32 devices in a mesh: dp: 2 (over x), ctx: 4 (over y, core), tensor: 4 (over z).
Axes of the slice: x: 2, y: 2, z: 4, core: 2. Of those that a mesh axis runs over, the one named last changes fastest.
Arguments:
- hidden_in: bfloat16 [4096, 2048], P(('dp', 'ctx')), may hold values from -6 to 6
- lengths: int32 [2], P('dp'), may hold values from 1537 to 2048, as said below
- attn_gain: float32 [2048], P(('dp', 'ctx')), may hold values from 0.5 to 1.5
- q_weight: float32 [2048, 2048], P(('dp', 'ctx'), 'tensor'), may hold values from -0.125 to 0.125
- gate_weight: float32 [2048, 2048], P(('dp', 'ctx'), 'tensor'), may hold values from -0.125 to 0.125
- k_weight: float32 [2048, 1024], P(('dp', 'ctx'), 'tensor'), may hold values from -0.125 to 0.125
- v_weight: float32 [2048, 1024], P(('dp', 'ctx'), 'tensor'), may hold values from -0.125 to 0.125
- q_gain: float32 [128], P(('dp', 'ctx')), may hold values from 0.5 to 1.5
- k_gain: float32 [128], P(('dp', 'ctx')), may hold values from 0.5 to 1.5
- o_weight: float32 [2048, 2048], P(('dp', 'ctx'), 'tensor'), may hold values from -3 to 3
- mlp_gain: float32 [2048], P(('dp', 'ctx')), may hold values from 0.5 to 1.5
- w_gate: float32 [2048, 6144], P(('dp', 'ctx'), 'tensor'), may hold values from -0.125 to 0.125
- w_up: float32 [2048, 6144], P(('dp', 'ctx'), 'tensor'), may hold values from -0.125 to 0.125
- w_down: float32 [2048, 6144], P(('dp', 'ctx'), 'tensor'), may hold values from -0.15625 to 0.15625
- out_grad: bfloat16 [4096, 2048], P(('dp', 'ctx')), may hold values from -6 to 6
Outputs:
- hidden_out: bfloat16 [4096, 2048], P(('dp', 'ctx'))
- grad_in: float32 [4096, 2048], P(('dp', 'ctx'))
- grad_attn_gain: float32 [2048], P(('dp', 'ctx'))
- grad_q_weight: float32 [2048, 2048], P(('dp', 'ctx'), 'tensor')
- grad_gate_weight: float32 [2048, 2048], P(('dp', 'ctx'), 'tensor')
- grad_k_weight: float32 [2048, 1024], P(('dp', 'ctx'), 'tensor')
- grad_v_weight: float32 [2048, 1024], P(('dp', 'ctx'), 'tensor')
- grad_q_gain: float32 [128], P(('dp', 'ctx'))
- grad_k_gain: float32 [128], P(('dp', 'ctx'))
- grad_o_weight: float32 [2048, 2048], P(('dp', 'ctx'), 'tensor')
- grad_mlp_gain: float32 [2048], P(('dp', 'ctx'))
- grad_w_gate: float32 [2048, 6144], P(('dp', 'ctx'), 'tensor')
- grad_w_up: float32 [2048, 6144], P(('dp', 'ctx'), 'tensor')
- grad_w_down: float32 [2048, 6144], P(('dp', 'ctx'), 'tensor')
The draws below stay inside these ranges and needn't reach their ends.
Inputs may be any that keep to these rules, and one draw needn't show every extreme that they name: `lengths`: positions at or past a sequence's length are padding; some sequence fills all 2048 of its slots.
All inputs are finite; a program needn't handle non-finite values.
Results may differ from the reference program's by a relative error of at most 0.015.
The reference program's roundings to bfloat16 on the way count: a program that leaves them out, or rounds other values in their place, can miss the bound.
Values may be sent and summed in bfloat16 or wider, within the bound.
No kernel may reach another device: no remote copies, remote signals or barrier semaphores. Data moves between devices by JAX's collectives and lax.ppermute only.
A program may use at most 256 MiB of HBM per device.

```python
import math
import jax
import jax.numpy as jnp
from jax import lax

D = 2048
HEADS = 16
KV_HEADS = 8
HD = 128
FF = 6144
SPAN = 512
SEQS = 2
BUCKET = 2048
TOKENS = 4096
Q_WIDTH = 2048
KV_WIDTH = 1024


def draw_lengths(key, part):
    first_key = jax.random.fold_in(key, 11)
    second_key = jax.random.fold_in(key, 23)
    spread = jax.random.randint(first_key, (SEQS,), 0, SPAN)
    extra = spread * spread // SPAN * spread // SPAN
    base_len = 3 * SPAN + 1 + extra
    chosen = jax.random.randint(second_key, (), 0, SEQS)
    return jnp.where(jnp.arange(SEQS) == chosen, BUCKET, base_len).astype(jnp.int32)


def level_of(stream_key, dims, pieces, low, largest):
    gain, own = 1.0, jax.random.fold_in(stream_key, 6)
    for dim, blocks in pieces:
        steps = jnp.exp(jax.random.uniform(jax.random.fold_in(own, dim), (blocks,), jnp.float32, low / len(pieces), largest / len(pieces)))
        gain = gain * jnp.repeat(steps, dims[dim] // blocks).reshape([-1 if axis == dim else 1 for axis in range(len(dims))])
    return gain


def centred(key, dims, scale, limit, split=(), kind=jnp.bfloat16):
    values = scale * jax.random.normal(key, dims, jnp.float32)
    if split:
        values = values * level_of(key, dims, split, -0.22, 0.18)
    return jnp.clip(values, -limit, limit).astype(kind)


def setup_inputs(seed: int = 0) -> dict:
    keys = jax.random.split(jax.random.key(seed), 16)
    hidden_in = centred(keys[0], (TOKENS, D), 1.0, 6.0, ((0, 8),))
    lengths = draw_lengths(jax.random.fold_in(keys[15], 71), 0)
    attn_gain = jnp.clip(1.0 + 0.1 * jax.random.normal(keys[2], (D,), jnp.float32), 0.5, 1.5)
    q_weight = centred(keys[3], (D, Q_WIDTH), D ** -0.5, 0.125, ((0, 8), (1, 4)), jnp.float32)
    gate_weight = centred(keys[4], (D, Q_WIDTH), D ** -0.5, 0.125, ((0, 8), (1, 4)), jnp.float32)
    k_weight = centred(keys[5], (D, KV_WIDTH), D ** -0.5, 0.125, ((0, 8), (1, 4)), jnp.float32)
    v_weight = centred(keys[6], (D, KV_WIDTH), D ** -0.5, 0.125, ((0, 8), (1, 4)), jnp.float32)
    q_gain = jnp.clip(1.0 + 0.1 * jax.random.normal(keys[7], (HD,), jnp.float32), 0.5, 1.5)
    k_gain = jnp.clip(1.0 + 0.1 * jax.random.normal(keys[8], (HD,), jnp.float32), 0.5, 1.5)
    o_weight = centred(keys[9], (D, Q_WIDTH), 4 ** -0.5, 3.0, ((0, 8), (1, 4)), jnp.float32)
    mlp_gain = jnp.clip(1.0 + 0.1 * jax.random.normal(keys[10], (D,), jnp.float32), 0.5, 1.5)
    w_gate = centred(keys[11], (D, FF), D ** -0.5, 0.125, ((0, 8), (1, 4)), jnp.float32)
    w_up = centred(keys[12], (D, FF), D ** -0.5, 0.125, ((0, 8), (1, 4)), jnp.float32)
    w_down = centred(keys[13], (D, FF), (FF // 4) ** -0.5, 0.15625, ((0, 8), (1, 4)), jnp.float32)
    out_grad = centred(keys[14], (TOKENS, D), 1.0, 6.0, ((0, 8),))
    return {"hidden_in": hidden_in, "lengths": lengths, "attn_gain": attn_gain, "q_weight": q_weight, "gate_weight": gate_weight, "k_weight": k_weight, "v_weight": v_weight, "q_gain": q_gain, "k_gain": k_gain, "o_weight": o_weight, "mlp_gain": mlp_gain, "w_gate": w_gate, "w_up": w_up, "w_down": w_down, "out_grad": out_grad}


EPSILON = 1e-06
ROPE_BASE = 1000000.0
MASKED = -1e+30

@jax.custom_vjp
def low(v):
    return lax.optimization_barrier(v.astype(jnp.bfloat16)).astype(jnp.float32)

@jax.custom_vjp
def low_back(v):
    return v

def low_keep(v):
    return (low(v), None)

def low_pass(kept, grad):
    return (grad,)

def back_keep(v):
    return (v, None)

def back_low(kept, grad):
    return (low(grad),)
low.defvjp(low_keep, low_pass)
low_back.defvjp(back_keep, back_low)

def matmul(operand, matrix):
    return jnp.dot(operand, matrix, precision=lax.Precision.HIGHEST, preferred_element_type=jnp.float32)

def rms_scale(vectors, gain_vec):
    return vectors * lax.rsqrt(lax.optimization_barrier(jnp.mean(vectors * vectors, axis=-1, keepdims=True)) + EPSILON) * gain_vec

def angles(positions, dim_size):
    freq_steps = jnp.arange(dim_size // 2, dtype=jnp.float32) * (2.0 / dim_size)
    inverse = jnp.exp(-math.log(ROPE_BASE) * freq_steps)
    turned = positions[:, None] * inverse[None, :]
    return (jnp.cos(turned)[:, None, :], jnp.sin(turned)[:, None, :])

def rotate(vectors, cosine, sine_table):
    half_width = vectors.shape[-1] // 2
    first_half = vectors[..., :half_width]
    second = vectors[..., half_width:]
    return jnp.concatenate([first_half * cosine - second * sine_table, second * cosine + first_half * sine_table], axis=-1)

def layer_forward(stream, parameters, length):
    attn_gain, q_weight, gate_weight, k_weight, v_weight, q_gain, k_gain, o_weight, mlp_gain, w_gate, w_up, w_down = tuple((low(param) for param in parameters))
    row_count = stream.shape[0]
    places = jnp.arange(row_count, dtype=jnp.int32)
    live_rows = (places < length).astype(jnp.float32)[:, None]
    cosine, sine_table = angles(places.astype(jnp.float32), HD)
    normed = low(rms_scale(stream, attn_gain))
    queries = low_back(matmul(normed, q_weight)).reshape(row_count, HEADS, HD)
    gates = low_back(matmul(normed, gate_weight))
    key_proj = low_back(matmul(normed, k_weight)).reshape(row_count, KV_HEADS, HD)
    values = low(low_back(matmul(normed, v_weight))).reshape(row_count, KV_HEADS, HD)
    query_rot = low(rotate(rms_scale(queries, q_gain), cosine, sine_table))
    key_rot = low(rotate(rms_scale(key_proj, k_gain), cosine, sine_table))
    allowed = (places[None, :] <= places[:, None]) & (places[None, :] < length)
    score_scale = HD ** (-0.5)
    group_size = HEADS // KV_HEADS

    def attend(inputs):
        query_head, key_head, value_head = inputs
        scores = low_back(matmul(query_head, key_head.T) * score_scale)
        scores = jnp.where(allowed, scores, MASKED)
        row_max = lax.optimization_barrier(jnp.max(scores, axis=-1, keepdims=True))
        exp_terms = jnp.exp(scores - row_max)
        prob_table = exp_terms / lax.optimization_barrier(jnp.sum(exp_terms, axis=-1, keepdims=True))
        return low_back(matmul(low(prob_table), value_head))
    per_head = lax.map(jax.checkpoint(attend), (query_rot.transpose(1, 0, 2), jnp.repeat(key_rot, group_size, axis=1).transpose(1, 0, 2), jnp.repeat(values, group_size, axis=1).transpose(1, 0, 2)))
    mixed_heads = per_head.transpose(1, 0, 2).reshape(row_count, Q_WIDTH)
    gated_heads = low(mixed_heads * jax.nn.sigmoid(gates))
    attn_out = low_back(matmul(gated_heads, o_weight.T) * live_rows)
    middle = stream + attn_out
    normed_two = low(rms_scale(middle, mlp_gain))
    gate_in = low_back(matmul(normed_two, w_gate))
    up_in = low_back(matmul(normed_two, w_up))
    hidden = low(jax.nn.silu(gate_in) * up_in)
    return middle + matmul(hidden, w_down.T) * live_rows

def reference(hidden_in, lengths, attn_gain, q_weight, gate_weight, k_weight, v_weight, q_gain, k_gain, o_weight, mlp_gain, w_gate, w_up, w_down, out_grad):
    parameters = (attn_gain, q_weight, gate_weight, k_weight, v_weight, q_gain, k_gain, o_weight, mlp_gain, w_gate, w_up, w_down)
    streams = hidden_in.reshape(SEQS, BUCKET, D).astype(jnp.float32)
    cotangents = out_grad.reshape(SEQS, BUCKET, D).astype(jnp.float32)

    def one_sequence(running, inputs):
        stream, cotangent, length = inputs

        def apply_layer(stream_in, params_in):
            return layer_forward(stream_in, params_in, length)
        result, pullback = jax.vjp(apply_layer, stream, parameters)
        grad_stream, grad_params = pullback(cotangent)
        running = jax.tree.map(lambda before, addend: before + addend, running, grad_params)
        return (running, (result.astype(jnp.bfloat16), grad_stream))
    initial = jax.tree.map(jnp.zeros_like, parameters)
    totals, (outputs, grad_rows) = lax.scan(one_sequence, initial, (streams, cotangents, lengths))
    return (outputs.reshape(TOKENS, D), grad_rows.reshape(TOKENS, D), totals[0], totals[1], totals[2], totals[3], totals[4], totals[5], totals[6], totals[7], totals[8], totals[9], totals[10], totals[11])
```

```python
import math

import jax
import jax.numpy as jnp
from jax import lax
from jax.sharding import PartitionSpec as P

EPSILON = 1e-06
ROPE_BASE = 1000000.0
MASKED = -1e30
CONTRACT_ROWS = (((0,), (0,)), ((), ()))
CONTRACT_COLS = (((1,), (1,)), ((), ()))
F32 = jnp.float32
BF16 = jnp.bfloat16


def angles(positions, dim_size):
    freq_steps = jnp.arange(dim_size // 2, dtype=F32) * (2.0 / dim_size)
    inverse = jnp.exp(-math.log(ROPE_BASE) * freq_steps)
    turned = positions[:, None] * inverse[None, :]
    return (jnp.cos(turned)[:, None, :], jnp.sin(turned)[:, None, :])


def rotate(vectors, cosine, sine_table):
    half_width = vectors.shape[-1] // 2
    first_half = vectors[..., :half_width]
    second = vectors[..., half_width:]
    return jnp.concatenate(
        [first_half * cosine - second * sine_table, second * cosine + first_half * sine_table],
        axis=-1,
    )


def rotate_back(gradient, cosine, sine_table):
    return rotate(gradient, cosine, -sine_table)


def norm_back(gradient, unit_vals, inverse, gain_vec):
    scaled = gradient * gain_vec
    return inverse * (scaled - unit_vals * jnp.mean(scaled * unit_vals, axis=-1, keepdims=True))


def project(operand, matrix):
    return jnp.dot(operand, matrix, preferred_element_type=F32)


def row_contract(first_op, second_op):
    return lax.dot_general(first_op, second_op, CONTRACT_ROWS, preferred_element_type=F32)


def col_contract(first_op, second_op):
    return lax.dot_general(first_op, second_op, CONTRACT_COLS, preferred_element_type=F32)


class Links:
    def __init__(self, sizes):
        self.dp, self.ctx, self.tensor = sizes["dp"], sizes["ctx"], sizes["tensor"]
        self.half = self.dp * self.ctx // 2
        ctx_bits = int(math.log2(self.ctx // 2))
        dp_bits = int(math.log2(self.dp))
        self.bits = [("ctx", 2 << i) for i in range(ctx_bits)] + [("dp", 1 << i) for i in range(dp_bits)]

    def swap(self, value, axis, mask):
        count = self.dp if axis == "dp" else self.ctx
        return lax.ppermute(value, axis, [(i, i ^ mask) for i in range(count)])

    def order(self, turn):
        places = list(range(len(self.bits)))
        return places if turn else places[::-1]

    def gather(self, block, turn):
        blocks = {0: block}
        for place in self.order(turn):
            axis, mask = self.bits[place]
            for q in list(blocks):
                blocks[q | (1 << place)] = self.swap(blocks[q], axis, mask)
        own = jnp.concatenate([blocks[q] for q in range(self.half)], axis=0)
        return own, self.swap(own, "ctx", 1)

    def reduce(self, own, other, turn):
        arrived = self.swap(other, "ctx", 1)
        total = own.astype(F32) + arrived.astype(F32)
        rows = total.shape[0] // self.half
        pieces = {q: total[q * rows : (q + 1) * rows] for q in range(self.half)}
        for place in self.order(turn):
            axis, mask = self.bits[place]
            bit = 1 << place
            kept = [q for q in pieces if not q & bit]
            sent = jnp.concatenate([pieces[q | bit].astype(BF16) for q in kept], axis=0)
            back = self.swap(sent, axis, mask).astype(F32)
            pieces = {q: pieces[q] + back[i * rows : (i + 1) * rows] for i, q in enumerate(kept)}
        return pieces[0]

    def place_of(self, position, dp_index, ctx_index):
        dp_far, ctx_far = position // self.ctx, position % self.ctx
        dp_far, ctx_far = dp_far ^ dp_index, ctx_far ^ ctx_index
        return (ctx_far % 2) * self.half + dp_far * (self.ctx // 2) + ctx_far // 2

    def owner_of(self, position, dp_index, ctx_index):
        h, q = position // self.half, position % self.half
        dp_far, ctx_far = q // (self.ctx // 2), (q % (self.ctx // 2)) * 2 + h
        return (dp_index ^ dp_far) * self.ctx + (ctx_index ^ ctx_far)

    def columns_in(self, value, dp_index, ctx_index):
        count = self.half * 2
        width = value.shape[1] // count
        return jnp.concatenate(
            [
                lax.dynamic_slice_in_dim(value, self.owner_of(p, dp_index, ctx_index) * width, width, axis=1)
                for p in range(count)
            ],
            axis=1,
        )

    def columns_out(self, value, dp_index, ctx_index):
        count = self.half * 2
        width = value.shape[1] // count
        return jnp.concatenate(
            [
                lax.dynamic_slice_in_dim(value, self.place_of(p, dp_index, ctx_index) * width, width, axis=1)
                for p in range(count)
            ],
            axis=1,
        )

    def tensor_sum(self, chunks):
        if self.tensor != 4:
            return [lax.psum(c.astype(F32), "tensor").astype(BF16) for c in chunks]
        place = lax.axis_index("tensor")
        end = (place == 0) | (place == 3)
        first = [lax.ppermute(c, "tensor", [(0, 1), (3, 2)]) for c in chunks]
        pairs = [(c.astype(F32) + a.astype(F32)).astype(BF16) for c, a in zip(chunks, first)]
        second = [lax.ppermute(c, "tensor", [(1, 2), (2, 1)]) for c in pairs]
        whole = [(c.astype(F32) + a.astype(F32)).astype(BF16) for c, a in zip(pairs, second)]
        third = [lax.ppermute(c, "tensor", [(1, 0), (2, 3)]) for c in whole]
        return [jnp.where(end, a, c) for c, a in zip(whole, third)]

    def token_sum(self, halves):
        rows = halves[0].shape[0] // 2
        chunks = [h[i * rows : (i + 1) * rows].astype(BF16) for i in range(2) for h in halves]
        done = self.tensor_sum(chunks)
        return jnp.concatenate(
            [jnp.concatenate(done[0:2], axis=1), jnp.concatenate(done[2:4], axis=1)], axis=0
        )


def masked_scores(query_grouped, keys_all, allowed, score_scale):
    scores = (
        jnp.einsum("qkgd,nkd->kgqn", query_grouped, keys_all, preferred_element_type=F32)
        * score_scale
    )
    return jnp.where(allowed[None, None], scores, MASKED)


def per_device(
    links,
    hidden_in,
    lengths,
    attn_gain,
    q_weight,
    gate_weight,
    k_weight,
    v_weight,
    q_gain,
    k_gain,
    o_weight,
    mlp_gain,
    w_gate,
    w_up,
    w_down,
    out_grad,
):
    dp_index, ctx_index = lax.axis_index("dp"), lax.axis_index("ctx")
    q_cols, k_cols, ff_cols = q_weight.shape[1], k_weight.shape[1], w_down.shape[1]
    ff_half = ff_cols // 2
    low = lambda *mats: jnp.concatenate([m.astype(BF16) for m in mats], axis=1)

    small = jnp.concatenate(
        [attn_gain.astype(BF16), mlp_gain.astype(BF16), q_gain.astype(BF16), k_gain.astype(BF16)]
    )
    gains = lax.all_gather(small, ("dp", "ctx"), axis=0, tiled=False)
    shard, head_shard = attn_gain.shape[0], q_gain.shape[0]
    attn_scale = links.columns_in(gains[:, :shard].reshape(1, -1), dp_index, ctx_index).astype(F32)
    mlp_scale = links.columns_in(
        gains[:, shard : 2 * shard].reshape(1, -1), dp_index, ctx_index
    ).astype(F32)
    query_scale = gains[:, 2 * shard : 2 * shard + head_shard].reshape(-1).astype(F32)
    key_scale = gains[:, 2 * shard + head_shard :].reshape(-1).astype(F32)

    qk_mat = links.gather(low(q_weight, k_weight), 0)
    gv_mat = links.gather(low(gate_weight, v_weight), 1)
    out_mat = links.gather(low(o_weight), 0)
    feed_gate = links.gather(low(w_gate), 0)
    feed_up = links.gather(low(w_up), 1)
    feed_down = [
        links.gather(low(w_down[:, :ff_half]), 0),
        links.gather(low(w_down[:, ff_half:]), 1),
    ]

    span_len, width = hidden_in.shape
    mid = width // 2
    head_dim = query_scale.shape[0]
    local_heads = q_cols // head_dim
    local_kv = k_cols // head_dim
    group_size = local_heads // local_kv
    positions = ctx_index * span_len + jnp.arange(span_len, dtype=jnp.int32)
    length = lengths[0]
    live_rows = (positions < length).astype(F32)[:, None]
    cosine, sine_table = angles(positions.astype(F32), head_dim)
    stream = links.columns_in(hidden_in, dp_index, ctx_index).astype(F32)
    grad_out = links.columns_in(out_grad, dp_index, ctx_index).astype(F32)
    inverse_one = lax.rsqrt(jnp.mean(stream * stream, axis=-1, keepdims=True) + EPSILON)
    unit_one = stream * inverse_one
    normed = (unit_one * attn_scale).astype(BF16)
    both = lambda value, mats: project(value[:, :mid], mats[0]) + project(value[:, mid:], mats[1])
    qk = both(normed, qk_mat)
    gv = both(normed, gv_mat)
    queries = qk[:, :q_cols].reshape(span_len, local_heads, head_dim)
    key_proj = qk[:, q_cols:].reshape(span_len, local_kv, head_dim)
    gates = gv[:, :q_cols]
    value_proj = gv[:, q_cols:].astype(BF16).reshape(span_len, local_kv, head_dim)
    query_inv = lax.rsqrt(jnp.mean(queries * queries, axis=-1, keepdims=True) + EPSILON)
    query_unit = queries * query_inv
    query_rot = rotate(query_unit * query_scale, cosine, sine_table).astype(BF16)
    key_inv = lax.rsqrt(jnp.mean(key_proj * key_proj, axis=-1, keepdims=True) + EPSILON)
    key_unit = key_proj * key_inv
    key_rot = rotate(key_unit * key_scale, cosine, sine_table).astype(BF16)

    both_kv = jnp.concatenate([key_rot, value_proj], axis=1)
    held = [both_kv]
    places = [0]
    mask = links.ctx // 2
    while mask:
        held = held + [links.swap(b, "ctx", mask) for b in held]
        places = places + [p ^ mask for p in places]
        mask //= 2
    kv_all = jnp.concatenate(held, axis=0)
    keys_all, values_all = kv_all[:, :local_kv], kv_all[:, local_kv:]
    key_places = jnp.concatenate(
        [(ctx_index ^ p) * span_len + jnp.arange(span_len, dtype=jnp.int32) for p in places]
    )
    allowed = (key_places[None, :] <= positions[:, None]) & (key_places[None, :] < length)
    score_scale = head_dim ** (-0.5)
    query_grouped = query_rot.reshape(span_len, local_kv, group_size, head_dim)
    scores = masked_scores(query_grouped, keys_all, allowed, score_scale)
    row_max = jnp.max(scores, axis=-1, keepdims=True)
    exp_terms = jnp.exp(scores - row_max)
    row_sum = jnp.sum(exp_terms, axis=-1, keepdims=True)
    prob_low = (exp_terms / row_sum).astype(BF16)
    mixed_heads = jnp.einsum(
        "kgqn,nkd->qkgd", prob_low, values_all, preferred_element_type=F32
    ).reshape(span_len, local_heads * head_dim)
    gate_sig = jax.nn.sigmoid(gates)
    gated_heads = (mixed_heads * gate_sig).astype(BF16)
    attn_out = links.token_sum([col_contract(gated_heads, m) for m in out_mat]).astype(F32)
    middle = stream + attn_out * live_rows
    inverse_two = lax.rsqrt(jnp.mean(middle * middle, axis=-1, keepdims=True) + EPSILON)
    unit_two = middle * inverse_two
    normed_two = (unit_two * mlp_scale).astype(BF16)
    gate_in = both(normed_two, feed_gate)
    up_in = both(normed_two, feed_up)
    hidden = (jax.nn.silu(gate_in) * up_in).astype(BF16)
    down_parts = [
        sum(
            col_contract(hidden[:, s * ff_half : (s + 1) * ff_half], feed_down[s][h])
            for s in range(2)
        )
        for h in range(2)
    ]
    down_grad = (grad_out * live_rows).astype(BF16)
    grad_hidden = jnp.concatenate([both(down_grad, feed_down[s]) for s in range(2)], axis=1)
    sig_ff = jax.nn.sigmoid(gate_in)
    grad_gate_in = (grad_hidden * up_in * sig_ff * (1.0 + gate_in * (1.0 - sig_ff))).astype(BF16)
    grad_up_in = (grad_hidden * (gate_in * sig_ff)).astype(BF16)

    def weight_grad(rows_of, cols_of, turn):
        other = row_contract(rows_of[:, mid:], cols_of).astype(BF16)
        own = row_contract(rows_of[:, :mid], cols_of).astype(BF16)
        return links.reduce(own, other, turn)

    back_parts = [
        col_contract(grad_gate_in, feed_gate[h]) + col_contract(grad_up_in, feed_up[h])
        for h in range(2)
    ]
    normed_two_grad = links.token_sum(back_parts).astype(F32)
    down_total = links.token_sum(down_parts).astype(F32)
    hidden_out = links.columns_out(
        (middle + down_total * live_rows).astype(BF16), dp_index, ctx_index
    )
    grad_feed_down = jnp.concatenate(
        [
            weight_grad(down_grad, hidden[:, s * ff_half : (s + 1) * ff_half], s)
            for s in range(2)
        ],
        axis=1,
    )
    grad_feed_gate = weight_grad(normed_two, grad_gate_in, 0)
    grad_feed_up = weight_grad(normed_two, grad_up_in, 1)

    grad_mlp_gain = jnp.sum(normed_two_grad * unit_two, axis=0)
    grad_middle = grad_out + norm_back(normed_two_grad, unit_two, inverse_two, mlp_scale)
    attn_grad = (grad_middle * live_rows).astype(BF16)
    grad_out_mat = weight_grad(attn_grad, gated_heads, 0)
    grad_gated = both(attn_grad, out_mat)
    grad_mixed = (grad_gated * gate_sig).astype(BF16)
    grad_gates = (grad_gated * mixed_heads * gate_sig * (1.0 - gate_sig)).astype(BF16)
    grad_mixed_grouped = grad_mixed.reshape(span_len, local_kv, group_size, head_dim)
    prob_table = (
        jnp.exp(masked_scores(query_grouped, keys_all, allowed, score_scale) - row_max) / row_sum
    )
    grad_probs = jnp.einsum(
        "qkgd,nkd->kgqn", grad_mixed_grouped, values_all, preferred_element_type=F32
    )
    row_dot = jnp.sum(grad_probs * prob_table, axis=-1, keepdims=True)
    grad_scores = (prob_table * (grad_probs - row_dot)).astype(BF16)
    grad_query_rot = (
        jnp.einsum("kgqn,nkd->qkgd", grad_scores, keys_all, preferred_element_type=F32).reshape(
            span_len, local_heads, head_dim
        )
        * score_scale
    )
    grad_key_all = (
        jnp.einsum("kgqn,qkgd->nkd", grad_scores, query_grouped, preferred_element_type=F32)
        * score_scale
    )
    grad_value_all = jnp.einsum(
        "kgqn,qkgd->nkd", prob_low, grad_mixed_grouped, preferred_element_type=F32
    )
    grad_kv = jnp.concatenate([grad_key_all, grad_value_all], axis=1)
    parts = [grad_kv[i * span_len : (i + 1) * span_len] for i in range(links.ctx)]
    mask = 1
    while len(parts) > 1:
        far = [i for i, p in enumerate(places) if p & mask]
        near = [i for i, p in enumerate(places) if not p & mask]
        sent = jnp.concatenate([parts[i].astype(BF16) for i in far], axis=0)
        back = links.swap(sent, "ctx", mask).astype(F32)
        by_place = {places[i] ^ mask: back[n * span_len : (n + 1) * span_len] for n, i in enumerate(far)}
        parts = [parts[i] + by_place[places[i]] for i in near]
        places = [places[i] for i in near]
        mask *= 2
    grad_key_own, grad_value_own = parts[0][:, :local_kv], parts[0][:, local_kv:]

    query_pre_grad = rotate_back(grad_query_rot, cosine, sine_table)
    query_gain_part = jnp.sum(query_pre_grad * query_unit, axis=(0, 1))
    grad_queries = (
        norm_back(query_pre_grad, query_unit, query_inv, query_scale)
        .astype(BF16)
        .reshape(span_len, local_heads * head_dim)
    )
    key_pre_grad = rotate_back(grad_key_own, cosine, sine_table)
    key_gain_part = jnp.sum(key_pre_grad * key_unit, axis=(0, 1))
    grad_keys = (
        norm_back(key_pre_grad, key_unit, key_inv, key_scale)
        .astype(BF16)
        .reshape(span_len, local_kv * head_dim)
    )
    grad_values = grad_value_own.astype(BF16).reshape(span_len, local_kv * head_dim)
    grad_qk = jnp.concatenate([grad_queries, grad_keys], axis=1)
    grad_gv = jnp.concatenate([grad_gates, grad_values], axis=1)
    normed_parts = [
        col_contract(grad_qk, qk_mat[h]) + col_contract(grad_gv, gv_mat[h]) for h in range(2)
    ]
    normed_grad = links.token_sum(normed_parts).astype(F32)
    qk_weight_grad = weight_grad(normed, grad_qk, 0)
    gv_weight_grad = weight_grad(normed, grad_gv, 1)
    grad_attn_gain = jnp.sum(normed_grad * unit_one, axis=0)
    grad_in = links.columns_out(
        grad_middle + norm_back(normed_grad, unit_one, inverse_one, attn_scale), dp_index, ctx_index
    )
    gain_cols = links.columns_out(
        jnp.stack([grad_attn_gain, grad_mlp_gain]) * (1.0 / links.tensor), dp_index, ctx_index
    )
    packed = jnp.concatenate([gain_cols[0], gain_cols[1], query_gain_part, key_gain_part])
    packed = lax.psum(packed, ("dp", "ctx", "tensor"))
    rank = dp_index * links.ctx + ctx_index
    pick = lambda start, size: lax.dynamic_slice_in_dim(packed, start + rank * size, size)
    return (
        hidden_out,
        grad_in,
        pick(0, shard),
        qk_weight_grad[:, :q_cols],
        gv_weight_grad[:, :q_cols],
        qk_weight_grad[:, q_cols:],
        gv_weight_grad[:, q_cols:],
        pick(2 * width, head_shard),
        pick(2 * width + head_dim, head_shard),
        grad_out_mat,
        pick(width, shard),
        grad_feed_gate,
        grad_feed_up,
        grad_feed_down,
    )


def solution(mesh):
    links = Links(dict(mesh.shape))
    rows = P(("dp", "ctx"))
    plain = P(("dp", "ctx"), None)
    split = P(("dp", "ctx"), "tensor")

    def step(*arrays):
        return per_device(links, *arrays)

    return jax.shard_map(
        step,
        mesh=mesh,
        in_specs=(plain, P("dp"), rows, split, split, split, split, rows, rows, split, rows, split, split, split, plain),
        out_specs=(plain, plain, rows, split, split, split, split, rows, rows, split, rows, split, split, split),
        check_vma=False,
    )
```

```python
import functools
import math

import jax
import jax.numpy as jnp
from jax import lax
from jax.experimental import pallas as pl
from jax.experimental.pallas import tpu as pltpu
from jax.sharding import PartitionSpec as P

EPSILON = 1e-06
ROPE_BASE = 1000000.0
CONTRACT_ROWS = (((0,), (0,)), ((), ()))
CONTRACT_COLS = (((1,), (1,)), ((), ()))
F32 = jnp.float32
BF16 = jnp.bfloat16
VMEM_BYTES = 56 * 1024 * 1024


def project(operand, matrix):
    return jnp.dot(operand, matrix, preferred_element_type=F32)


def row_contract(first_op, second_op):
    return lax.dot_general(first_op, second_op, CONTRACT_ROWS, preferred_element_type=F32)


def col_contract(first_op, second_op):
    return lax.dot_general(first_op, second_op, CONTRACT_COLS, preferred_element_type=F32)


def sigmoid(value):
    return 1.0 / (1.0 + jnp.exp(-value))


def cost(flops, moved, exps=0):
    return pl.CostEstimate(flops=int(flops), bytes_accessed=int(moved), transcendentals=int(exps))


def params(**kwargs):
    return pltpu.CompilerParams(vmem_limit_bytes=VMEM_BYTES, **kwargs)


class Links:
    def __init__(self, sizes):
        self.dp, self.ctx, self.tensor = sizes["dp"], sizes["ctx"], sizes["tensor"]
        self.half = self.dp * self.ctx // 2
        ctx_bits = int(math.log2(self.ctx // 2))
        dp_bits = int(math.log2(self.dp))
        self.bits = [("ctx", 2 << i) for i in range(ctx_bits)] + [("dp", 1 << i) for i in range(dp_bits)]
        self.masks = [1 << i for i in range(int(math.log2(self.tensor)))]
        self.turns = [0]
        for mask in reversed(self.masks):
            self.turns = self.turns + [j ^ mask for j in self.turns]

    def swap(self, value, axis, mask):
        count = {"dp": self.dp, "ctx": self.ctx, "tensor": self.tensor}[axis]
        return lax.ppermute(value, axis, [(i, i ^ mask) for i in range(count)])

    def order(self, turn):
        places = list(range(len(self.bits)))
        return places if turn else places[::-1]

    def gather(self, block):
        mid = block.shape[1] // 2
        single = {1 << p: self.swap(block, *self.bits[p]) for p in self.order(0)}
        left = {q: b[:, :mid] for q, b in single.items()}
        right = {q: b[:, mid:] for q, b in single.items()}
        for side, places in ((left, self.order(0)), (right, self.order(1))):
            for q in range(self.half):
                if q and q not in single:
                    self.reach(side, q, places)
        rows = [block]
        for q in range(1, self.half):
            rows.append(single[q] if q in single else jnp.concatenate([left[q], right[q]], axis=1))
        own = jnp.concatenate(rows, axis=0)
        return own, self.swap(own, "ctx", 1)

    def reach(self, side, q, places):
        if q not in side:
            last = [p for p in places if q & (1 << p)][-1]
            self.reach(side, q ^ (1 << last), places)
            side[q] = self.swap(side[q ^ (1 << last)], *self.bits[last])

    def reduce(self, own, other):
        arrived = self.swap(other, "ctx", 1)
        total = own.astype(F32) + arrived.astype(F32)
        rows, mid = total.shape[0] // self.half, total.shape[1] // 2
        done = []
        for turn in range(2):
            cols = slice(turn * mid, (turn + 1) * mid)
            pieces = {q: total[q * rows : (q + 1) * rows, cols] for q in range(self.half)}
            for place in self.order(turn):
                bit = 1 << place
                kept = [q for q in pieces if not q & bit]
                sent = jnp.concatenate([pieces[q | bit].astype(BF16) for q in kept], axis=0)
                back = self.swap(sent, *self.bits[place]).astype(F32)
                pieces = {q: pieces[q] + back[i * rows : (i + 1) * rows] for i, q in enumerate(kept)}
            done.append(pieces[0])
        return jnp.concatenate(done, axis=1)

    def small_gather(self, row):
        rows = {0: row}
        for place in self.order(0):
            for q in list(rows):
                rows[q | (1 << place)] = None
            grown = jnp.concatenate([rows[q] for q in rows if rows[q] is not None], axis=0)
            came = self.swap(grown, *self.bits[place])
            old = [q for q in rows if rows[q] is not None]
            for i, q in enumerate(old):
                rows[q | (1 << place)] = came[i : i + 1]
        own = jnp.concatenate([rows[q] for q in range(self.half)], axis=0)
        return jnp.concatenate([own, self.swap(own, "ctx", 1)], axis=0)

    def owner_of(self, position, dp_index, ctx_index):
        h, q = position // self.half, position % self.half
        dp_far, ctx_far = q // (self.ctx // 2), (q % (self.ctx // 2)) * 2 + h
        return (dp_index ^ dp_far) * self.ctx + (ctx_index ^ ctx_far)

    def scatter_rows(self, part):
        kept, rows = part, part.shape[0]
        for mask in self.masks:
            rows //= 2
            came = self.swap(kept[rows:].astype(BF16), "tensor", mask)
            kept = kept[:rows].astype(F32) + came.astype(F32)
        return kept

    def gather_rows(self, shard):
        for mask in reversed(self.masks):
            shard = jnp.concatenate([shard, self.swap(shard, "tensor", mask)], axis=0)
        return shard

    def add_all(self, value):
        for mask in self.masks:
            value = value + self.swap(value, "tensor", mask)
        value = value + self.swap(value, "ctx", 1)
        for axis, mask in self.bits:
            value = value + self.swap(value, axis, mask)
        return value


def still(scalars, count, parts):
    owners = scalars[parts : parts + count]
    return owners, lax.dynamic_update_slice(scalars, jnp.arange(count, dtype=scalars.dtype), (parts,))


def columns(value, owners):
    count = owners.shape[0]
    blocks = value.reshape(value.shape[0], count, value.shape[1] // count)
    return jnp.take(blocks, owners, axis=1).reshape(value.shape)


def column_place(scalars, parts, p, size):
    if size % 128:
        return pl.ds(p * size, size)
    return pl.ds(pl.multiple_of(scalars[parts + p] * size, size), size)


def enter_kernel(count, parts, span, scalars, x_ref, g_ref, gain_ref, x_out, g_out, m_out, n_out):
    step = pl.program_id(0)
    rows, width = x_ref.shape
    size = width // count
    x_cols, g_cols = [], []
    for p in range(count):
        place = column_place(scalars, parts, p, size)
        x_cols.append(x_ref[:, place])
        g_cols.append(g_ref[:, place])
    x = jnp.concatenate(x_cols, axis=1)
    g = jnp.concatenate(g_cols, axis=1)
    x_out[...] = x
    g_out[...] = g
    spot = scalars[parts + count] + scalars[step] * rows + lax.broadcasted_iota(jnp.int32, (rows, 1), 0)
    live = spot < scalars[parts + count + 1]
    m_out[...] = jnp.where(live, g.astype(F32), 0.0).astype(BF16)
    wide = x.astype(F32)
    inverse = lax.rsqrt(jnp.mean(wide * wide, axis=-1, keepdims=True) + EPSILON)
    n_out[...] = (wide * inverse * gain_ref[...]).astype(BF16)


def enter(scalars, count, parts, span, hidden_in, out_grad, gain):
    rows, width = span // parts, hidden_in.shape[1]
    if width // count % 128:
        owners, scalars = still(scalars, count, parts)
        hidden_in, out_grad = columns(hidden_in, owners), columns(out_grad, owners)
    moved = pl.BlockSpec((rows, width), lambda i, s: (s[i], 0))
    plain = pl.BlockSpec((rows, width), lambda i, s: (i, 0))
    shape = jax.ShapeDtypeStruct((span, width), BF16)
    return pl.pallas_call(
        functools.partial(enter_kernel, count, parts, span),
        out_shape=(shape,) * 4,
        grid_spec=pltpu.PrefetchScalarGridSpec(
            num_scalar_prefetch=1,
            grid=(parts,),
            in_specs=[moved, moved, pl.BlockSpec((1, width), lambda i, s: (0, 0))],
            out_specs=(plain,) * 4,
        ),
        compiler_params=params(),
        cost_estimate=cost(10 * span * width, 12 * span * width),
        name="enter",
    )(scalars, hidden_in, out_grad, gain)


def leave_kernel(count, parts, scalars, in_ref, out_ref):
    size = in_ref.shape[1] // count
    for p in range(count):
        place = column_place(scalars, parts, p, size)
        out_ref[:, place] = in_ref[:, p * size : (p + 1) * size].astype(out_ref.dtype)


def leave(scalars, count, parts, value, dtype):
    span, width = value.shape
    rows = span // parts
    if width // count % 128:
        owners, scalars = still(scalars, count, parts)
        value = columns(value, jnp.argsort(owners))
    return pl.pallas_call(
        functools.partial(leave_kernel, count, parts),
        out_shape=jax.ShapeDtypeStruct((span, width), dtype),
        grid_spec=pltpu.PrefetchScalarGridSpec(
            num_scalar_prefetch=1,
            grid=(parts,),
            in_specs=[pl.BlockSpec((rows, width), lambda i, s: (i, 0))],
            out_specs=pl.BlockSpec((rows, width), lambda i, s: (s[i], 0)),
        ),
        compiler_params=params(),
        cost_estimate=cost(0, 6 * span * width),
        name="leave",
    )(scalars, value)


def unit_of(value):
    inverse = lax.rsqrt(jnp.mean(value * value, axis=-1, keepdims=True) + EPSILON)
    return value * inverse, inverse


def turn(value, cos_ref, sin_ref, sign):
    half = value.shape[-1] // 2
    return value * cos_ref[...] + sign * pltpu.roll(value, half, 1) * sin_ref[...]


def prepare_kernel(heads, kv_heads, head_dim, p_ref, cos_ref, sin_ref, qg_ref, kg_ref, q_out, kv_out):
    group = heads // kv_heads
    q_cols, k_cols = heads * head_dim, kv_heads * head_dim
    for h in range(heads + kv_heads):
        unit, _ = unit_of(p_ref[:, h * head_dim : (h + 1) * head_dim])
        gain = qg_ref[...] if h < heads else kg_ref[...]
        turned = turn(unit * gain, cos_ref, sin_ref, 1.0).astype(BF16)
        if h < heads:
            q_out[:, h * head_dim : (h + 1) * head_dim] = turned
        else:
            place = (h - heads) * 2 * head_dim
            kv_out[:, place : place + head_dim] = turned
    for h in range(kv_heads):
        place = (2 * h + 1) * head_dim
        start = 2 * q_cols + k_cols + h * head_dim
        kv_out[:, place : place + head_dim] = p_ref[:, start : start + head_dim].astype(BF16)


def prepare(heads, kv_heads, head_dim, proj, cos, sin, q_gain, k_gain):
    span = proj.shape[0]
    rows = span // 2
    spec = lambda n: pl.BlockSpec((rows, n), lambda i: (i, 0))
    whole = pl.BlockSpec((1, head_dim), lambda i: (0, 0))
    return pl.pallas_call(
        functools.partial(prepare_kernel, heads, kv_heads, head_dim),
        out_shape=(
            jax.ShapeDtypeStruct((span, heads * head_dim), BF16),
            jax.ShapeDtypeStruct((span, 2 * kv_heads * head_dim), BF16),
        ),
        grid=(2,),
        in_specs=[spec(proj.shape[1]), spec(head_dim), spec(head_dim), whole, whole],
        out_specs=(spec(heads * head_dim), spec(2 * kv_heads * head_dim)),
        compiler_params=params(),
        cost_estimate=cost(20 * proj.size, 5 * proj.size),
        name="prepare",
    )(proj, cos, sin, q_gain, k_gain)


def attend_kernel(group, head_dim, turns, scalars, q_ref, gate_ref, spot_ref, key_ref, *refs):
    blocks = len(turns)
    kv_refs = refs[:blocks]
    mixed_out, gated_out, sum_out, acc_ref, total_ref = refs[blocks:]
    scale = head_dim**-0.5 * math.log2(math.e)
    own = scalars[0]
    for h in range(group):
        cols = slice(h * head_dim, (h + 1) * head_dim)
        query = q_ref[:, cols]

        def scores(ref):
            return lax.dot_general(query, ref[:, :head_dim], CONTRACT_COLS, preferred_element_type=F32)

        allowed = (key_ref[...] <= spot_ref[...]) & (key_ref[...] < scalars[1])
        terms = jnp.where(allowed, jnp.exp2(scores(kv_refs[0]) * scale), 0.0)
        total_ref[...] = jnp.sum(terms, axis=-1, keepdims=True)
        acc_ref[...] = project(terms.astype(BF16), kv_refs[0][:, head_dim:])
        for place in range(1, blocks):

            @pl.when((own ^ turns[place]) < own)
            def _(ref=kv_refs[place]):
                terms = jnp.exp2(scores(ref) * scale)
                total_ref[...] += jnp.sum(terms, axis=-1, keepdims=True)
                acc_ref[...] += project(terms.astype(BF16), ref[:, head_dim:])

        mixed = acc_ref[...] / total_ref[...]
        mixed_out[:, cols] = mixed
        gated_out[:, cols] = (mixed * sigmoid(gate_ref[:, cols])).astype(BF16)
        sum_out[:, cols] = jnp.broadcast_to(total_ref[...], mixed.shape)


def attend(scalars, part, parts, group, head_dim, turns, query, proj, gate_at, spots, keys, kvs):
    span, width = query.shape
    rows, wide = span // parts, group * head_dim
    head = pl.BlockSpec((rows, wide), lambda g, s: (part, g))
    out = pl.BlockSpec((rows, wide), lambda g, s: (0, g))
    gate_block = gate_at // wide
    return pl.pallas_call(
        functools.partial(attend_kernel, group, head_dim, turns),
        out_shape=(
            jax.ShapeDtypeStruct((rows, width), F32),
            jax.ShapeDtypeStruct((rows, width), BF16),
            jax.ShapeDtypeStruct((rows, width), F32),
        ),
        grid_spec=pltpu.PrefetchScalarGridSpec(
            num_scalar_prefetch=1,
            grid=(width // wide,),
            in_specs=[
                head,
                pl.BlockSpec((rows, wide), lambda g, s: (part, gate_block + g)),
                pl.BlockSpec((rows, 1), lambda g, s: (part, 0)),
                pl.BlockSpec((1, span), lambda g, s: (0, 0)),
            ]
            + [pl.BlockSpec((span, 2 * head_dim), lambda g, s: (0, g))] * len(kvs),
            out_specs=(out,) * 3,
            scratch_shapes=[pltpu.VMEM((rows, head_dim), F32), pltpu.VMEM((rows, 1), F32)],
        ),
        compiler_params=params(),
        cost_estimate=cost(
            4 * rows * width * span * len(kvs),
            4 * span * width * len(kvs) + 20 * rows * width,
            rows * span * len(kvs) * width // head_dim,
        ),
        name="attend",
    )(scalars, query, proj, spots, keys, *kvs)


def attend_back_kernel(group, head_dim, turns, first, scalars, *refs):
    blocks = len(turns)
    q_ref, query_ref, gate_ref, mixed_ref, sum_ref, gg_ref, spot_ref, key_ref, cos_ref, sin_ref, gain_ref = refs[:11]
    kv_refs = refs[11 : 11 + blocks]
    rest = refs[11 + blocks :]
    old_refs = () if first else rest[:blocks]
    rest = rest if first else rest[blocks:]
    gq_out, ggate_out, gain_out = rest[:3]
    new_refs = rest[3 : 3 + blocks]
    gq_ref, gk_ref = rest[3 + blocks :]
    score_scale = head_dim**-0.5
    scale = score_scale * math.log2(math.e)
    own = scalars[0]
    rows = q_ref.shape[0]

    def as_row(column):
        return jnp.transpose(jnp.broadcast_to(column, (rows, head_dim)))[:1, :]

    for place in range(blocks):
        if first:
            new_refs[place][...] = jnp.zeros_like(new_refs[place])
        else:
            new_refs[place][...] = old_refs[place][...]
    gain_total = jnp.zeros((1, head_dim), F32)
    for h in range(group):
        cols = slice(h * head_dim, (h + 1) * head_dim)
        query = q_ref[:, cols]
        gate = sigmoid(gate_ref[:, cols])
        grad_gated, mixed = gg_ref[:, cols], mixed_ref[:, cols]
        grad_mixed = (grad_gated * gate).astype(BF16)
        ggate_out[:, cols] = (grad_gated * mixed * gate * (1.0 - gate)).astype(BF16)
        row_dot = as_row(jnp.sum(grad_mixed.astype(F32) * mixed, axis=-1, keepdims=True))
        row_log = as_row(jnp.log2(sum_ref[:, cols][:, :1]))
        gq_ref[...] = jnp.zeros_like(gq_ref)

        def block(kv_ref, new_ref, masked):
            key, value = kv_ref[:, :head_dim], kv_ref[:, head_dim:]
            scores = lax.dot_general(key, query, CONTRACT_COLS, preferred_element_type=F32)
            probs = jnp.exp2(scores * scale - row_log)
            if masked:
                allowed = (key_ref[...] <= spot_ref[...]) & (key_ref[...] < scalars[1])
                probs = jnp.where(allowed, probs, 0.0)
            grad_probs = lax.dot_general(value, grad_mixed, CONTRACT_COLS, preferred_element_type=F32)
            grad_scores = (probs * (grad_probs - row_dot)).astype(BF16)
            new_ref[:, head_dim:] += project(probs.astype(BF16), grad_mixed)
            new_ref[:, :head_dim] += project(grad_scores, query)
            gq_ref[...] += lax.dot_general(grad_scores, key, CONTRACT_ROWS, preferred_element_type=F32)

        block(kv_refs[0], new_refs[0], True)
        for place in range(1, blocks):

            @pl.when((own ^ turns[place]) < own)
            def _(place=place):
                block(kv_refs[place], new_refs[place], False)

        unit, inverse = unit_of(query_ref[:, cols])
        back = turn(gq_ref[...] * score_scale, cos_ref, sin_ref, -1.0)
        gain_total = gain_total + jnp.sum(back * unit, axis=0, keepdims=True)
        scaled = back * gain_ref[...]
        gq_out[:, cols] = (
            inverse * (scaled - unit * jnp.mean(scaled * unit, axis=-1, keepdims=True))
        ).astype(BF16)
    gain_out[...] = jnp.broadcast_to(gain_total, gain_out.shape)


def attend_back(
    scalars, part, parts, group, head_dim, turns, query, proj, gate_at, mixed, sums, grad_gated, spots, keys, cos, sin, gain, kvs, olds
):
    span, width = query.shape
    rows, wide = span // parts, group * head_dim
    blocks = len(kvs)
    gate_block = gate_at // wide
    mine = pl.BlockSpec((rows, wide), lambda g, s: (part, g))
    local = pl.BlockSpec((rows, wide), lambda g, s: (0, g))
    table = pl.BlockSpec((rows, head_dim), lambda g, s: (part, 0))
    pair = pl.BlockSpec((span, 2 * head_dim), lambda g, s: (0, g))
    first = olds is None
    olds = () if first else tuple(olds)
    kv_shape = jax.ShapeDtypeStruct(kvs[0].shape, F32)
    steps = width // wide
    out = pl.pallas_call(
        functools.partial(attend_back_kernel, group, head_dim, turns, first),
        out_shape=(
            jax.ShapeDtypeStruct((rows, width), BF16),
            jax.ShapeDtypeStruct((rows, width), BF16),
            jax.ShapeDtypeStruct((8 * steps, head_dim), F32),
        )
        + (kv_shape,) * blocks,
        grid_spec=pltpu.PrefetchScalarGridSpec(
            num_scalar_prefetch=1,
            grid=(steps,),
            in_specs=[
                mine,
                mine,
                pl.BlockSpec((rows, wide), lambda g, s: (part, gate_block + g)),
                local,
                local,
                local,
                pl.BlockSpec((1, rows), lambda g, s: (0, part)),
                pl.BlockSpec((span, 1), lambda g, s: (0, 0)),
                table,
                table,
                pl.BlockSpec((1, head_dim), lambda g, s: (0, 0)),
            ]
            + [pair] * (blocks + len(olds)),
            out_specs=(local, local, pl.BlockSpec((8, head_dim), lambda g, s: (g, 0))) + (pair,) * blocks,
            scratch_shapes=[pltpu.VMEM((rows, head_dim), F32), pltpu.VMEM((8, head_dim), F32)],
        ),
        input_output_aliases={12 + blocks + i: 3 + i for i in range(len(olds))},
        compiler_params=params(),
        cost_estimate=cost(
            10 * rows * width * span * blocks,
            20 * span * width * blocks,
            rows * span * blocks * width // head_dim,
        ),
        name="attend_back",
    )(scalars, query, proj, proj, mixed, sums, grad_gated, spots, keys, cos, sin, gain, *kvs, *olds)
    gain_part = sum(out[2][8 * g] for g in range(steps))
    return out[0], out[1], gain_part, out[3:]


def keys_back_kernel(kv_heads, head_dim, g_ref, p_ref, cos_ref, sin_ref, gain_ref, k_out, v_out, gain_out):
    gain_total = jnp.zeros((1, head_dim), F32)
    for h in range(kv_heads):
        cols = slice(h * head_dim, (h + 1) * head_dim)
        unit, inverse = unit_of(p_ref[:, cols])
        grad = g_ref[:, 2 * h * head_dim : (2 * h + 1) * head_dim] * head_dim**-0.5
        back = turn(grad, cos_ref, sin_ref, -1.0)
        gain_total = gain_total + jnp.sum(back * unit, axis=0, keepdims=True)
        scaled = back * gain_ref[...]
        k_out[:, cols] = (
            inverse * (scaled - unit * jnp.mean(scaled * unit, axis=-1, keepdims=True))
        ).astype(BF16)
        v_out[:, cols] = g_ref[:, (2 * h + 1) * head_dim : (2 * h + 2) * head_dim].astype(BF16)
    gain_out[...] = jnp.broadcast_to(gain_total, gain_out.shape)


def keys_back(kv_heads, head_dim, grad_kv, proj, key_at, cos, sin, gain):
    span = proj.shape[0]
    cols = kv_heads * head_dim
    key_block = key_at // cols
    whole = lambda a, b: pl.BlockSpec((a, b), lambda i: (0, 0))
    out = pl.pallas_call(
        functools.partial(keys_back_kernel, kv_heads, head_dim),
        out_shape=(
            jax.ShapeDtypeStruct((span, cols), BF16),
            jax.ShapeDtypeStruct((span, cols), BF16),
            jax.ShapeDtypeStruct((8, head_dim), F32),
        ),
        grid=(1,),
        in_specs=[
            whole(span, 2 * cols),
            pl.BlockSpec((span, cols), lambda i: (0, key_block)),
            whole(span, head_dim),
            whole(span, head_dim),
            whole(1, head_dim),
        ],
        out_specs=(whole(span, cols), whole(span, cols), whole(8, head_dim)),
        compiler_params=params(),
        cost_estimate=cost(40 * span * cols, 16 * span * cols),
        name="keys_back",
    )(grad_kv, proj, cos, sin, gain)
    return out[0], out[1], out[2][0]


def norm_back(gradient, unit_vals, inverse, gain_vec):
    scaled = gradient * gain_vec
    return inverse * (scaled - unit_vals * jnp.mean(scaled * unit_vals, axis=-1, keepdims=True))


def per_device(
    links,
    hidden_in,
    lengths,
    attn_gain,
    q_weight,
    gate_weight,
    k_weight,
    v_weight,
    q_gain,
    k_gain,
    o_weight,
    mlp_gain,
    w_gate,
    w_up,
    w_down,
    out_grad,
):
    dp_index, ctx_index, z_index = (lax.axis_index(a) for a in ("dp", "ctx", "tensor"))
    q_cols, k_cols, ff_cols = q_weight.shape[1], k_weight.shape[1], w_down.shape[1]
    span, width = hidden_in.shape
    mid, count = width // 2, 2 * links.half
    shard, head_shard = attn_gain.shape[0], q_gain.shape[0]
    head_dim = head_shard * count
    heads, kv_heads = q_cols // head_dim, k_cols // head_dim
    group = heads // kv_heads
    length = lengths[0]
    low = lambda *mats: jnp.concatenate([m.astype(BF16) for m in mats], axis=1)

    small = jnp.concatenate([attn_gain, mlp_gain, q_gain, k_gain]).astype(BF16)[None, :]
    first_mat = links.gather(low(q_weight, k_weight, gate_weight, v_weight, o_weight))
    gains = links.small_gather(small)
    feed_mat = links.gather(low(w_gate, w_up))
    down_mat = links.gather(low(w_down))
    attn_scale = gains[:, :shard].reshape(1, width).astype(F32)
    mlp_scale = gains[:, shard : 2 * shard].reshape(1, width).astype(F32)
    owners = jnp.stack([links.owner_of(p, dp_index, ctx_index) for p in range(count)])
    pick = (owners[None, :] == jnp.arange(count)[:, None]).astype(BF16)
    head_gains = project(pick, gains[:, 2 * shard :])
    query_scale = head_gains[:, :head_shard].reshape(1, head_dim)
    key_scale = head_gains[:, head_shard:].reshape(1, head_dim)

    parts = 2 * links.tensor
    row_block = span // parts
    row_places = jnp.stack(
        [part * links.tensor + (z_index ^ j) for part in range(2) for j in links.turns]
    ).astype(jnp.int32)
    start = ctx_index * span
    scalars = jnp.concatenate(
        [row_places, owners.astype(jnp.int32), jnp.stack([start, length]).astype(jnp.int32)]
    )
    spots = (start + row_places[:, None] * row_block + jnp.arange(row_block)[None, :]).reshape(span)
    spots = spots.astype(jnp.int32)
    freq_steps = jnp.arange(head_dim // 2, dtype=F32) * (2.0 / head_dim)
    turned = spots.astype(F32)[:, None] * jnp.exp(-math.log(ROPE_BASE) * freq_steps)[None, :]
    cosine, sine = jnp.cos(turned), jnp.sin(turned)
    cos = jnp.concatenate([cosine, cosine], axis=1)
    sin = jnp.concatenate([-sine, sine], axis=1)
    spot_col, spot_row = spots[:, None], spots[None, :]

    stream, grad_out, down_grad, normed = enter(scalars, count, parts, span, hidden_in, out_grad, attn_scale)

    proj_cols = 2 * (q_cols + k_cols)
    both = lambda value, mats, a, b: project(value[:, :mid], mats[0][:, a:b]) + project(
        value[:, mid:], mats[1][:, a:b]
    )
    proj = both(normed, first_mat, 0, proj_cols)
    gate_at = q_cols + k_cols
    query, kv = prepare(heads, kv_heads, head_dim, proj, cos, sin, query_scale, key_scale)
    kvs, turns = [kv], [0]
    mask = links.ctx // 2
    while mask:
        kvs = kvs + [links.swap(b, "ctx", mask) for b in kvs]
        turns = turns + [p ^ mask for p in turns]
        mask //= 2
    at = jnp.stack([ctx_index, length]).astype(jnp.int32)
    half_rows = span // 2
    mixed, gated, sums, middle, normed_two, unit_two, inverse_two = ([None] * 2 for _ in range(7))
    out_mat = [m[:, proj_cols:] for m in first_mat]
    shard_rows = half_rows // links.tensor
    own_rows = lambda value, t: value[t * half_rows : t * half_rows + shard_rows]
    live = [(own_rows(spot_col, t) < length).astype(F32) for t in range(2)]
    for t in range(2):
        mixed[t], gated[t], sums[t] = attend(
            at, t, 2, group, head_dim, turns, query, proj, gate_at, spot_col, spot_row, kvs
        )
        part = jnp.concatenate([col_contract(gated[t], m).astype(BF16) for m in out_mat], axis=1)
        attn_out = links.scatter_rows(part)
        middle[t] = own_rows(stream, t).astype(F32) + attn_out * live[t]
        inverse_two[t] = lax.rsqrt(jnp.mean(middle[t] * middle[t], axis=-1, keepdims=True) + EPSILON)
        unit_two[t] = middle[t] * inverse_two[t]
        normed_two[t] = links.gather_rows((unit_two[t] * mlp_scale).astype(BF16))

    hidden, grad_feed, grad_middle, attn_grad = ([None] * 2 for _ in range(4))
    down_shard = [None] * 2
    for t in range(2):
        rows = slice(t * half_rows, (t + 1) * half_rows)
        gate_in = both(normed_two[t], feed_mat, 0, ff_cols)
        up_in = both(normed_two[t], feed_mat, ff_cols, 2 * ff_cols)
        grad_hidden = both(down_grad[rows], down_mat, 0, ff_cols)
        sig = jax.nn.sigmoid(gate_in)
        hidden[t] = (gate_in * sig * up_in).astype(BF16)
        grad_gate_in = (grad_hidden * up_in * sig * (1.0 + gate_in * (1.0 - sig))).astype(BF16)
        grad_up_in = (grad_hidden * (gate_in * sig)).astype(BF16)
        grad_feed[t] = jnp.concatenate([grad_gate_in, grad_up_in], axis=1)
        part = jnp.concatenate([col_contract(grad_feed[t], m).astype(BF16) for m in feed_mat], axis=1)
        back = links.scatter_rows(part)
        grad_mlp = jnp.sum(back * unit_two[t], axis=0)
        grad_mlp_gain = grad_mlp if t == 0 else grad_mlp_gain + grad_mlp
        grad_middle[t] = own_rows(grad_out, t).astype(F32) + norm_back(
            back, unit_two[t], inverse_two[t], mlp_scale
        )
        attn_grad[t] = links.gather_rows((grad_middle[t] * live[t]).astype(BF16))
    for t in range(2):
        part = jnp.concatenate([col_contract(hidden[t], m).astype(BF16) for m in down_mat], axis=1)
        down = links.scatter_rows(part)
        down_shard[t] = links.gather_rows((middle[t] + down * live[t]).astype(BF16))
    hidden_out = leave(scalars, count, parts, jnp.concatenate(down_shard, axis=0), BF16)

    def weight_grad(rows_of, cols_of):
        other = row_contract(rows_of[:, mid:], cols_of).astype(BF16)
        own = row_contract(rows_of[:, :mid], cols_of).astype(BF16)
        return own, other

    rows_two = jnp.concatenate(normed_two, axis=0)
    down_pair = weight_grad(down_grad, jnp.concatenate(hidden, axis=0))
    grad_w_down = links.reduce(*down_pair)
    feed_pair = weight_grad(rows_two, jnp.concatenate(grad_feed, axis=0))
    grad_feed_mat = links.reduce(*feed_pair)

    olds = None
    grad_query, grad_gates, q_gain_part = [None] * 2, [None] * 2, 0.0
    for t in range(2):
        grad_gated = both(attn_grad[t], out_mat, 0, q_cols)
        grad_query[t], grad_gates[t], gain_part, olds = attend_back(
            at, t, 2, group, head_dim, turns, query, proj, gate_at, mixed[t], sums[t], grad_gated,
            spot_row, spot_col, cos, sin, query_scale, kvs, olds,
        )
        q_gain_part = q_gain_part + gain_part
    pieces = dict(zip(turns, olds))
    mask = 1
    while len(pieces) > 1:
        near = [p for p in pieces if not p & mask]
        sent = jnp.concatenate([pieces[p ^ mask].astype(BF16) for p in near], axis=0)
        came = links.swap(sent, "ctx", mask).astype(F32)
        pieces = {p: pieces[p] + came[i * span : (i + 1) * span] for i, p in enumerate(near)}
        mask *= 2
    grad_key, grad_value, k_gain_part = keys_back(
        kv_heads, head_dim, pieces[0], proj, q_cols, cos, sin, key_scale
    )
    grad_proj = jnp.concatenate(
        [
            jnp.concatenate(grad_query, axis=0),
            grad_key,
            jnp.concatenate(grad_gates, axis=0),
            grad_value,
        ],
        axis=1,
    )
    grad_in, attn_gain_part = [None] * 2, 0.0
    for t in range(2):
        rows = slice(t * half_rows, (t + 1) * half_rows)
        part = jnp.concatenate(
            [col_contract(grad_proj[rows], m[:, :proj_cols]).astype(BF16) for m in first_mat], axis=1
        )
        back = links.scatter_rows(part)
        x = own_rows(stream, t).astype(F32)
        inverse = lax.rsqrt(jnp.mean(x * x, axis=-1, keepdims=True) + EPSILON)
        unit = x * inverse
        attn_gain_part = attn_gain_part + jnp.sum(back * unit, axis=0)
        grad_in[t] = links.gather_rows(
            (grad_middle[t] + norm_back(back, unit, inverse, attn_scale)).astype(BF16)
        )
    grad_in = leave(scalars, count, parts, jnp.concatenate(grad_in, axis=0), F32)
    proj_pair = weight_grad(normed, grad_proj)
    out_pair = weight_grad(jnp.concatenate(attn_grad, axis=0), jnp.concatenate(gated, axis=0))
    grad_first = links.reduce(
        *(jnp.concatenate([a, b], axis=1) for a, b in zip(proj_pair, out_pair))
    )

    blocks = jnp.stack([attn_gain_part.reshape(count, shard), grad_mlp_gain.reshape(count, shard)])
    to_mesh = (owners[None, :] == jnp.arange(count)[:, None]).astype(F32)
    blocks = jnp.einsum("ap,kpn->kan", to_mesh, blocks, precision=lax.Precision.HIGHEST)
    packed = jnp.concatenate([blocks.reshape(1, -1), q_gain_part[None, :], k_gain_part[None, :]], axis=1)
    packed = links.add_all(packed)[0]
    rank = dp_index * links.ctx + ctx_index
    take = lambda at, size: lax.dynamic_slice_in_dim(packed, at + rank * size, size)
    cut = [q_cols, q_cols + k_cols, 2 * q_cols + k_cols, proj_cols]
    grads = jnp.split(grad_first, cut, axis=1)
    return (
        hidden_out,
        grad_in,
        take(0, shard),
        grads[0],
        grads[2],
        grads[1],
        grads[3],
        take(2 * width, head_shard),
        take(2 * width + head_dim, head_shard),
        grads[4],
        take(width, shard),
        grad_feed_mat[:, :ff_cols],
        grad_feed_mat[:, ff_cols:],
        grad_w_down,
    )


def solution(mesh):
    links = Links(dict(mesh.shape))
    rows = P(("dp", "ctx"))
    plain = P(("dp", "ctx"), None)
    split = P(("dp", "ctx"), "tensor")

    def step(*arrays):
        return per_device(links, *arrays)

    return jax.shard_map(
        step,
        mesh=mesh,
        in_specs=(plain, P("dp"), rows, split, split, split, split, rows, rows, split, rows, split, split, split, plain),
        out_specs=(plain, plain, rows, split, split, split, split, rows, rows, split, rows, split, split, split),
        check_vma=False,
    )
```

```python
import functools
import math

import jax
import jax.numpy as jnp
from jax import lax
from jax.experimental import pallas as pl
from jax.experimental.pallas import tpu as pltpu
from jax.sharding import PartitionSpec as P

EPSILON = 1e-06
ROPE_BASE = 1000000.0
CONTRACT_ROWS = (((0,), (0,)), ((), ()))
CONTRACT_COLS = (((1,), (1,)), ((), ()))
F32 = jnp.float32
BF16 = jnp.bfloat16
VMEM_BYTES = 56 * 1024 * 1024


def project(operand, matrix):
    return jnp.dot(operand, matrix, preferred_element_type=F32)


def row_contract(first_op, second_op):
    return lax.dot_general(first_op, second_op, CONTRACT_ROWS, preferred_element_type=F32)


def col_contract(first_op, second_op):
    return lax.dot_general(first_op, second_op, CONTRACT_COLS, preferred_element_type=F32)


def sigmoid(value):
    return 1.0 / (1.0 + jnp.exp(-value))


def after(value, *others):
    return lax.optimization_barrier((value,) + others)[0]


def cost(flops, moved, exps=0):
    return pl.CostEstimate(flops=int(flops), bytes_accessed=int(moved), transcendentals=int(exps))


def params(**kwargs):
    return pltpu.CompilerParams(vmem_limit_bytes=VMEM_BYTES, **kwargs)


class Links:
    def __init__(self, sizes):
        self.dp, self.ctx, self.tensor = sizes["dp"], sizes["ctx"], sizes["tensor"]
        self.half = self.dp * self.ctx // 2
        ctx_bits = int(math.log2(self.ctx // 2))
        dp_bits = int(math.log2(self.dp))
        self.bits = [("ctx", 2 << i) for i in range(ctx_bits)] + [("dp", 1 << i) for i in range(dp_bits)]
        self.masks = [(2 << i) - 1 for i in range(int(math.log2(self.tensor)))]
        self.turns = [0]
        for mask in reversed(self.masks):
            self.turns = self.turns + [j ^ mask for j in self.turns]

    def swap(self, value, axis, mask):
        count = {"dp": self.dp, "ctx": self.ctx, "tensor": self.tensor}[axis]
        return lax.ppermute(value, axis, [(i, i ^ mask) for i in range(count)])

    def order(self, turn):
        places = list(range(len(self.bits)))
        return places if turn else places[::-1]

    def send_own(self, block):
        return {1 << p: self.swap(block, *self.bits[p]) for p in self.order(0)}

    def send_on(self, single):
        mid = next(iter(single.values())).shape[1] // 2
        left = {q: b[:, :mid] for q, b in single.items()}
        right = {q: b[:, mid:] for q, b in single.items()}
        for side, places in ((left, self.order(0)), (right, self.order(1))):
            for q in range(1, self.half):
                if q not in single:
                    self.reach(side, q, places)
        return {q: (left[q], right[q]) for q in left if q not in single}

    def assemble(self, block, single, pairs):
        blocks, groups = [], []
        for q in range(self.half):
            members = [block] if q == 0 else [single[q]] if q in single else list(pairs[q])
            groups.append(tuple(range(len(blocks), len(blocks) + len(members))))
            blocks += members
        return stack_blocks(groups, blocks)

    def reach(self, side, q, places):
        if q not in side:
            last = [p for p in places if q & (1 << p)][-1]
            self.reach(side, q ^ (1 << last), places)
            side[q] = self.swap(side[q ^ (1 << last)], *self.bits[last])

    def first_sum(self, own, other):
        return (own + self.swap(other, "ctx", 1).astype(F32)).astype(BF16)

    def reduce_step(self, pieces, turn, step):
        rows = pieces[0].shape[0]
        place = self.order(turn)[step]
        bit = 1 << place
        kept = [q for q in pieces if not q & bit]
        sent = jnp.concatenate([pieces[q | bit].astype(BF16) for q in kept], axis=0)
        came = self.swap(sent, *self.bits[place])
        return came, {
            q: pieces[q].astype(F32) + came[i * rows : (i + 1) * rows].astype(F32) for i, q in enumerate(kept)
        }

    def reduce(self, total, turn):
        rows = total.shape[0] // self.half
        pieces = {q: total[q * rows : (q + 1) * rows] for q in range(self.half)}
        seen = []
        for step in range(len(self.bits)):
            came, pieces = self.reduce_step(pieces, turn, step)
            seen.append(came)
        return pieces[0], seen

    def small_gather(self, row):
        count = self.dp * self.ctx
        rows = [row]
        for q in range(1, self.half):
            far = (q // (self.ctx // 2)) * self.ctx + (q % (self.ctx // 2)) * 2
            rows.append(lax.ppermute(row, ("dp", "ctx"), [(i, i ^ far) for i in range(count)]))
        own = jnp.concatenate(rows, axis=0)
        return jnp.concatenate([own, self.swap(own, "ctx", 1)], axis=0), rows[1:]

    def owner_of(self, position, dp_index, ctx_index):
        h, q = position // self.half, position % self.half
        dp_far, ctx_far = q // (self.ctx // 2), (q % (self.ctx // 2)) * 2 + h
        return (dp_index ^ dp_far) * self.ctx + (ctx_index ^ ctx_far)

    def scatter_rows(self, part):
        kept, rows = part, part.shape[0]
        for mask in self.masks:
            rows //= 2
            came = self.swap(kept[rows:].astype(BF16), "tensor", mask)
            kept = kept[:rows].astype(F32) + came.astype(F32)
        return kept

    def gather_rows(self, shard):
        for mask in reversed(self.masks):
            shard = jnp.concatenate([shard, self.swap(shard, "tensor", mask)], axis=0)
        return shard

    def add_all(self, value):
        for mask in self.masks:
            value = value + self.swap(value, "tensor", mask)
        value = value + self.swap(value, "ctx", 1)
        for axis, mask in self.bits:
            value = value + self.swap(value, axis, mask)
        return value


def still(scalars, count, parts):
    owners = scalars[parts : parts + count]
    return owners, lax.dynamic_update_slice(scalars, jnp.arange(count, dtype=scalars.dtype), (parts,))


def columns(value, owners):
    count = owners.shape[0]
    blocks = value.reshape(value.shape[0], count, value.shape[1] // count)
    return jnp.take(blocks, owners, axis=1).reshape(value.shape)


def column_place(scalars, parts, p, size):
    if size % 128:
        return pl.ds(p * size, size)
    return pl.ds(pl.multiple_of(scalars[parts + p] * size, size), size)


def stack_kernel(groups, *refs):
    out_ref = refs[-1]
    for q, group in enumerate(groups):

        @pl.when(pl.program_id(0) == q)
        def _(group=group):
            col = 0
            for i in group:
                out_ref[:, col : col + refs[i].shape[1]] = refs[i][...]
                col += refs[i].shape[1]


def stack_blocks(groups, blocks):
    rows, n = blocks[0].shape
    held = lambda b: pl.BlockSpec(b.shape, lambda i: (0, 0), pipeline_mode=pl.Buffered(1))
    return pl.pallas_call(
        functools.partial(stack_kernel, groups),
        out_shape=jax.ShapeDtypeStruct((rows * len(groups), n), blocks[0].dtype),
        grid=(len(groups),),
        in_specs=[held(b) for b in blocks],
        out_specs=pl.BlockSpec((rows, n), lambda i: (i, 0)),
        compiler_params=params(),
        cost_estimate=cost(0, 4 * rows * len(groups) * n),
        name="stack",
    )(*blocks)


def enter_kernel(count, parts, scalars, xa_ref, xb_ref, ga_ref, gb_ref, gain_ref, x_out, g_out, m_out, n_out):
    step = pl.program_id(0)
    rows, width = xa_ref.shape
    size = width // count
    for part, (x_ref, g_ref) in enumerate(((xa_ref, ga_ref), (xb_ref, gb_ref))):
        places = [column_place(scalars, parts, p, size) for p in range(count)]
        x = jnp.concatenate([x_ref[:, place] for place in places], axis=1)
        g = jnp.concatenate([g_ref[:, place] for place in places], axis=1)
        if part == 0:

            @pl.when(step % (parts // 4) == 0)
            def _(x=x, g=g):
                x_out[...] = x
                g_out[...] = g

        place = slice(part * rows, (part + 1) * rows)
        spot = scalars[parts + count] + scalars[2 * step + part] * rows
        live = spot + lax.broadcasted_iota(jnp.int32, (rows, 1), 0) < scalars[parts + count + 1]
        m_out[place, :] = jnp.where(live, g.astype(F32), 0.0).astype(BF16)
        wide = x.astype(F32)
        inverse = lax.rsqrt(jnp.mean(wide * wide, axis=-1, keepdims=True) + EPSILON)
        n_out[place, :] = (wide * inverse * gain_ref[...]).astype(BF16)


def enter(scalars, count, parts, span, hidden_in, out_grad, gain):
    rows, width = span // parts, hidden_in.shape[1]
    if width // count % 128:
        owners, scalars = still(scalars, count, parts)
        hidden_in, out_grad = columns(hidden_in, owners), columns(out_grad, owners)
    upper = pl.BlockSpec((rows, width), lambda i, s: (s[2 * i], 0))
    lower = pl.BlockSpec((rows, width), lambda i, s: (s[2 * i + 1], 0))
    own = pl.BlockSpec((rows, width), lambda i, s: (i // (parts // 4), 0))
    plain = pl.BlockSpec((2 * rows, width), lambda i, s: (i, 0))
    shape = jax.ShapeDtypeStruct((span, width), BF16)
    short = jax.ShapeDtypeStruct((2 * rows, width), BF16)
    return pl.pallas_call(
        functools.partial(enter_kernel, count, parts),
        out_shape=(short, short, shape, shape),
        grid_spec=pltpu.PrefetchScalarGridSpec(
            num_scalar_prefetch=1,
            grid=(parts // 2,),
            in_specs=[upper, lower, upper, lower, pl.BlockSpec((1, width), lambda i, s: (0, 0))],
            out_specs=(own, own, plain, plain),
        ),
        compiler_params=params(),
        cost_estimate=cost(10 * span * width, 8 * span * width),
        name="enter",
    )(scalars, hidden_in, hidden_in, out_grad, out_grad, gain)


def leave_kernel(count, parts, scalars, in_ref, out_ref):
    rows, size = in_ref.shape[0] // 2, in_ref.shape[1] // count
    step = pl.program_id(0)
    for part in range(2):
        at = pl.ds(pl.multiple_of(scalars[2 * step + part] * rows, rows), rows)
        for p in range(count):
            place = column_place(scalars, parts, p, size)
            block = in_ref[part * rows : (part + 1) * rows, p * size : (p + 1) * size]
            out_ref[at, place] = block.astype(out_ref.dtype)


def leave(scalars, count, parts, value, dtype):
    span, width = value.shape
    rows = span // parts
    if width // count % 128:
        owners, scalars = still(scalars, count, parts)
        value = columns(value, jnp.argsort(owners))
    return pl.pallas_call(
        functools.partial(leave_kernel, count, parts),
        out_shape=jax.ShapeDtypeStruct((span, width), dtype),
        grid_spec=pltpu.PrefetchScalarGridSpec(
            num_scalar_prefetch=1,
            grid=(parts // 2,),
            in_specs=[pl.BlockSpec((2 * rows, width), lambda i, s: (i, 0))],
            out_specs=pl.BlockSpec((span, width), lambda i, s: (0, 0)),
        ),
        compiler_params=params(),
        cost_estimate=cost(0, 6 * span * width),
        name="leave",
    )(scalars, value)


def unit_of(value):
    inverse = lax.rsqrt(jnp.mean(value * value, axis=-1, keepdims=True) + EPSILON)
    return value * inverse, inverse


def turn(value, cos_ref, sin_ref, sign):
    half = value.shape[-1] // 2
    return value * cos_ref[...] + sign * pltpu.roll(value, half, 1) * sin_ref[...]


def prepare_kernel(heads, kv_heads, head_dim, p_ref, cos_ref, sin_ref, qg_ref, kg_ref, q_out, kv_out):
    group = heads // kv_heads
    q_cols, k_cols = heads * head_dim, kv_heads * head_dim
    for h in range(heads + kv_heads):
        unit, _ = unit_of(p_ref[:, h * head_dim : (h + 1) * head_dim])
        gain = qg_ref[...] if h < heads else kg_ref[...]
        turned = turn(unit * gain, cos_ref, sin_ref, 1.0).astype(BF16)
        if h < heads:
            q_out[:, h * head_dim : (h + 1) * head_dim] = turned
        else:
            place = (h - heads) * 2 * head_dim
            kv_out[:, place : place + head_dim] = turned
    for h in range(kv_heads):
        place = (2 * h + 1) * head_dim
        start = 2 * q_cols + k_cols + h * head_dim
        kv_out[:, place : place + head_dim] = p_ref[:, start : start + head_dim].astype(BF16)


def prepare(heads, kv_heads, head_dim, proj, cos, sin, q_gain, k_gain):
    span = proj.shape[0]
    rows = span // 2
    spec = lambda n: pl.BlockSpec((rows, n), lambda i: (i, 0))
    whole = pl.BlockSpec((1, head_dim), lambda i: (0, 0))
    return pl.pallas_call(
        functools.partial(prepare_kernel, heads, kv_heads, head_dim),
        out_shape=(
            jax.ShapeDtypeStruct((span, heads * head_dim), BF16),
            jax.ShapeDtypeStruct((span, 2 * kv_heads * head_dim), BF16),
        ),
        grid=(2,),
        in_specs=[spec(proj.shape[1]), spec(head_dim), spec(head_dim), whole, whole],
        out_specs=(spec(heads * head_dim), spec(2 * kv_heads * head_dim)),
        compiler_params=params(),
        cost_estimate=cost(20 * proj.size, 5 * proj.size),
        name="prepare",
    )(proj, cos, sin, q_gain, k_gain)


def attend_kernel(group, head_dim, turns, scalars, q_ref, gate_ref, spot_ref, key_ref, *refs):
    blocks = len(turns)
    kv_refs = refs[:blocks]
    mixed_out, gated_out, sum_out, acc_ref, total_ref = refs[blocks:]
    scale = head_dim**-0.5 * math.log2(math.e)
    own = scalars[0]
    for h in range(group):
        cols = slice(h * head_dim, (h + 1) * head_dim)
        query = q_ref[:, cols]

        def scores(ref):
            return lax.dot_general(query, ref[:, :head_dim], CONTRACT_COLS, preferred_element_type=F32)

        allowed = (key_ref[...] <= spot_ref[...]) & (key_ref[...] < scalars[1])
        terms = jnp.where(allowed, jnp.exp2(scores(kv_refs[0]) * scale), 0.0)
        total_ref[...] = jnp.sum(terms, axis=-1, keepdims=True)
        acc_ref[...] = project(terms.astype(BF16), kv_refs[0][:, head_dim:])
        for place in range(1, blocks):

            @pl.when((own ^ turns[place]) < own)
            def _(ref=kv_refs[place]):
                terms = jnp.exp2(scores(ref) * scale)
                total_ref[...] += jnp.sum(terms, axis=-1, keepdims=True)
                acc_ref[...] += project(terms.astype(BF16), ref[:, head_dim:])

        mixed = acc_ref[...] / total_ref[...]
        mixed_out[:, cols] = mixed
        gated_out[:, cols] = (mixed * sigmoid(gate_ref[:, cols])).astype(BF16)
        sum_out[:, cols] = jnp.broadcast_to(total_ref[...], mixed.shape)


def attend(scalars, part, parts, group, head_dim, turns, query, proj, gate_at, spots, keys, kvs):
    span, width = query.shape
    rows, wide = span // parts, group * head_dim
    head = pl.BlockSpec((rows, wide), lambda g, s: (part, g))
    out = pl.BlockSpec((rows, wide), lambda g, s: (0, g))
    gate_block = gate_at // wide
    return pl.pallas_call(
        functools.partial(attend_kernel, group, head_dim, turns),
        out_shape=(
            jax.ShapeDtypeStruct((rows, width), F32),
            jax.ShapeDtypeStruct((rows, width), BF16),
            jax.ShapeDtypeStruct((rows, width), F32),
        ),
        grid_spec=pltpu.PrefetchScalarGridSpec(
            num_scalar_prefetch=1,
            grid=(width // wide,),
            in_specs=[
                head,
                pl.BlockSpec((rows, wide), lambda g, s: (part, gate_block + g)),
                pl.BlockSpec((rows, 1), lambda g, s: (part, 0)),
                pl.BlockSpec((1, span), lambda g, s: (0, 0)),
            ]
            + [pl.BlockSpec((span, 2 * head_dim), lambda g, s: (0, g))] * len(kvs),
            out_specs=(out,) * 3,
            scratch_shapes=[pltpu.VMEM((rows, head_dim), F32), pltpu.VMEM((rows, 1), F32)],
        ),
        compiler_params=params(),
        cost_estimate=cost(
            4 * rows * width * span * len(kvs),
            4 * span * width * len(kvs) + 20 * rows * width,
            rows * span * len(kvs) * width // head_dim,
        ),
        name="attend",
    )(scalars, query, proj, spots, keys, *kvs)


def attend_back_kernel(group, head_dim, turns, first, scalars, *refs):
    blocks = len(turns)
    q_ref, query_ref, gate_ref, mixed_ref, sum_ref, gg_ref, spot_ref, key_ref, cos_ref, sin_ref, gain_ref = refs[:11]
    kv_refs = refs[11 : 11 + blocks]
    rest = refs[11 + blocks :]
    old_refs = () if first else rest[:blocks]
    rest = rest if first else rest[blocks:]
    gq_out, ggate_out, gain_out = rest[:3]
    new_refs = rest[3 : 3 + blocks]
    gq_ref, gk_ref = rest[3 + blocks :]
    score_scale = head_dim**-0.5
    scale = score_scale * math.log2(math.e)
    own = scalars[0]
    rows = q_ref.shape[0]

    def as_row(column):
        return jnp.transpose(jnp.broadcast_to(column, (rows, head_dim)))[:1, :]

    for place in range(blocks):
        if first:
            new_refs[place][...] = jnp.zeros_like(new_refs[place])
        else:
            new_refs[place][...] = old_refs[place][...]
    gain_total = jnp.zeros((1, head_dim), F32)
    for h in range(group):
        cols = slice(h * head_dim, (h + 1) * head_dim)
        query = q_ref[:, cols]
        gate = sigmoid(gate_ref[:, cols])
        grad_gated, mixed = gg_ref[:, cols], mixed_ref[:, cols]
        grad_mixed = (grad_gated * gate).astype(BF16)
        ggate_out[:, cols] = (grad_gated * mixed * gate * (1.0 - gate)).astype(BF16)
        row_dot = as_row(jnp.sum(grad_mixed.astype(F32) * mixed, axis=-1, keepdims=True))
        row_log = as_row(jnp.log2(sum_ref[:, cols][:, :1]))
        gq_ref[...] = jnp.zeros_like(gq_ref)

        def block(kv_ref, new_ref, masked):
            key, value = kv_ref[:, :head_dim], kv_ref[:, head_dim:]
            scores = lax.dot_general(key, query, CONTRACT_COLS, preferred_element_type=F32)
            probs = jnp.exp2(scores * scale - row_log)
            if masked:
                allowed = (key_ref[...] <= spot_ref[...]) & (key_ref[...] < scalars[1])
                probs = jnp.where(allowed, probs, 0.0)
            grad_probs = lax.dot_general(value, grad_mixed, CONTRACT_COLS, preferred_element_type=F32)
            grad_scores = (probs * (grad_probs - row_dot)).astype(BF16)
            new_ref[:, head_dim:] += project(probs.astype(BF16), grad_mixed)
            new_ref[:, :head_dim] += project(grad_scores, query)
            gq_ref[...] += lax.dot_general(grad_scores, key, CONTRACT_ROWS, preferred_element_type=F32)

        block(kv_refs[0], new_refs[0], True)
        for place in range(1, blocks):

            @pl.when((own ^ turns[place]) < own)
            def _(place=place):
                block(kv_refs[place], new_refs[place], False)

        unit, inverse = unit_of(query_ref[:, cols])
        back = turn(gq_ref[...] * score_scale, cos_ref, sin_ref, -1.0)
        gain_total = gain_total + jnp.sum(back * unit, axis=0, keepdims=True)
        scaled = back * gain_ref[...]
        gq_out[:, cols] = (
            inverse * (scaled - unit * jnp.mean(scaled * unit, axis=-1, keepdims=True))
        ).astype(BF16)
    gain_out[...] = jnp.broadcast_to(gain_total, gain_out.shape)


def attend_back(
    scalars, part, parts, group, head_dim, turns, query, proj, gate_at, mixed, sums, grad_gated, spots, keys, cos, sin, gain, kvs, olds
):
    span, width = query.shape
    rows, wide = span // parts, group * head_dim
    blocks = len(kvs)
    gate_block = gate_at // wide
    mine = pl.BlockSpec((rows, wide), lambda g, s: (part, g))
    local = pl.BlockSpec((rows, wide), lambda g, s: (0, g))
    table = pl.BlockSpec((rows, head_dim), lambda g, s: (part, 0))
    pair = pl.BlockSpec((span, 2 * head_dim), lambda g, s: (0, g))
    first = olds is None
    olds = () if first else tuple(olds)
    kv_shape = jax.ShapeDtypeStruct(kvs[0].shape, F32)
    steps = width // wide
    out = pl.pallas_call(
        functools.partial(attend_back_kernel, group, head_dim, turns, first),
        out_shape=(
            jax.ShapeDtypeStruct((rows, width), BF16),
            jax.ShapeDtypeStruct((rows, width), BF16),
            jax.ShapeDtypeStruct((8 * steps, head_dim), F32),
        )
        + (kv_shape,) * blocks,
        grid_spec=pltpu.PrefetchScalarGridSpec(
            num_scalar_prefetch=1,
            grid=(steps,),
            in_specs=[
                mine,
                mine,
                pl.BlockSpec((rows, wide), lambda g, s: (part, gate_block + g)),
                local,
                local,
                local,
                pl.BlockSpec((1, rows), lambda g, s: (0, part)),
                pl.BlockSpec((span, 1), lambda g, s: (0, 0)),
                table,
                table,
                pl.BlockSpec((1, head_dim), lambda g, s: (0, 0)),
            ]
            + [pair] * (blocks + len(olds)),
            out_specs=(local, local, pl.BlockSpec((8, head_dim), lambda g, s: (g, 0))) + (pair,) * blocks,
            scratch_shapes=[pltpu.VMEM((rows, head_dim), F32), pltpu.VMEM((8, head_dim), F32)],
        ),
        input_output_aliases={12 + blocks + i: 3 + i for i in range(len(olds))},
        compiler_params=params(),
        cost_estimate=cost(
            10 * rows * width * span * blocks,
            20 * span * width * blocks,
            rows * span * blocks * width // head_dim,
        ),
        name="attend_back",
    )(scalars, query, proj, proj, mixed, sums, grad_gated, spots, keys, cos, sin, gain, *kvs, *olds)
    gain_part = sum(out[2][8 * g] for g in range(steps))
    return out[0], out[1], gain_part, out[3:]


def keys_back_kernel(kv_heads, head_dim, g_ref, p_ref, cos_ref, sin_ref, gain_ref, k_out, v_out, gain_out):
    gain_total = jnp.zeros((1, head_dim), F32)
    for h in range(kv_heads):
        cols = slice(h * head_dim, (h + 1) * head_dim)
        unit, inverse = unit_of(p_ref[:, cols])
        grad = g_ref[:, 2 * h * head_dim : (2 * h + 1) * head_dim] * head_dim**-0.5
        back = turn(grad, cos_ref, sin_ref, -1.0)
        gain_total = gain_total + jnp.sum(back * unit, axis=0, keepdims=True)
        scaled = back * gain_ref[...]
        k_out[:, cols] = (
            inverse * (scaled - unit * jnp.mean(scaled * unit, axis=-1, keepdims=True))
        ).astype(BF16)
        v_out[:, cols] = g_ref[:, (2 * h + 1) * head_dim : (2 * h + 2) * head_dim].astype(BF16)
    gain_out[...] = jnp.broadcast_to(gain_total, gain_out.shape)


def keys_back(kv_heads, head_dim, grad_kv, proj, key_at, cos, sin, gain):
    span = proj.shape[0]
    cols = kv_heads * head_dim
    key_block = key_at // cols
    whole = lambda a, b: pl.BlockSpec((a, b), lambda i: (0, 0))
    out = pl.pallas_call(
        functools.partial(keys_back_kernel, kv_heads, head_dim),
        out_shape=(
            jax.ShapeDtypeStruct((span, cols), BF16),
            jax.ShapeDtypeStruct((span, cols), BF16),
            jax.ShapeDtypeStruct((8, head_dim), F32),
        ),
        grid=(1,),
        in_specs=[
            whole(span, 2 * cols),
            pl.BlockSpec((span, cols), lambda i: (0, key_block)),
            whole(span, head_dim),
            whole(span, head_dim),
            whole(1, head_dim),
        ],
        out_specs=(whole(span, cols), whole(span, cols), whole(8, head_dim)),
        compiler_params=params(),
        cost_estimate=cost(40 * span * cols, 16 * span * cols),
        name="keys_back",
    )(grad_kv, proj, cos, sin, gain)
    return out[0], out[1], out[2][0]


def norm_back(gradient, unit_vals, inverse, gain_vec):
    scaled = gradient * gain_vec
    return inverse * (scaled - unit_vals * jnp.mean(scaled * unit_vals, axis=-1, keepdims=True))


def per_device(
    links,
    hidden_in,
    lengths,
    attn_gain,
    q_weight,
    gate_weight,
    k_weight,
    v_weight,
    q_gain,
    k_gain,
    o_weight,
    mlp_gain,
    w_gate,
    w_up,
    w_down,
    out_grad,
):
    dp_index, ctx_index, z_index = (lax.axis_index(a) for a in ("dp", "ctx", "tensor"))
    q_cols, k_cols, ff_cols = q_weight.shape[1], k_weight.shape[1], w_down.shape[1]
    span, width = hidden_in.shape
    mid, count = width // 2, 2 * links.half
    shard, head_shard = attn_gain.shape[0], q_gain.shape[0]
    head_dim = head_shard * count
    heads, kv_heads = q_cols // head_dim, k_cols // head_dim
    group = heads // kv_heads
    length = lengths[0]
    low = lambda *mats: jnp.concatenate([m.astype(BF16) for m in mats], axis=1)

    small = jnp.concatenate([attn_gain, mlp_gain, q_gain, k_gain]).astype(BF16)[None, :]
    gains, seen = links.small_gather(small)
    first_own = after(low(q_weight, k_weight, gate_weight, v_weight, o_weight), *seen)
    first_single = links.send_own(first_own)
    first_pairs = links.send_on(first_single)
    feed_own = after(low(w_gate, w_up), *first_single.values())
    feed_single = links.send_own(feed_own)
    feed_pairs = links.send_on(feed_single)
    down_own = after(low(w_down), *feed_single.values())
    down_single = links.send_own(down_own)
    down_pairs = links.send_on(down_single)
    first_half = links.assemble(first_own, first_single, first_pairs)
    first_mat = (first_half, links.swap(first_half, "ctx", 1))
    feed_half = links.assemble(feed_own, feed_single, feed_pairs)
    feed_mat = (feed_half, links.swap(feed_half, "ctx", 1))
    down_half = links.assemble(down_own, down_single, down_pairs)
    down_mat = (down_half, links.swap(down_half, "ctx", 1))
    attn_scale = gains[:, :shard].reshape(1, width).astype(F32)
    mlp_scale = gains[:, shard : 2 * shard].reshape(1, width).astype(F32)
    owners = jnp.stack([links.owner_of(p, dp_index, ctx_index) for p in range(count)])
    pick = (owners[None, :] == jnp.arange(count)[:, None]).astype(BF16)
    head_gains = project(pick, gains[:, 2 * shard :])
    query_scale = head_gains[:, :head_shard].reshape(1, head_dim)
    key_scale = head_gains[:, head_shard:].reshape(1, head_dim)

    parts = 2 * links.tensor
    row_block = span // parts
    row_places = jnp.stack(
        [part * links.tensor + (z_index ^ j) for part in range(2) for j in links.turns]
    ).astype(jnp.int32)
    start = ctx_index * span
    scalars = jnp.concatenate(
        [row_places, owners.astype(jnp.int32), jnp.stack([start, length]).astype(jnp.int32)]
    )
    spots = (start + row_places[:, None] * row_block + jnp.arange(row_block)[None, :]).reshape(span)
    spots = spots.astype(jnp.int32)
    freq_steps = jnp.arange(head_dim // 2, dtype=F32) * (2.0 / head_dim)
    turned = spots.astype(F32)[:, None] * jnp.exp(-math.log(ROPE_BASE) * freq_steps)[None, :]
    cosine, sine = jnp.cos(turned), jnp.sin(turned)
    cos = jnp.concatenate([cosine, cosine], axis=1)
    sin = jnp.concatenate([-sine, sine], axis=1)
    spot_col, spot_row = spots[:, None], spots[None, :]

    stream, grad_out, down_grad, normed = enter(scalars, count, parts, span, hidden_in, out_grad, attn_scale)

    proj_cols = 2 * (q_cols + k_cols)
    both = lambda value, mats, a, b: project(value[:, :mid], mats[0][:, a:b]) + project(
        value[:, mid:], mats[1][:, a:b]
    )
    across = lambda value, mats: jnp.concatenate([col_contract(value, m).astype(BF16) for m in mats], axis=1)
    proj = both(normed, first_mat, 0, proj_cols)
    gate_at = q_cols + k_cols
    query, kv = prepare(heads, kv_heads, head_dim, proj, cos, sin, query_scale, key_scale)
    kvs, turns = [kv], [0]
    mask = links.ctx // 2
    while mask:
        kvs = kvs + [links.swap(b, "ctx", mask) for b in kvs]
        turns = turns + [p ^ mask for p in turns]
        mask //= 2
    at = jnp.stack([ctx_index, length]).astype(jnp.int32)
    half_rows = span // 2
    mixed, gated, sums, middle, normed_two, unit_two, inverse_two = ([None] * 2 for _ in range(7))
    out_mat = [m[:, proj_cols:] for m in first_mat]
    shard_rows = half_rows // links.tensor
    part_of = lambda value, t: value[t * half_rows : (t + 1) * half_rows]
    own_rows = lambda value, t: value[t * shard_rows : (t + 1) * shard_rows]
    live = [(part_of(spot_col, t)[:shard_rows] < length).astype(F32) for t in range(2)]
    query_now = after(query, *feed_single.values())
    for t in range(2):
        mixed[t], gated[t], sums[t] = attend(
            at, t, 2, group, head_dim, turns, query_now, proj, gate_at, spot_col, spot_row, kvs
        )
        attn_out = links.scatter_rows(across(gated[t], out_mat))
        middle[t] = own_rows(stream, t).astype(F32) + attn_out * live[t]
        if t == 0:
            middle[t] = after(middle[t], feed_half)
        inverse_two[t] = lax.rsqrt(jnp.mean(middle[t] * middle[t], axis=-1, keepdims=True) + EPSILON)
        unit_two[t] = middle[t] * inverse_two[t]
        normed_two[t] = links.gather_rows((unit_two[t] * mlp_scale).astype(BF16))

    grad_hidden = both(down_grad, down_mat, 0, ff_cols)
    normed_two[0] = after(normed_two[0], grad_hidden)
    hidden, grad_gate_in, grad_up_in, grad_middle, attn_grad = ([None] * 2 for _ in range(5))
    for t in range(2):
        gate_in = both(normed_two[t], feed_mat, 0, ff_cols)
        up_in = both(normed_two[t], feed_mat, ff_cols, 2 * ff_cols)
        grad_hid = part_of(grad_hidden, t)
        sig = jax.nn.sigmoid(gate_in)
        hidden[t] = (gate_in * sig * up_in).astype(BF16)
        grad_gate_in[t] = (grad_hid * up_in * sig * (1.0 + gate_in * (1.0 - sig))).astype(BF16)
        grad_up_in[t] = (grad_hid * (gate_in * sig)).astype(BF16)
        grad_feed = jnp.concatenate([grad_gate_in[t], grad_up_in[t]], axis=1)
        part = across(grad_feed, feed_mat)
        if t == 0:
            normed_two[1] = after(normed_two[1], part)
        back = links.scatter_rows(part)
        grad_mlp = jnp.sum(back * unit_two[t], axis=0)
        grad_mlp_gain = grad_mlp if t == 0 else grad_mlp_gain + grad_mlp
        grad_middle[t] = own_rows(grad_out, t).astype(F32) + norm_back(
            back, unit_two[t], inverse_two[t], mlp_scale
        )
        attn_grad[t] = links.gather_rows((grad_middle[t] * live[t]).astype(BF16))

    def weight_grad(rows_of, cols_of, turn):
        other = row_contract(rows_of[:, mid:], cols_of).astype(BF16)
        total = links.first_sum(row_contract(rows_of[:, :mid], cols_of), other)
        grad, seen = links.reduce(total, turn)
        return grad, total, seen

    whole = lambda pair: jnp.concatenate(pair, axis=0)
    rows_two, hidden_all = whole(normed_two), whole(hidden)
    ff_half = ff_cols // 2
    down_grads = [weight_grad(down_grad, hidden_all[:, i * ff_half : (i + 1) * ff_half], i) for i in range(2)]
    feed_grads = [weight_grad(rows_two, whole(g), i) for i, g in enumerate((grad_gate_in, grad_up_in))]

    olds = None
    grad_query, grad_gates, q_gain_part = [None] * 2, [None] * 2, 0.0
    attn_grad[0] = after(attn_grad[0], *(g[2][0] for g in down_grads), *(g[1] for g in feed_grads))
    down_part = after(across(hidden_all, down_mat), attn_grad[0])
    down_shard = [
        links.gather_rows((middle[t] + links.scatter_rows(part_of(down_part, t)) * live[t]).astype(BF16))
        for t in range(2)
    ]
    attn_grad[1] = after(attn_grad[1], *(g[0] for g in down_grads), *(g[2][0] for g in feed_grads))
    for t in range(2):
        grad_gated = both(attn_grad[t], out_mat, 0, q_cols)
        grad_query[t], grad_gates[t], gain_part, olds = attend_back(
            at, t, 2, group, head_dim, turns, query, proj, gate_at, mixed[t], sums[t], grad_gated,
            spot_row, spot_col, cos, sin, query_scale, kvs, olds,
        )
        q_gain_part = q_gain_part + gain_part
    pieces = dict(zip(turns, olds))
    mask = 1
    while len(pieces) > 1:
        near = [p for p in pieces if not p & mask]
        sent = jnp.concatenate([pieces[p ^ mask].astype(BF16) for p in near], axis=0)
        came = links.swap(sent, "ctx", mask).astype(F32)
        pieces = {p: pieces[p] + came[i * span : (i + 1) * span] for i, p in enumerate(near)}
        mask *= 2
    grad_kv = pieces[0]
    grad_key, grad_value, k_gain_part = keys_back(
        kv_heads, head_dim, grad_kv, proj, q_cols, cos, sin, key_scale
    )
    grad_proj = jnp.concatenate([whole(grad_query), grad_key, whole(grad_gates), grad_value], axis=1)
    out_half = q_cols // 2
    attn_all, gated_all = whole(attn_grad), whole(gated)
    out_grads = [weight_grad(attn_all, gated_all[:, i * out_half : (i + 1) * out_half], i) for i in range(2)]
    proj_half = proj_cols // 2
    proj_grads = [
        weight_grad(normed, grad_proj[:, i * proj_half : (i + 1) * proj_half], i) for i in range(2)
    ]
    grad_in, attn_gain_part = [None] * 2, 0.0
    for t in range(2):
        back = links.scatter_rows(across(part_of(grad_proj, t), [m[:, :proj_cols] for m in first_mat]))
        if t == 0:
            back = after(back, *(g[0] for g in feed_grads), *down_shard)
        x = own_rows(stream, t).astype(F32)
        inverse = lax.rsqrt(jnp.mean(x * x, axis=-1, keepdims=True) + EPSILON)
        unit = x * inverse
        attn_gain_part = attn_gain_part + jnp.sum(back * unit, axis=0)
        grad_in[t] = links.gather_rows(
            (grad_middle[t] + norm_back(back, unit, inverse, attn_scale)).astype(BF16)
        )
    hidden_out = leave(scalars, count, parts, whole(down_shard), BF16)
    grad_in = leave(scalars, count, parts, whole(grad_in), F32)

    blocks = jnp.stack([attn_gain_part.reshape(count, shard), grad_mlp_gain.reshape(count, shard)])
    to_mesh = (owners[None, :] == jnp.arange(count)[:, None]).astype(F32)
    blocks = jnp.einsum("ap,kpn->kan", to_mesh, blocks, precision=lax.Precision.HIGHEST)
    packed = jnp.concatenate([blocks.reshape(1, -1), q_gain_part[None, :], k_gain_part[None, :]], axis=1)
    packed = links.add_all(packed)[0]
    rank = dp_index * links.ctx + ctx_index
    take = lambda at, size: lax.dynamic_slice_in_dim(packed, at + rank * size, size)
    return (
        hidden_out,
        grad_in,
        take(0, shard),
        proj_grads[0][0][:, :q_cols],
        proj_grads[1][0][:, :q_cols],
        proj_grads[0][0][:, q_cols:],
        proj_grads[1][0][:, q_cols:],
        take(2 * width, head_shard),
        take(2 * width + head_dim, head_shard),
        jnp.concatenate([g[0] for g in out_grads], axis=1),
        take(width, shard),
        feed_grads[0][0],
        feed_grads[1][0],
        jnp.concatenate([g[0] for g in down_grads], axis=1),
    )


def solution(mesh):
    links = Links(dict(mesh.shape))
    rows = P(("dp", "ctx"))
    plain = P(("dp", "ctx"), None)
    split = P(("dp", "ctx"), "tensor")

    def step(*arrays):
        return per_device(links, *arrays)

    return jax.shard_map(
        step,
        mesh=mesh,
        in_specs=(plain, P("dp"), rows, split, split, split, split, rows, rows, split, rows, split, split, split, plain),
        out_specs=(plain, plain, rows, split, split, split, split, rows, rows, split, rows, split, split, split),
        check_vma=False,
    )
```

```python
import functools
import math

import jax
import jax.numpy as jnp
from jax import lax
from jax.experimental import pallas as pl
from jax.experimental.pallas import tpu as pltpu
from jax.sharding import PartitionSpec as P

EPSILON = 1e-06
ROPE_BASE = 1000000.0
CONTRACT_ROWS = (((0,), (0,)), ((), ()))
CONTRACT_COLS = (((1,), (1,)), ((), ()))
F32 = jnp.float32
BF16 = jnp.bfloat16
VMEM_BYTES = 56 * 1024 * 1024


def project(operand, matrix):
    return jnp.dot(operand, matrix, preferred_element_type=F32)


def row_contract(first_op, second_op):
    return lax.dot_general(first_op, second_op, CONTRACT_ROWS, preferred_element_type=F32)


def col_contract(first_op, second_op):
    return lax.dot_general(first_op, second_op, CONTRACT_COLS, preferred_element_type=F32)


def sigmoid(value):
    return 1.0 / (1.0 + jnp.exp(-value))


def after(value, *others):
    if not others:
        return value
    return lax.optimization_barrier((value,) + others)[0]


def cost(flops, moved, exps=0):
    return pl.CostEstimate(flops=int(flops) // 64, bytes_accessed=int(moved) // 64, transcendentals=int(exps) // 64)


def params(**kwargs):
    return pltpu.CompilerParams(vmem_limit_bytes=VMEM_BYTES, **kwargs)


class Links:
    def __init__(self, sizes):
        self.dp, self.ctx, self.tensor = sizes["dp"], sizes["ctx"], sizes["tensor"]
        self.half = self.dp * self.ctx // 2
        ctx_bits = int(math.log2(self.ctx // 2))
        dp_bits = int(math.log2(self.dp))
        self.bits = [("ctx", 2 << i) for i in range(ctx_bits)] + [("dp", 1 << i) for i in range(dp_bits)]
        self.masks = [(2 << i) - 1 for i in range(int(math.log2(self.tensor)))]
        self.turns = [0]
        for mask in reversed(self.masks):
            self.turns = self.turns + [j ^ mask for j in self.turns]

    def swap(self, value, axis, mask):
        count = {"dp": self.dp, "ctx": self.ctx, "tensor": self.tensor}[axis]
        return lax.ppermute(value, axis, [(i, i ^ mask) for i in range(count)])

    def order(self, turn):
        places = list(range(len(self.bits)))
        return places if turn else places[::-1]

    def send_own(self, blocks):
        return {1 << p: self.swap(blocks[p], *self.bits[p]) for p in self.order(0)}

    def send_far(self, block):
        count = self.dp * self.ctx
        single = {}
        for q in range(1, self.half):
            far = (q // (self.ctx // 2)) * self.ctx + (q % (self.ctx // 2)) * 2
            single[q] = lax.ppermute(block, ("dp", "ctx"), [(i, i ^ far) for i in range(count)])
        return single

    def send_on(self, single):
        mid = next(iter(single.values())).shape[1] // 2
        left = {q: b[:, :mid] for q, b in single.items()}
        right = {q: b[:, mid:] for q, b in single.items()}
        for side, places in ((left, self.order(0)), (right, self.order(1))):
            for q in range(1, self.half):
                if q not in single:
                    self.reach(side, q, places)
        return {q: (left[q], right[q]) for q in left if q not in single}

    def assemble(self, block, single, pairs):
        blocks, groups = [], []
        for q in range(self.half):
            members = [block] if q == 0 else [single[q]] if q in single else list(pairs[q])
            groups.append(tuple(range(len(blocks), len(blocks) + len(members))))
            blocks += members
        return stack_blocks(groups, blocks)

    def reach(self, side, q, places):
        if q not in side:
            last = [p for p in places if q & (1 << p)][-1]
            self.reach(side, q ^ (1 << last), places)
            side[q] = self.swap(side[q ^ (1 << last)], *self.bits[last])

    def reduce_first(self, total, turn, *hold):
        rows = total.shape[0] // self.half
        pieces = {q: total[q * rows : (q + 1) * rows] for q in range(self.half)}
        return self.reduce_step(pieces, turn, 0, *hold)

    def reduce_step(self, pieces, turn, step, *hold):
        place = self.order(turn)[step]
        bit = 1 << place
        kept = {q: b for q, b in pieces.items() if not q & bit}
        gone = [pieces[q | bit].astype(BF16) for q in kept]
        gone[0] = after(gone[0], *hold)
        return kept, gone, self.swap(jnp.concatenate(gone, axis=0), *self.bits[place])

    def reduce_rest(self, kept, came, turn):
        gone = []
        for step in range(1, len(self.bits) + 1):
            rows = came.shape[0] // len(kept)
            pieces = {
                q: b.astype(F32) + came[i * rows : (i + 1) * rows].astype(F32) for i, (q, b) in enumerate(kept.items())
            }
            if step < len(self.bits):
                kept, sent, came = self.reduce_step(pieces, turn, step)
                gone += sent
        return pieces[0], gone, came

    def small_gather(self, row):
        far = self.send_far(row)
        own = jnp.concatenate([row] + [far[q] for q in range(1, self.half)], axis=0)
        return jnp.concatenate([own, self.swap(own, "ctx", 1)], axis=0), list(far.values())

    def owner_of(self, position, dp_index, ctx_index):
        h, q = position // self.half, position % self.half
        dp_far, ctx_far = q // (self.ctx // 2), (q % (self.ctx // 2)) * 2 + h
        return (dp_index ^ dp_far) * self.ctx + (ctx_index ^ ctx_far)

    def scatter_first(self, part):
        rows = part.shape[0] // 2
        return part[:rows], self.swap(part[rows:], "tensor", self.masks[0])

    def scatter_rest(self, kept, came, before=(), late=()):
        gone = seen = came
        kept = kept.astype(F32) + came.astype(F32)
        for mask in self.masks[1:]:
            rows = kept.shape[0] // 2
            gone = kept[rows:].astype(BF16)
            seen = self.swap(after(gone, *before), "tensor", mask)
            kept = kept[:rows] + after(seen, *late).astype(F32)
        return kept, seen

    def gather_first(self, shard):
        return shard, self.swap(shard, "tensor", self.masks[-1])

    def gather_rest(self, shard, came, late=()):
        came = after(came, *late)
        for mask in self.masks[-2::-1]:
            shard = jnp.concatenate([shard, came], axis=0)
            came = self.swap(shard, "tensor", mask)
        return shard, came

    def add_all(self, value, *before):
        value = value + self.swap(value, "ctx", 1)
        for axis, mask in self.bits:
            value = value + self.swap(value, axis, mask)
        value = after(value, *before)
        for mask in self.masks:
            value = value + self.swap(value, "tensor", mask)
        return value


def still(scalars, count, parts):
    owners = scalars[parts : parts + count]
    return owners, lax.dynamic_update_slice(scalars, jnp.arange(count, dtype=scalars.dtype), (parts,))


def columns(value, owners):
    count = owners.shape[0]
    blocks = value.reshape(value.shape[0], count, value.shape[1] // count)
    return jnp.take(blocks, owners, axis=1).reshape(value.shape)


def column_place(scalars, parts, p, size):
    if size % 128:
        return pl.ds(p * size, size)
    return pl.ds(pl.multiple_of(scalars[parts + p] * size, size), size)


def stack_kernel(groups, *refs):
    out_ref = refs[-1]
    for q, group in enumerate(groups):

        @pl.when(pl.program_id(0) == q)
        def _(group=group):
            col = 0
            for i in group:
                out_ref[:, col : col + refs[i].shape[1]] = refs[i][...]
                col += refs[i].shape[1]


def stack_blocks(groups, blocks):
    rows, n = blocks[0].shape
    held = lambda b: pl.BlockSpec(b.shape, lambda i: (0, 0), pipeline_mode=pl.Buffered(1))
    return pl.pallas_call(
        functools.partial(stack_kernel, groups),
        out_shape=jax.ShapeDtypeStruct((rows * len(groups), n), blocks[0].dtype),
        grid=(len(groups),),
        in_specs=[held(b) for b in blocks],
        out_specs=pl.BlockSpec((rows, n), lambda i: (i, 0)),
        compiler_params=params(),
        cost_estimate=cost(0, 4 * rows * len(groups) * n),
        name="stack",
    )(*blocks)


def enter_kernel(count, parts, scalars, xa_ref, xb_ref, ga_ref, gb_ref, gain_ref, x_out, g_out, m_out, n_out):
    step = pl.program_id(0)
    rows, width = xa_ref.shape
    size = width // count
    for part, (x_ref, g_ref) in enumerate(((xa_ref, ga_ref), (xb_ref, gb_ref))):
        places = [column_place(scalars, parts, p, size) for p in range(count)]
        x = jnp.concatenate([x_ref[:, place] for place in places], axis=1)
        g = jnp.concatenate([g_ref[:, place] for place in places], axis=1)
        if part == 0:

            @pl.when(step % (parts // 4) == 0)
            def _(x=x, g=g):
                x_out[...] = x
                g_out[...] = g

        place = slice(part * rows, (part + 1) * rows)
        spot = scalars[parts + count] + scalars[2 * step + part] * rows
        live = spot + lax.broadcasted_iota(jnp.int32, (rows, 1), 0) < scalars[parts + count + 1]
        m_out[place, :] = jnp.where(live, g.astype(F32), 0.0).astype(BF16)
        wide = x.astype(F32)
        inverse = lax.rsqrt(jnp.mean(wide * wide, axis=-1, keepdims=True) + EPSILON)
        n_out[place, :] = (wide * inverse * gain_ref[...]).astype(BF16)


def enter(scalars, count, parts, span, hidden_in, out_grad, gain):
    rows, width = span // parts, hidden_in.shape[1]
    if width // count % 128:
        owners, scalars = still(scalars, count, parts)
        hidden_in, out_grad = columns(hidden_in, owners), columns(out_grad, owners)
    upper = pl.BlockSpec((rows, width), lambda i, s: (s[2 * i], 0))
    lower = pl.BlockSpec((rows, width), lambda i, s: (s[2 * i + 1], 0))
    own = pl.BlockSpec((rows, width), lambda i, s: (i // (parts // 4), 0))
    plain = pl.BlockSpec((2 * rows, width), lambda i, s: (i, 0))
    shape = jax.ShapeDtypeStruct((span, width), BF16)
    short = jax.ShapeDtypeStruct((2 * rows, width), BF16)
    return pl.pallas_call(
        functools.partial(enter_kernel, count, parts),
        out_shape=(short, short, shape, shape),
        grid_spec=pltpu.PrefetchScalarGridSpec(
            num_scalar_prefetch=1,
            grid=(parts // 2,),
            in_specs=[upper, lower, upper, lower, pl.BlockSpec((1, width), lambda i, s: (0, 0))],
            out_specs=(own, own, plain, plain),
        ),
        compiler_params=params(),
        cost_estimate=cost(10 * span * width, 8 * span * width),
        name="enter",
    )(scalars, hidden_in, hidden_in, out_grad, out_grad, gain)


def leave_kernel(count, parts, scalars, *refs):
    pieces, out_ref = refs[:4], refs[4]
    blocks, size = parts // 4, out_ref.shape[1] // count
    rows = out_ref.shape[0] // parts
    for i, in_ref in enumerate(pieces):

        @pl.when(pl.program_id(0) == i)
        def _(i=i, in_ref=in_ref):
            for part in range(blocks):
                at = pl.ds(pl.multiple_of(scalars[i * blocks + part] * rows, rows), rows)
                for p in range(count):
                    block = in_ref[part * rows : (part + 1) * rows, p * size : (p + 1) * size]
                    out_ref[at, column_place(scalars, parts, p, size)] = block.astype(out_ref.dtype)


def leave(scalars, count, parts, pieces, dtype):
    rows, width = pieces[0].shape
    place = lambda k: lambda i, s: (0, 0)
    if len(pieces) == 1:
        rows, pieces = rows // 4, pieces * 4
        place = lambda k: lambda i, s: (k, 0)
    if width // count % 128:
        owners, scalars = still(scalars, count, parts)
        pieces = [columns(piece, jnp.argsort(owners)) for piece in pieces]
    return pl.pallas_call(
        functools.partial(leave_kernel, count, parts),
        out_shape=jax.ShapeDtypeStruct((4 * rows, width), dtype),
        grid_spec=pltpu.PrefetchScalarGridSpec(
            num_scalar_prefetch=1,
            grid=(4,),
            in_specs=[pl.BlockSpec((rows, width), place(k)) for k in range(4)],
            out_specs=pl.BlockSpec((4 * rows, width), lambda i, s: (0, 0)),
        ),
        compiler_params=params(),
        cost_estimate=cost(0, 24 * rows * width),
        name="leave",
    )(scalars, *pieces)


def spread_kernel(tiles, count, parts, summed, *refs):
    homes, refs = (refs[0], refs[1:]) if parts else (None, refs)
    values, out_ref = refs[:count], refs[3 * count + summed]
    for h in range(2):

        @pl.when(pl.program_id(0) // tiles == h)
        def _(h=h):
            total = None
            for k in range(count):
                term = lax.dot_general(
                    values[k][...], refs[count + 2 * k + h][...], CONTRACT_COLS, preferred_element_type=F32
                )
                total = term if total is None else total + term
            if summed:
                norm_ref, sum_ref = refs[3 * count], refs[3 * count + 2]
                gain = jnp.sum(total * norm_ref[...].astype(F32), axis=0, keepdims=True)
                sum_ref[...] = jnp.broadcast_to(gain, sum_ref.shape)
            if parts:
                rows = out_ref.shape[0] // parts
                for i in range(parts):
                    at = pl.ds(pl.multiple_of(homes[i] * rows, rows), rows)
                    out_ref[at, :] = total[i * rows : (i + 1) * rows].astype(BF16)
            else:
                out_ref[...] = total.astype(BF16)


def spread(name, terms, part=0, parts=1, homes=None, normed=None):
    rows = terms[0][0].shape[0] // parts
    mid = terms[0][1][0].shape[0]
    tile = mid // 2
    specs, mats = [], []
    for value, pair, start in terms:
        n = value.shape[1]
        specs += [
            pl.BlockSpec((tile, n), lambda j, *s, c=start // n: (jnp.minimum(j, 1), c)),
            pl.BlockSpec((tile, n), lambda j, *s, c=start // n: (jnp.maximum(j - 2, 0), c)),
        ]
        mats += list(pair)
    held = [pl.BlockSpec((rows, v.shape[1]), lambda j, *s: (part, 0)) for v, _, _ in terms]
    wide = sum(v.shape[1] for v, _, _ in terms)
    summed = normed is not None
    shapes = [jax.ShapeDtypeStruct((rows, 2 * mid), BF16)]
    outs = [pl.BlockSpec((rows, tile), lambda j, *s: (0, j))]
    extra = []
    if summed:
        extra = [normed]
        specs.append(pl.BlockSpec((rows, tile), lambda j, *s: (part, j)))
        shapes.append(jax.ShapeDtypeStruct((8, 2 * mid), F32))
        outs.append(pl.BlockSpec((8, tile), lambda j, *s: (0, j)))
    out = pl.pallas_call(
        functools.partial(spread_kernel, 2, len(terms), 0 if homes is None else homes.shape[0], summed),
        out_shape=shapes,
        grid_spec=pltpu.PrefetchScalarGridSpec(
            num_scalar_prefetch=0 if homes is None else 1, grid=(4,), in_specs=held + specs, out_specs=outs
        ),
        compiler_params=params(),
        cost_estimate=cost(4 * rows * mid * wide, 2 * wide * (rows + 2 * mid) + 4 * rows * mid),
        name=name,
    )(*(() if homes is None else (homes,)), *(v for v, _, _ in terms), *mats, *extra)
    return out if summed else out[0]


def feed_kernel(first, a_ref, b_ref, go_ref, gf_ref, uo_ref, uf_ref, gh_ref, *refs):
    refs = refs if first else refs[4:]
    hidden_out, gate_out, up_out, rows_out, part_out, x_ref, acc_ref = refs
    step, mid = pl.program_id(0), x_ref.shape[1] // 2

    @pl.when(step == 0)
    def _():
        rows = a_ref.shape[0]
        x_ref[:rows, :] = a_ref[...]
        x_ref[rows:, :] = b_ref[...]
        rows_out[...] = x_ref[...]
        acc_ref[...] = jnp.zeros_like(acc_ref)

    near, far = x_ref[:, :mid], x_ref[:, mid:]
    gate = project(near, go_ref[...]) + project(far, gf_ref[...])
    up = project(near, uo_ref[...]) + project(far, uf_ref[...])
    grad = gh_ref[...]
    sig = sigmoid(gate)
    hidden_out[...] = (gate * sig * up).astype(BF16)
    grad_gate = (grad * up * sig * (1.0 + gate * (1.0 - sig))).astype(BF16)
    grad_up = (grad * (gate * sig)).astype(BF16)
    gate_out[...] = grad_gate
    up_out[...] = grad_up
    acc_ref[:, :mid] += col_contract(grad_gate, go_ref[...]) + col_contract(grad_up, uo_ref[...])
    acc_ref[:, mid:] += col_contract(grad_gate, gf_ref[...]) + col_contract(grad_up, uf_ref[...])

    @pl.when(step == pl.num_programs(0) - 1)
    def _():
        part_out[...] = acc_ref[...].astype(BF16)


def feed(part, pieces, mats, grad_hidden, olds):
    span, ff = grad_hidden.shape
    piece, width = pieces[0].shape
    rows, mid = 2 * piece, width // 2
    tile = 256 if ff % 256 == 0 else ff
    steps = ff // tile
    held = pl.BlockSpec((piece, width), lambda j: (0, 0))
    mat = lambda shift: pl.BlockSpec((mid, tile), lambda j: (0, shift + j))
    cols = pl.BlockSpec((rows, tile), lambda j: (part, j))
    first = olds is None
    olds = () if first else tuple(olds)
    wide = jax.ShapeDtypeStruct((span, ff), BF16)
    out = pl.pallas_call(
        functools.partial(feed_kernel, first),
        out_shape=(
            wide,
            wide,
            wide,
            jax.ShapeDtypeStruct((span, width), BF16),
            jax.ShapeDtypeStruct((rows, width), BF16),
        ),
        grid=(steps,),
        in_specs=[held, held, mat(0), mat(0), mat(steps), mat(steps), cols]
        + [pl.BlockSpec(memory_space=pl.ANY)] * len(olds),
        out_specs=(
            cols,
            cols,
            cols,
            pl.BlockSpec((rows, width), lambda j: (part, 0)),
            pl.BlockSpec((rows, width), lambda j: (0, 0)),
        ),
        scratch_shapes=[pltpu.VMEM((rows, width), BF16), pltpu.VMEM((rows, width), F32)],
        input_output_aliases={7 + i: i for i in range(len(olds))},
        compiler_params=params(),
        cost_estimate=cost(8 * rows * width * ff, 8 * width * ff, 2 * rows * ff),
        name="feed",
    )(*pieces, mats[0], mats[1], mats[0], mats[1], grad_hidden, *olds)
    return out[:4], out[4]


def unit_of(value):
    inverse = lax.rsqrt(jnp.mean(value * value, axis=-1, keepdims=True) + EPSILON)
    return value * inverse, inverse


def turn(value, cos_ref, sin_ref, sign):
    half = value.shape[-1] // 2
    return value * cos_ref[...] + sign * pltpu.roll(value, half, 1) * sin_ref[...]


def prepare_queries_kernel(head_dim, p_ref, cos_ref, sin_ref, gain_ref, out_ref):
    for h in range(p_ref.shape[1] // head_dim):
        cols = slice(h * head_dim, (h + 1) * head_dim)
        unit, _ = unit_of(p_ref[:, cols])
        out_ref[:, cols] = turn(unit * gain_ref[...], cos_ref, sin_ref, 1.0).astype(BF16)


def prepare_keys_kernel(head_dim, p_ref, cos_ref, sin_ref, gain_ref, out_ref):
    heads = p_ref.shape[1] // head_dim // 2
    for h in range(heads):
        unit, _ = unit_of(p_ref[:, h * head_dim : (h + 1) * head_dim])
        turned = turn(unit * gain_ref[...], cos_ref, sin_ref, 1.0).astype(BF16)
        out_ref[:, 2 * h * head_dim : (2 * h + 1) * head_dim] = turned
        value = p_ref[:, (heads + h) * head_dim : (heads + h + 1) * head_dim]
        out_ref[:, (2 * h + 1) * head_dim : (2 * h + 2) * head_dim] = value.astype(BF16)


def prepare(body, name, head_dim, cols, proj, cos, sin, gain):
    span = proj.shape[0]
    rows = span // 2
    spec = lambda n: pl.BlockSpec((rows, n), lambda i: (i, 0))
    return pl.pallas_call(
        functools.partial(body, head_dim),
        out_shape=jax.ShapeDtypeStruct((span, cols), BF16),
        grid=(2,),
        in_specs=[spec(cols), spec(head_dim), spec(head_dim), pl.BlockSpec((1, head_dim), lambda i: (0, 0))],
        out_specs=spec(cols),
        compiler_params=params(),
        cost_estimate=cost(20 * span * cols, 6 * span * cols),
        name=name,
    )(proj, cos, sin, gain)


def attend_kernel(group, head_dim, turns, first, scalars, q_ref, gate_ref, spot_ref, key_ref, oo_ref, of_ref, *refs):
    blocks = len(turns)
    kv_refs = refs[:blocks]
    rest = refs[blocks:] if first else refs[blocks + 1 :]
    mixed_out, sum_out, gated_out, part_out, acc_ref, total_ref, out_acc = rest
    scale = head_dim**-0.5 * math.log2(math.e)
    own = scalars[0]
    step, mid = pl.program_id(0), out_acc.shape[1] // 2

    @pl.when(step == 0)
    def _():
        out_acc[...] = jnp.zeros_like(out_acc)

    for h in range(group):
        cols = slice(h * head_dim, (h + 1) * head_dim)
        query = q_ref[:, cols]

        def scores(ref):
            return lax.dot_general(query, ref[:, :head_dim], CONTRACT_COLS, preferred_element_type=F32)

        allowed = (key_ref[...] <= spot_ref[...]) & (key_ref[...] < scalars[1])
        terms = jnp.where(allowed, jnp.exp2(scores(kv_refs[0]) * scale), 0.0)
        total_ref[...] = jnp.sum(terms, axis=-1, keepdims=True)
        acc_ref[...] = project(terms.astype(BF16), kv_refs[0][:, head_dim:])
        for place in range(1, blocks):

            @pl.when((own ^ turns[place]) < own)
            def _(ref=kv_refs[place]):
                terms = jnp.exp2(scores(ref) * scale)
                total_ref[...] += jnp.sum(terms, axis=-1, keepdims=True)
                acc_ref[...] += project(terms.astype(BF16), ref[:, head_dim:])

        mixed = acc_ref[...] / total_ref[...]
        mixed_out[:, cols] = mixed
        gated_out[:, cols] = (mixed * sigmoid(gate_ref[:, cols])).astype(BF16)
        sum_out[:, cols] = jnp.broadcast_to(total_ref[...], mixed.shape)
    gated = gated_out[...]
    out_acc[:, :mid] += col_contract(gated, oo_ref[...])
    out_acc[:, mid:] += col_contract(gated, of_ref[...])

    @pl.when(step == pl.num_programs(0) - 1)
    def _():
        part_out[...] = out_acc[...].astype(BF16)


def attend(scalars, part, parts, group, head_dim, turns, query, proj, gate_at, spots, keys, mats, out_at, kvs, old):
    span, width = query.shape
    rows, wide, mid = span // parts, group * head_dim, mats[0].shape[0]
    head = pl.BlockSpec((rows, wide), lambda g, s: (part, g))
    out = pl.BlockSpec((rows, wide), lambda g, s: (0, g))
    mat = pl.BlockSpec((mid, wide), lambda g, s: (0, out_at // wide + g))
    first = old is None
    olds = () if first else (old,)
    return pl.pallas_call(
        functools.partial(attend_kernel, group, head_dim, turns, first),
        out_shape=(
            jax.ShapeDtypeStruct((rows, width), F32),
            jax.ShapeDtypeStruct((rows, width), F32),
            jax.ShapeDtypeStruct((span, width), BF16),
            jax.ShapeDtypeStruct((rows, 2 * mid), BF16),
        ),
        grid_spec=pltpu.PrefetchScalarGridSpec(
            num_scalar_prefetch=1,
            grid=(width // wide,),
            in_specs=[
                head,
                pl.BlockSpec((rows, wide), lambda g, s: (part, gate_at // wide + g)),
                pl.BlockSpec((rows, 1), lambda g, s: (part, 0)),
                pl.BlockSpec((1, span), lambda g, s: (0, 0)),
                mat,
                mat,
            ]
            + [pl.BlockSpec((span, 2 * head_dim), lambda g, s: (0, g))] * len(kvs)
            + [pl.BlockSpec(memory_space=pl.ANY)] * len(olds),
            out_specs=(out, out, head, pl.BlockSpec((rows, 2 * mid), lambda g, s: (0, 0))),
            scratch_shapes=[
                pltpu.VMEM((rows, head_dim), F32),
                pltpu.VMEM((rows, 1), F32),
                pltpu.VMEM((rows, 2 * mid), F32),
            ],
        ),
        input_output_aliases={7 + len(kvs): 2} if olds else {},
        compiler_params=params(),
        cost_estimate=cost(
            4 * rows * width * span * len(kvs) + 4 * rows * width * mid,
            4 * span * width * len(kvs) + 20 * rows * width + 4 * mid * width,
            rows * span * len(kvs) * width // head_dim,
        ),
        name="attend",
    )(scalars, query, proj, spots, keys, *mats, *kvs, *olds)


def attend_back_kernel(group, head_dim, turns, first, scalars, *refs):
    blocks = len(turns)
    q_ref, query_ref, gate_ref, mixed_ref, sum_ref, a_ref, b_ref, oo_ref, of_ref = refs[:9]
    spot_ref, key_ref, cos_ref, sin_ref, gain_ref = refs[9:14]
    kv_refs = refs[14 : 14 + blocks]
    rest = refs[14 + blocks :]
    old_refs = () if first else rest[:blocks]
    rest = rest if first else rest[blocks + 3 :]
    gq_out, ggate_out, rows_out, gain_out = rest[:4]
    new_refs = rest[4 : 4 + blocks]
    gq_ref, x_ref = rest[4 + blocks :]
    mid = x_ref.shape[1] // 2

    @pl.when(pl.program_id(0) == 0)
    def _():
        piece = a_ref.shape[0]
        x_ref[:piece, :] = a_ref[...]
        x_ref[piece:, :] = b_ref[...]
        rows_out[...] = x_ref[...]

    all_gated = project(x_ref[:, :mid], oo_ref[...]) + project(x_ref[:, mid:], of_ref[...])
    score_scale = head_dim**-0.5
    scale = score_scale * math.log2(math.e)
    own = scalars[0]
    rows = q_ref.shape[0]

    def as_row(column):
        return jnp.transpose(jnp.broadcast_to(column, (rows, head_dim)))[:1, :]

    for place in range(blocks):
        if first:
            new_refs[place][...] = jnp.zeros_like(new_refs[place])
        else:
            new_refs[place][...] = old_refs[place][...]
    gain_total = jnp.zeros((1, head_dim), F32)
    for h in range(group):
        cols = slice(h * head_dim, (h + 1) * head_dim)
        query = q_ref[:, cols]
        gate = sigmoid(gate_ref[:, cols])
        grad_gated, mixed = all_gated[:, cols], mixed_ref[:, cols]
        grad_mixed = (grad_gated * gate).astype(BF16)
        ggate_out[:, cols] = (grad_gated * mixed * gate * (1.0 - gate)).astype(BF16)
        row_dot = as_row(jnp.sum(grad_mixed.astype(F32) * mixed, axis=-1, keepdims=True))
        row_log = as_row(jnp.log2(sum_ref[:, cols][:, :1]))
        gq_ref[...] = jnp.zeros_like(gq_ref)

        def block(kv_ref, new_ref, masked):
            key, value = kv_ref[:, :head_dim], kv_ref[:, head_dim:]
            scores = lax.dot_general(key, query, CONTRACT_COLS, preferred_element_type=F32)
            probs = jnp.exp2(scores * scale - row_log)
            if masked:
                allowed = (key_ref[...] <= spot_ref[...]) & (key_ref[...] < scalars[1])
                probs = jnp.where(allowed, probs, 0.0)
            grad_probs = lax.dot_general(value, grad_mixed, CONTRACT_COLS, preferred_element_type=F32)
            grad_scores = (probs * (grad_probs - row_dot)).astype(BF16)
            new_ref[:, head_dim:] += project(probs.astype(BF16), grad_mixed)
            new_ref[:, :head_dim] += project(grad_scores, query)
            gq_ref[...] += lax.dot_general(grad_scores, key, CONTRACT_ROWS, preferred_element_type=F32)

        block(kv_refs[0], new_refs[0], True)
        for place in range(1, blocks):

            @pl.when((own ^ turns[place]) < own)
            def _(place=place):
                block(kv_refs[place], new_refs[place], False)

        unit, inverse = unit_of(query_ref[:, cols])
        back = turn(gq_ref[...] * score_scale, cos_ref, sin_ref, -1.0)
        gain_total = gain_total + jnp.sum(back * unit, axis=0, keepdims=True)
        scaled = back * gain_ref[...]
        gq_out[:, cols] = (
            inverse * (scaled - unit * jnp.mean(scaled * unit, axis=-1, keepdims=True))
        ).astype(BF16)
    gain_out[...] = jnp.broadcast_to(gain_total, gain_out.shape)


def attend_back(
    scalars, part, parts, group, head_dim, turns, query, proj, gate_at, mixed, sums, pieces, mats, out_at, spots, keys, cos, sin, gain, kvs, olds
):
    span, width = query.shape
    rows, wide = span // parts, group * head_dim
    blocks, mid = len(kvs), mats[0].shape[0]
    mine = pl.BlockSpec((rows, wide), lambda g, s: (part, g))
    local = pl.BlockSpec((rows, wide), lambda g, s: (0, g))
    table = pl.BlockSpec((rows, head_dim), lambda g, s: (part, 0))
    pair = pl.BlockSpec((span, 2 * head_dim), lambda g, s: (0, g))
    piece = pl.BlockSpec(pieces[0].shape, lambda g, s: (0, 0))
    mat = pl.BlockSpec((mid, wide), lambda g, s: (0, out_at // wide + g))
    first = olds is None
    olds = () if first else tuple(olds)
    kv_shape = jax.ShapeDtypeStruct(kvs[0].shape, F32)
    steps = width // wide
    before = 15 + blocks
    out = pl.pallas_call(
        functools.partial(attend_back_kernel, group, head_dim, turns, first),
        out_shape=(
            jax.ShapeDtypeStruct((span, width), BF16),
            jax.ShapeDtypeStruct((span, width), BF16),
            jax.ShapeDtypeStruct((span, 2 * mid), BF16),
            jax.ShapeDtypeStruct((8 * steps, head_dim), F32),
        )
        + (kv_shape,) * blocks,
        grid_spec=pltpu.PrefetchScalarGridSpec(
            num_scalar_prefetch=1,
            grid=(steps,),
            in_specs=[
                mine,
                mine,
                pl.BlockSpec((rows, wide), lambda g, s: (part, gate_at // wide + g)),
                local,
                local,
                piece,
                piece,
                mat,
                mat,
                pl.BlockSpec((1, rows), lambda g, s: (0, part)),
                pl.BlockSpec((span, 1), lambda g, s: (0, 0)),
                table,
                table,
                pl.BlockSpec((1, head_dim), lambda g, s: (0, 0)),
            ]
            + [pair] * (blocks + min(len(olds), blocks))
            + [pl.BlockSpec(memory_space=pl.ANY)] * max(len(olds) - blocks, 0),
            out_specs=(
                mine,
                mine,
                pl.BlockSpec((rows, 2 * mid), lambda g, s: (part, 0)),
                pl.BlockSpec((8, head_dim), lambda g, s: (g, 0)),
            )
            + (pair,) * blocks,
            scratch_shapes=[pltpu.VMEM((rows, head_dim), F32), pltpu.VMEM((rows, 2 * mid), BF16)],
        ),
        input_output_aliases={}
        if first
        else {**{before + i: 4 + i for i in range(blocks)}, **{before + blocks + i: i for i in range(3)}},
        compiler_params=params(),
        cost_estimate=cost(
            10 * rows * width * span * blocks + 4 * rows * width * mid,
            20 * span * width * blocks,
            rows * span * blocks * width // head_dim,
        ),
        name="attend_back",
    )(scalars, query, proj, proj, mixed, sums, *pieces, *mats, spots, keys, cos, sin, gain, *kvs, *olds)
    gain_part = sum(out[3][8 * g] for g in range(steps))
    return out[4:], out[:3], gain_part


def keys_back_kernel(kv_heads, head_dim, g_ref, p_ref, cos_ref, sin_ref, gain_ref, k_out, v_out, gain_out):
    gain_total = jnp.zeros((1, head_dim), F32)
    for h in range(kv_heads):
        cols = slice(h * head_dim, (h + 1) * head_dim)
        unit, inverse = unit_of(p_ref[:, cols])
        grad = g_ref[:, 2 * h * head_dim : (2 * h + 1) * head_dim] * head_dim**-0.5
        back = turn(grad, cos_ref, sin_ref, -1.0)
        gain_total = gain_total + jnp.sum(back * unit, axis=0, keepdims=True)
        scaled = back * gain_ref[...]
        k_out[:, cols] = (
            inverse * (scaled - unit * jnp.mean(scaled * unit, axis=-1, keepdims=True))
        ).astype(BF16)
        v_out[:, cols] = g_ref[:, (2 * h + 1) * head_dim : (2 * h + 2) * head_dim].astype(BF16)
    gain_out[...] = jnp.broadcast_to(gain_total, gain_out.shape)


def keys_back(kv_heads, head_dim, grad_kv, proj, key_at, cos, sin, gain):
    span = proj.shape[0]
    cols = kv_heads * head_dim
    key_block = key_at // cols
    whole = lambda a, b: pl.BlockSpec((a, b), lambda i: (0, 0))
    out = pl.pallas_call(
        functools.partial(keys_back_kernel, kv_heads, head_dim),
        out_shape=(
            jax.ShapeDtypeStruct((span, cols), BF16),
            jax.ShapeDtypeStruct((span, cols), BF16),
            jax.ShapeDtypeStruct((8, head_dim), F32),
        ),
        grid=(1,),
        in_specs=[
            whole(span, 2 * cols),
            pl.BlockSpec((span, cols), lambda i: (0, key_block)),
            whole(span, head_dim),
            whole(span, head_dim),
            whole(1, head_dim),
        ],
        out_specs=(whole(span, cols), whole(span, cols), whole(8, head_dim)),
        compiler_params=params(),
        cost_estimate=cost(40 * span * cols, 16 * span * cols),
        name="keys_back",
    )(grad_kv, proj, cos, sin, gain)
    return out[0], out[1], out[2][0]


def norm_back(gradient, unit_vals, inverse, gain_vec):
    scaled = gradient * gain_vec
    return inverse * (scaled - unit_vals * jnp.mean(scaled * unit_vals, axis=-1, keepdims=True))


def per_device(
    links,
    hidden_in,
    lengths,
    attn_gain,
    q_weight,
    gate_weight,
    k_weight,
    v_weight,
    q_gain,
    k_gain,
    o_weight,
    mlp_gain,
    w_gate,
    w_up,
    w_down,
    out_grad,
):
    dp_index, ctx_index, z_index = (lax.axis_index(a) for a in ("dp", "ctx", "tensor"))
    q_cols, k_cols, ff_cols = q_weight.shape[1], k_weight.shape[1], w_down.shape[1]
    span, width = hidden_in.shape
    mid, count = width // 2, 2 * links.half
    shard, head_shard = attn_gain.shape[0], q_gain.shape[0]
    head_dim = head_shard * count
    heads, kv_heads = q_cols // head_dim, k_cols // head_dim
    group = heads // kv_heads
    length = lengths[0]
    low = lambda *mats: jnp.concatenate([m.astype(BF16) for m in mats], axis=1)

    small = jnp.concatenate([attn_gain, mlp_gain, q_gain, k_gain]).astype(BF16)[None, :]
    gains, seen = links.small_gather(small)
    feed_low, down_low = low(w_gate, w_up), low(w_down)
    everywhere = lambda block: {p: block for p in range(len(links.bits))}
    paired = lambda half: (half, links.swap(half, "ctx", 1))
    kv_own = after(low(k_weight, v_weight), *seen)
    kv_far = links.send_far(kv_own)
    attn_scale = gains[:, :shard].reshape(1, width).astype(F32)
    mlp_scale = gains[:, shard : 2 * shard].reshape(1, width).astype(F32)
    owners = jnp.stack([links.owner_of(p, dp_index, ctx_index) for p in range(count)])
    pick = (owners[None, :] == jnp.arange(count)[:, None]).astype(BF16)
    head_gains = project(pick, gains[:, 2 * shard :])
    query_scale = head_gains[:, :head_shard].reshape(1, head_dim)
    key_scale = head_gains[:, head_shard:].reshape(1, head_dim)

    parts = 2 * links.tensor
    row_block = span // parts
    row_places = jnp.stack(
        [part * links.tensor + (z_index ^ j) for part in range(2) for j in links.turns]
    ).astype(jnp.int32)
    start = ctx_index * span
    scalars = jnp.concatenate(
        [row_places, owners.astype(jnp.int32), jnp.stack([start, length]).astype(jnp.int32)]
    )
    spots = (start + row_places[:, None] * row_block + jnp.arange(row_block)[None, :]).reshape(span)
    spots = spots.astype(jnp.int32)
    freq_steps = jnp.arange(head_dim // 2, dtype=F32) * (2.0 / head_dim)
    turned = spots.astype(F32)[:, None] * jnp.exp(-math.log(ROPE_BASE) * freq_steps)[None, :]
    cosine, sine = jnp.cos(turned), jnp.sin(turned)
    cos = jnp.concatenate([cosine, cosine], axis=1)
    sin = jnp.concatenate([-sine, sine], axis=1)
    spot_col, spot_row = spots[:, None], spots[None, :]

    first_own = after(low(q_weight, gate_weight, o_weight), kv_far[1])
    stream, grad_out, down_grad, normed = enter(
        scalars, count, parts, span, hidden_in, out_grad, after(attn_scale, first_own)
    )

    both = lambda value, mats, a, b: project(value[:, :mid], mats[0][:, a:b]) + project(
        value[:, mid:], mats[1][:, a:b]
    )
    kv_mat = paired(links.assemble(after(kv_own, normed), kv_far, {}))
    first_single = links.send_own(everywhere(first_own))
    kv_proj = both(normed, kv_mat, 0, 2 * k_cols)
    kv = prepare(prepare_keys_kernel, "prepare_keys", head_dim, 2 * k_cols, kv_proj, cos, sin, key_scale)
    first_ready = {q: after(b, kv, feed_low, down_low) for q, b in first_single.items()}
    first_pairs = links.send_on(first_ready)
    first_seen = [b for pair in first_pairs.values() for b in pair]
    feed_own = after(feed_low, *first_seen)
    feed_single = links.send_own(everywhere(feed_own))
    down_own = after(down_low, *first_seen)
    down_single = links.send_own(everywhere(down_own))
    first_mat = paired(links.assemble(first_own, first_ready, first_pairs))
    gate_at, proj_cols = q_cols, 2 * q_cols
    proj = both(normed, first_mat, 0, proj_cols)
    kvs, turns = [after(kv, *first_single.values())], [0]
    mask = links.ctx // 2
    while mask:
        kvs = kvs + [links.swap(b if i == 0 else after(b, proj), "ctx", mask) for i, b in enumerate(kvs)]
        turns = turns + [p ^ mask for p in turns]
        mask //= 2
    query = prepare(prepare_queries_kernel, "prepare_queries", head_dim, q_cols, proj, cos, sin, query_scale)
    at = jnp.stack([ctx_index, length]).astype(jnp.int32)
    half_rows = span // 2
    shard_rows = half_rows // links.tensor
    part_of = lambda value, t: value[t * half_rows : (t + 1) * half_rows]
    own_rows = lambda value, t: value[t * shard_rows : (t + 1) * shard_rows]
    live = [(part_of(spot_col, t)[:shard_rows] < length).astype(F32) for t in range(2)]
    mixed, sums, out_part, one = ([None] * 2 for _ in range(4))
    query_now, gated_all = query, None
    for t in range(2):
        mixed[t], sums[t], gated_all, out_part[t] = attend(
            at, t, 2, group, head_dim, turns, query_now, proj, gate_at, spot_col, spot_row, first_mat, proj_cols, kvs, gated_all
        )
        one[t] = links.scatter_first(out_part[t])
    feed_ready = {q: after(b, out_part[1], one[1][1], *down_single.values()) for q, b in feed_single.items()}
    feed_pairs = links.send_on(feed_ready)
    middle, normed_two, unit_two, inverse_two, two = ([None] * 2 for _ in range(5))
    late = (one[1][1],)
    for t in range(2):
        attn_out, _ = links.scatter_rest(*one[t], late=late)
        middle[t] = own_rows(stream, t).astype(F32) + attn_out * live[t]
        inverse_two[t] = lax.rsqrt(jnp.mean(middle[t] * middle[t], axis=-1, keepdims=True) + EPSILON)
        unit_two[t] = middle[t] * inverse_two[t]
        normed_two[t] = (unit_two[t] * mlp_scale).astype(BF16)
        two[t] = links.gather_first(normed_two[t])
        late = (normed_two[t],)
    feed_mat = paired(links.assemble(after(feed_own, normed_two[1]), feed_ready, feed_pairs))
    pieces_two = [links.gather_rest(*two[0], late=late)]
    down_pairs = links.send_on(down_single)
    down_mat = paired(links.assemble(after(down_own, two[1][1]), down_single, down_pairs))
    pieces_two.append(links.gather_rest(*two[1], late=(pieces_two[0][0],)))

    grad_hidden = both(after(down_grad, pieces_two[0][1]), down_mat, 0, ff_cols)
    back_part, three = [None] * 2, [None] * 2
    held = None
    for t in range(2):
        held, back_part[t] = feed(t, pieces_two[t], feed_mat, grad_hidden, held)
        three[t] = links.scatter_first(back_part[t])
    hidden_all, grad_gate_all, grad_up_all, rows_two = held

    halves = lambda value: (value[:, : value.shape[1] // 2], value[:, value.shape[1] // 2 :])

    def grad_others(rows_of, cols, *before):
        left = after(rows_of[:, mid:], *before)
        parts = [row_contract(left, c).astype(BF16) for c in cols]
        return parts, [links.swap(p, "ctx", 1) for p in parts]

    def grad_totals(rows_of, cols, arrived, *before, holds=((), ())):
        left = after(rows_of[:, :mid], *before)
        totals = [(row_contract(left, c) + a.astype(F32)).astype(BF16) for c, a in zip(cols, arrived)]
        return totals, [links.reduce_first(x, turn, *holds[turn]) for turn, x in enumerate(totals)]

    def grad_rest(firsts, *before):
        return [
            links.reduce_rest(kept, after(came, *before), turn) for turn, (kept, _, came) in enumerate(firsts)
        ]

    scaled_back = lambda back, t: own_rows(grad_out, t).astype(F32) + norm_back(
        back, unit_two[t], inverse_two[t], mlp_scale
    )
    grad_middle, attn_grad, four = ([None] * 2 for _ in range(3))
    down_cols = halves(hidden_all)
    down_others, down_came = grad_others(down_grad, down_cols, three[0][1])
    feed_cols = [grad_gate_all, grad_up_all]
    feed_others, feed_came = grad_others(rows_two, feed_cols, *down_others)
    back_a, seen_a = links.scatter_rest(*three[0], before=(hidden_all,))
    back_b, seen_b = links.scatter_rest(*three[1], before=())
    down_totals, down_first = grad_totals(down_grad, down_cols, down_came, three[1][1], seen_a, *feed_others)
    for t, back in enumerate((back_a, back_b)):
        back = after(back, *((down_totals[1],) if t == 0 else (attn_grad[0],)))
        grad_middle[t] = scaled_back(back, t)
        attn_grad[t] = (grad_middle[t] * live[t]).astype(BF16)
        four[t] = links.gather_first(attn_grad[t])
    feed_totals, feed_first = grad_totals(rows_two, feed_cols, feed_came, attn_grad[1])
    grad_mlp_gain = sum(jnp.sum(b * unit_two[t], axis=0) for t, b in enumerate((back_a, back_b)))
    attn_shard = attn_grad[1]
    pieces_four = [links.gather_rest(*four[0], late=(attn_shard,))]
    homes = jnp.stack([(z_index ^ j) * 2 + part for part in range(2) for j in links.turns]).astype(jnp.int32)
    down_part = spread("spread_down", [(after(hidden_all, pieces_four[0][0], *feed_totals), down_mat, 0)], homes=homes)
    down_rest = grad_rest(down_first, down_part)
    down_gone = [b for r in down_rest for b in r[1]]
    pieces_four.append(links.gather_rest(*four[1], late=(pieces_four[0][0],)))
    down_sum = lax.psum_scatter(down_part, "tensor", scatter_dimension=0, tiled=True).astype(F32)
    down_shard = jnp.concatenate(middle, axis=0) + down_sum * jnp.concatenate(live, axis=0)
    down_all = lax.all_gather(down_shard.astype(BF16), "tensor", axis=0, tiled=True)
    back_places = jnp.array(
        [part * links.tensor + o for o in range(links.tensor) for part in range(2)], dtype=jnp.int32
    )
    hidden_out = leave(jnp.concatenate([back_places, scalars[parts:]]), count, parts, [down_all], BF16)

    backward = lambda t, pieces, olds: attend_back(
        at, t, 2, group, head_dim, turns, query, proj, gate_at, mixed[t], sums[t], pieces, first_mat, proj_cols,
        spot_row, spot_col, cos, sin, query_scale, kvs, olds,
    )
    grad_kvs, held, gain_a = backward(0, (pieces_four[0][0], after(pieces_four[0][1], pieces_four[1][0], down_part)), None)
    grad_query = held[0]
    last = (pieces_four[1][0], after(pieces_four[1][1], *down_gone, *(f[2] for f in feed_first)))
    grad_kvs, held, gain_b = backward(1, last, (*grad_kvs, *held))
    grad_query, grad_gates, attn_all = held
    q_gain_part = gain_a + gain_b
    pieces = dict(zip(turns, grad_kvs))
    mask = 1
    kv_gone, kv_seen = [], []
    while len(pieces) > 1:
        near = [p for p in pieces if not p & mask]
        gone = [pieces[p ^ mask].astype(BF16) for p in near]
        came = links.swap(jnp.concatenate(gone, axis=0), "ctx", mask)
        kv_gone.append(gone)
        kv_seen.append(came)
        pieces = {
            p: pieces[p].astype(F32) + came[i * span : (i + 1) * span].astype(F32) for i, p in enumerate(near)
        }
        mask *= 2
    feed_rest = grad_rest(feed_first, kv_seen[0])
    feed_last = [(r[2],) for r in feed_rest]
    out_cols, proj_cols_of = halves(gated_all), (grad_query, grad_gates)
    proj_others, proj_came = grad_others(normed, proj_cols_of, *kv_gone[-1])
    proj_totals, proj_first = grad_totals(normed, proj_cols_of, proj_came, *proj_others, holds=feed_last)
    out_others, out_came = grad_others(attn_all, out_cols, *proj_totals)
    proj_seen = [(f[2],) for f in proj_first]
    out_totals, out_first = grad_totals(attn_all, out_cols, out_came, *out_others, holds=proj_seen)
    grad_key, grad_value, k_gain_part = keys_back(
        kv_heads, head_dim, after(pieces[0], down_shard), kv_proj, 0, cos, sin, key_scale
    )
    seven, eight, in_part, grad_in, attn_gain_part = ([None] * 2 for _ in range(5))
    for t in range(2):
        terms = [
            (grad_query, first_mat, 0),
            (grad_gates, first_mat, q_cols),
            (grad_key, kv_mat, 0),
            (grad_value, kv_mat, k_cols),
        ]
        in_part[t], gain = spread("spread_in", terms, t, 2, normed=normed)
        attn_gain_part[t] = gain[0] / attn_scale[0]
        seven[t] = links.scatter_first(in_part[t])
    kv_others, kv_came = grad_others(normed, (grad_key, grad_value), seven[0][1])
    summed = [links.scatter_rest(*seven[t]) for t in range(2)]
    kv_totals, kv_first = grad_totals(
        normed, (grad_key, grad_value), kv_came, seven[1][1], summed[0][1], holds=[(f[2],) for f in out_first]
    )
    late = (*kv_totals, down_all)
    for t in range(2):
        back = after(summed[t][0], *late)
        x = own_rows(stream, t).astype(F32)
        inverse = lax.rsqrt(jnp.mean(x * x, axis=-1, keepdims=True) + EPSILON)
        unit = x * inverse
        grad_in[t] = (grad_middle[t] + norm_back(back, unit, inverse, attn_scale)).astype(BF16)
        eight[t] = links.gather_first(grad_in[t])
        late = (grad_in[t],)
    proj_rest, out_rest, kv_rest = grad_rest(proj_first), grad_rest(out_first), grad_rest(kv_first)
    in_pieces = [*links.gather_rest(*eight[0], late=late)]
    in_pieces += links.gather_rest(*eight[1], late=(in_pieces[0],))
    attn_gain_part, grad_shards = sum(attn_gain_part), (eight[1][0],)
    in_pieces[1] = after(in_pieces[1], hidden_out)
    grad_in = leave(scalars, count, parts, in_pieces, F32)
    side = lambda rest: jnp.concatenate([r[0] for r in rest], axis=1)

    blocks = jnp.stack([attn_gain_part.reshape(count, shard), grad_mlp_gain.reshape(count, shard)])
    to_mesh = (owners[None, :] == jnp.arange(count)[:, None]).astype(F32)
    blocks = jnp.einsum("ap,kpn->kan", to_mesh, blocks, precision=lax.Precision.HIGHEST)
    packed = jnp.concatenate([blocks.reshape(1, -1), q_gain_part[None, :], k_gain_part[None, :]], axis=1)
    packed = links.add_all(packed, *grad_shards)[0]
    rank = dp_index * links.ctx + ctx_index
    take = lambda at, size: lax.dynamic_slice_in_dim(packed, at + rank * size, size)
    return (
        hidden_out,
        grad_in,
        take(0, shard),
        proj_rest[0][0],
        proj_rest[1][0],
        kv_rest[0][0],
        kv_rest[1][0],
        take(2 * width, head_shard),
        take(2 * width + head_dim, head_shard),
        side(out_rest),
        take(width, shard),
        feed_rest[0][0],
        feed_rest[1][0],
        side(down_rest),
    )


def solution(mesh):
    links = Links(dict(mesh.shape))
    rows = P(("dp", "ctx"))
    plain = P(("dp", "ctx"), None)
    split = P(("dp", "ctx"), "tensor")

    def step(*arrays):
        return per_device(links, *arrays)

    return jax.shard_map(
        step,
        mesh=mesh,
        in_specs=(plain, P("dp"), rows, split, split, split, split, rows, rows, split, rows, split, split, split, plain),
        out_specs=(plain, plain, rows, split, split, split, split, rows, rows, split, rows, split, split, split),
        check_vma=False,
    )
```

```python
import functools
import math

import jax
import jax.numpy as jnp
from jax import lax
from jax.experimental import pallas as pl
from jax.experimental.pallas import tpu as pltpu
from jax.sharding import PartitionSpec as P

EPSILON = 1e-06
ROPE_BASE = 1000000.0
CONTRACT_ROWS = (((0,), (0,)), ((), ()))
CONTRACT_COLS = (((1,), (1,)), ((), ()))
F32 = jnp.float32
BF16 = jnp.bfloat16
VMEM_BYTES = 56 * 1024 * 1024


def project(operand, matrix):
    return jnp.dot(operand, matrix, preferred_element_type=F32)


def row_contract(first_op, second_op):
    return lax.dot_general(first_op, second_op, CONTRACT_ROWS, preferred_element_type=F32)


def col_contract(first_op, second_op):
    return lax.dot_general(first_op, second_op, CONTRACT_COLS, preferred_element_type=F32)


def sigmoid(value):
    return 1.0 / (1.0 + jnp.exp(-value))


def after(value, *others):
    if not others:
        return value
    return lax.optimization_barrier((value,) + others)[0]


def cost(flops, moved, exps=0):
    return pl.CostEstimate(flops=int(flops), bytes_accessed=int(moved), transcendentals=int(exps))


def params(**kwargs):
    return pltpu.CompilerParams(vmem_limit_bytes=VMEM_BYTES, **kwargs)


class Links:
    def __init__(self, sizes):
        self.dp, self.ctx, self.tensor = sizes["dp"], sizes["ctx"], sizes["tensor"]
        self.half = self.dp * self.ctx // 2
        ctx_bits = int(math.log2(self.ctx // 2))
        dp_bits = int(math.log2(self.dp))
        self.bits = [("ctx", 2 << i) for i in range(ctx_bits)] + [("dp", 1 << i) for i in range(dp_bits)]
        self.masks = [(2 << i) - 1 for i in range(int(math.log2(self.tensor)))]
        self.turns = [0]
        for mask in reversed(self.masks):
            self.turns = self.turns + [j ^ mask for j in self.turns]

    def swap(self, value, axis, mask):
        count = {"dp": self.dp, "ctx": self.ctx, "tensor": self.tensor}[axis]
        return lax.ppermute(value, axis, [(i, i ^ mask) for i in range(count)])

    def order(self, turn):
        places = list(range(len(self.bits)))
        return places if turn else places[::-1]

    def send_own(self, blocks):
        return {1 << p: self.swap(blocks[p], *self.bits[p]) for p in self.order(0)}

    def send_far(self, block):
        count = self.dp * self.ctx
        single = {}
        for q in range(1, self.half):
            far = (q // (self.ctx // 2)) * self.ctx + (q % (self.ctx // 2)) * 2
            single[q] = lax.ppermute(block, ("dp", "ctx"), [(i, i ^ far) for i in range(count)])
        return single

    def send_on(self, single):
        mid = next(iter(single.values())).shape[1] // 2
        left = {q: b[:, :mid] for q, b in single.items()}
        right = {q: b[:, mid:] for q, b in single.items()}
        for side, places in ((left, self.order(0)), (right, self.order(1))):
            for q in range(1, self.half):
                if q not in single:
                    self.reach(side, q, places)
        return {q: (left[q], right[q]) for q in left if q not in single}

    def assemble(self, block, single, pairs):
        blocks, groups = [], []
        for q in range(self.half):
            members = [block] if q == 0 else [single[q]] if q in single else list(pairs[q])
            groups.append(tuple(range(len(blocks), len(blocks) + len(members))))
            blocks += members
        return stack_blocks(groups, blocks)

    def reach(self, side, q, places):
        if q not in side:
            last = [p for p in places if q & (1 << p)][-1]
            self.reach(side, q ^ (1 << last), places)
            side[q] = self.swap(side[q ^ (1 << last)], *self.bits[last])

    def reduce_first(self, total, turn, *hold):
        rows = total.shape[0] // self.half
        pieces = {q: total[q * rows : (q + 1) * rows] for q in range(self.half)}
        return self.reduce_step(pieces, turn, 0, *hold)

    def reduce_step(self, pieces, turn, step, *hold):
        place = self.order(turn)[step]
        bit = 1 << place
        kept = {q: b for q, b in pieces.items() if not q & bit}
        gone = [pieces[q | bit].astype(BF16) for q in kept]
        gone[0] = after(gone[0], *hold)
        return kept, gone, self.swap(jnp.concatenate(gone, axis=0), *self.bits[place])

    def reduce_rest(self, kept, came, turn):
        gone = []
        for step in range(1, len(self.bits) + 1):
            rows = came.shape[0] // len(kept)
            pieces = {
                q: b.astype(F32) + came[i * rows : (i + 1) * rows].astype(F32) for i, (q, b) in enumerate(kept.items())
            }
            if step < len(self.bits):
                kept, sent, came = self.reduce_step(pieces, turn, step)
                gone += sent
        return pieces[0], gone, came

    def small_gather(self, row):
        far = self.send_far(row)
        own = jnp.concatenate([row] + [far[q] for q in range(1, self.half)], axis=0)
        return jnp.concatenate([own, self.swap(own, "ctx", 1)], axis=0), list(far.values())

    def owner_of(self, position, dp_index, ctx_index):
        h, q = position // self.half, position % self.half
        dp_far, ctx_far = q // (self.ctx // 2), (q % (self.ctx // 2)) * 2 + h
        return (dp_index ^ dp_far) * self.ctx + (ctx_index ^ ctx_far)

    def scatter_first(self, part):
        rows = part.shape[0] // 2
        return part[:rows], self.swap(part[rows:], "tensor", self.masks[0])

    def scatter_rest(self, kept, came, before=(), late=()):
        gone = seen = came
        kept = kept.astype(F32) + came.astype(F32)
        for mask in self.masks[1:]:
            rows = kept.shape[0] // 2
            gone = kept[rows:].astype(BF16)
            seen = self.swap(after(gone, *before), "tensor", mask)
            kept = kept[:rows] + after(seen, *late).astype(F32)
        return kept, seen

    def gather_first(self, shard):
        return shard, self.swap(shard, "tensor", self.masks[-1])

    def gather_rest(self, shard, came, late=()):
        came = after(came, *late)
        for mask in self.masks[-2::-1]:
            shard = jnp.concatenate([shard, came], axis=0)
            came = self.swap(shard, "tensor", mask)
        return shard, came

    def add_all(self, value, *before):
        value = value + self.swap(value, "ctx", 1)
        for axis, mask in self.bits:
            value = value + self.swap(value, axis, mask)
        value = after(value, *before)
        for mask in self.masks:
            value = value + self.swap(value, "tensor", mask)
        return value


def still(scalars, count, parts):
    owners = scalars[parts : parts + count]
    return owners, lax.dynamic_update_slice(scalars, jnp.arange(count, dtype=scalars.dtype), (parts,))


def columns(value, owners):
    count = owners.shape[0]
    blocks = value.reshape(value.shape[0], count, value.shape[1] // count)
    return jnp.take(blocks, owners, axis=1).reshape(value.shape)


def column_place(scalars, parts, p, size):
    if size % 128:
        return pl.ds(p * size, size)
    return pl.ds(pl.multiple_of(scalars[parts + p] * size, size), size)


def stack_kernel(groups, *refs):
    out_ref = refs[-1]
    for q, group in enumerate(groups):

        @pl.when(pl.program_id(0) == q)
        def _(group=group):
            col = 0
            for i in group:
                out_ref[:, col : col + refs[i].shape[1]] = refs[i][...]
                col += refs[i].shape[1]


def stack_blocks(groups, blocks):
    rows, n = blocks[0].shape
    held = lambda b: pl.BlockSpec(b.shape, lambda i: (0, 0), pipeline_mode=pl.Buffered(1))
    return pl.pallas_call(
        functools.partial(stack_kernel, groups),
        out_shape=jax.ShapeDtypeStruct((rows * len(groups), n), blocks[0].dtype),
        grid=(len(groups),),
        in_specs=[held(b) for b in blocks],
        out_specs=pl.BlockSpec((rows, n), lambda i: (i, 0)),
        compiler_params=params(),
        cost_estimate=cost(0, 4 * rows * len(groups) * n),
        name="stack",
    )(*blocks)


def enter_kernel(
    count, parts, scalars, xa_ref, xb_ref, ga_ref, gb_ref, gain_ref, x_out, g_out, m_out, mine_out, plain_out, n_out
):
    step = pl.program_id(0)
    rows, width = xa_ref.shape
    size = width // count
    moved = [column_place(scalars, parts, p, size) for p in range(count)]
    for part, (x_ref, g_ref) in enumerate(((xa_ref, ga_ref), (xb_ref, gb_ref))):
        if part == 0:

            @pl.when(step % (parts // 4) == 0)
            def _(x_ref=x_ref, g_ref=g_ref):
                for p in range(count):
                    x_out[:, p * size : (p + 1) * size] = x_ref[:, moved[p]]
                    g_out[:, p * size : (p + 1) * size] = g_ref[:, moved[p]]

        place = slice(part * rows, (part + 1) * rows)
        spot = scalars[parts + count] + scalars[2 * step + part] * rows
        live = spot + lax.broadcasted_iota(jnp.int32, (rows, 1), 0) < scalars[parts + count + 1]
        m_out[place, :] = jnp.where(live, g_ref[...].astype(F32), 0.0).astype(BF16)
        wide = x_ref[...].astype(F32)
        inverse = lax.rsqrt(jnp.mean(wide * wide, axis=-1, keepdims=True) + EPSILON)
        plain_out[place, :] = (wide * inverse * gain_ref[...]).astype(BF16)
        for p in range(count):
            n_out[place, p * size : (p + 1) * size] = plain_out[place, moved[p]]
            mine_out[place, p * size : (p + 1) * size] = m_out[place, moved[p]]


def enter(scalars, count, parts, span, hidden_in, out_grad, gain):
    rows, width = span // parts, hidden_in.shape[1]
    narrow = width // count % 128
    owners = scalars[parts : parts + count]
    upper = pl.BlockSpec((rows, width), lambda i, s: (s[2 * i], 0))
    lower = pl.BlockSpec((rows, width), lambda i, s: (s[2 * i + 1], 0))
    own = pl.BlockSpec((rows, width), lambda i, s: (i // (parts // 4), 0))
    plain = pl.BlockSpec((2 * rows, width), lambda i, s: (i, 0))
    shape = jax.ShapeDtypeStruct((span, width), BF16)
    short = jax.ShapeDtypeStruct((2 * rows, width), BF16)
    x, g, m, mine, unmoved, normed = pl.pallas_call(
        functools.partial(enter_kernel, count, parts),
        out_shape=(short, short, shape, shape, shape, shape),
        grid_spec=pltpu.PrefetchScalarGridSpec(
            num_scalar_prefetch=1,
            grid=(parts // 2,),
            in_specs=[upper, lower, upper, lower, pl.BlockSpec((1, width), lambda i, s: (0, 0))],
            out_specs=(own, own, plain, plain, plain, plain),
        ),
        compiler_params=params(),
        cost_estimate=cost(10 * span * width, 8 * span * width),
        name="enter",
    )(scalars, hidden_in, hidden_in, out_grad, out_grad, gain)
    if narrow:
        x, g, mine, normed = (columns(v, owners) for v in (x, g, mine, normed))
    return x, g, m, mine, unmoved, normed


def leave_kernel(count, parts, scalars, *refs):
    pieces, out_ref = refs[:4], refs[4]
    blocks, size = parts // 4, out_ref.shape[1] // count
    rows = out_ref.shape[0] // parts
    for i, in_ref in enumerate(pieces):

        @pl.when(pl.program_id(0) == i)
        def _(i=i, in_ref=in_ref):
            for part in range(blocks):
                at = pl.ds(pl.multiple_of(scalars[i * blocks + part] * rows, rows), rows)
                for p in range(count):
                    block = in_ref[part * rows : (part + 1) * rows, p * size : (p + 1) * size]
                    out_ref[at, column_place(scalars, parts, p, size)] = block.astype(out_ref.dtype)


def leave(scalars, count, parts, pieces, dtype):
    rows, width = pieces[0].shape
    place = lambda k: lambda i, s: (0, 0)
    if len(pieces) == 1:
        rows, pieces = rows // 4, pieces * 4
        place = lambda k: lambda i, s: (k, 0)
    if width // count % 128:
        owners, scalars = still(scalars, count, parts)
        pieces = [columns(piece, jnp.argsort(owners)) for piece in pieces]
    return pl.pallas_call(
        functools.partial(leave_kernel, count, parts),
        out_shape=jax.ShapeDtypeStruct((4 * rows, width), dtype),
        grid_spec=pltpu.PrefetchScalarGridSpec(
            num_scalar_prefetch=1,
            grid=(4,),
            in_specs=[pl.BlockSpec((rows, width), place(k)) for k in range(4)],
            out_specs=pl.BlockSpec((4 * rows, width), lambda i, s: (0, 0)),
        ),
        compiler_params=params(),
        cost_estimate=cost(0, 24 * rows * width),
        name="leave",
    )(scalars, *pieces)


def spread_kernel(tiles, count, parts, summed, *refs):
    homes, refs = (refs[0], refs[1:]) if parts else (None, refs)
    values, out_ref = refs[:count], refs[3 * count + summed]
    for h in range(2):

        @pl.when(pl.program_id(0) // tiles == h)
        def _(h=h):
            total = None
            for k in range(count):
                term = lax.dot_general(
                    values[k][...], refs[count + 2 * k + h][...], CONTRACT_COLS, preferred_element_type=F32
                )
                total = term if total is None else total + term
            if summed:
                norm_ref, sum_ref = refs[3 * count], refs[3 * count + 2]
                gain = jnp.sum(total * norm_ref[...].astype(F32), axis=0, keepdims=True)
                sum_ref[...] = jnp.broadcast_to(gain, sum_ref.shape)
            if parts:
                rows = out_ref.shape[0] // parts
                for i in range(parts):
                    at = pl.ds(pl.multiple_of(homes[i] * rows, rows), rows)
                    out_ref[at, :] = total[i * rows : (i + 1) * rows].astype(BF16)
            else:
                out_ref[...] = total.astype(BF16)


def spread(name, terms, part=0, parts=1, homes=None, normed=None):
    rows = terms[0][0].shape[0] // parts
    mid = terms[0][1][0].shape[0]
    tile = mid // 2
    specs, mats = [], []
    for value, pair, start in terms:
        n = value.shape[1]
        specs += [
            pl.BlockSpec((tile, n), lambda j, *s, c=start // n: (jnp.minimum(j, 1), c)),
            pl.BlockSpec((tile, n), lambda j, *s, c=start // n: (jnp.maximum(j - 2, 0), c)),
        ]
        mats += list(pair)
    held = [pl.BlockSpec((rows, v.shape[1]), lambda j, *s: (part, 0)) for v, _, _ in terms]
    wide = sum(v.shape[1] for v, _, _ in terms)
    summed = normed is not None
    shapes = [jax.ShapeDtypeStruct((rows, 2 * mid), BF16)]
    outs = [pl.BlockSpec((rows, tile), lambda j, *s: (0, j))]
    extra = []
    if summed:
        extra = [normed]
        specs.append(pl.BlockSpec((rows, tile), lambda j, *s: (part, j)))
        shapes.append(jax.ShapeDtypeStruct((8, 2 * mid), F32))
        outs.append(pl.BlockSpec((8, tile), lambda j, *s: (0, j)))
    out = pl.pallas_call(
        functools.partial(spread_kernel, 2, len(terms), 0 if homes is None else homes.shape[0], summed),
        out_shape=shapes,
        grid_spec=pltpu.PrefetchScalarGridSpec(
            num_scalar_prefetch=0 if homes is None else 1, grid=(4,), in_specs=held + specs, out_specs=outs
        ),
        compiler_params=params(),
        cost_estimate=cost(4 * rows * mid * wide, 2 * wide * (rows + 2 * mid) + 4 * rows * mid),
        name=name,
    )(*(() if homes is None else (homes,)), *(v for v, _, _ in terms), *mats, *extra)
    return out if summed else out[0]


def feed_kernel(first, count, parts, scalars, a_ref, b_ref, gate_ref, up_ref, gh_ref, *refs):
    refs = refs if first else refs[4:]
    hidden_out, gate_out, up_out, rows_out, part_out, x_ref, acc_ref = refs
    step, size = pl.program_id(0), x_ref.shape[1] // count
    moved = [column_place(scalars, parts, p, size) for p in range(count)]

    @pl.when(step == 0)
    def _():
        rows = a_ref.shape[0]
        rows_out[:rows, :] = a_ref[...]
        rows_out[rows:, :] = b_ref[...]
        for p in range(count):
            x_ref[:rows, moved[p]] = a_ref[:, p * size : (p + 1) * size]
            x_ref[rows:, moved[p]] = b_ref[:, p * size : (p + 1) * size]
        acc_ref[...] = jnp.zeros_like(acc_ref)

    gate = project(x_ref[...], gate_ref[...])
    up = project(x_ref[...], up_ref[...])
    grad = gh_ref[...]
    sig = sigmoid(gate)
    hidden_out[...] = (gate * sig * up).astype(BF16)
    grad_gate = (grad * up * sig * (1.0 + gate * (1.0 - sig))).astype(BF16)
    grad_up = (grad * (gate * sig)).astype(BF16)
    gate_out[...] = grad_gate
    up_out[...] = grad_up
    acc_ref[...] += col_contract(grad_gate, gate_ref[...]) + col_contract(grad_up, up_ref[...])

    @pl.when(step == pl.num_programs(0) - 1)
    def _():
        for p in range(count):
            part_out[:, p * size : (p + 1) * size] = acc_ref[:, moved[p]].astype(BF16)


def feed(scalars, count, parts, part, pieces, mat, grad_hidden, olds):
    span, ff = grad_hidden.shape
    piece, width = pieces[0].shape
    rows = 2 * piece
    tile = 256 if ff % 256 == 0 else ff
    steps = ff // tile
    narrow = width // count % 128
    owners = scalars[parts : parts + count]
    given = [columns(x, jnp.argsort(owners)) for x in pieces] if narrow else pieces
    held = pl.BlockSpec((piece, width), lambda j, s: (0, 0))
    columns_of = lambda shift: pl.BlockSpec((width, tile), lambda j, s: (0, shift + j))
    cols = pl.BlockSpec((rows, tile), lambda j, s: (part, j))
    first = olds is None
    olds = () if first else tuple(olds)
    wide = jax.ShapeDtypeStruct((span, ff), BF16)
    out = pl.pallas_call(
        functools.partial(feed_kernel, first, count, parts),
        out_shape=(
            wide,
            wide,
            wide,
            jax.ShapeDtypeStruct((span, width), BF16),
            jax.ShapeDtypeStruct((rows, width), BF16),
        ),
        grid_spec=pltpu.PrefetchScalarGridSpec(
            num_scalar_prefetch=1,
            grid=(steps,),
            in_specs=[held, held, columns_of(0), columns_of(steps), cols]
            + [pl.BlockSpec(memory_space=pl.ANY)] * len(olds),
            out_specs=(
                cols,
                cols,
                cols,
                pl.BlockSpec((rows, width), lambda j, s: (part, 0)),
                pl.BlockSpec((rows, width), lambda j, s: (0, 0)),
            ),
            scratch_shapes=[pltpu.VMEM((rows, width), BF16), pltpu.VMEM((rows, width), F32)],
        ),
        input_output_aliases={6 + i: i for i in range(len(olds))},
        compiler_params=params(),
        cost_estimate=cost(8 * rows * width * ff, 8 * width * ff, 2 * rows * ff),
        name="feed",
    )(scalars, *given, mat, mat, grad_hidden, *olds)
    return out[:4], columns(out[4], owners) if narrow else out[4]


def descend_kernel(parts, homes, value_ref, mat_ref, out_ref):
    total = col_contract(value_ref[...], mat_ref[...])
    rows = out_ref.shape[0] // parts
    for i in range(parts):
        at = pl.ds(pl.multiple_of(homes[i] * rows, rows), rows)
        out_ref[at, :] = total[i * rows : (i + 1) * rows].astype(BF16)


def descend(homes, owners, value, mat):
    rows, n = value.shape
    width, count, parts = mat.shape[0], owners.shape[0], homes.shape[0]
    narrow = width // count % 128
    steps = 4 if narrow else count
    out = pl.pallas_call(
        functools.partial(descend_kernel, parts),
        out_shape=jax.ShapeDtypeStruct((rows, width), BF16),
        grid_spec=pltpu.PrefetchScalarGridSpec(
            num_scalar_prefetch=1,
            grid=(steps,),
            in_specs=[
                pl.BlockSpec((rows, n), lambda j, s: (0, 0)),
                pl.BlockSpec((width // steps, n), lambda j, s: (s[parts + j], 0)),
            ],
            out_specs=pl.BlockSpec((rows, width // steps), lambda j, s: (0, j)),
        ),
        compiler_params=params(),
        cost_estimate=cost(2 * rows * width * n, 2 * (rows + width) * n + 2 * rows * width),
        name="descend",
    )(jnp.concatenate([homes, jnp.arange(4, dtype=jnp.int32) if narrow else owners]), value, mat)
    return columns(out, owners) if narrow else out


def plane_grads_kernel(count, *refs):
    out_ref, start = refs[-1], 0
    for left, right in zip(refs[:count], refs[count : 2 * count]):
        size = right.shape[1]
        out_ref[:, start : start + size] = row_contract(left[...], right[...]).astype(BF16)
        start += size


def plane_grads(name, terms, total, old=None):
    span, width = terms[0][0].shape
    tile = 256
    cols = sum(g.shape[1] for _, g in terms)
    at = 0 if old is None else total // cols - 1
    left = pl.BlockSpec((span, tile), lambda j: (0, j))
    held = [pl.BlockSpec(g.shape, lambda j: (0, 0)) for _, g in terms]
    olds = () if old is None else (old,)
    return pl.pallas_call(
        functools.partial(plane_grads_kernel, len(terms)),
        out_shape=jax.ShapeDtypeStruct((width, total), BF16),
        grid=(width // tile,),
        in_specs=[left] * len(terms) + held + [pl.BlockSpec(memory_space=pl.ANY)] * len(olds),
        out_specs=pl.BlockSpec((tile, cols), lambda j: (j, at)),
        input_output_aliases={2 * len(terms): 0} if olds else {},
        compiler_params=params(),
        cost_estimate=cost(2 * span * width * cols, 2 * span * (2 * width + cols) + 2 * width * cols),
        name=name,
    )(*(a for a, _ in terms), *(g for _, g in terms), *olds)


def enter_heads_kernel(heads, head_dim, paired, x_ref, near_ref, far_ref, cos_ref, sin_ref, gain_ref, p_out, r_out):
    mid = x_ref.shape[1] // 2
    proj = project(x_ref[:, :mid], near_ref[...]) + project(x_ref[:, mid:], far_ref[...])
    p_out[...] = proj
    for h in range(heads):
        unit, _ = unit_of(proj[:, h * head_dim : (h + 1) * head_dim])
        turned = turn(unit * gain_ref[...], cos_ref, sin_ref, 1.0).astype(BF16)
        at = (2 * h if paired else h) * head_dim
        r_out[:, at : at + head_dim] = turned
        if paired:
            value = proj[:, (heads + h) * head_dim : (heads + h + 1) * head_dim]
            r_out[:, at + head_dim : at + 2 * head_dim] = value.astype(BF16)


def enter_heads(name, heads, head_dim, paired, normed, mats, at, cols, cos, sin, gain):
    span, width = normed.shape
    rows = span // 2
    spec = lambda n: pl.BlockSpec((rows, n), lambda i: (i, 0))
    mat = pl.BlockSpec((width // 2, cols), lambda i: (0, at // cols))
    turned = heads * head_dim * (2 if paired else 1)
    return pl.pallas_call(
        functools.partial(enter_heads_kernel, heads, head_dim, paired),
        out_shape=(jax.ShapeDtypeStruct((span, cols), F32), jax.ShapeDtypeStruct((span, turned), BF16)),
        grid=(2,),
        in_specs=[spec(width), mat, mat, spec(head_dim), spec(head_dim), pl.BlockSpec((1, head_dim), lambda i: (0, 0))],
        out_specs=(spec(cols), spec(turned)),
        compiler_params=params(),
        cost_estimate=cost(2 * span * width * cols, 2 * width * (span + cols) + 6 * span * cols),
        name=name,
    )(normed, *mats, cos, sin, gain)


def unit_of(value):
    inverse = lax.rsqrt(jnp.mean(value * value, axis=-1, keepdims=True) + EPSILON)
    return value * inverse, inverse


def turn(value, cos_ref, sin_ref, sign):
    half = value.shape[-1] // 2
    return value * cos_ref[...] + sign * pltpu.roll(value, half, 1) * sin_ref[...]


def attend_kernel(group, head_dim, turns, first, scalars, q_ref, gate_ref, spot_ref, key_ref, oo_ref, of_ref, *refs):
    blocks = len(turns)
    kv_refs = refs[:blocks]
    rest = refs[blocks:] if first else refs[blocks + 1 :]
    mixed_out, sum_out, gated_out, part_out, acc_ref, total_ref, out_acc = rest
    scale = head_dim**-0.5 * math.log2(math.e)
    own = scalars[0]
    step, mid = pl.program_id(0), out_acc.shape[1] // 2

    @pl.when(step == 0)
    def _():
        out_acc[...] = jnp.zeros_like(out_acc)

    for h in range(group):
        cols = slice(h * head_dim, (h + 1) * head_dim)
        query = q_ref[:, cols]

        def scores(ref):
            return lax.dot_general(query, ref[:, :head_dim], CONTRACT_COLS, preferred_element_type=F32)

        allowed = (key_ref[...] <= spot_ref[...]) & (key_ref[...] < scalars[1])
        terms = jnp.where(allowed, jnp.exp2(scores(kv_refs[0]) * scale), 0.0)
        total_ref[...] = jnp.sum(terms, axis=-1, keepdims=True)
        acc_ref[...] = project(terms.astype(BF16), kv_refs[0][:, head_dim:])
        for place in range(1, blocks):

            @pl.when((own ^ turns[place]) < own)
            def _(ref=kv_refs[place]):
                terms = jnp.exp2(scores(ref) * scale)
                total_ref[...] += jnp.sum(terms, axis=-1, keepdims=True)
                acc_ref[...] += project(terms.astype(BF16), ref[:, head_dim:])

        mixed = acc_ref[...] / total_ref[...]
        mixed_out[:, cols] = mixed
        gated_out[:, cols] = (mixed * sigmoid(gate_ref[:, cols])).astype(BF16)
        sum_out[:, cols] = jnp.broadcast_to(total_ref[...], mixed.shape)
    gated = gated_out[...]
    out_acc[:, :mid] += col_contract(gated, oo_ref[...])
    out_acc[:, mid:] += col_contract(gated, of_ref[...])

    @pl.when(step == pl.num_programs(0) - 1)
    def _():
        part_out[...] = out_acc[...].astype(BF16)


def attend(scalars, part, parts, group, head_dim, turns, query, proj, gate_at, spots, keys, mats, out_at, kvs, old):
    span, width = query.shape
    rows, wide, mid = span // parts, group * head_dim, mats[0].shape[0]
    head = pl.BlockSpec((rows, wide), lambda g, s: (part, g))
    out = pl.BlockSpec((rows, wide), lambda g, s: (0, g))
    mat = pl.BlockSpec((mid, wide), lambda g, s: (0, out_at // wide + g))
    first = old is None
    olds = () if first else (old,)
    return pl.pallas_call(
        functools.partial(attend_kernel, group, head_dim, turns, first),
        out_shape=(
            jax.ShapeDtypeStruct((rows, width), F32),
            jax.ShapeDtypeStruct((rows, width), F32),
            jax.ShapeDtypeStruct((span, width), BF16),
            jax.ShapeDtypeStruct((rows, 2 * mid), BF16),
        ),
        grid_spec=pltpu.PrefetchScalarGridSpec(
            num_scalar_prefetch=1,
            grid=(width // wide,),
            in_specs=[
                head,
                pl.BlockSpec((rows, wide), lambda g, s: (part, gate_at // wide + g)),
                pl.BlockSpec((rows, 1), lambda g, s: (part, 0)),
                pl.BlockSpec((1, span), lambda g, s: (0, 0)),
                mat,
                mat,
            ]
            + [pl.BlockSpec((span, 2 * head_dim), lambda g, s: (0, g))] * len(kvs)
            + [pl.BlockSpec(memory_space=pl.ANY)] * len(olds),
            out_specs=(out, out, head, pl.BlockSpec((rows, 2 * mid), lambda g, s: (0, 0))),
            scratch_shapes=[
                pltpu.VMEM((rows, head_dim), F32),
                pltpu.VMEM((rows, 1), F32),
                pltpu.VMEM((rows, 2 * mid), F32),
            ],
        ),
        input_output_aliases={7 + len(kvs): 2} if olds else {},
        compiler_params=params(),
        cost_estimate=cost(
            4 * rows * width * span * len(kvs) + 4 * rows * width * mid,
            4 * span * width * len(kvs) + 20 * rows * width + 4 * mid * width,
            rows * span * len(kvs) * width // head_dim,
        ),
        name="attend",
    )(scalars, query, proj, spots, keys, *mats, *kvs, *olds)


def attend_back_kernel(group, head_dim, turns, first, count, scalars, *refs):
    blocks = len(turns)
    q_ref, query_ref, gate_ref, mixed_ref, sum_ref, a_ref, b_ref, oo_ref, of_ref = refs[:9]
    spot_ref, key_ref, cos_ref, sin_ref, gain_ref = refs[9:14]
    kv_refs = refs[14 : 14 + blocks]
    rest = refs[14 + blocks :]
    old_refs = () if first else rest[:blocks]
    rest = rest if first else rest[blocks + 3 :]
    gq_out, ggate_out, rows_out, gain_out = rest[:4]
    new_refs = rest[4 : 4 + blocks]
    gq_ref, x_ref = rest[4 + blocks :]
    mid = x_ref.shape[1] // 2

    @pl.when(pl.program_id(0) == 0)
    def _():
        piece = a_ref.shape[0]
        x_ref[:piece, :] = a_ref[...]
        x_ref[piece:, :] = b_ref[...]
        size = x_ref.shape[1] // count
        for p in range(count):
            rows_out[:, column_place(scalars, 2, p, size)] = x_ref[:, p * size : (p + 1) * size]

    all_gated = project(x_ref[:, :mid], oo_ref[...]) + project(x_ref[:, mid:], of_ref[...])
    score_scale = head_dim**-0.5
    scale = score_scale * math.log2(math.e)
    own = scalars[0]
    rows = q_ref.shape[0]

    def as_row(column):
        return jnp.transpose(jnp.broadcast_to(column, (rows, head_dim)))[:1, :]

    for place in range(blocks):
        if first:
            new_refs[place][...] = jnp.zeros_like(new_refs[place])
        else:
            new_refs[place][...] = old_refs[place][...]
    gain_total = jnp.zeros((1, head_dim), F32)
    for h in range(group):
        cols = slice(h * head_dim, (h + 1) * head_dim)
        query = q_ref[:, cols]
        gate = sigmoid(gate_ref[:, cols])
        grad_gated, mixed = all_gated[:, cols], mixed_ref[:, cols]
        grad_mixed = (grad_gated * gate).astype(BF16)
        ggate_out[:, cols] = (grad_gated * mixed * gate * (1.0 - gate)).astype(BF16)
        row_dot = as_row(jnp.sum(grad_mixed.astype(F32) * mixed, axis=-1, keepdims=True))
        row_log = as_row(jnp.log2(sum_ref[:, cols][:, :1]))
        gq_ref[...] = jnp.zeros_like(gq_ref)

        def block(kv_ref, new_ref, masked):
            key, value = kv_ref[:, :head_dim], kv_ref[:, head_dim:]
            scores = lax.dot_general(key, query, CONTRACT_COLS, preferred_element_type=F32)
            probs = jnp.exp2(scores * scale - row_log)
            if masked:
                allowed = (key_ref[...] <= spot_ref[...]) & (key_ref[...] < scalars[1])
                probs = jnp.where(allowed, probs, 0.0)
            grad_probs = lax.dot_general(value, grad_mixed, CONTRACT_COLS, preferred_element_type=F32)
            grad_scores = (probs * (grad_probs - row_dot)).astype(BF16)
            new_ref[:, head_dim:] += project(probs.astype(BF16), grad_mixed)
            new_ref[:, :head_dim] += project(grad_scores, query)
            gq_ref[...] += lax.dot_general(grad_scores, key, CONTRACT_ROWS, preferred_element_type=F32)

        block(kv_refs[0], new_refs[0], True)
        for place in range(1, blocks):

            @pl.when((own ^ turns[place]) < own)
            def _(place=place):
                block(kv_refs[place], new_refs[place], False)

        unit, inverse = unit_of(query_ref[:, cols])
        back = turn(gq_ref[...] * score_scale, cos_ref, sin_ref, -1.0)
        gain_total = gain_total + jnp.sum(back * unit, axis=0, keepdims=True)
        scaled = back * gain_ref[...]
        gq_out[:, cols] = (
            inverse * (scaled - unit * jnp.mean(scaled * unit, axis=-1, keepdims=True))
        ).astype(BF16)
    gain_out[...] = jnp.broadcast_to(gain_total, gain_out.shape)


def attend_back(
    scalars, count, part, parts, group, head_dim, turns, query, proj, gate_at, mixed, sums, pieces, mats, out_at, spots, keys, cos, sin, gain, kvs, olds
):
    span, width = query.shape
    rows, wide = span // parts, group * head_dim
    blocks, mid = len(kvs), mats[0].shape[0]
    mine = pl.BlockSpec((rows, wide), lambda g, s: (part, g))
    local = pl.BlockSpec((rows, wide), lambda g, s: (0, g))
    table = pl.BlockSpec((rows, head_dim), lambda g, s: (part, 0))
    pair = pl.BlockSpec((span, 2 * head_dim), lambda g, s: (0, g))
    piece = pl.BlockSpec(pieces[0].shape, lambda g, s: (0, 0))
    mat = pl.BlockSpec((mid, wide), lambda g, s: (0, out_at // wide + g))
    first = olds is None
    olds = () if first else tuple(olds)
    kv_shape = jax.ShapeDtypeStruct(kvs[0].shape, F32)
    steps = width // wide
    before = 15 + blocks
    out = pl.pallas_call(
        functools.partial(attend_back_kernel, group, head_dim, turns, first, count),
        out_shape=(
            jax.ShapeDtypeStruct((span, width), BF16),
            jax.ShapeDtypeStruct((span, width), BF16),
            jax.ShapeDtypeStruct((span, 2 * mid), BF16),
            jax.ShapeDtypeStruct((8 * steps, head_dim), F32),
        )
        + (kv_shape,) * blocks,
        grid_spec=pltpu.PrefetchScalarGridSpec(
            num_scalar_prefetch=1,
            grid=(steps,),
            in_specs=[
                mine,
                mine,
                pl.BlockSpec((rows, wide), lambda g, s: (part, gate_at // wide + g)),
                local,
                local,
                piece,
                piece,
                mat,
                mat,
                pl.BlockSpec((1, rows), lambda g, s: (0, part)),
                pl.BlockSpec((span, 1), lambda g, s: (0, 0)),
                table,
                table,
                pl.BlockSpec((1, head_dim), lambda g, s: (0, 0)),
            ]
            + [pair] * (blocks + min(len(olds), blocks))
            + [pl.BlockSpec(memory_space=pl.ANY)] * max(len(olds) - blocks, 0),
            out_specs=(
                mine,
                mine,
                pl.BlockSpec((rows, 2 * mid), lambda g, s: (part, 0)),
                pl.BlockSpec((8, head_dim), lambda g, s: (g, 0)),
            )
            + (pair,) * blocks,
            scratch_shapes=[pltpu.VMEM((rows, head_dim), F32), pltpu.VMEM((rows, 2 * mid), BF16)],
        ),
        input_output_aliases={}
        if first
        else {**{before + i: 4 + i for i in range(blocks)}, **{before + blocks + i: i for i in range(3)}},
        compiler_params=params(),
        cost_estimate=cost(
            10 * rows * width * span * blocks + 4 * rows * width * mid,
            20 * span * width * blocks,
            rows * span * blocks * width // head_dim,
        ),
        name="attend_back",
    )(scalars, query, proj, proj, mixed, sums, *pieces, *mats, spots, keys, cos, sin, gain, *kvs, *olds)
    gain_part = sum(out[3][8 * g] for g in range(steps))
    return out[4:], out[:3], gain_part


def keys_back_kernel(kv_heads, head_dim, g_ref, p_ref, cos_ref, sin_ref, gain_ref, k_out, v_out, gain_out):
    gain_total = jnp.zeros((1, head_dim), F32)
    for h in range(kv_heads):
        cols = slice(h * head_dim, (h + 1) * head_dim)
        unit, inverse = unit_of(p_ref[:, cols])
        grad = g_ref[:, 2 * h * head_dim : (2 * h + 1) * head_dim] * head_dim**-0.5
        back = turn(grad, cos_ref, sin_ref, -1.0)
        gain_total = gain_total + jnp.sum(back * unit, axis=0, keepdims=True)
        scaled = back * gain_ref[...]
        k_out[:, cols] = (
            inverse * (scaled - unit * jnp.mean(scaled * unit, axis=-1, keepdims=True))
        ).astype(BF16)
        v_out[:, cols] = g_ref[:, (2 * h + 1) * head_dim : (2 * h + 2) * head_dim].astype(BF16)
    gain_out[...] = jnp.broadcast_to(gain_total, gain_out.shape)


def keys_back(kv_heads, head_dim, grad_kv, proj, key_at, cos, sin, gain):
    span = proj.shape[0]
    cols = kv_heads * head_dim
    key_block = key_at // cols
    whole = lambda a, b: pl.BlockSpec((a, b), lambda i: (0, 0))
    out = pl.pallas_call(
        functools.partial(keys_back_kernel, kv_heads, head_dim),
        out_shape=(
            jax.ShapeDtypeStruct((span, cols), BF16),
            jax.ShapeDtypeStruct((span, cols), BF16),
            jax.ShapeDtypeStruct((8, head_dim), F32),
        ),
        grid=(1,),
        in_specs=[
            whole(span, 2 * cols),
            pl.BlockSpec((span, cols), lambda i: (0, key_block)),
            whole(span, head_dim),
            whole(span, head_dim),
            whole(1, head_dim),
        ],
        out_specs=(whole(span, cols), whole(span, cols), whole(8, head_dim)),
        compiler_params=params(),
        cost_estimate=cost(40 * span * cols, 16 * span * cols),
        name="keys_back",
    )(grad_kv, proj, cos, sin, gain)
    return out[0], out[1], out[2][0]


def norm_back(gradient, unit_vals, inverse, gain_vec):
    scaled = gradient * gain_vec
    return inverse * (scaled - unit_vals * jnp.mean(scaled * unit_vals, axis=-1, keepdims=True))


def per_device(
    links,
    hidden_in,
    lengths,
    attn_gain,
    q_weight,
    gate_weight,
    k_weight,
    v_weight,
    q_gain,
    k_gain,
    o_weight,
    mlp_gain,
    w_gate,
    w_up,
    w_down,
    out_grad,
):
    dp_index, ctx_index, z_index = (lax.axis_index(a) for a in ("dp", "ctx", "tensor"))
    q_cols, k_cols, ff_cols = q_weight.shape[1], k_weight.shape[1], w_down.shape[1]
    span, width = hidden_in.shape
    mid, count = width // 2, 2 * links.half
    shard, head_shard = attn_gain.shape[0], q_gain.shape[0]
    head_dim = head_shard * count
    heads, kv_heads = q_cols // head_dim, k_cols // head_dim
    group = heads // kv_heads
    length = lengths[0]
    low = lambda *mats: jnp.concatenate([m.astype(BF16) for m in mats], axis=1)

    small = jnp.concatenate([attn_gain, mlp_gain, q_gain, k_gain]).astype(BF16)[None, :]
    gains, seen = links.small_gather(small)
    everywhere = lambda block: {p: block for p in range(len(links.bits))}
    paired = lambda half: (half, links.swap(half, "ctx", 1))
    plane = ("dp", "ctx")
    first_own = after(low(q_weight, gate_weight, k_weight, v_weight, o_weight), *seen)
    first_single = links.send_own(everywhere(first_own))
    attn_scale = gains[:, :shard].reshape(1, width).astype(F32)
    mlp_scale = gains[:, shard : 2 * shard].reshape(1, width).astype(F32)
    owners = jnp.stack([links.owner_of(p, dp_index, ctx_index) for p in range(count)]).astype(jnp.int32)
    pick = (owners[None, :] == jnp.arange(count)[:, None]).astype(BF16)
    mesh_gains = project(pick, gains)
    mesh_scale = mesh_gains[:, :shard].reshape(1, width)
    query_scale = mesh_gains[:, 2 * shard : 2 * shard + head_shard].reshape(1, head_dim)
    key_scale = mesh_gains[:, 2 * shard + head_shard :].reshape(1, head_dim)

    parts = 2 * links.tensor
    row_block = span // parts
    row_places = jnp.stack(
        [part * links.tensor + (z_index ^ j) for part in range(2) for j in links.turns]
    ).astype(jnp.int32)
    start = ctx_index * span
    scalars = jnp.concatenate(
        [row_places, owners.astype(jnp.int32), jnp.stack([start, length]).astype(jnp.int32)]
    )
    spots = (start + row_places[:, None] * row_block + jnp.arange(row_block)[None, :]).reshape(span)
    spots = spots.astype(jnp.int32)
    freq_steps = jnp.arange(head_dim // 2, dtype=F32) * (2.0 / head_dim)
    turned = spots.astype(F32)[:, None] * jnp.exp(-math.log(ROPE_BASE) * freq_steps)[None, :]
    cosine, sine = jnp.cos(turned), jnp.sin(turned)
    cos = jnp.concatenate([cosine, cosine], axis=1)
    sin = jnp.concatenate([-sine, sine], axis=1)
    spot_col, spot_row = spots[:, None], spots[None, :]

    stream, grad_out, plain_down, down_grad, plain_normed, normed = enter(
        scalars, count, parts, span, hidden_in, out_grad, after(mesh_scale, first_own)
    )
    first_single = {q: after(b, normed) for q, b in first_single.items()}
    feed_mat = lax.all_gather(after(low(w_gate, w_up), normed), plane, axis=0, tiled=True)
    down_mat = lax.all_gather(after(low(w_down), *first_single.values()), plane, axis=0, tiled=True)

    first_pairs = links.send_on(first_single)
    first_mat = paired(links.assemble(first_own, first_single, first_pairs))
    gate_at, key_at = q_cols, 2 * q_cols
    value_at, out_at = key_at + k_cols, key_at + 2 * k_cols
    kv_proj, kv = enter_heads(
        "enter_keys", kv_heads, head_dim, True, normed, first_mat, key_at, 2 * k_cols, cos, sin, key_scale
    )
    proj, query = enter_heads(
        "enter_queries", heads, head_dim, False, after(normed, kv), first_mat, 0, 2 * q_cols, cos, sin, query_scale
    )
    kvs, turns = [kv], [0]
    mask = links.ctx // 2
    while mask:
        kvs = kvs + [links.swap(b if i == 0 else after(b, query), "ctx", mask) for i, b in enumerate(kvs)]
        turns = turns + [p ^ mask for p in turns]
        mask //= 2
    at = jnp.concatenate([jnp.stack([ctx_index, length]).astype(jnp.int32), owners])
    half_rows = span // 2
    shard_rows = half_rows // links.tensor
    part_of = lambda value, t: value[t * half_rows : (t + 1) * half_rows]
    own_rows = lambda value, t: value[t * shard_rows : (t + 1) * shard_rows]
    live = [(part_of(spot_col, t)[:shard_rows] < length).astype(F32) for t in range(2)]
    mixed, sums, out_part, one = ([None] * 2 for _ in range(4))
    query_now, gated_all = query, None
    for t in range(2):
        mixed[t], sums[t], gated_all, out_part[t] = attend(
            at, t, 2, group, head_dim, turns, query_now, proj, gate_at, spot_col, spot_row, first_mat, out_at, kvs, gated_all
        )
        one[t] = links.scatter_first(out_part[t])
    middle, normed_two, unit_two, inverse_two, two = ([None] * 2 for _ in range(5))
    late = (one[1][1],)
    for t in range(2):
        attn_out, _ = links.scatter_rest(*one[t], late=late)
        middle[t] = own_rows(stream, t).astype(F32) + attn_out * live[t]
        inverse_two[t] = lax.rsqrt(jnp.mean(middle[t] * middle[t], axis=-1, keepdims=True) + EPSILON)
        unit_two[t] = middle[t] * inverse_two[t]
        normed_two[t] = (unit_two[t] * mlp_scale).astype(BF16)
        two[t] = links.gather_first(normed_two[t])
        late = (normed_two[t],)
    pieces_two = [links.gather_rest(*two[0], late=late)]
    pieces_two.append(links.gather_rest(*two[1], late=(pieces_two[0][0],)))

    grad_hidden = project(after(plain_down, one[1][1]), down_mat)
    back_part, three = [None] * 2, [None] * 2
    held = None
    for t in range(2):
        held, back_part[t] = feed(scalars, count, parts, t, pieces_two[t], feed_mat, grad_hidden, held)
        three[t] = links.scatter_first(back_part[t])
    hidden_all, grad_gate_all, grad_up_all, rows_two = held

    halves = lambda value: (value[:, : value.shape[1] // 2], value[:, value.shape[1] // 2 :])

    def grad_others(rows_of, cols, *before):
        left = after(rows_of[:, mid:], *before)
        parts = [row_contract(left, c).astype(BF16) for c in cols]
        return parts, [links.swap(p, "ctx", 1) for p in parts]

    def grad_totals(rows_of, cols, arrived, *before, holds=((), ())):
        left = after(rows_of[:, :mid], *before)
        totals = [(row_contract(left, c) + a.astype(F32)).astype(BF16) for c, a in zip(cols, arrived)]
        return totals, [links.reduce_first(x, turn, *holds[turn]) for turn, x in enumerate(totals)]

    def grad_rest(firsts, *before):
        return [
            links.reduce_rest(kept, after(came, *before), turn) for turn, (kept, _, came) in enumerate(firsts)
        ]

    scaled_back = lambda back, t: own_rows(grad_out, t).astype(F32) + norm_back(
        back, unit_two[t], inverse_two[t], mlp_scale
    )
    grad_middle, attn_grad, four = ([None] * 2 for _ in range(3))
    back_a, seen_a = links.scatter_rest(*three[0], before=(hidden_all,))
    back_b, seen_b = links.scatter_rest(*three[1])
    feed_cols = [grad_gate_all, grad_up_all]
    over_plane = lambda part: lax.psum_scatter(part, plane, scatter_dimension=0, tiled=True).astype(F32)
    down_grad_part = row_contract(after(plain_down, three[0][1]), hidden_all).astype(BF16)
    grad_down = over_plane(down_grad_part)
    feed_others, feed_came = grad_others(rows_two, feed_cols, down_grad_part)
    homes = jnp.stack([(z_index ^ j) * 2 + part for part in range(2) for j in links.turns]).astype(jnp.int32)
    down_part = descend(homes, owners, after(hidden_all, *feed_others, three[1][1]), down_mat)
    for t, back in enumerate((back_a, back_b)):
        back = after(back, *((down_part,) if t == 0 else (attn_grad[0],)))
        grad_middle[t] = scaled_back(back, t)
        attn_grad[t] = (grad_middle[t] * live[t]).astype(BF16)
        four[t] = links.gather_first(attn_grad[t])
    grad_mlp_gain = sum(jnp.sum(b * unit_two[t], axis=0) for t, b in enumerate((back_a, back_b)))
    attn_shard = attn_grad[1]
    pieces_four = [links.gather_rest(*four[0], late=(attn_shard,))]
    pieces_four.append(links.gather_rest(*four[1]))
    down_sum = lax.psum_scatter(after(down_part, grad_down), "tensor", scatter_dimension=0, tiled=True).astype(F32)
    backward = lambda t, pieces, olds: attend_back(
        at, count, t, 2, group, head_dim, turns, query, proj, gate_at, mixed[t], sums[t], pieces, first_mat, out_at,
        spot_row, spot_col, cos, sin, query_scale, kvs, olds,
    )
    feed_totals, feed_first = grad_totals(rows_two, feed_cols, feed_came, pieces_four[0][1])
    ready = after(pieces_four[0][1], pieces_four[1][0], *feed_totals, grad_down)
    grad_kvs, held, gain_a = backward(0, (pieces_four[0][0], ready), None)
    down_sum = after(down_sum, grad_kvs[0])
    down_shard = jnp.concatenate(middle, axis=0) + down_sum * jnp.concatenate(live, axis=0)
    down_all = lax.all_gather(down_shard.astype(BF16), "tensor", axis=0, tiled=True)
    back_places = jnp.array(
        [part * links.tensor + o for o in range(links.tensor) for part in range(2)], dtype=jnp.int32
    )
    last = pieces_four[1]
    grad_kvs, held, gain_b = backward(1, last, (*grad_kvs, *held))
    grad_query, grad_gates, attn_all = held
    if width // count % 128:
        attn_all = columns(attn_all, jnp.argsort(owners))
    q_gain_part = gain_a + gain_b
    pieces = dict(zip(turns, grad_kvs))
    mask = 1
    kv_gone, kv_seen = [], []
    while len(pieces) > 1:
        near = [p for p in pieces if not p & mask]
        gone = [pieces[p ^ mask].astype(BF16) for p in near]
        came = links.swap(jnp.concatenate(gone, axis=0), "ctx", mask)
        kv_gone.append(gone)
        kv_seen.append(came)
        pieces = {
            p: pieces[p].astype(F32) + came[i * span : (i + 1) * span].astype(F32) for i, p in enumerate(near)
        }
        mask *= 2
    outer_part = plane_grads(
        "outer_grads", [(after(plain_normed, *kv_gone[-1], *(f[2] for f in feed_first)), grad_query), (plain_normed, grad_gates), (attn_all, gated_all)],
        3 * q_cols + 2 * k_cols,
    )
    feed_rest = grad_rest(feed_first, grad_query)
    grad_key, grad_value, k_gain_part = keys_back(
        kv_heads, head_dim, after(pieces[0], outer_part, down_shard), kv_proj, 0, cos, sin, key_scale
    )
    seven, eight, in_part, grad_in, attn_gain_part = ([None] * 2 for _ in range(5))
    for t in range(2):
        terms = [
            (grad_query, first_mat, 0),
            (grad_gates, first_mat, gate_at),
            (grad_key, first_mat, key_at),
            (grad_value, first_mat, value_at),
        ]
        in_part[t], gain = spread("spread_in", terms, t, 2, normed=normed)
        attn_gain_part[t] = gain[0] / attn_scale[0]
        seven[t] = links.scatter_first(in_part[t])
    summed = [links.scatter_rest(*seven[t]) for t in range(2)]
    plain_late = after(plain_normed, in_part[1], seven[0][1], *(r[2] for r in feed_rest))
    inner_part = plane_grads(
        "inner_grads", [(plain_late, grad_key), (plain_late, grad_value)], 3 * q_cols + 2 * k_cols, outer_part
    )
    inner_sum = over_plane(inner_part)
    late = (inner_part,)
    for t in range(2):
        back = after(summed[t][0], *late)
        x = own_rows(stream, t).astype(F32)
        inverse = lax.rsqrt(jnp.mean(x * x, axis=-1, keepdims=True) + EPSILON)
        unit = x * inverse
        grad_in[t] = (grad_middle[t] + norm_back(back, unit, inverse, attn_scale)).astype(BF16)
        eight[t] = links.gather_first(grad_in[t])
        late = (grad_in[t],)
    hidden_out = leave(jnp.concatenate([back_places, scalars[parts:]]), count, parts, [after(down_all, in_part[1])], BF16)
    in_pieces = [*links.gather_rest(*eight[0], late=late)]
    in_pieces += links.gather_rest(*eight[1], late=(in_pieces[0],))
    attn_gain_part, grad_shards = sum(attn_gain_part), (eight[1][0],)
    in_pieces[1] = after(in_pieces[1], hidden_out, *(r[0] for r in feed_rest))
    grad_in = leave(scalars, count, parts, in_pieces, F32)

    blocks = jnp.stack([attn_gain_part.reshape(count, shard), grad_mlp_gain.reshape(count, shard)])
    to_mesh = (owners[None, :] == jnp.arange(count)[:, None]).astype(F32)
    blocks = jnp.einsum("ap,kpn->kan", to_mesh, blocks, precision=lax.Precision.HIGHEST)
    packed = jnp.concatenate([blocks.reshape(1, -1), q_gain_part[None, :], k_gain_part[None, :]], axis=1)
    packed = links.add_all(packed, *grad_shards)[0]
    rank = dp_index * links.ctx + ctx_index
    take = lambda at, size: lax.dynamic_slice_in_dim(packed, at + rank * size, size)
    return (
        hidden_out,
        grad_in,
        take(0, shard),
        inner_sum[:, :q_cols],
        inner_sum[:, q_cols : 2 * q_cols],
        inner_sum[:, 3 * q_cols : 3 * q_cols + k_cols],
        inner_sum[:, 3 * q_cols + k_cols :],
        take(2 * width, head_shard),
        take(2 * width + head_dim, head_shard),
        inner_sum[:, 2 * q_cols : 3 * q_cols],
        take(width, shard),
        feed_rest[0][0],
        feed_rest[1][0],
        grad_down,
    )


def solution(mesh):
    links = Links(dict(mesh.shape))
    rows = P(("dp", "ctx"))
    plain = P(("dp", "ctx"), None)
    split = P(("dp", "ctx"), "tensor")

    def step(*arrays):
        return per_device(links, *arrays)

    return jax.shard_map(
        step,
        mesh=mesh,
        in_specs=(plain, P("dp"), rows, split, split, split, split, rows, rows, split, rows, split, split, split, plain),
        out_specs=(plain, plain, rows, split, split, split, split, rows, rows, split, rows, split, split, split),
        check_vma=False,
    )
```

```python
import functools
import math

import jax
import jax.numpy as jnp
from jax import lax
from jax.experimental import pallas as pl
from jax.experimental.pallas import tpu as pltpu
from jax.sharding import PartitionSpec as P

EPSILON = 1e-06
ROPE_BASE = 1000000.0
CONTRACT_ROWS = (((0,), (0,)), ((), ()))
CONTRACT_COLS = (((1,), (1,)), ((), ()))
F32 = jnp.float32
BF16 = jnp.bfloat16
VMEM_BYTES = 56 * 1024 * 1024


def project(operand, matrix):
    return jnp.dot(operand, matrix, preferred_element_type=F32)


def row_contract(first_op, second_op):
    return lax.dot_general(first_op, second_op, CONTRACT_ROWS, preferred_element_type=F32)


def col_contract(first_op, second_op):
    return lax.dot_general(first_op, second_op, CONTRACT_COLS, preferred_element_type=F32)


def sigmoid(value):
    return 1.0 / (1.0 + jnp.exp(-value))


def after(value, *others):
    if not others:
        return value
    return lax.optimization_barrier((value,) + others)[0]


def cost(flops, moved, exps=0):
    return pl.CostEstimate(flops=int(flops), bytes_accessed=int(moved), transcendentals=int(exps))


def params(**kwargs):
    return pltpu.CompilerParams(vmem_limit_bytes=VMEM_BYTES, **kwargs)


class Links:
    def __init__(self, sizes):
        self.dp, self.ctx, self.tensor = sizes["dp"], sizes["ctx"], sizes["tensor"]
        self.half = self.dp * self.ctx // 2
        ctx_bits = int(math.log2(self.ctx // 2))
        dp_bits = int(math.log2(self.dp))
        self.bits = [("ctx", 2 << i) for i in range(ctx_bits)] + [("dp", 1 << i) for i in range(dp_bits)]
        self.masks = [(2 << i) - 1 for i in range(int(math.log2(self.tensor)))]
        self.turns = [0]
        for mask in reversed(self.masks):
            self.turns = self.turns + [j ^ mask for j in self.turns]

    def swap(self, value, axis, mask):
        count = {"dp": self.dp, "ctx": self.ctx, "tensor": self.tensor}[axis]
        return lax.ppermute(value, axis, [(i, i ^ mask) for i in range(count)])

    def order(self, turn):
        places = list(range(len(self.bits)))
        return places if turn else places[::-1]

    def send_own(self, blocks):
        return {1 << p: self.swap(blocks[p], *self.bits[p]) for p in self.order(0)}

    def send_far(self, block):
        count = self.dp * self.ctx
        single = {}
        for q in range(1, self.half):
            far = (q // (self.ctx // 2)) * self.ctx + (q % (self.ctx // 2)) * 2
            single[q] = lax.ppermute(block, ("dp", "ctx"), [(i, i ^ far) for i in range(count)])
        return single

    def send_on(self, single):
        mid = next(iter(single.values())).shape[1] // 2
        left = {q: b[:, :mid] for q, b in single.items()}
        right = {q: b[:, mid:] for q, b in single.items()}
        for side, places in ((left, self.order(0)), (right, self.order(1))):
            for q in range(1, self.half):
                if q not in single:
                    self.reach(side, q, places)
        return {q: (left[q], right[q]) for q in left if q not in single}

    def assemble(self, block, single, pairs):
        blocks, groups = [], []
        for q in range(self.half):
            members = [block] if q == 0 else [single[q]] if q in single else list(pairs[q])
            groups.append(tuple(range(len(blocks), len(blocks) + len(members))))
            blocks += members
        return stack_blocks(groups, blocks)

    def reach(self, side, q, places):
        if q not in side:
            last = [p for p in places if q & (1 << p)][-1]
            self.reach(side, q ^ (1 << last), places)
            side[q] = self.swap(side[q ^ (1 << last)], *self.bits[last])

    def reduce_first(self, total, turn, *hold):
        rows = total.shape[0] // self.half
        pieces = {q: total[q * rows : (q + 1) * rows] for q in range(self.half)}
        return self.reduce_step(pieces, turn, 0, *hold)

    def reduce_step(self, pieces, turn, step, *hold):
        place = self.order(turn)[step]
        bit = 1 << place
        kept = {q: b for q, b in pieces.items() if not q & bit}
        gone = [pieces[q | bit].astype(BF16) for q in kept]
        sent = after(jnp.concatenate(gone, axis=0), *hold)
        return kept, [sent], self.swap(sent, *self.bits[place])

    def reduce_rest(self, kept, came, turn):
        gone = []
        for step in range(1, len(self.bits) + 1):
            rows = came.shape[0] // len(kept)
            pieces = {
                q: b.astype(F32) + came[i * rows : (i + 1) * rows].astype(F32) for i, (q, b) in enumerate(kept.items())
            }
            if step < len(self.bits):
                kept, sent, came = self.reduce_step(pieces, turn, step)
                gone += sent
        return pieces[0], gone, came

    def small_gather(self, row):
        far = self.send_far(row)
        own = jnp.concatenate([row] + [far[q] for q in range(1, self.half)], axis=0)
        return jnp.concatenate([own, self.swap(own, "ctx", 1)], axis=0), list(far.values())

    def owner_of(self, position, dp_index, ctx_index):
        h, q = position // self.half, position % self.half
        dp_far, ctx_far = q // (self.ctx // 2), (q % (self.ctx // 2)) * 2 + h
        return (dp_index ^ dp_far) * self.ctx + (ctx_index ^ ctx_far)

    def scatter_first(self, part):
        rows = part.shape[0] // 2
        return part[:rows], self.swap(part[rows:], "tensor", self.masks[0])

    def scatter_rest(self, kept, came, before=(), late=()):
        gone = seen = came
        kept = kept.astype(F32) + came.astype(F32)
        for mask in self.masks[1:]:
            rows = kept.shape[0] // 2
            gone = kept[rows:].astype(BF16)
            seen = self.swap(after(gone, *before), "tensor", mask)
            kept = kept[:rows] + after(seen, *late).astype(F32)
        return kept, seen

    def gather_first(self, shard):
        return shard, self.swap(shard, "tensor", self.masks[-1])

    def gather_rest(self, shard, came, late=()):
        came = after(came, *late)
        for mask in self.masks[-2::-1]:
            shard = jnp.concatenate([shard, came], axis=0)
            came = self.swap(shard, "tensor", mask)
        return shard, came

    def add_all(self, value, *before):
        value = after(value, *before)
        value = value + self.swap(value, "ctx", 1)
        for axis, mask in self.bits:
            value = value + self.swap(value, axis, mask)
        return value + sum(self.swap(value, "tensor", mask) for mask in range(1, self.tensor))


def still(scalars, count, parts):
    owners = scalars[parts : parts + count]
    return owners, lax.dynamic_update_slice(scalars, jnp.arange(count, dtype=scalars.dtype), (parts,))


def columns(value, owners):
    count = owners.shape[0]
    blocks = value.reshape(value.shape[0], count, value.shape[1] // count)
    return jnp.take(blocks, owners, axis=1).reshape(value.shape)


def column_place(scalars, parts, p, size):
    if size % 128:
        return pl.ds(p * size, size)
    return pl.ds(pl.multiple_of(scalars[parts + p] * size, size), size)


def stack_kernel(groups, *refs):
    out_ref = refs[-1]
    for q, group in enumerate(groups):

        @pl.when(pl.program_id(0) == q)
        def _(group=group):
            col = 0
            for i in group:
                out_ref[:, col : col + refs[i].shape[1]] = refs[i][...]
                col += refs[i].shape[1]


def stack_blocks(groups, blocks):
    rows, n = blocks[0].shape
    held = lambda b: pl.BlockSpec(b.shape, lambda i: (0, 0), pipeline_mode=pl.Buffered(1))
    return pl.pallas_call(
        functools.partial(stack_kernel, groups),
        out_shape=jax.ShapeDtypeStruct((rows * len(groups), n), blocks[0].dtype),
        grid=(len(groups),),
        in_specs=[held(b) for b in blocks],
        out_specs=pl.BlockSpec((rows, n), lambda i: (i, 0)),
        compiler_params=params(),
        cost_estimate=cost(0, 4 * rows * len(groups) * n),
        name="stack",
    )(*blocks)


def enter_kernel(
    count, parts, scalars, xa_ref, xb_ref, ga_ref, gb_ref, gain_ref, x_out, g_out, m_out, mine_out, plain_out, n_out
):
    step = pl.program_id(0)
    rows, width = xa_ref.shape
    size = width // count
    moved = [column_place(scalars, parts, p, size) for p in range(count)]
    for part, (x_ref, g_ref) in enumerate(((xa_ref, ga_ref), (xb_ref, gb_ref))):
        if part == 0:

            @pl.when(step % (parts // 4) == 0)
            def _(x_ref=x_ref, g_ref=g_ref):
                for p in range(count):
                    x_out[:, p * size : (p + 1) * size] = x_ref[:, moved[p]]
                    g_out[:, p * size : (p + 1) * size] = g_ref[:, moved[p]]

        place = slice(part * rows, (part + 1) * rows)
        spot = scalars[parts + count] + scalars[2 * step + part] * rows
        live = spot + lax.broadcasted_iota(jnp.int32, (rows, 1), 0) < scalars[parts + count + 1]
        m_out[place, :] = jnp.where(live, g_ref[...].astype(F32), 0.0).astype(BF16)
        wide = x_ref[...].astype(F32)
        inverse = lax.rsqrt(jnp.mean(wide * wide, axis=-1, keepdims=True) + EPSILON)
        plain_out[place, :] = (wide * inverse * gain_ref[...]).astype(BF16)
        for p in range(count):
            n_out[place, p * size : (p + 1) * size] = plain_out[place, moved[p]]
            mine_out[place, p * size : (p + 1) * size] = m_out[place, moved[p]]


def enter(scalars, count, parts, span, hidden_in, out_grad, gain):
    rows, width = span // parts, hidden_in.shape[1]
    narrow = width // count % 128
    owners = scalars[parts : parts + count]
    upper = pl.BlockSpec((rows, width), lambda i, s: (s[2 * i], 0))
    lower = pl.BlockSpec((rows, width), lambda i, s: (s[2 * i + 1], 0))
    own = pl.BlockSpec((rows, width), lambda i, s: (i // (parts // 4), 0))
    plain = pl.BlockSpec((2 * rows, width), lambda i, s: (i, 0))
    shape = jax.ShapeDtypeStruct((span, width), BF16)
    short = jax.ShapeDtypeStruct((2 * rows, width), BF16)
    x, g, m, mine, unmoved, normed = pl.pallas_call(
        functools.partial(enter_kernel, count, parts),
        out_shape=(short, short, shape, shape, shape, shape),
        grid_spec=pltpu.PrefetchScalarGridSpec(
            num_scalar_prefetch=1,
            grid=(parts // 2,),
            in_specs=[upper, lower, upper, lower, pl.BlockSpec((1, width), lambda i, s: (0, 0))],
            out_specs=(own, own, plain, plain, plain, plain),
        ),
        compiler_params=params(),
        cost_estimate=cost(10 * span * width, 8 * span * width),
        name="enter",
    )(scalars, hidden_in, hidden_in, out_grad, out_grad, gain)
    if narrow:
        x, g, mine, normed = (columns(v, owners) for v in (x, g, mine, normed))
    return x, g, m, mine, unmoved, normed


def leave_kernel(count, parts, scalars, *refs):
    pieces, out_ref = refs[:4], refs[4]
    blocks, size = parts // 4, out_ref.shape[1] // count
    rows = out_ref.shape[0] // parts
    for i, in_ref in enumerate(pieces):

        @pl.when(pl.program_id(0) == i)
        def _(i=i, in_ref=in_ref):
            for part in range(blocks):
                at = pl.ds(pl.multiple_of(scalars[i * blocks + part] * rows, rows), rows)
                for p in range(count):
                    block = in_ref[part * rows : (part + 1) * rows, p * size : (p + 1) * size]
                    out_ref[at, column_place(scalars, parts, p, size)] = block.astype(out_ref.dtype)


def leave(scalars, count, parts, pieces, dtype):
    rows, width = pieces[0].shape
    place = lambda k: lambda i, s: (0, 0)
    if len(pieces) == 1:
        rows, pieces = rows // 4, pieces * 4
        place = lambda k: lambda i, s: (k, 0)
    if width // count % 128:
        owners, scalars = still(scalars, count, parts)
        pieces = [columns(piece, jnp.argsort(owners)) for piece in pieces]
    return pl.pallas_call(
        functools.partial(leave_kernel, count, parts),
        out_shape=jax.ShapeDtypeStruct((4 * rows, width), dtype),
        grid_spec=pltpu.PrefetchScalarGridSpec(
            num_scalar_prefetch=1,
            grid=(4,),
            in_specs=[pl.BlockSpec((rows, width), place(k)) for k in range(4)],
            out_specs=pl.BlockSpec((4 * rows, width), lambda i, s: (0, 0)),
        ),
        compiler_params=params(),
        cost_estimate=cost(0, 24 * rows * width),
        name="leave",
    )(scalars, *pieces)


def spread_kernel(tiles, count, parts, summed, *refs):
    homes, refs = (refs[0], refs[1:]) if parts else (None, refs)
    values, out_ref = refs[:count], refs[3 * count + summed]
    for h in range(2):

        @pl.when(pl.program_id(0) // tiles == h)
        def _(h=h):
            total = None
            for k in range(count):
                term = lax.dot_general(
                    values[k][...], refs[count + 2 * k + h][...], CONTRACT_COLS, preferred_element_type=F32
                )
                total = term if total is None else total + term
            if summed:
                norm_ref, sum_ref = refs[3 * count], refs[3 * count + 2]
                gain = jnp.sum(total * norm_ref[...].astype(F32), axis=0, keepdims=True)
                sum_ref[...] = jnp.broadcast_to(gain, sum_ref.shape)
            if parts:
                rows = out_ref.shape[0] // parts
                for i in range(parts):
                    at = pl.ds(pl.multiple_of(homes[i] * rows, rows), rows)
                    out_ref[at, :] = total[i * rows : (i + 1) * rows].astype(BF16)
            else:
                out_ref[...] = total.astype(BF16)


def spread(name, terms, part=0, parts=1, homes=None, normed=None):
    rows = terms[0][0].shape[0] // parts
    mid = terms[0][1][0].shape[0]
    tile = mid // 2
    specs, mats = [], []
    for value, pair, start in terms:
        n = value.shape[1]
        specs += [
            pl.BlockSpec((tile, n), lambda j, *s, c=start // n: (jnp.minimum(j, 1), c)),
            pl.BlockSpec((tile, n), lambda j, *s, c=start // n: (jnp.maximum(j - 2, 0), c)),
        ]
        mats += list(pair)
    held = [pl.BlockSpec((rows, v.shape[1]), lambda j, *s: (part, 0)) for v, _, _ in terms]
    wide = sum(v.shape[1] for v, _, _ in terms)
    summed = normed is not None
    shapes = [jax.ShapeDtypeStruct((rows, 2 * mid), BF16)]
    outs = [pl.BlockSpec((rows, tile), lambda j, *s: (0, j))]
    extra = []
    if summed:
        extra = [normed]
        specs.append(pl.BlockSpec((rows, tile), lambda j, *s: (part, j)))
        shapes.append(jax.ShapeDtypeStruct((8, 2 * mid), F32))
        outs.append(pl.BlockSpec((8, tile), lambda j, *s: (0, j)))
    out = pl.pallas_call(
        functools.partial(spread_kernel, 2, len(terms), 0 if homes is None else homes.shape[0], summed),
        out_shape=shapes,
        grid_spec=pltpu.PrefetchScalarGridSpec(
            num_scalar_prefetch=0 if homes is None else 1, grid=(4,), in_specs=held + specs, out_specs=outs
        ),
        compiler_params=params(),
        cost_estimate=cost(4 * rows * mid * wide, 2 * wide * (rows + 2 * mid) + 4 * rows * mid),
        name=name,
    )(*(() if homes is None else (homes,)), *(v for v, _, _ in terms), *mats, *extra)
    return out if summed else out[0]


def feed_kernel(first, count, parts, scalars, a_ref, b_ref, gate_ref, up_ref, gh_ref, *refs):
    refs = refs if first else refs[4:]
    hidden_out, gate_out, up_out, rows_out, part_out, x_ref, acc_ref = refs
    step, size = pl.program_id(0), x_ref.shape[1] // count
    moved = [column_place(scalars, parts, p, size) for p in range(count)]

    @pl.when(step == 0)
    def _():
        rows = a_ref.shape[0]
        rows_out[:rows, :] = a_ref[...]
        rows_out[rows:, :] = b_ref[...]
        for p in range(count):
            x_ref[:rows, moved[p]] = a_ref[:, p * size : (p + 1) * size]
            x_ref[rows:, moved[p]] = b_ref[:, p * size : (p + 1) * size]
        acc_ref[...] = jnp.zeros_like(acc_ref)

    gate = project(x_ref[...], gate_ref[...])
    up = project(x_ref[...], up_ref[...])
    grad = gh_ref[...]
    sig = sigmoid(gate)
    hidden_out[...] = (gate * sig * up).astype(BF16)
    grad_gate = (grad * up * sig * (1.0 + gate * (1.0 - sig))).astype(BF16)
    grad_up = (grad * (gate * sig)).astype(BF16)
    gate_out[...] = grad_gate
    up_out[...] = grad_up
    acc_ref[...] += col_contract(grad_gate, gate_ref[...]) + col_contract(grad_up, up_ref[...])

    @pl.when(step == pl.num_programs(0) - 1)
    def _():
        for p in range(count):
            part_out[:, p * size : (p + 1) * size] = acc_ref[:, moved[p]].astype(BF16)


def feed(scalars, count, parts, part, pieces, mat, grad_hidden, olds):
    span, ff = grad_hidden.shape
    piece, width = pieces[0].shape
    rows = 2 * piece
    tile = 256 if ff % 256 == 0 else ff
    steps = ff // tile
    narrow = width // count % 128
    owners = scalars[parts : parts + count]
    given = [columns(x, jnp.argsort(owners)) for x in pieces] if narrow else pieces
    held = pl.BlockSpec((piece, width), lambda j, s: (0, 0))
    columns_of = lambda shift: pl.BlockSpec((width, tile), lambda j, s: (0, shift + j))
    cols = pl.BlockSpec((rows, tile), lambda j, s: (part, j))
    first = olds is None
    olds = () if first else tuple(olds)
    wide = jax.ShapeDtypeStruct((span, ff), BF16)
    out = pl.pallas_call(
        functools.partial(feed_kernel, first, count, parts),
        out_shape=(
            wide,
            wide,
            wide,
            jax.ShapeDtypeStruct((span, width), BF16),
            jax.ShapeDtypeStruct((rows, width), BF16),
        ),
        grid_spec=pltpu.PrefetchScalarGridSpec(
            num_scalar_prefetch=1,
            grid=(steps,),
            in_specs=[held, held, columns_of(0), columns_of(steps), cols]
            + [pl.BlockSpec(memory_space=pl.ANY)] * len(olds),
            out_specs=(
                cols,
                cols,
                cols,
                pl.BlockSpec((rows, width), lambda j, s: (part, 0)),
                pl.BlockSpec((rows, width), lambda j, s: (0, 0)),
            ),
            scratch_shapes=[pltpu.VMEM((rows, width), BF16), pltpu.VMEM((rows, width), F32)],
        ),
        input_output_aliases={6 + i: i for i in range(len(olds))},
        compiler_params=params(),
        cost_estimate=cost(8 * rows * width * ff, 8 * width * ff, 2 * rows * ff),
        name="feed",
    )(scalars, *given, mat, mat, grad_hidden, *olds)
    return out[:4], columns(out[4], owners) if narrow else out[4]


def descend_kernel(parts, homes, value_ref, mat_ref, out_ref):
    total = col_contract(value_ref[...], mat_ref[...])
    rows = out_ref.shape[0] // parts
    for i in range(parts):
        at = pl.ds(pl.multiple_of(homes[i] * rows, rows), rows)
        out_ref[at, :] = total[i * rows : (i + 1) * rows].astype(BF16)


def descend(homes, owners, value, mat):
    rows, n = value.shape
    width, count, parts = mat.shape[0], owners.shape[0], homes.shape[0]
    narrow = width // count % 128
    steps = 4 if narrow else count
    out = pl.pallas_call(
        functools.partial(descend_kernel, parts),
        out_shape=jax.ShapeDtypeStruct((rows, width), BF16),
        grid_spec=pltpu.PrefetchScalarGridSpec(
            num_scalar_prefetch=1,
            grid=(steps,),
            in_specs=[
                pl.BlockSpec((rows, n), lambda j, s: (0, 0)),
                pl.BlockSpec((width // steps, n), lambda j, s: (s[parts + j], 0)),
            ],
            out_specs=pl.BlockSpec((rows, width // steps), lambda j, s: (0, j)),
        ),
        compiler_params=params(),
        cost_estimate=cost(2 * rows * width * n, 2 * (rows + width) * n + 2 * rows * width),
        name="descend",
    )(jnp.concatenate([homes, jnp.arange(4, dtype=jnp.int32) if narrow else owners]), value, mat)
    return columns(out, owners) if narrow else out


def plane_grads_kernel(count, *refs):
    out_ref, start = refs[-1], 0
    for left, right in zip(refs[:count], refs[count : 2 * count]):
        size = right.shape[1]
        out_ref[:, start : start + size] = row_contract(left[...], right[...]).astype(BF16)
        start += size


def plane_grads(name, terms, total, old=None):
    span, width = terms[0][0].shape
    tile = 256
    cols = sum(g.shape[1] for _, g in terms)
    at = 0 if old is None else total // cols - 1
    left = pl.BlockSpec((span, tile), lambda j: (0, j))
    held = [pl.BlockSpec(g.shape, lambda j: (0, 0)) for _, g in terms]
    olds = () if old is None else (old,)
    return pl.pallas_call(
        functools.partial(plane_grads_kernel, len(terms)),
        out_shape=jax.ShapeDtypeStruct((width, total), BF16),
        grid=(width // tile,),
        in_specs=[left] * len(terms) + held + [pl.BlockSpec(memory_space=pl.ANY)] * len(olds),
        out_specs=pl.BlockSpec((tile, cols), lambda j: (j, at)),
        input_output_aliases={2 * len(terms): 0} if olds else {},
        compiler_params=params(),
        cost_estimate=cost(2 * span * width * cols, 2 * span * (2 * width + cols) + 2 * width * cols),
        name=name,
    )(*(a for a, _ in terms), *(g for _, g in terms), *olds)


def enter_heads_kernel(heads, head_dim, paired, x_ref, near_ref, far_ref, cos_ref, sin_ref, gain_ref, p_out, r_out):
    mid = x_ref.shape[1] // 2
    proj = project(x_ref[:, :mid], near_ref[...]) + project(x_ref[:, mid:], far_ref[...])
    p_out[...] = proj
    for h in range(heads):
        unit, _ = unit_of(proj[:, h * head_dim : (h + 1) * head_dim])
        turned = turn(unit * gain_ref[...], cos_ref, sin_ref, 1.0).astype(BF16)
        at = (2 * h if paired else h) * head_dim
        r_out[:, at : at + head_dim] = turned
        if paired:
            value = proj[:, (heads + h) * head_dim : (heads + h + 1) * head_dim]
            r_out[:, at + head_dim : at + 2 * head_dim] = value.astype(BF16)


def enter_heads(name, heads, head_dim, paired, normed, mats, at, cols, cos, sin, gain):
    span, width = normed.shape
    rows = span // 2
    spec = lambda n: pl.BlockSpec((rows, n), lambda i: (i, 0))
    mat = pl.BlockSpec((width // 2, cols), lambda i: (0, at // cols))
    turned = heads * head_dim * (2 if paired else 1)
    return pl.pallas_call(
        functools.partial(enter_heads_kernel, heads, head_dim, paired),
        out_shape=(jax.ShapeDtypeStruct((span, cols), F32), jax.ShapeDtypeStruct((span, turned), BF16)),
        grid=(2,),
        in_specs=[spec(width), mat, mat, spec(head_dim), spec(head_dim), pl.BlockSpec((1, head_dim), lambda i: (0, 0))],
        out_specs=(spec(cols), spec(turned)),
        compiler_params=params(),
        cost_estimate=cost(2 * span * width * cols, 2 * width * (span + cols) + 6 * span * cols),
        name=name,
    )(normed, *mats, cos, sin, gain)


def unit_of(value):
    inverse = lax.rsqrt(jnp.mean(value * value, axis=-1, keepdims=True) + EPSILON)
    return value * inverse, inverse


def turn(value, cos_ref, sin_ref, sign):
    half = value.shape[-1] // 2
    return value * cos_ref[...] + sign * pltpu.roll(value, half, 1) * sin_ref[...]


def attend_kernel(group, head_dim, turns, first, scalars, q_ref, gate_ref, spot_ref, key_ref, oo_ref, of_ref, *refs):
    blocks = len(turns)
    kv_refs = refs[:blocks]
    rest = refs[blocks:] if first else refs[blocks + 1 :]
    mixed_out, sum_out, gated_out, part_out, acc_ref, total_ref, out_acc = rest
    scale = head_dim**-0.5 * math.log2(math.e)
    own = scalars[0]
    step, mid = pl.program_id(0), out_acc.shape[1] // 2

    @pl.when(step == 0)
    def _():
        out_acc[...] = jnp.zeros_like(out_acc)

    for h in range(group):
        cols = slice(h * head_dim, (h + 1) * head_dim)
        query = q_ref[:, cols]

        def scores(ref):
            return lax.dot_general(query, ref[:, :head_dim], CONTRACT_COLS, preferred_element_type=F32)

        allowed = (key_ref[...] <= spot_ref[...]) & (key_ref[...] < scalars[1])
        terms = jnp.where(allowed, jnp.exp2(scores(kv_refs[0]) * scale), 0.0)
        total_ref[...] = jnp.sum(terms, axis=-1, keepdims=True)
        acc_ref[...] = project(terms.astype(BF16), kv_refs[0][:, head_dim:])
        for place in range(1, blocks):

            @pl.when((own ^ turns[place]) < own)
            def _(ref=kv_refs[place]):
                terms = jnp.exp2(scores(ref) * scale)
                total_ref[...] += jnp.sum(terms, axis=-1, keepdims=True)
                acc_ref[...] += project(terms.astype(BF16), ref[:, head_dim:])

        mixed = acc_ref[...] / total_ref[...]
        mixed_out[:, cols] = mixed
        gated_out[:, cols] = (mixed * sigmoid(gate_ref[:, cols])).astype(BF16)
        sum_out[:, cols] = jnp.broadcast_to(total_ref[...], mixed.shape)
    gated = gated_out[...]
    out_acc[:, :mid] += col_contract(gated, oo_ref[...])
    out_acc[:, mid:] += col_contract(gated, of_ref[...])

    @pl.when(step == pl.num_programs(0) - 1)
    def _():
        part_out[...] = out_acc[...].astype(BF16)


def attend(scalars, part, parts, group, head_dim, turns, query, proj, gate_at, spots, keys, mats, out_at, kvs, old):
    span, width = query.shape
    rows, wide, mid = span // parts, group * head_dim, mats[0].shape[0]
    head = pl.BlockSpec((rows, wide), lambda g, s: (part, g))
    out = pl.BlockSpec((rows, wide), lambda g, s: (0, g))
    mat = pl.BlockSpec((mid, wide), lambda g, s: (0, out_at // wide + g))
    first = old is None
    olds = () if first else (old,)
    return pl.pallas_call(
        functools.partial(attend_kernel, group, head_dim, turns, first),
        out_shape=(
            jax.ShapeDtypeStruct((rows, width), F32),
            jax.ShapeDtypeStruct((rows, width), F32),
            jax.ShapeDtypeStruct((span, width), BF16),
            jax.ShapeDtypeStruct((rows, 2 * mid), BF16),
        ),
        grid_spec=pltpu.PrefetchScalarGridSpec(
            num_scalar_prefetch=1,
            grid=(width // wide,),
            in_specs=[
                head,
                pl.BlockSpec((rows, wide), lambda g, s: (part, gate_at // wide + g)),
                pl.BlockSpec((rows, 1), lambda g, s: (part, 0)),
                pl.BlockSpec((1, span), lambda g, s: (0, 0)),
                mat,
                mat,
            ]
            + [pl.BlockSpec((span, 2 * head_dim), lambda g, s: (0, g))] * len(kvs)
            + [pl.BlockSpec(memory_space=pl.ANY)] * len(olds),
            out_specs=(out, out, head, pl.BlockSpec((rows, 2 * mid), lambda g, s: (0, 0))),
            scratch_shapes=[
                pltpu.VMEM((rows, head_dim), F32),
                pltpu.VMEM((rows, 1), F32),
                pltpu.VMEM((rows, 2 * mid), F32),
            ],
        ),
        input_output_aliases={7 + len(kvs): 2} if olds else {},
        compiler_params=params(),
        cost_estimate=cost(
            4 * rows * width * span * len(kvs) + 4 * rows * width * mid,
            4 * span * width * len(kvs) + 20 * rows * width + 4 * mid * width,
            rows * span * len(kvs) * width // head_dim,
        ),
        name="attend",
    )(scalars, query, proj, spots, keys, *mats, *kvs, *olds)


def attend_back_kernel(group, head_dim, turns, first, count, scalars, *refs):
    blocks = len(turns)
    q_ref, query_ref, gate_ref, mixed_ref, sum_ref, a_ref, b_ref, oo_ref, of_ref = refs[:9]
    spot_ref, key_ref, cos_ref, sin_ref, gain_ref = refs[9:14]
    kv_refs = refs[14 : 14 + blocks]
    rest = refs[14 + blocks :]
    old_refs = () if first else rest[:blocks]
    rest = rest if first else rest[blocks + 3 :]
    gq_out, ggate_out, rows_out, gain_out = rest[:4]
    new_refs = rest[4 : 4 + blocks]
    gq_ref, x_ref = rest[4 + blocks :]
    mid = x_ref.shape[1] // 2

    @pl.when(pl.program_id(0) == 0)
    def _():
        piece = a_ref.shape[0]
        x_ref[:piece, :] = a_ref[...]
        x_ref[piece:, :] = b_ref[...]
        size = x_ref.shape[1] // count
        for p in range(count):
            rows_out[:, column_place(scalars, 2, p, size)] = x_ref[:, p * size : (p + 1) * size]

    all_gated = project(x_ref[:, :mid], oo_ref[...]) + project(x_ref[:, mid:], of_ref[...])
    score_scale = head_dim**-0.5
    scale = score_scale * math.log2(math.e)
    own = scalars[0]
    rows = q_ref.shape[0]

    def as_row(column):
        return jnp.transpose(jnp.broadcast_to(column, (rows, head_dim)))[:1, :]

    for place in range(blocks):
        if first:
            new_refs[place][...] = jnp.zeros_like(new_refs[place])
        else:
            new_refs[place][...] = old_refs[place][...]
    gain_total = jnp.zeros((1, head_dim), F32)
    for h in range(group):
        cols = slice(h * head_dim, (h + 1) * head_dim)
        query = q_ref[:, cols]
        gate = sigmoid(gate_ref[:, cols])
        grad_gated, mixed = all_gated[:, cols], mixed_ref[:, cols]
        grad_mixed = (grad_gated * gate).astype(BF16)
        ggate_out[:, cols] = (grad_gated * mixed * gate * (1.0 - gate)).astype(BF16)
        row_dot = as_row(jnp.sum(grad_mixed.astype(F32) * mixed, axis=-1, keepdims=True))
        row_log = as_row(jnp.log2(sum_ref[:, cols][:, :1]))
        gq_ref[...] = jnp.zeros_like(gq_ref)

        def block(kv_ref, new_ref, masked):
            key, value = kv_ref[:, :head_dim], kv_ref[:, head_dim:]
            scores = lax.dot_general(key, query, CONTRACT_COLS, preferred_element_type=F32)
            probs = jnp.exp2(scores * scale - row_log)
            if masked:
                allowed = (key_ref[...] <= spot_ref[...]) & (key_ref[...] < scalars[1])
                probs = jnp.where(allowed, probs, 0.0)
            grad_probs = lax.dot_general(value, grad_mixed, CONTRACT_COLS, preferred_element_type=F32)
            grad_scores = (probs * (grad_probs - row_dot)).astype(BF16)
            new_ref[:, head_dim:] += project(probs.astype(BF16), grad_mixed)
            new_ref[:, :head_dim] += project(grad_scores, query)
            gq_ref[...] += lax.dot_general(grad_scores, key, CONTRACT_ROWS, preferred_element_type=F32)

        block(kv_refs[0], new_refs[0], True)
        for place in range(1, blocks):

            @pl.when((own ^ turns[place]) < own)
            def _(place=place):
                block(kv_refs[place], new_refs[place], False)

        unit, inverse = unit_of(query_ref[:, cols])
        back = turn(gq_ref[...] * score_scale, cos_ref, sin_ref, -1.0)
        gain_total = gain_total + jnp.sum(back * unit, axis=0, keepdims=True)
        scaled = back * gain_ref[...]
        gq_out[:, cols] = (
            inverse * (scaled - unit * jnp.mean(scaled * unit, axis=-1, keepdims=True))
        ).astype(BF16)
    gain_out[...] = jnp.broadcast_to(gain_total, gain_out.shape)


def attend_back(
    scalars, count, part, parts, group, head_dim, turns, query, proj, gate_at, mixed, sums, pieces, mats, out_at, spots, keys, cos, sin, gain, kvs, olds
):
    span, width = query.shape
    rows, wide = span // parts, group * head_dim
    blocks, mid = len(kvs), mats[0].shape[0]
    mine = pl.BlockSpec((rows, wide), lambda g, s: (part, g))
    local = pl.BlockSpec((rows, wide), lambda g, s: (0, g))
    table = pl.BlockSpec((rows, head_dim), lambda g, s: (part, 0))
    pair = pl.BlockSpec((span, 2 * head_dim), lambda g, s: (0, g))
    piece = pl.BlockSpec(pieces[0].shape, lambda g, s: (0, 0))
    mat = pl.BlockSpec((mid, wide), lambda g, s: (0, out_at // wide + g))
    first = olds is None
    olds = () if first else tuple(olds)
    kv_shape = jax.ShapeDtypeStruct(kvs[0].shape, F32)
    steps = width // wide
    before = 15 + blocks
    out = pl.pallas_call(
        functools.partial(attend_back_kernel, group, head_dim, turns, first, count),
        out_shape=(
            jax.ShapeDtypeStruct((span, width), BF16),
            jax.ShapeDtypeStruct((span, width), BF16),
            jax.ShapeDtypeStruct((span, 2 * mid), BF16),
            jax.ShapeDtypeStruct((8 * steps, head_dim), F32),
        )
        + (kv_shape,) * blocks,
        grid_spec=pltpu.PrefetchScalarGridSpec(
            num_scalar_prefetch=1,
            grid=(steps,),
            in_specs=[
                mine,
                mine,
                pl.BlockSpec((rows, wide), lambda g, s: (part, gate_at // wide + g)),
                local,
                local,
                piece,
                piece,
                mat,
                mat,
                pl.BlockSpec((1, rows), lambda g, s: (0, part)),
                pl.BlockSpec((span, 1), lambda g, s: (0, 0)),
                table,
                table,
                pl.BlockSpec((1, head_dim), lambda g, s: (0, 0)),
            ]
            + [pair] * (blocks + min(len(olds), blocks))
            + [pl.BlockSpec(memory_space=pl.ANY)] * max(len(olds) - blocks, 0),
            out_specs=(
                mine,
                mine,
                pl.BlockSpec((rows, 2 * mid), lambda g, s: (part, 0)),
                pl.BlockSpec((8, head_dim), lambda g, s: (g, 0)),
            )
            + (pair,) * blocks,
            scratch_shapes=[pltpu.VMEM((rows, head_dim), F32), pltpu.VMEM((rows, 2 * mid), BF16)],
        ),
        input_output_aliases={}
        if first
        else {**{before + i: 4 + i for i in range(blocks)}, **{before + blocks + i: i for i in range(3)}},
        compiler_params=params(),
        cost_estimate=cost(
            10 * rows * width * span * blocks + 4 * rows * width * mid,
            20 * span * width * blocks,
            rows * span * blocks * width // head_dim,
        ),
        name="attend_back",
    )(scalars, query, proj, proj, mixed, sums, *pieces, *mats, spots, keys, cos, sin, gain, *kvs, *olds)
    gain_part = sum(out[3][8 * g] for g in range(steps))
    return out[4:], out[:3], gain_part


def keys_back_kernel(kv_heads, head_dim, g_ref, p_ref, cos_ref, sin_ref, gain_ref, k_out, v_out, gain_out):
    gain_total = jnp.zeros((1, head_dim), F32)
    for h in range(kv_heads):
        cols = slice(h * head_dim, (h + 1) * head_dim)
        unit, inverse = unit_of(p_ref[:, cols])
        grad = g_ref[:, 2 * h * head_dim : (2 * h + 1) * head_dim] * head_dim**-0.5
        back = turn(grad, cos_ref, sin_ref, -1.0)
        gain_total = gain_total + jnp.sum(back * unit, axis=0, keepdims=True)
        scaled = back * gain_ref[...]
        k_out[:, cols] = (
            inverse * (scaled - unit * jnp.mean(scaled * unit, axis=-1, keepdims=True))
        ).astype(BF16)
        v_out[:, cols] = g_ref[:, (2 * h + 1) * head_dim : (2 * h + 2) * head_dim].astype(BF16)
    gain_out[...] = jnp.broadcast_to(gain_total, gain_out.shape)


def keys_back(kv_heads, head_dim, grad_kv, proj, key_at, cos, sin, gain):
    span = proj.shape[0]
    cols = kv_heads * head_dim
    key_block = key_at // cols
    whole = lambda a, b: pl.BlockSpec((a, b), lambda i: (0, 0))
    out = pl.pallas_call(
        functools.partial(keys_back_kernel, kv_heads, head_dim),
        out_shape=(
            jax.ShapeDtypeStruct((span, cols), BF16),
            jax.ShapeDtypeStruct((span, cols), BF16),
            jax.ShapeDtypeStruct((8, head_dim), F32),
        ),
        grid=(1,),
        in_specs=[
            whole(span, 2 * cols),
            pl.BlockSpec((span, cols), lambda i: (0, key_block)),
            whole(span, head_dim),
            whole(span, head_dim),
            whole(1, head_dim),
        ],
        out_specs=(whole(span, cols), whole(span, cols), whole(8, head_dim)),
        compiler_params=params(),
        cost_estimate=cost(40 * span * cols, 16 * span * cols),
        name="keys_back",
    )(grad_kv, proj, cos, sin, gain)
    return out[0], out[1], out[2][0]


def norm_back(gradient, unit_vals, inverse, gain_vec):
    scaled = gradient * gain_vec
    return inverse * (scaled - unit_vals * jnp.mean(scaled * unit_vals, axis=-1, keepdims=True))


def per_device(
    links,
    hidden_in,
    lengths,
    attn_gain,
    q_weight,
    gate_weight,
    k_weight,
    v_weight,
    q_gain,
    k_gain,
    o_weight,
    mlp_gain,
    w_gate,
    w_up,
    w_down,
    out_grad,
):
    dp_index, ctx_index, z_index = (lax.axis_index(a) for a in ("dp", "ctx", "tensor"))
    q_cols, k_cols, ff_cols = q_weight.shape[1], k_weight.shape[1], w_down.shape[1]
    span, width = hidden_in.shape
    mid, count = width // 2, 2 * links.half
    shard, head_shard = attn_gain.shape[0], q_gain.shape[0]
    head_dim = head_shard * count
    heads, kv_heads = q_cols // head_dim, k_cols // head_dim
    group = heads // kv_heads
    length = lengths[0]
    low = lambda *mats: jnp.concatenate([m.astype(BF16) for m in mats], axis=1)

    small = jnp.concatenate([attn_gain, mlp_gain, q_gain, k_gain]).astype(BF16)[None, :]
    gains, seen = links.small_gather(small)
    everywhere = lambda block: {p: block for p in range(len(links.bits))}
    paired = lambda half: (half, links.swap(half, "ctx", 1))
    plane = ("dp", "ctx")
    first_own = after(low(q_weight, gate_weight, k_weight, v_weight, o_weight), *seen)
    first_single = links.send_own(everywhere(first_own))
    attn_scale = gains[:, :shard].reshape(1, width).astype(F32)
    mlp_scale = gains[:, shard : 2 * shard].reshape(1, width).astype(F32)
    owners = jnp.stack([links.owner_of(p, dp_index, ctx_index) for p in range(count)]).astype(jnp.int32)
    pick = (owners[None, :] == jnp.arange(count)[:, None]).astype(BF16)
    mesh_gains = project(pick, gains)
    mesh_scale = mesh_gains[:, :shard].reshape(1, width)
    query_scale = mesh_gains[:, 2 * shard : 2 * shard + head_shard].reshape(1, head_dim)
    key_scale = mesh_gains[:, 2 * shard + head_shard :].reshape(1, head_dim)

    parts = 2 * links.tensor
    row_block = span // parts
    row_places = jnp.stack(
        [part * links.tensor + (z_index ^ j) for part in range(2) for j in links.turns]
    ).astype(jnp.int32)
    start = ctx_index * span
    scalars = jnp.concatenate(
        [row_places, owners.astype(jnp.int32), jnp.stack([start, length]).astype(jnp.int32)]
    )
    spots = (start + row_places[:, None] * row_block + jnp.arange(row_block)[None, :]).reshape(span)
    spots = spots.astype(jnp.int32)
    freq_steps = jnp.arange(head_dim // 2, dtype=F32) * (2.0 / head_dim)
    turned = spots.astype(F32)[:, None] * jnp.exp(-math.log(ROPE_BASE) * freq_steps)[None, :]
    cosine, sine = jnp.cos(turned), jnp.sin(turned)
    cos = jnp.concatenate([cosine, cosine], axis=1)
    sin = jnp.concatenate([-sine, sine], axis=1)
    spot_col, spot_row = spots[:, None], spots[None, :]

    stream, grad_out, plain_down, down_grad, plain_normed, normed = enter(
        scalars, count, parts, span, hidden_in, out_grad, after(mesh_scale, first_own)
    )
    first_single = {q: after(b, normed) for q, b in first_single.items()}
    feed_mat = lax.all_gather(after(low(w_gate, w_up), normed), plane, axis=0, tiled=True)
    down_mat = lax.all_gather(after(low(w_down), *first_single.values()), plane, axis=0, tiled=True)

    first_pairs = links.send_on(first_single)
    first_mat = paired(links.assemble(first_own, first_single, first_pairs))
    gate_at, key_at = q_cols, 2 * q_cols
    value_at, out_at = key_at + k_cols, key_at + 2 * k_cols
    kv_proj, kv = enter_heads(
        "enter_keys", kv_heads, head_dim, True, normed, first_mat, key_at, 2 * k_cols, cos, sin, key_scale
    )
    proj, query = enter_heads(
        "enter_queries", heads, head_dim, False, after(normed, kv), first_mat, 0, 2 * q_cols, cos, sin, query_scale
    )
    kvs, turns = [kv], [0]
    mask = links.ctx // 2
    while mask:
        kvs = kvs + [links.swap(b if i == 0 else after(b, query), "ctx", mask) for i, b in enumerate(kvs)]
        turns = turns + [p ^ mask for p in turns]
        mask //= 2
    at = jnp.concatenate([jnp.stack([ctx_index, length]).astype(jnp.int32), owners])
    half_rows = span // 2
    shard_rows = half_rows // links.tensor
    part_of = lambda value, t: value[t * half_rows : (t + 1) * half_rows]
    own_rows = lambda value, t: value[t * shard_rows : (t + 1) * shard_rows]
    live = [(part_of(spot_col, t)[:shard_rows] < length).astype(F32) for t in range(2)]
    mixed, sums, out_part, one = ([None] * 2 for _ in range(4))
    query_now, gated_all = query, None
    for t in range(2):
        mixed[t], sums[t], gated_all, out_part[t] = attend(
            at, t, 2, group, head_dim, turns, query_now, proj, gate_at, spot_col, spot_row, first_mat, out_at, kvs, gated_all
        )
        one[t] = links.scatter_first(out_part[t])
    middle, normed_two, unit_two, inverse_two, two = ([None] * 2 for _ in range(5))
    late = (one[1][1],)
    for t in range(2):
        attn_out, _ = links.scatter_rest(*one[t], late=late)
        middle[t] = own_rows(stream, t).astype(F32) + attn_out * live[t]
        inverse_two[t] = lax.rsqrt(jnp.mean(middle[t] * middle[t], axis=-1, keepdims=True) + EPSILON)
        unit_two[t] = middle[t] * inverse_two[t]
        normed_two[t] = (unit_two[t] * mlp_scale).astype(BF16)
        two[t] = links.gather_first(normed_two[t])
        late = (normed_two[t],)
    pieces_two = [links.gather_rest(*two[0], late=late)]
    pieces_two.append(links.gather_rest(*two[1], late=(pieces_two[0][0],)))

    grad_hidden = project(after(plain_down, one[1][1]), down_mat)
    back_part, three = [None] * 2, [None] * 2
    held = None
    for t in range(2):
        held, back_part[t] = feed(scalars, count, parts, t, pieces_two[t], feed_mat, grad_hidden, held)
        three[t] = links.scatter_first(back_part[t])
    hidden_all, grad_gate_all, grad_up_all, rows_two = held

    halves = lambda value: (value[:, : value.shape[1] // 2], value[:, value.shape[1] // 2 :])

    def grad_others(rows_of, cols, *before):
        left = after(rows_of[:, mid:], *before)
        parts = [row_contract(left, c).astype(BF16) for c in cols]
        return parts, [links.swap(p, "ctx", 1) for p in parts]

    def grad_totals(rows_of, cols, arrived, *before):
        left = after(rows_of[:, :mid], *before)
        return [(row_contract(left, c) + a.astype(F32)).astype(BF16) for c, a in zip(cols, arrived)]

    def grad_rest(firsts, *before):
        return [
            links.reduce_rest(kept, after(came, *before), turn) for turn, (kept, _, came) in enumerate(firsts)
        ]

    scaled_back = lambda back, t: own_rows(grad_out, t).astype(F32) + norm_back(
        back, unit_two[t], inverse_two[t], mlp_scale
    )
    grad_middle, attn_grad, four = ([None] * 2 for _ in range(3))
    back_a, seen_a = links.scatter_rest(*three[0], before=(hidden_all,))
    back_b, seen_b = links.scatter_rest(*three[1])
    feed_cols = [grad_gate_all, grad_up_all]
    over_plane = lambda part: lax.psum_scatter(part, plane, scatter_dimension=0, tiled=True).astype(F32)
    down_grad_part = row_contract(after(plain_down, three[0][1]), hidden_all).astype(BF16)
    grad_down = over_plane(down_grad_part)
    feed_others, feed_came = grad_others(rows_two, feed_cols, down_grad_part)
    homes = jnp.stack([(z_index ^ j) * 2 + part for part in range(2) for j in links.turns]).astype(jnp.int32)
    down_part = descend(homes, owners, after(hidden_all, *feed_others, three[1][1]), down_mat)
    for t, back in enumerate((back_a, back_b)):
        back = after(back, *((down_part,) if t == 0 else (attn_grad[0],)))
        grad_middle[t] = scaled_back(back, t)
        attn_grad[t] = (grad_middle[t] * live[t]).astype(BF16)
        four[t] = links.gather_first(attn_grad[t])
    grad_mlp_gain = sum(jnp.sum(b * unit_two[t], axis=0) for t, b in enumerate((back_a, back_b)))
    attn_shard = attn_grad[1]
    pieces_four = [links.gather_rest(*four[0], late=(attn_shard,))]
    pieces_four.append(links.gather_rest(*four[1]))
    down_sum = lax.psum_scatter(after(down_part, grad_down, pieces_four[0][1], pieces_four[1][0]), "tensor", scatter_dimension=0, tiled=True).astype(F32)
    backward = lambda t, pieces, olds: attend_back(
        at, count, t, 2, group, head_dim, turns, query, proj, gate_at, mixed[t], sums[t], pieces, first_mat, out_at,
        spot_row, spot_col, cos, sin, query_scale, kvs, olds,
    )
    feed_totals = grad_totals(rows_two, feed_cols, feed_came, pieces_four[0][1])
    ready = after(pieces_four[0][1], pieces_four[1][0], grad_down, *feed_totals)
    grad_kvs, held, gain_a = backward(0, (pieces_four[0][0], ready), None)
    back_places = jnp.array(
        [part * links.tensor + o for o in range(links.tensor) for part in range(2)], dtype=jnp.int32
    )
    last = pieces_four[1]
    grad_kvs, held, gain_b = backward(1, last, (*grad_kvs, *held))
    grad_query, grad_gates, attn_all = held
    down_sum = after(down_sum, grad_kvs[0])
    down_shard = jnp.concatenate(middle, axis=0) + down_sum * jnp.concatenate(live, axis=0)
    down_all = lax.all_gather(down_shard.astype(BF16), "tensor", axis=0, tiled=True)
    if width // count % 128:
        attn_all = columns(attn_all, jnp.argsort(owners))
    q_gain_part = gain_a + gain_b
    pieces = dict(zip(turns, grad_kvs))
    mask = 1
    kv_gone, kv_seen = [], []
    while len(pieces) > 1:
        near = [p for p in pieces if not p & mask]
        gone = [pieces[p ^ mask].astype(BF16) for p in near]
        came = links.swap(jnp.concatenate(gone, axis=0), "ctx", mask)
        kv_gone.append(gone)
        kv_seen.append(came)
        pieces = {
            p: pieces[p].astype(F32) + came[i * span : (i + 1) * span].astype(F32) for i, p in enumerate(near)
        }
        mask *= 2
    outer_part = plane_grads(
        "outer_grads", [(after(plain_normed, *kv_gone[-1]), grad_query), (plain_normed, grad_gates), (attn_all, gated_all)],
        3 * q_cols + 2 * k_cols,
    )
    grad_key, grad_value, k_gain_part = keys_back(
        kv_heads, head_dim, after(pieces[0], outer_part, down_shard), kv_proj, 0, cos, sin, key_scale
    )
    feed_first = [links.reduce_first(x, turn, *((grad_key,) if turn else ())) for turn, x in enumerate(feed_totals)]
    seven, eight, in_part, grad_in, attn_gain_part = ([None] * 2 for _ in range(5))
    late_query = grad_query
    for t in range(2):
        terms = [
            (late_query, first_mat, 0),
            (grad_gates, first_mat, gate_at),
            (grad_key, first_mat, key_at),
            (grad_value, first_mat, value_at),
        ]
        in_part[t], gain = spread("spread_in", terms, t, 2, normed=normed)
        attn_gain_part[t] = gain[0] / attn_scale[0]
        seven[t] = links.scatter_first(in_part[t] if t == 0 else after(in_part[1], seven[0][1]))
    inner_part = plane_grads(
        "inner_grads", [(after(plain_normed, attn_gain_part[1]), grad_key), (plain_normed, grad_value)], 3 * q_cols + 2 * k_cols, outer_part
    )
    inner_sum = over_plane(inner_part)
    summed = [links.scatter_rest(*seven[t]) for t in range(2)]
    late = ()
    for t in range(2):
        back = after(summed[t][0], *late)
        x = own_rows(stream, t).astype(F32)
        inverse = lax.rsqrt(jnp.mean(x * x, axis=-1, keepdims=True) + EPSILON)
        unit = x * inverse
        grad_in[t] = (grad_middle[t] + norm_back(back, unit, inverse, attn_scale)).astype(BF16)
        eight[t] = links.gather_first(grad_in[t])
        late = (grad_in[t],)
    feed_rest = grad_rest(feed_first, grad_in[0])
    hidden_out = leave(jnp.concatenate([back_places, scalars[parts:]]), count, parts, [after(down_all, in_part[1])], BF16)
    in_pieces = [*links.gather_rest(*eight[0], late=late)]
    in_pieces += links.gather_rest(*eight[1], late=(in_pieces[0],))
    attn_gain_part = sum(attn_gain_part)
    arrived_one = in_pieces[1]
    in_pieces[1] = after(in_pieces[1], hidden_out, *(r[0] for r in feed_rest))
    grad_in = leave(scalars, count, parts, in_pieces, F32)

    blocks = jnp.stack([attn_gain_part.reshape(count, shard), grad_mlp_gain.reshape(count, shard)])
    to_mesh = (owners[None, :] == jnp.arange(count)[:, None]).astype(F32)
    blocks = jnp.einsum("ap,kpn->kan", to_mesh, blocks, precision=lax.Precision.HIGHEST)
    packed = jnp.concatenate([blocks.reshape(1, -1), q_gain_part[None, :], k_gain_part[None, :]], axis=1)
    packed = links.add_all(packed, in_pieces[3], arrived_one, hidden_out, *(r[2] for r in feed_rest))[0]
    rank = dp_index * links.ctx + ctx_index
    take = lambda at, size: lax.dynamic_slice_in_dim(packed, at + rank * size, size)
    return (
        hidden_out,
        grad_in,
        take(0, shard),
        inner_sum[:, :q_cols],
        inner_sum[:, q_cols : 2 * q_cols],
        inner_sum[:, 3 * q_cols : 3 * q_cols + k_cols],
        inner_sum[:, 3 * q_cols + k_cols :],
        take(2 * width, head_shard),
        take(2 * width + head_dim, head_shard),
        inner_sum[:, 2 * q_cols : 3 * q_cols],
        take(width, shard),
        feed_rest[0][0],
        feed_rest[1][0],
        grad_down,
    )


def solution(mesh):
    links = Links(dict(mesh.shape))
    rows = P(("dp", "ctx"))
    plain = P(("dp", "ctx"), None)
    split = P(("dp", "ctx"), "tensor")

    def step(*arrays):
        return per_device(links, *arrays)

    return jax.shard_map(
        step,
        mesh=mesh,
        in_specs=(plain, P("dp"), rows, split, split, split, split, rows, rows, split, rows, split, split, split, plain),
        out_specs=(plain, plain, rows, split, split, split, split, rows, rows, split, rows, split, split, split),
        check_vma=False,
    )
```

```python
import functools
import math

import jax
import jax.numpy as jnp
from jax import lax
from jax.experimental import pallas as pl
from jax.experimental.pallas import tpu as pltpu
from jax.sharding import PartitionSpec as P

EPSILON = 1e-06
ROPE_BASE = 1000000.0
CONTRACT_ROWS = (((0,), (0,)), ((), ()))
CONTRACT_COLS = (((1,), (1,)), ((), ()))
F32 = jnp.float32
BF16 = jnp.bfloat16
VMEM_BYTES = 56 * 1024 * 1024


def project(operand, matrix):
    return jnp.dot(operand, matrix, preferred_element_type=F32)


def row_contract(first_op, second_op):
    return lax.dot_general(first_op, second_op, CONTRACT_ROWS, preferred_element_type=F32)


def col_contract(first_op, second_op):
    return lax.dot_general(first_op, second_op, CONTRACT_COLS, preferred_element_type=F32)


def sigmoid(value):
    return 1.0 / (1.0 + jnp.exp(-value))


def after(value, *others):
    if not others:
        return value
    return lax.optimization_barrier((value,) + others)[0]


def cost(flops, moved, exps=0):
    return pl.CostEstimate(flops=int(flops), bytes_accessed=int(moved), transcendentals=int(exps))


def params(**kwargs):
    return pltpu.CompilerParams(vmem_limit_bytes=VMEM_BYTES, **kwargs)


class Links:
    def __init__(self, sizes):
        self.dp, self.ctx, self.tensor = sizes["dp"], sizes["ctx"], sizes["tensor"]
        self.half = self.dp * self.ctx // 2
        ctx_bits = int(math.log2(self.ctx // 2))
        dp_bits = int(math.log2(self.dp))
        self.bits = [("ctx", 2 << i) for i in range(ctx_bits)] + [("dp", 1 << i) for i in range(dp_bits)]
        self.masks = [(2 << i) - 1 for i in range(int(math.log2(self.tensor)))]
        self.turns = [0]
        for mask in reversed(self.masks):
            self.turns = self.turns + [j ^ mask for j in self.turns]

    def swap(self, value, axis, mask):
        count = {"dp": self.dp, "ctx": self.ctx, "tensor": self.tensor}[axis]
        return lax.ppermute(value, axis, [(i, i ^ mask) for i in range(count)])

    def order(self, turn):
        places = list(range(len(self.bits)))
        return places if turn else places[::-1]

    def send_own(self, blocks):
        return {1 << p: self.swap(blocks[p], *self.bits[p]) for p in self.order(0)}

    def send_far(self, block):
        count = self.dp * self.ctx
        single = {}
        for q in range(1, self.half):
            far = (q // (self.ctx // 2)) * self.ctx + (q % (self.ctx // 2)) * 2
            single[q] = lax.ppermute(block, ("dp", "ctx"), [(i, i ^ far) for i in range(count)])
        return single

    def send_on(self, single):
        mid = next(iter(single.values())).shape[1] // 2
        left = {q: b[:, :mid] for q, b in single.items()}
        right = {q: b[:, mid:] for q, b in single.items()}
        for side, places in ((left, self.order(0)), (right, self.order(1))):
            for q in range(1, self.half):
                if q not in single:
                    self.reach(side, q, places)
        return {q: (left[q], right[q]) for q in left if q not in single}

    def assemble(self, block, single, pairs):
        blocks, groups = [], []
        for q in range(self.half):
            members = [block] if q == 0 else [single[q]] if q in single else list(pairs[q])
            groups.append(tuple(range(len(blocks), len(blocks) + len(members))))
            blocks += members
        return stack_blocks(groups, blocks)

    def reach(self, side, q, places):
        if q not in side:
            last = [p for p in places if q & (1 << p)][-1]
            self.reach(side, q ^ (1 << last), places)
            side[q] = self.swap(side[q ^ (1 << last)], *self.bits[last])

    def reduce_first(self, total, turn, *hold):
        rows = total.shape[0] // self.half
        pieces = {q: total[q * rows : (q + 1) * rows] for q in range(self.half)}
        return self.reduce_step(pieces, turn, 0, *hold)

    def reduce_step(self, pieces, turn, step, *hold):
        place = self.order(turn)[step]
        bit = 1 << place
        kept = {q: b for q, b in pieces.items() if not q & bit}
        gone = [pieces[q | bit].astype(BF16) for q in kept]
        sent = after(jnp.concatenate(gone, axis=0), *hold)
        return kept, [sent], self.swap(sent, *self.bits[place])

    def reduce_rest(self, kept, came, turn):
        gone = []
        for step in range(1, len(self.bits) + 1):
            rows = came.shape[0] // len(kept)
            pieces = {
                q: b.astype(F32) + came[i * rows : (i + 1) * rows].astype(F32) for i, (q, b) in enumerate(kept.items())
            }
            if step < len(self.bits):
                kept, sent, came = self.reduce_step(pieces, turn, step)
                gone += sent
        return pieces[0], gone, came

    def small_gather(self, row):
        far = self.send_far(row)
        own = jnp.concatenate([row] + [far[q] for q in range(1, self.half)], axis=0)
        return jnp.concatenate([own, self.swap(own, "ctx", 1)], axis=0), list(far.values())

    def owner_of(self, position, dp_index, ctx_index):
        h, q = position // self.half, position % self.half
        dp_far, ctx_far = q // (self.ctx // 2), (q % (self.ctx // 2)) * 2 + h
        return (dp_index ^ dp_far) * self.ctx + (ctx_index ^ ctx_far)

    def scatter_first(self, part):
        rows = part.shape[0] // 2
        return part[:rows], self.swap(part[rows:], "tensor", self.masks[0])

    def scatter_rest(self, kept, came, before=(), late=()):
        gone = seen = came
        kept = kept.astype(F32) + came.astype(F32)
        for mask in self.masks[1:]:
            rows = kept.shape[0] // 2
            gone = kept[rows:].astype(BF16)
            seen = self.swap(after(gone, *before), "tensor", mask)
            kept = kept[:rows] + after(seen, *late).astype(F32)
        return kept, seen

    def gather_first(self, shard):
        return shard, self.swap(shard, "tensor", self.masks[-1])

    def gather_rest(self, shard, came, late=()):
        came = after(came, *late)
        for mask in self.masks[-2::-1]:
            shard = jnp.concatenate([shard, came], axis=0)
            came = self.swap(shard, "tensor", mask)
        return shard, came

    def add_all(self, value, *before):
        value = after(value, *before)
        value = value + self.swap(value, "ctx", 1)
        for axis, mask in self.bits:
            value = value + self.swap(value, axis, mask)
        return value + sum(self.swap(value, "tensor", mask) for mask in range(1, self.tensor))


def still(scalars, count, parts):
    owners = scalars[parts : parts + count]
    return owners, lax.dynamic_update_slice(scalars, jnp.arange(count, dtype=scalars.dtype), (parts,))


def columns(value, owners):
    count = owners.shape[0]
    blocks = value.reshape(value.shape[0], count, value.shape[1] // count)
    return jnp.take(blocks, owners, axis=1).reshape(value.shape)


def column_place(scalars, parts, p, size):
    if size % 128:
        return pl.ds(p * size, size)
    return pl.ds(pl.multiple_of(scalars[parts + p] * size, size), size)


def stack_kernel(groups, *refs):
    out_ref = refs[-1]
    for q, group in enumerate(groups):

        @pl.when(pl.program_id(0) == q)
        def _(group=group):
            col = 0
            for i in group:
                out_ref[:, col : col + refs[i].shape[1]] = refs[i][...]
                col += refs[i].shape[1]


def stack_blocks(groups, blocks):
    rows, n = blocks[0].shape
    held = lambda b: pl.BlockSpec(b.shape, lambda i: (0, 0), pipeline_mode=pl.Buffered(1))
    return pl.pallas_call(
        functools.partial(stack_kernel, groups),
        out_shape=jax.ShapeDtypeStruct((rows * len(groups), n), blocks[0].dtype),
        grid=(len(groups),),
        in_specs=[held(b) for b in blocks],
        out_specs=pl.BlockSpec((rows, n), lambda i: (i, 0)),
        compiler_params=params(),
        cost_estimate=cost(0, 4 * rows * len(groups) * n),
        name="stack",
    )(*blocks)


def enter_kernel(
    count, parts, scalars, xa_ref, xb_ref, ga_ref, gb_ref, gain_ref, x_out, g_out, m_out, mine_out, plain_out, n_out
):
    step = pl.program_id(0)
    rows, width = xa_ref.shape
    size = width // count
    moved = [column_place(scalars, parts, p, size) for p in range(count)]
    for part, (x_ref, g_ref) in enumerate(((xa_ref, ga_ref), (xb_ref, gb_ref))):
        if part == 0:

            @pl.when(step % (parts // 4) == 0)
            def _(x_ref=x_ref, g_ref=g_ref):
                for p in range(count):
                    x_out[:, p * size : (p + 1) * size] = x_ref[:, moved[p]]
                    g_out[:, p * size : (p + 1) * size] = g_ref[:, moved[p]]

        place = slice(part * rows, (part + 1) * rows)
        spot = scalars[parts + count] + scalars[2 * step + part] * rows
        live = spot + lax.broadcasted_iota(jnp.int32, (rows, 1), 0) < scalars[parts + count + 1]
        m_out[place, :] = jnp.where(live, g_ref[...].astype(F32), 0.0).astype(BF16)
        wide = x_ref[...].astype(F32)
        inverse = lax.rsqrt(jnp.mean(wide * wide, axis=-1, keepdims=True) + EPSILON)
        plain_out[place, :] = (wide * inverse * gain_ref[...]).astype(BF16)
        for p in range(count):
            n_out[place, p * size : (p + 1) * size] = plain_out[place, moved[p]]
            mine_out[place, p * size : (p + 1) * size] = m_out[place, moved[p]]


def enter(scalars, count, parts, span, hidden_in, out_grad, gain):
    rows, width = span // parts, hidden_in.shape[1]
    narrow = width // count % 128
    owners = scalars[parts : parts + count]
    upper = pl.BlockSpec((rows, width), lambda i, s: (s[2 * i], 0))
    lower = pl.BlockSpec((rows, width), lambda i, s: (s[2 * i + 1], 0))
    own = pl.BlockSpec((rows, width), lambda i, s: (i // (parts // 4), 0))
    plain = pl.BlockSpec((2 * rows, width), lambda i, s: (i, 0))
    shape = jax.ShapeDtypeStruct((span, width), BF16)
    short = jax.ShapeDtypeStruct((2 * rows, width), BF16)
    x, g, m, mine, unmoved, normed = pl.pallas_call(
        functools.partial(enter_kernel, count, parts),
        out_shape=(short, short, shape, shape, shape, shape),
        grid_spec=pltpu.PrefetchScalarGridSpec(
            num_scalar_prefetch=1,
            grid=(parts // 2,),
            in_specs=[upper, lower, upper, lower, pl.BlockSpec((1, width), lambda i, s: (0, 0))],
            out_specs=(own, own, plain, plain, plain, plain),
        ),
        compiler_params=params(),
        cost_estimate=cost(10 * span * width, 8 * span * width),
        name="enter",
    )(scalars, hidden_in, hidden_in, out_grad, out_grad, gain)
    if narrow:
        x, g, mine, normed = (columns(v, owners) for v in (x, g, mine, normed))
    return x, g, m, mine, unmoved, normed


def leave_kernel(count, parts, scalars, *refs):
    pieces, out_ref = refs[:4], refs[4]
    blocks, size = parts // 4, out_ref.shape[1] // count
    rows = out_ref.shape[0] // parts
    for i, in_ref in enumerate(pieces):

        @pl.when(pl.program_id(0) == i)
        def _(i=i, in_ref=in_ref):
            for part in range(blocks):
                at = pl.ds(pl.multiple_of(scalars[i * blocks + part] * rows, rows), rows)
                for p in range(count):
                    block = in_ref[part * rows : (part + 1) * rows, p * size : (p + 1) * size]
                    out_ref[at, column_place(scalars, parts, p, size)] = block.astype(out_ref.dtype)


def leave(scalars, count, parts, pieces, dtype):
    rows, width = pieces[0].shape
    place = lambda k: lambda i, s: (0, 0)
    if len(pieces) == 1:
        rows, pieces = rows // 4, pieces * 4
        place = lambda k: lambda i, s: (k, 0)
    if width // count % 128:
        owners, scalars = still(scalars, count, parts)
        pieces = [columns(piece, jnp.argsort(owners)) for piece in pieces]
    return pl.pallas_call(
        functools.partial(leave_kernel, count, parts),
        out_shape=jax.ShapeDtypeStruct((4 * rows, width), dtype),
        grid_spec=pltpu.PrefetchScalarGridSpec(
            num_scalar_prefetch=1,
            grid=(4,),
            in_specs=[pl.BlockSpec((rows, width), place(k)) for k in range(4)],
            out_specs=pl.BlockSpec((4 * rows, width), lambda i, s: (0, 0)),
        ),
        compiler_params=params(),
        cost_estimate=cost(0, 24 * rows * width),
        name="leave",
    )(scalars, *pieces)


def spread_kernel(tiles, count, parts, summed, *refs):
    homes, refs = (refs[0], refs[1:]) if parts else (None, refs)
    values, out_ref = refs[:count], refs[3 * count + summed]
    for h in range(2):

        @pl.when(pl.program_id(0) // tiles == h)
        def _(h=h):
            total = None
            for k in range(count):
                term = lax.dot_general(
                    values[k][...], refs[count + 2 * k + h][...], CONTRACT_COLS, preferred_element_type=F32
                )
                total = term if total is None else total + term
            if summed:
                norm_ref, sum_ref = refs[3 * count], refs[3 * count + 2]
                gain = jnp.sum(total * norm_ref[...].astype(F32), axis=0, keepdims=True)
                sum_ref[...] = jnp.broadcast_to(gain, sum_ref.shape)
            if parts:
                rows = out_ref.shape[0] // parts
                for i in range(parts):
                    at = pl.ds(pl.multiple_of(homes[i] * rows, rows), rows)
                    out_ref[at, :] = total[i * rows : (i + 1) * rows].astype(BF16)
            else:
                out_ref[...] = total.astype(BF16)


def spread(name, terms, part=0, parts=1, homes=None, normed=None):
    rows = terms[0][0].shape[0] // parts
    mid = terms[0][1][0].shape[0]
    tile = mid // 2
    specs, mats = [], []
    for value, pair, start in terms:
        n = value.shape[1]
        specs += [
            pl.BlockSpec((tile, n), lambda j, *s, c=start // n: (jnp.minimum(j, 1), c)),
            pl.BlockSpec((tile, n), lambda j, *s, c=start // n: (jnp.maximum(j - 2, 0), c)),
        ]
        mats += list(pair)
    held = [pl.BlockSpec((rows, v.shape[1]), lambda j, *s: (part, 0)) for v, _, _ in terms]
    wide = sum(v.shape[1] for v, _, _ in terms)
    summed = normed is not None
    shapes = [jax.ShapeDtypeStruct((rows, 2 * mid), BF16)]
    outs = [pl.BlockSpec((rows, tile), lambda j, *s: (0, j))]
    extra = []
    if summed:
        extra = [normed]
        specs.append(pl.BlockSpec((rows, tile), lambda j, *s: (part, j)))
        shapes.append(jax.ShapeDtypeStruct((8, 2 * mid), F32))
        outs.append(pl.BlockSpec((8, tile), lambda j, *s: (0, j)))
    out = pl.pallas_call(
        functools.partial(spread_kernel, 2, len(terms), 0 if homes is None else homes.shape[0], summed),
        out_shape=shapes,
        grid_spec=pltpu.PrefetchScalarGridSpec(
            num_scalar_prefetch=0 if homes is None else 1, grid=(4,), in_specs=held + specs, out_specs=outs
        ),
        compiler_params=params(),
        cost_estimate=cost(4 * rows * mid * wide, 2 * wide * (rows + 2 * mid) + 4 * rows * mid),
        name=name,
    )(*(() if homes is None else (homes,)), *(v for v, _, _ in terms), *mats, *extra)
    return out if summed else out[0]


def feed_kernel(first, count, parts, scalars, a_ref, b_ref, gate_ref, up_ref, gh_ref, *refs):
    refs = refs if first else refs[4:]
    hidden_out, gate_out, up_out, rows_out, part_out, x_ref, acc_ref = refs
    step, size = pl.program_id(0), x_ref.shape[1] // count
    moved = [column_place(scalars, parts, p, size) for p in range(count)]

    @pl.when(step == 0)
    def _():
        rows = a_ref.shape[0]
        rows_out[:rows, :] = a_ref[...]
        rows_out[rows:, :] = b_ref[...]
        for p in range(count):
            x_ref[:rows, moved[p]] = a_ref[:, p * size : (p + 1) * size]
            x_ref[rows:, moved[p]] = b_ref[:, p * size : (p + 1) * size]
        acc_ref[...] = jnp.zeros_like(acc_ref)

    gate = project(x_ref[...], gate_ref[...])
    up = project(x_ref[...], up_ref[...])
    grad = gh_ref[...]
    sig = sigmoid(gate)
    hidden_out[...] = (gate * sig * up).astype(BF16)
    grad_gate = (grad * up * sig * (1.0 + gate * (1.0 - sig))).astype(BF16)
    grad_up = (grad * (gate * sig)).astype(BF16)
    gate_out[...] = grad_gate
    up_out[...] = grad_up
    acc_ref[...] += col_contract(grad_gate, gate_ref[...]) + col_contract(grad_up, up_ref[...])

    @pl.when(step == pl.num_programs(0) - 1)
    def _():
        for p in range(count):
            part_out[:, p * size : (p + 1) * size] = acc_ref[:, moved[p]].astype(BF16)


def feed(scalars, count, parts, part, pieces, mat, grad_hidden, olds):
    span, ff = grad_hidden.shape
    piece, width = pieces[0].shape
    rows = 2 * piece
    tile = 512 if ff % 512 == 0 else ff
    steps = ff // tile
    narrow = width // count % 128
    owners = scalars[parts : parts + count]
    given = [columns(x, jnp.argsort(owners)) for x in pieces] if narrow else pieces
    held = pl.BlockSpec((piece, width), lambda j, s: (0, 0))
    columns_of = lambda shift: pl.BlockSpec((width, tile), lambda j, s: (0, shift + j))
    cols = pl.BlockSpec((rows, tile), lambda j, s: (part, j))
    first = olds is None
    olds = () if first else tuple(olds)
    wide = jax.ShapeDtypeStruct((span, ff), BF16)
    out = pl.pallas_call(
        functools.partial(feed_kernel, first, count, parts),
        out_shape=(
            wide,
            wide,
            wide,
            jax.ShapeDtypeStruct((span, width), BF16),
            jax.ShapeDtypeStruct((rows, width), BF16),
        ),
        grid_spec=pltpu.PrefetchScalarGridSpec(
            num_scalar_prefetch=1,
            grid=(steps,),
            in_specs=[held, held, columns_of(0), columns_of(steps), cols]
            + [pl.BlockSpec(memory_space=pl.ANY)] * len(olds),
            out_specs=(
                cols,
                cols,
                cols,
                pl.BlockSpec((rows, width), lambda j, s: (part, 0)),
                pl.BlockSpec((rows, width), lambda j, s: (0, 0)),
            ),
            scratch_shapes=[pltpu.VMEM((rows, width), BF16), pltpu.VMEM((rows, width), F32)],
        ),
        input_output_aliases={6 + i: i for i in range(len(olds))},
        compiler_params=params(),
        cost_estimate=cost(8 * rows * width * ff, 8 * width * ff, 2 * rows * ff),
        name="feed",
    )(scalars, *given, mat, mat, grad_hidden, *olds)
    return out[:4], columns(out[4], owners) if narrow else out[4]


def descend_kernel(parts, homes, value_ref, mat_ref, out_ref):
    total = col_contract(value_ref[...], mat_ref[...])
    rows = out_ref.shape[0] // parts
    for i in range(parts):
        at = pl.ds(pl.multiple_of(homes[i] * rows, rows), rows)
        out_ref[at, :] = total[i * rows : (i + 1) * rows].astype(BF16)


def descend(homes, owners, value, mat):
    rows, n = value.shape
    width, count, parts = mat.shape[0], owners.shape[0], homes.shape[0]
    narrow = width // count % 128
    steps = 4 if narrow else count
    out = pl.pallas_call(
        functools.partial(descend_kernel, parts),
        out_shape=jax.ShapeDtypeStruct((rows, width), BF16),
        grid_spec=pltpu.PrefetchScalarGridSpec(
            num_scalar_prefetch=1,
            grid=(steps,),
            in_specs=[
                pl.BlockSpec((rows, n), lambda j, s: (0, 0)),
                pl.BlockSpec((width // steps, n), lambda j, s: (s[parts + j], 0)),
            ],
            out_specs=pl.BlockSpec((rows, width // steps), lambda j, s: (0, j)),
        ),
        compiler_params=params(),
        cost_estimate=cost(2 * rows * width * n, 2 * (rows + width) * n + 2 * rows * width),
        name="descend",
    )(jnp.concatenate([homes, jnp.arange(4, dtype=jnp.int32) if narrow else owners]), value, mat)
    return columns(out, owners) if narrow else out


def plane_grads_kernel(count, *refs):
    out_ref, start = refs[-1], 0
    for left, right in zip(refs[:count], refs[count : 2 * count]):
        size = right.shape[1]
        out_ref[:, start : start + size] = row_contract(left[...], right[...]).astype(BF16)
        start += size


def plane_grads(name, terms, total, old=None):
    span, width = terms[0][0].shape
    tile = 256
    cols = sum(g.shape[1] for _, g in terms)
    at = 0 if old is None else total // cols - 1
    left = pl.BlockSpec((span, tile), lambda j: (0, j))
    held = [pl.BlockSpec(g.shape, lambda j: (0, 0)) for _, g in terms]
    olds = () if old is None else (old,)
    return pl.pallas_call(
        functools.partial(plane_grads_kernel, len(terms)),
        out_shape=jax.ShapeDtypeStruct((width, total), BF16),
        grid=(width // tile,),
        in_specs=[left] * len(terms) + held + [pl.BlockSpec(memory_space=pl.ANY)] * len(olds),
        out_specs=pl.BlockSpec((tile, cols), lambda j: (j, at)),
        input_output_aliases={2 * len(terms): 0} if olds else {},
        compiler_params=params(),
        cost_estimate=cost(2 * span * width * cols, 2 * span * (2 * width + cols) + 2 * width * cols),
        name=name,
    )(*(a for a, _ in terms), *(g for _, g in terms), *olds)


def enter_heads_kernel(heads, head_dim, paired, x_ref, near_ref, far_ref, cos_ref, sin_ref, gain_ref, p_out, r_out):
    mid = x_ref.shape[1] // 2
    proj = project(x_ref[:, :mid], near_ref[...]) + project(x_ref[:, mid:], far_ref[...])
    p_out[...] = proj
    for h in range(heads):
        unit, _ = unit_of(proj[:, h * head_dim : (h + 1) * head_dim])
        turned = turn(unit * gain_ref[...], cos_ref, sin_ref, 1.0).astype(BF16)
        at = (2 * h if paired else h) * head_dim
        r_out[:, at : at + head_dim] = turned
        if paired:
            value = proj[:, (heads + h) * head_dim : (heads + h + 1) * head_dim]
            r_out[:, at + head_dim : at + 2 * head_dim] = value.astype(BF16)


def enter_heads(name, heads, head_dim, paired, normed, mats, at, cols, cos, sin, gain):
    span, width = normed.shape
    rows = span // 2
    spec = lambda n: pl.BlockSpec((rows, n), lambda i: (i, 0))
    mat = pl.BlockSpec((width // 2, cols), lambda i: (0, at // cols))
    turned = heads * head_dim * (2 if paired else 1)
    return pl.pallas_call(
        functools.partial(enter_heads_kernel, heads, head_dim, paired),
        out_shape=(jax.ShapeDtypeStruct((span, cols), F32), jax.ShapeDtypeStruct((span, turned), BF16)),
        grid=(2,),
        in_specs=[spec(width), mat, mat, spec(head_dim), spec(head_dim), pl.BlockSpec((1, head_dim), lambda i: (0, 0))],
        out_specs=(spec(cols), spec(turned)),
        compiler_params=params(),
        cost_estimate=cost(2 * span * width * cols, 2 * width * (span + cols) + 6 * span * cols),
        name=name,
    )(normed, *mats, cos, sin, gain)


def unit_of(value):
    inverse = lax.rsqrt(jnp.mean(value * value, axis=-1, keepdims=True) + EPSILON)
    return value * inverse, inverse


def turn(value, cos_ref, sin_ref, sign):
    half = value.shape[-1] // 2
    return value * cos_ref[...] + sign * pltpu.roll(value, half, 1) * sin_ref[...]


def attend_kernel(group, head_dim, turns, first, scalars, q_ref, gate_ref, spot_ref, key_ref, oo_ref, of_ref, *refs):
    blocks = len(turns)
    kv_refs = refs[:blocks]
    rest = refs[blocks:] if first else refs[blocks + 1 :]
    mixed_out, sum_out, gated_out, part_out, acc_ref, total_ref, out_acc = rest
    scale = head_dim**-0.5 * math.log2(math.e)
    own = scalars[0]
    step, mid = pl.program_id(0), out_acc.shape[1] // 2

    @pl.when(step == 0)
    def _():
        out_acc[...] = jnp.zeros_like(out_acc)

    for h in range(group):
        cols = slice(h * head_dim, (h + 1) * head_dim)
        query = q_ref[:, cols]

        def scores(ref):
            return lax.dot_general(query, ref[:, :head_dim], CONTRACT_COLS, preferred_element_type=F32)

        allowed = (key_ref[...] <= spot_ref[...]) & (key_ref[...] < scalars[1])
        terms = jnp.where(allowed, jnp.exp2(scores(kv_refs[0]) * scale), 0.0)
        total_ref[...] = jnp.sum(terms, axis=-1, keepdims=True)
        acc_ref[...] = project(terms.astype(BF16), kv_refs[0][:, head_dim:])
        for place in range(1, blocks):

            @pl.when((own ^ turns[place]) < own)
            def _(ref=kv_refs[place]):
                terms = jnp.exp2(scores(ref) * scale)
                total_ref[...] += jnp.sum(terms, axis=-1, keepdims=True)
                acc_ref[...] += project(terms.astype(BF16), ref[:, head_dim:])

        mixed = acc_ref[...] / total_ref[...]
        mixed_out[:, cols] = mixed
        gated_out[:, cols] = (mixed * sigmoid(gate_ref[:, cols])).astype(BF16)
        sum_out[:, cols] = jnp.broadcast_to(total_ref[...], mixed.shape)
    gated = gated_out[...]
    out_acc[:, :mid] += col_contract(gated, oo_ref[...])
    out_acc[:, mid:] += col_contract(gated, of_ref[...])

    @pl.when(step == pl.num_programs(0) - 1)
    def _():
        part_out[...] = out_acc[...].astype(BF16)


def attend(scalars, part, parts, group, head_dim, turns, query, proj, gate_at, spots, keys, mats, out_at, kvs, old):
    span, width = query.shape
    rows, wide, mid = span // parts, group * head_dim, mats[0].shape[0]
    head = pl.BlockSpec((rows, wide), lambda g, s: (part, g))
    out = pl.BlockSpec((rows, wide), lambda g, s: (0, g))
    mat = pl.BlockSpec((mid, wide), lambda g, s: (0, out_at // wide + g))
    first = old is None
    olds = () if first else (old,)
    return pl.pallas_call(
        functools.partial(attend_kernel, group, head_dim, turns, first),
        out_shape=(
            jax.ShapeDtypeStruct((rows, width), F32),
            jax.ShapeDtypeStruct((rows, width), F32),
            jax.ShapeDtypeStruct((span, width), BF16),
            jax.ShapeDtypeStruct((rows, 2 * mid), BF16),
        ),
        grid_spec=pltpu.PrefetchScalarGridSpec(
            num_scalar_prefetch=1,
            grid=(width // wide,),
            in_specs=[
                head,
                pl.BlockSpec((rows, wide), lambda g, s: (part, gate_at // wide + g)),
                pl.BlockSpec((rows, 1), lambda g, s: (part, 0)),
                pl.BlockSpec((1, span), lambda g, s: (0, 0)),
                mat,
                mat,
            ]
            + [pl.BlockSpec((span, 2 * head_dim), lambda g, s: (0, g))] * len(kvs)
            + [pl.BlockSpec(memory_space=pl.ANY)] * len(olds),
            out_specs=(out, out, head, pl.BlockSpec((rows, 2 * mid), lambda g, s: (0, 0))),
            scratch_shapes=[
                pltpu.VMEM((rows, head_dim), F32),
                pltpu.VMEM((rows, 1), F32),
                pltpu.VMEM((rows, 2 * mid), F32),
            ],
        ),
        input_output_aliases={7 + len(kvs): 2} if olds else {},
        compiler_params=params(),
        cost_estimate=cost(
            4 * rows * width * span * len(kvs) + 4 * rows * width * mid,
            4 * span * width * len(kvs) + 20 * rows * width + 4 * mid * width,
            rows * span * len(kvs) * width // head_dim,
        ),
        name="attend",
    )(scalars, query, proj, spots, keys, *mats, *kvs, *olds)


def attend_back_kernel(group, head_dim, turns, first, count, scalars, *refs):
    blocks = len(turns)
    q_ref, query_ref, gate_ref, mixed_ref, sum_ref, a_ref, b_ref, oo_ref, of_ref = refs[:9]
    spot_ref, key_ref, cos_ref, sin_ref, gain_ref = refs[9:14]
    kv_refs = refs[14 : 14 + blocks]
    rest = refs[14 + blocks :]
    old_refs = () if first else rest[:blocks]
    rest = rest if first else rest[blocks + 3 :]
    gq_out, ggate_out, rows_out, gain_out = rest[:4]
    new_refs = rest[4 : 4 + blocks]
    gq_ref, x_ref = rest[4 + blocks :]
    mid = x_ref.shape[1] // 2

    @pl.when(pl.program_id(0) == 0)
    def _():
        piece = a_ref.shape[0]
        x_ref[:piece, :] = a_ref[...]
        x_ref[piece:, :] = b_ref[...]
        size = x_ref.shape[1] // count
        for p in range(count):
            rows_out[:, column_place(scalars, 2, p, size)] = x_ref[:, p * size : (p + 1) * size]

    all_gated = project(x_ref[:, :mid], oo_ref[...]) + project(x_ref[:, mid:], of_ref[...])
    score_scale = head_dim**-0.5
    scale = score_scale * math.log2(math.e)
    own = scalars[0]
    rows = q_ref.shape[0]

    def as_row(column):
        return jnp.transpose(jnp.broadcast_to(column, (rows, head_dim)))[:1, :]

    for place in range(blocks):
        if first:
            new_refs[place][...] = jnp.zeros_like(new_refs[place])
        else:
            new_refs[place][...] = old_refs[place][...]
    gain_total = jnp.zeros((1, head_dim), F32)
    for h in range(group):
        cols = slice(h * head_dim, (h + 1) * head_dim)
        query = q_ref[:, cols]
        gate = sigmoid(gate_ref[:, cols])
        grad_gated, mixed = all_gated[:, cols], mixed_ref[:, cols]
        grad_mixed = (grad_gated * gate).astype(BF16)
        ggate_out[:, cols] = (grad_gated * mixed * gate * (1.0 - gate)).astype(BF16)
        row_dot = as_row(jnp.sum(grad_mixed.astype(F32) * mixed, axis=-1, keepdims=True))
        row_log = as_row(jnp.log2(sum_ref[:, cols][:, :1]))
        gq_ref[...] = jnp.zeros_like(gq_ref)

        def block(kv_ref, new_ref, masked):
            key, value = kv_ref[:, :head_dim], kv_ref[:, head_dim:]
            scores = lax.dot_general(key, query, CONTRACT_COLS, preferred_element_type=F32)
            probs = jnp.exp2(scores * scale - row_log)
            if masked:
                allowed = (key_ref[...] <= spot_ref[...]) & (key_ref[...] < scalars[1])
                probs = jnp.where(allowed, probs, 0.0)
            grad_probs = lax.dot_general(value, grad_mixed, CONTRACT_COLS, preferred_element_type=F32)
            grad_scores = (probs * (grad_probs - row_dot)).astype(BF16)
            new_ref[:, head_dim:] += project(probs.astype(BF16), grad_mixed)
            new_ref[:, :head_dim] += project(grad_scores, query)
            gq_ref[...] += lax.dot_general(grad_scores, key, CONTRACT_ROWS, preferred_element_type=F32)

        block(kv_refs[0], new_refs[0], True)
        for place in range(1, blocks):

            @pl.when((own ^ turns[place]) < own)
            def _(place=place):
                block(kv_refs[place], new_refs[place], False)

        unit, inverse = unit_of(query_ref[:, cols])
        back = turn(gq_ref[...] * score_scale, cos_ref, sin_ref, -1.0)
        gain_total = gain_total + jnp.sum(back * unit, axis=0, keepdims=True)
        scaled = back * gain_ref[...]
        gq_out[:, cols] = (
            inverse * (scaled - unit * jnp.mean(scaled * unit, axis=-1, keepdims=True))
        ).astype(BF16)
    gain_out[...] = jnp.broadcast_to(gain_total, gain_out.shape)


def attend_back(
    scalars, count, part, parts, group, head_dim, turns, query, proj, gate_at, mixed, sums, pieces, mats, out_at, spots, keys, cos, sin, gain, kvs, olds
):
    span, width = query.shape
    rows, wide = span // parts, group * head_dim
    blocks, mid = len(kvs), mats[0].shape[0]
    mine = pl.BlockSpec((rows, wide), lambda g, s: (part, g))
    local = pl.BlockSpec((rows, wide), lambda g, s: (0, g))
    table = pl.BlockSpec((rows, head_dim), lambda g, s: (part, 0))
    pair = pl.BlockSpec((span, 2 * head_dim), lambda g, s: (0, g))
    piece = pl.BlockSpec(pieces[0].shape, lambda g, s: (0, 0))
    mat = pl.BlockSpec((mid, wide), lambda g, s: (0, out_at // wide + g))
    first = olds is None
    olds = () if first else tuple(olds)
    kv_shape = jax.ShapeDtypeStruct(kvs[0].shape, F32)
    steps = width // wide
    before = 15 + blocks
    out = pl.pallas_call(
        functools.partial(attend_back_kernel, group, head_dim, turns, first, count),
        out_shape=(
            jax.ShapeDtypeStruct((span, width), BF16),
            jax.ShapeDtypeStruct((span, width), BF16),
            jax.ShapeDtypeStruct((span, 2 * mid), BF16),
            jax.ShapeDtypeStruct((8 * steps, head_dim), F32),
        )
        + (kv_shape,) * blocks,
        grid_spec=pltpu.PrefetchScalarGridSpec(
            num_scalar_prefetch=1,
            grid=(steps,),
            in_specs=[
                mine,
                mine,
                pl.BlockSpec((rows, wide), lambda g, s: (part, gate_at // wide + g)),
                local,
                local,
                piece,
                piece,
                mat,
                mat,
                pl.BlockSpec((1, rows), lambda g, s: (0, part)),
                pl.BlockSpec((span, 1), lambda g, s: (0, 0)),
                table,
                table,
                pl.BlockSpec((1, head_dim), lambda g, s: (0, 0)),
            ]
            + [pair] * (blocks + min(len(olds), blocks))
            + [pl.BlockSpec(memory_space=pl.ANY)] * max(len(olds) - blocks, 0),
            out_specs=(
                mine,
                mine,
                pl.BlockSpec((rows, 2 * mid), lambda g, s: (part, 0)),
                pl.BlockSpec((8, head_dim), lambda g, s: (g, 0)),
            )
            + (pair,) * blocks,
            scratch_shapes=[pltpu.VMEM((rows, head_dim), F32), pltpu.VMEM((rows, 2 * mid), BF16)],
        ),
        input_output_aliases={}
        if first
        else {**{before + i: 4 + i for i in range(blocks)}, **{before + blocks + i: i for i in range(3)}},
        compiler_params=params(),
        cost_estimate=cost(
            10 * rows * width * span * blocks + 4 * rows * width * mid,
            20 * span * width * blocks,
            rows * span * blocks * width // head_dim,
        ),
        name="attend_back",
    )(scalars, query, proj, proj, mixed, sums, *pieces, *mats, spots, keys, cos, sin, gain, *kvs, *olds)
    gain_part = sum(out[3][8 * g] for g in range(steps))
    return out[4:], out[:3], gain_part


def keys_back_kernel(kv_heads, head_dim, g_ref, p_ref, cos_ref, sin_ref, gain_ref, k_out, v_out, gain_out):
    gain_total = jnp.zeros((1, head_dim), F32)
    for h in range(kv_heads):
        cols = slice(h * head_dim, (h + 1) * head_dim)
        unit, inverse = unit_of(p_ref[:, cols])
        grad = g_ref[:, 2 * h * head_dim : (2 * h + 1) * head_dim] * head_dim**-0.5
        back = turn(grad, cos_ref, sin_ref, -1.0)
        gain_total = gain_total + jnp.sum(back * unit, axis=0, keepdims=True)
        scaled = back * gain_ref[...]
        k_out[:, cols] = (
            inverse * (scaled - unit * jnp.mean(scaled * unit, axis=-1, keepdims=True))
        ).astype(BF16)
        v_out[:, cols] = g_ref[:, (2 * h + 1) * head_dim : (2 * h + 2) * head_dim].astype(BF16)
    gain_out[...] = jnp.broadcast_to(gain_total, gain_out.shape)


def keys_back(kv_heads, head_dim, grad_kv, proj, key_at, cos, sin, gain):
    span = proj.shape[0]
    cols = kv_heads * head_dim
    key_block = key_at // cols
    whole = lambda a, b: pl.BlockSpec((a, b), lambda i: (0, 0))
    out = pl.pallas_call(
        functools.partial(keys_back_kernel, kv_heads, head_dim),
        out_shape=(
            jax.ShapeDtypeStruct((span, cols), BF16),
            jax.ShapeDtypeStruct((span, cols), BF16),
            jax.ShapeDtypeStruct((8, head_dim), F32),
        ),
        grid=(1,),
        in_specs=[
            whole(span, 2 * cols),
            pl.BlockSpec((span, cols), lambda i: (0, key_block)),
            whole(span, head_dim),
            whole(span, head_dim),
            whole(1, head_dim),
        ],
        out_specs=(whole(span, cols), whole(span, cols), whole(8, head_dim)),
        compiler_params=params(),
        cost_estimate=cost(40 * span * cols, 16 * span * cols),
        name="keys_back",
    )(grad_kv, proj, cos, sin, gain)
    return out[0], out[1], out[2][0]


def norm_back(gradient, unit_vals, inverse, gain_vec):
    scaled = gradient * gain_vec
    return inverse * (scaled - unit_vals * jnp.mean(scaled * unit_vals, axis=-1, keepdims=True))


def per_device(
    links,
    hidden_in,
    lengths,
    attn_gain,
    q_weight,
    gate_weight,
    k_weight,
    v_weight,
    q_gain,
    k_gain,
    o_weight,
    mlp_gain,
    w_gate,
    w_up,
    w_down,
    out_grad,
):
    dp_index, ctx_index, z_index = (lax.axis_index(a) for a in ("dp", "ctx", "tensor"))
    q_cols, k_cols, ff_cols = q_weight.shape[1], k_weight.shape[1], w_down.shape[1]
    span, width = hidden_in.shape
    mid, count = width // 2, 2 * links.half
    shard, head_shard = attn_gain.shape[0], q_gain.shape[0]
    head_dim = head_shard * count
    heads, kv_heads = q_cols // head_dim, k_cols // head_dim
    group = heads // kv_heads
    length = lengths[0]
    low = lambda *mats: jnp.concatenate([m.astype(BF16) for m in mats], axis=1)

    small = jnp.concatenate([attn_gain, mlp_gain, q_gain, k_gain]).astype(BF16)[None, :]
    gains, seen = links.small_gather(small)
    everywhere = lambda block: {p: block for p in range(len(links.bits))}
    paired = lambda half: (half, links.swap(half, "ctx", 1))
    plane = ("dp", "ctx")
    first_own = after(low(q_weight, gate_weight, k_weight, v_weight, o_weight), *seen)
    first_single = links.send_own(everywhere(first_own))
    attn_scale = gains[:, :shard].reshape(1, width).astype(F32)
    mlp_scale = gains[:, shard : 2 * shard].reshape(1, width).astype(F32)
    owners = jnp.stack([links.owner_of(p, dp_index, ctx_index) for p in range(count)]).astype(jnp.int32)
    pick = (owners[None, :] == jnp.arange(count)[:, None]).astype(BF16)
    mesh_gains = project(pick, gains)
    mesh_scale = mesh_gains[:, :shard].reshape(1, width)
    query_scale = mesh_gains[:, 2 * shard : 2 * shard + head_shard].reshape(1, head_dim)
    key_scale = mesh_gains[:, 2 * shard + head_shard :].reshape(1, head_dim)

    parts = 2 * links.tensor
    row_block = span // parts
    row_places = jnp.stack(
        [part * links.tensor + (z_index ^ j) for part in range(2) for j in links.turns]
    ).astype(jnp.int32)
    start = ctx_index * span
    scalars = jnp.concatenate(
        [row_places, owners.astype(jnp.int32), jnp.stack([start, length]).astype(jnp.int32)]
    )
    spots = (start + row_places[:, None] * row_block + jnp.arange(row_block)[None, :]).reshape(span)
    spots = spots.astype(jnp.int32)
    freq_steps = jnp.arange(head_dim // 2, dtype=F32) * (2.0 / head_dim)
    turned = spots.astype(F32)[:, None] * jnp.exp(-math.log(ROPE_BASE) * freq_steps)[None, :]
    cosine, sine = jnp.cos(turned), jnp.sin(turned)
    cos = jnp.concatenate([cosine, cosine], axis=1)
    sin = jnp.concatenate([-sine, sine], axis=1)
    spot_col, spot_row = spots[:, None], spots[None, :]

    stream, grad_out, plain_down, down_grad, plain_normed, normed = enter(
        scalars, count, parts, span, hidden_in, out_grad, after(mesh_scale, first_own)
    )
    feed_low, down_low = low(w_gate, w_up), low(w_down)
    first_single = {q: after(b, normed, feed_low, down_low) for q, b in first_single.items()}
    feed_mat = lax.all_gather(after(feed_low, normed), plane, axis=0, tiled=True)
    down_mat = lax.all_gather(after(down_low, *first_single.values()), plane, axis=0, tiled=True)

    first_pairs = links.send_on(first_single)
    first_mat = paired(links.assemble(first_own, first_single, first_pairs))
    gate_at, key_at = q_cols, 2 * q_cols
    value_at, out_at = key_at + k_cols, key_at + 2 * k_cols
    kv_proj, kv = enter_heads(
        "enter_keys", kv_heads, head_dim, True, normed, first_mat, key_at, 2 * k_cols, cos, sin, key_scale
    )
    proj, query = enter_heads(
        "enter_queries", heads, head_dim, False, after(normed, kv), first_mat, 0, 2 * q_cols, cos, sin, query_scale
    )
    kvs, turns = [kv], [0]
    mask = links.ctx // 2
    while mask:
        kvs = kvs + [links.swap(b if i == 0 else after(b, query), "ctx", mask) for i, b in enumerate(kvs)]
        turns = turns + [p ^ mask for p in turns]
        mask //= 2
    at = jnp.concatenate([jnp.stack([ctx_index, length]).astype(jnp.int32), owners])
    half_rows = span // 2
    shard_rows = half_rows // links.tensor
    part_of = lambda value, t: value[t * half_rows : (t + 1) * half_rows]
    own_rows = lambda value, t: value[t * shard_rows : (t + 1) * shard_rows]
    live = [(part_of(spot_col, t)[:shard_rows] < length).astype(F32) for t in range(2)]
    mixed, sums, out_part, one = ([None] * 2 for _ in range(4))
    query_now, gated_all = query, None
    for t in range(2):
        mixed[t], sums[t], gated_all, out_part[t] = attend(
            at, t, 2, group, head_dim, turns, query_now, proj, gate_at, spot_col, spot_row, first_mat, out_at, kvs, gated_all
        )
        one[t] = links.scatter_first(out_part[t])
    middle, normed_two, unit_two, inverse_two, two = ([None] * 2 for _ in range(5))
    late = (one[1][1],)
    for t in range(2):
        attn_out, _ = links.scatter_rest(*one[t], late=late)
        middle[t] = own_rows(stream, t).astype(F32) + attn_out * live[t]
        inverse_two[t] = lax.rsqrt(jnp.mean(middle[t] * middle[t], axis=-1, keepdims=True) + EPSILON)
        unit_two[t] = middle[t] * inverse_two[t]
        normed_two[t] = (unit_two[t] * mlp_scale).astype(BF16)
        two[t] = links.gather_first(normed_two[t])
        late = (normed_two[t],)
    pieces_two = [links.gather_rest(*two[0], late=late)]
    pieces_two.append(links.gather_rest(*two[1], late=(pieces_two[0][0],)))

    grad_hidden = project(after(plain_down, one[1][1]), down_mat)
    back_part, three = [None] * 2, [None] * 2
    held = None
    for t in range(2):
        held, back_part[t] = feed(scalars, count, parts, t, pieces_two[t], feed_mat, grad_hidden, held)
        three[t] = links.scatter_first(back_part[t])
    hidden_all, grad_gate_all, grad_up_all, rows_two = held

    halves = lambda value: (value[:, : value.shape[1] // 2], value[:, value.shape[1] // 2 :])

    def grad_others(rows_of, cols, *before):
        left = after(rows_of[:, mid:], *before)
        parts = [row_contract(left, c).astype(BF16) for c in cols]
        return parts, [links.swap(p, "ctx", 1) for p in parts]

    def grad_totals(rows_of, cols, arrived, *before):
        left = after(rows_of[:, :mid], *before)
        return [(row_contract(left, c) + a.astype(F32)).astype(BF16) for c, a in zip(cols, arrived)]

    def grad_rest(firsts, *before):
        return [
            links.reduce_rest(kept, after(came, *before), turn) for turn, (kept, _, came) in enumerate(firsts)
        ]

    scaled_back = lambda back, t: own_rows(grad_out, t).astype(F32) + norm_back(
        back, unit_two[t], inverse_two[t], mlp_scale
    )
    grad_middle, attn_grad, four = ([None] * 2 for _ in range(3))
    back_a, seen_a = links.scatter_rest(*three[0], before=(hidden_all,))
    back_b, seen_b = links.scatter_rest(*three[1])
    feed_cols = [grad_gate_all, grad_up_all]
    over_plane = lambda part: lax.psum_scatter(part, plane, scatter_dimension=0, tiled=True).astype(F32)
    down_grad_part = row_contract(after(plain_down, three[0][1]), hidden_all).astype(BF16)
    grad_down = over_plane(down_grad_part)
    feed_others, feed_came = grad_others(rows_two, feed_cols, down_grad_part)
    homes = jnp.stack([(z_index ^ j) * 2 + part for part in range(2) for j in links.turns]).astype(jnp.int32)
    down_part = descend(homes, owners, after(hidden_all, *feed_others, three[1][1]), down_mat)
    for t, back in enumerate((back_a, back_b)):
        back = after(back, *((down_part,) if t == 0 else (attn_grad[0],)))
        grad_middle[t] = scaled_back(back, t)
        attn_grad[t] = (grad_middle[t] * live[t]).astype(BF16)
        four[t] = links.gather_first(attn_grad[t])
    grad_mlp_gain = sum(jnp.sum(b * unit_two[t], axis=0) for t, b in enumerate((back_a, back_b)))
    attn_shard = attn_grad[1]
    pieces_four = [links.gather_rest(*four[0], late=(attn_shard,))]
    pieces_four.append(links.gather_rest(*four[1]))
    down_sum = lax.psum_scatter(after(down_part, grad_down, pieces_four[0][1], pieces_four[1][0]), "tensor", scatter_dimension=0, tiled=True).astype(F32)
    backward = lambda t, pieces, olds: attend_back(
        at, count, t, 2, group, head_dim, turns, query, proj, gate_at, mixed[t], sums[t], pieces, first_mat, out_at,
        spot_row, spot_col, cos, sin, query_scale, kvs, olds,
    )
    feed_totals = grad_totals(rows_two, feed_cols, feed_came, pieces_four[0][1])
    ready = after(pieces_four[0][1], pieces_four[1][0], grad_down, *feed_totals)
    grad_kvs, held, gain_a = backward(0, (pieces_four[0][0], ready), None)
    back_places = jnp.array(
        [part * links.tensor + o for o in range(links.tensor) for part in range(2)], dtype=jnp.int32
    )
    last = pieces_four[1]
    grad_kvs, held, gain_b = backward(1, last, (*grad_kvs, *held))
    grad_query, grad_gates, attn_all = held
    down_sum = after(down_sum, grad_kvs[0])
    down_shard = jnp.concatenate(middle, axis=0) + down_sum * jnp.concatenate(live, axis=0)
    down_all = lax.all_gather(down_shard.astype(BF16), "tensor", axis=0, tiled=True)
    if width // count % 128:
        attn_all = columns(attn_all, jnp.argsort(owners))
    q_gain_part = gain_a + gain_b
    pieces = dict(zip(turns, grad_kvs))
    mask = 1
    kv_gone, kv_seen = [], []
    while len(pieces) > 1:
        near = [p for p in pieces if not p & mask]
        gone = [pieces[p ^ mask].astype(BF16) for p in near]
        came = links.swap(jnp.concatenate(gone, axis=0), "ctx", mask)
        kv_gone.append(gone)
        kv_seen.append(came)
        pieces = {
            p: pieces[p].astype(F32) + came[i * span : (i + 1) * span].astype(F32) for i, p in enumerate(near)
        }
        mask *= 2
    outer_part = plane_grads(
        "outer_grads", [(after(plain_normed, *kv_gone[-1]), grad_query), (plain_normed, grad_gates), (attn_all, gated_all)],
        3 * q_cols + 2 * k_cols,
    )
    grad_key, grad_value, k_gain_part = keys_back(
        kv_heads, head_dim, after(pieces[0], outer_part, down_shard), kv_proj, 0, cos, sin, key_scale
    )
    feed_first = [links.reduce_first(x, turn, *((grad_key,) if turn else ())) for turn, x in enumerate(feed_totals)]
    seven, eight, in_part, grad_in, attn_gain_part = ([None] * 2 for _ in range(5))
    late_query = grad_query
    for t in range(2):
        terms = [
            (late_query, first_mat, 0),
            (grad_gates, first_mat, gate_at),
            (grad_key, first_mat, key_at),
            (grad_value, first_mat, value_at),
        ]
        in_part[t], gain = spread("spread_in", terms, t, 2, normed=normed)
        attn_gain_part[t] = gain[0] / attn_scale[0]
        seven[t] = links.scatter_first(in_part[t] if t == 0 else after(in_part[1], seven[0][1]))
    inner_part = plane_grads(
        "inner_grads", [(after(plain_normed, attn_gain_part[1]), grad_key), (plain_normed, grad_value)], 3 * q_cols + 2 * k_cols, outer_part
    )
    inner_sum = over_plane(inner_part)
    summed = [links.scatter_rest(*seven[t]) for t in range(2)]
    late = ()
    for t in range(2):
        back = after(summed[t][0], *late)
        x = own_rows(stream, t).astype(F32)
        inverse = lax.rsqrt(jnp.mean(x * x, axis=-1, keepdims=True) + EPSILON)
        unit = x * inverse
        grad_in[t] = (grad_middle[t] + norm_back(back, unit, inverse, attn_scale)).astype(BF16)
        eight[t] = links.gather_first(grad_in[t])
        late = (grad_in[t],)
    feed_rest = grad_rest(feed_first, grad_in[0])
    hidden_out = leave(jnp.concatenate([back_places, scalars[parts:]]), count, parts, [after(down_all, in_part[1])], BF16)
    in_pieces = [*links.gather_rest(*eight[0], late=late)]
    in_pieces += links.gather_rest(*eight[1], late=(in_pieces[0],))
    attn_gain_part = sum(attn_gain_part)
    arrived_one = in_pieces[1]
    in_pieces[1] = after(in_pieces[1], hidden_out, *(r[0] for r in feed_rest))
    grad_in = leave(scalars, count, parts, in_pieces, F32)

    blocks = jnp.stack([attn_gain_part.reshape(count, shard), grad_mlp_gain.reshape(count, shard)])
    to_mesh = (owners[None, :] == jnp.arange(count)[:, None]).astype(F32)
    blocks = jnp.einsum("ap,kpn->kan", to_mesh, blocks, precision=lax.Precision.HIGHEST)
    packed = jnp.concatenate([blocks.reshape(1, -1), q_gain_part[None, :], k_gain_part[None, :]], axis=1)
    packed = links.add_all(packed, arrived_one, hidden_out, *(r[2] for r in feed_rest))[0]
    rank = dp_index * links.ctx + ctx_index
    take = lambda at, size: lax.dynamic_slice_in_dim(packed, at + rank * size, size)
    return (
        hidden_out,
        grad_in,
        take(0, shard),
        inner_sum[:, :q_cols],
        inner_sum[:, q_cols : 2 * q_cols],
        inner_sum[:, 3 * q_cols : 3 * q_cols + k_cols],
        inner_sum[:, 3 * q_cols + k_cols :],
        take(2 * width, head_shard),
        take(2 * width + head_dim, head_shard),
        inner_sum[:, 2 * q_cols : 3 * q_cols],
        take(width, shard),
        feed_rest[0][0],
        feed_rest[1][0],
        grad_down,
    )


def solution(mesh):
    links = Links(dict(mesh.shape))
    rows = P(("dp", "ctx"))
    plain = P(("dp", "ctx"), None)
    split = P(("dp", "ctx"), "tensor")

    def step(*arrays):
        return per_device(links, *arrays)

    return jax.shard_map(
        step,
        mesh=mesh,
        in_specs=(plain, P("dp"), rows, split, split, split, split, rows, rows, split, rows, split, split, split, plain),
        out_specs=(plain, plain, rows, split, split, split, split, rows, rows, split, rows, split, split, split),
        check_vma=False,
    )
```

```python
import functools
import math

import jax
import jax.numpy as jnp
from jax import lax
from jax.experimental import pallas as pl
from jax.experimental.pallas import tpu as pltpu
from jax.sharding import PartitionSpec as P

EPSILON = 1e-06
ROPE_BASE = 1000000.0
CONTRACT_ROWS = (((0,), (0,)), ((), ()))
CONTRACT_COLS = (((1,), (1,)), ((), ()))
F32 = jnp.float32
BF16 = jnp.bfloat16
VMEM_BYTES = 56 * 1024 * 1024


def project(operand, matrix):
    return jnp.dot(operand, matrix, preferred_element_type=F32)


def row_contract(first_op, second_op):
    return lax.dot_general(first_op, second_op, CONTRACT_ROWS, preferred_element_type=F32)


def col_contract(first_op, second_op):
    return lax.dot_general(first_op, second_op, CONTRACT_COLS, preferred_element_type=F32)


def sigmoid(value):
    return 1.0 / (1.0 + jnp.exp(-value))


def after(value, *others):
    if not others:
        return value
    return lax.optimization_barrier((value,) + others)[0]


def cost(flops, moved, exps=0):
    return pl.CostEstimate(flops=int(flops), bytes_accessed=int(moved), transcendentals=int(exps))


def params(**kwargs):
    return pltpu.CompilerParams(vmem_limit_bytes=VMEM_BYTES, **kwargs)


class Links:
    def __init__(self, sizes):
        self.dp, self.ctx, self.tensor = sizes["dp"], sizes["ctx"], sizes["tensor"]
        self.half = self.dp * self.ctx // 2
        ctx_bits = int(math.log2(self.ctx // 2))
        dp_bits = int(math.log2(self.dp))
        self.bits = [("ctx", 2 << i) for i in range(ctx_bits)] + [("dp", 1 << i) for i in range(dp_bits)]
        self.masks = [(2 << i) - 1 for i in range(int(math.log2(self.tensor)))]
        self.turns = [0]
        for mask in reversed(self.masks):
            self.turns = self.turns + [j ^ mask for j in self.turns]

    def swap(self, value, axis, mask):
        count = {"dp": self.dp, "ctx": self.ctx, "tensor": self.tensor}[axis]
        return lax.ppermute(value, axis, [(i, i ^ mask) for i in range(count)])

    def order(self, turn):
        places = list(range(len(self.bits)))
        return places if turn else places[::-1]

    def send_own(self, blocks):
        return {1 << p: self.swap(blocks[p], *self.bits[p]) for p in self.order(0)}

    def send_far(self, block):
        count = self.dp * self.ctx
        single = {}
        for q in range(1, self.half):
            far = (q // (self.ctx // 2)) * self.ctx + (q % (self.ctx // 2)) * 2
            single[q] = lax.ppermute(block, ("dp", "ctx"), [(i, i ^ far) for i in range(count)])
        return single

    def send_on(self, single):
        mid = next(iter(single.values())).shape[1] // 2
        left = {q: b[:, :mid] for q, b in single.items()}
        right = {q: b[:, mid:] for q, b in single.items()}
        for side, places in ((left, self.order(0)), (right, self.order(1))):
            for q in range(1, self.half):
                if q not in single:
                    self.reach(side, q, places)
        return {q: (left[q], right[q]) for q in left if q not in single}

    def assemble(self, block, single, pairs):
        blocks, groups = [], []
        for q in range(self.half):
            members = [block] if q == 0 else [single[q]] if q in single else list(pairs[q])
            groups.append(tuple(range(len(blocks), len(blocks) + len(members))))
            blocks += members
        return stack_blocks(groups, blocks)

    def reach(self, side, q, places):
        if q not in side:
            last = [p for p in places if q & (1 << p)][-1]
            self.reach(side, q ^ (1 << last), places)
            side[q] = self.swap(side[q ^ (1 << last)], *self.bits[last])

    def reduce_first(self, total, turn, *hold):
        rows = total.shape[0] // self.half
        pieces = {q: total[q * rows : (q + 1) * rows] for q in range(self.half)}
        return self.reduce_step(pieces, turn, 0, *hold)

    def reduce_step(self, pieces, turn, step, *hold):
        place = self.order(turn)[step]
        bit = 1 << place
        kept = {q: b for q, b in pieces.items() if not q & bit}
        gone = [pieces[q | bit].astype(BF16) for q in kept]
        sent = after(jnp.concatenate(gone, axis=0), *hold)
        return kept, [sent], self.swap(sent, *self.bits[place])

    def reduce_rest(self, kept, came, turn):
        gone = []
        for step in range(1, len(self.bits) + 1):
            rows = came.shape[0] // len(kept)
            pieces = {
                q: b.astype(F32) + came[i * rows : (i + 1) * rows].astype(F32) for i, (q, b) in enumerate(kept.items())
            }
            if step < len(self.bits):
                kept, sent, came = self.reduce_step(pieces, turn, step)
                gone += sent
        return pieces[0], gone, came

    def small_gather(self, row):
        far = self.send_far(row)
        own = jnp.concatenate([row] + [far[q] for q in range(1, self.half)], axis=0)
        return jnp.concatenate([own, self.swap(own, "ctx", 1)], axis=0), list(far.values())

    def owner_of(self, position, dp_index, ctx_index):
        h, q = position // self.half, position % self.half
        dp_far, ctx_far = q // (self.ctx // 2), (q % (self.ctx // 2)) * 2 + h
        return (dp_index ^ dp_far) * self.ctx + (ctx_index ^ ctx_far)

    def scatter_first(self, part):
        rows = part.shape[0] // 2
        return part[:rows], self.swap(part[rows:], "tensor", self.masks[0])

    def scatter_rest(self, kept, came, before=(), late=()):
        gone = seen = came
        kept = kept.astype(F32) + came.astype(F32)
        for mask in self.masks[1:]:
            rows = kept.shape[0] // 2
            gone = kept[rows:].astype(BF16)
            seen = self.swap(after(gone, *before), "tensor", mask)
            kept = kept[:rows] + after(seen, *late).astype(F32)
        return kept, seen

    def gather_first(self, shard):
        return shard, self.swap(shard, "tensor", self.masks[-1])

    def gather_rest(self, shard, came, late=()):
        came = after(came, *late)
        for mask in self.masks[-2::-1]:
            shard = jnp.concatenate([shard, came], axis=0)
            came = self.swap(shard, "tensor", mask)
        return shard, came

    def add_all(self, value, *before):
        value = after(value, *before)
        value = value + self.swap(value, "ctx", 1)
        for axis, mask in self.bits:
            value = value + self.swap(value, axis, mask)
        return value + sum(self.swap(value, "tensor", mask) for mask in range(1, self.tensor))


def still(scalars, count, parts):
    owners = scalars[parts : parts + count]
    return owners, lax.dynamic_update_slice(scalars, jnp.arange(count, dtype=scalars.dtype), (parts,))


def columns(value, owners):
    count = owners.shape[0]
    blocks = value.reshape(value.shape[0], count, value.shape[1] // count)
    return jnp.take(blocks, owners, axis=1).reshape(value.shape)


def column_place(scalars, parts, p, size):
    if size % 128:
        return pl.ds(p * size, size)
    return pl.ds(pl.multiple_of(scalars[parts + p] * size, size), size)


def stack_kernel(groups, *refs):
    out_ref = refs[-1]
    for q, group in enumerate(groups):

        @pl.when(pl.program_id(0) == q)
        def _(group=group):
            col = 0
            for i in group:
                out_ref[:, col : col + refs[i].shape[1]] = refs[i][...]
                col += refs[i].shape[1]


def stack_blocks(groups, blocks):
    rows, n = blocks[0].shape
    held = lambda b: pl.BlockSpec(b.shape, lambda i: (0, 0), pipeline_mode=pl.Buffered(1))
    return pl.pallas_call(
        functools.partial(stack_kernel, groups),
        out_shape=jax.ShapeDtypeStruct((rows * len(groups), n), blocks[0].dtype),
        grid=(len(groups),),
        in_specs=[held(b) for b in blocks],
        out_specs=pl.BlockSpec((rows, n), lambda i: (i, 0)),
        compiler_params=params(),
        cost_estimate=cost(0, 4 * rows * len(groups) * n),
        name="stack",
    )(*blocks)


def enter_kernel(
    count, parts, scalars, xa_ref, xb_ref, ga_ref, gb_ref, gain_ref, x_out, g_out, m_out, mine_out, plain_out, n_out
):
    step = pl.program_id(0)
    rows, width = xa_ref.shape
    size = width // count
    moved = [column_place(scalars, parts, p, size) for p in range(count)]
    for part, (x_ref, g_ref) in enumerate(((xa_ref, ga_ref), (xb_ref, gb_ref))):
        if part == 0:

            @pl.when(step % (parts // 4) == 0)
            def _(x_ref=x_ref, g_ref=g_ref):
                for p in range(count):
                    x_out[:, p * size : (p + 1) * size] = x_ref[:, moved[p]]
                    g_out[:, p * size : (p + 1) * size] = g_ref[:, moved[p]]

        place = slice(part * rows, (part + 1) * rows)
        spot = scalars[parts + count] + scalars[2 * step + part] * rows
        live = spot + lax.broadcasted_iota(jnp.int32, (rows, 1), 0) < scalars[parts + count + 1]
        m_out[place, :] = jnp.where(live, g_ref[...].astype(F32), 0.0).astype(BF16)
        wide = x_ref[...].astype(F32)
        inverse = lax.rsqrt(jnp.mean(wide * wide, axis=-1, keepdims=True) + EPSILON)
        plain_out[place, :] = (wide * inverse * gain_ref[...]).astype(BF16)
        for p in range(count):
            n_out[place, p * size : (p + 1) * size] = plain_out[place, moved[p]]
            mine_out[place, p * size : (p + 1) * size] = m_out[place, moved[p]]


def enter(scalars, count, parts, span, hidden_in, out_grad, gain):
    rows, width = span // parts, hidden_in.shape[1]
    narrow = width // count % 128
    owners = scalars[parts : parts + count]
    upper = pl.BlockSpec((rows, width), lambda i, s: (s[2 * i], 0))
    lower = pl.BlockSpec((rows, width), lambda i, s: (s[2 * i + 1], 0))
    own = pl.BlockSpec((rows, width), lambda i, s: (i // (parts // 4), 0))
    plain = pl.BlockSpec((2 * rows, width), lambda i, s: (i, 0))
    shape = jax.ShapeDtypeStruct((span, width), BF16)
    short = jax.ShapeDtypeStruct((2 * rows, width), BF16)
    x, g, m, mine, unmoved, normed = pl.pallas_call(
        functools.partial(enter_kernel, count, parts),
        out_shape=(short, short, shape, shape, shape, shape),
        grid_spec=pltpu.PrefetchScalarGridSpec(
            num_scalar_prefetch=1,
            grid=(parts // 2,),
            in_specs=[upper, lower, upper, lower, pl.BlockSpec((1, width), lambda i, s: (0, 0))],
            out_specs=(own, own, plain, plain, plain, plain),
        ),
        compiler_params=params(),
        cost_estimate=cost(10 * span * width, 8 * span * width),
        name="enter",
    )(scalars, hidden_in, hidden_in, out_grad, out_grad, gain)
    if narrow:
        x, g, mine, normed = (columns(v, owners) for v in (x, g, mine, normed))
    return x, g, m, mine, unmoved, normed


def leave_kernel(count, parts, scalars, *refs):
    pieces, out_ref = refs[:4], refs[4]
    blocks, size = parts // 4, out_ref.shape[1] // count
    rows = out_ref.shape[0] // parts
    for i, in_ref in enumerate(pieces):

        @pl.when(pl.program_id(0) == i)
        def _(i=i, in_ref=in_ref):
            for part in range(blocks):
                at = pl.ds(pl.multiple_of(scalars[i * blocks + part] * rows, rows), rows)
                for p in range(count):
                    block = in_ref[part * rows : (part + 1) * rows, p * size : (p + 1) * size]
                    out_ref[at, column_place(scalars, parts, p, size)] = block.astype(out_ref.dtype)


def leave(scalars, count, parts, pieces, dtype):
    rows, width = pieces[0].shape
    place = lambda k: lambda i, s: (0, 0)
    if len(pieces) == 1:
        rows, pieces = rows // 4, pieces * 4
        place = lambda k: lambda i, s: (k, 0)
    if width // count % 128:
        owners, scalars = still(scalars, count, parts)
        pieces = [columns(piece, jnp.argsort(owners)) for piece in pieces]
    return pl.pallas_call(
        functools.partial(leave_kernel, count, parts),
        out_shape=jax.ShapeDtypeStruct((4 * rows, width), dtype),
        grid_spec=pltpu.PrefetchScalarGridSpec(
            num_scalar_prefetch=1,
            grid=(4,),
            in_specs=[pl.BlockSpec((rows, width), place(k)) for k in range(4)],
            out_specs=pl.BlockSpec((4 * rows, width), lambda i, s: (0, 0)),
        ),
        compiler_params=params(),
        cost_estimate=cost(0, 24 * rows * width),
        name="leave",
    )(scalars, *pieces)


def spread_kernel(tiles, count, parts, summed, *refs):
    homes, refs = (refs[0], refs[1:]) if parts else (None, refs)
    values, out_ref = refs[:count], refs[3 * count + summed]
    for h in range(2):

        @pl.when(pl.program_id(0) // tiles == h)
        def _(h=h):
            total = None
            for k in range(count):
                term = lax.dot_general(
                    values[k][...], refs[count + 2 * k + h][...], CONTRACT_COLS, preferred_element_type=F32
                )
                total = term if total is None else total + term
            if summed:
                norm_ref, sum_ref = refs[3 * count], refs[3 * count + 2]
                gain = jnp.sum(total * norm_ref[...].astype(F32), axis=0, keepdims=True)
                sum_ref[...] = jnp.broadcast_to(gain, sum_ref.shape)
            if parts:
                rows = out_ref.shape[0] // parts
                for i in range(parts):
                    at = pl.ds(pl.multiple_of(homes[i] * rows, rows), rows)
                    out_ref[at, :] = total[i * rows : (i + 1) * rows].astype(BF16)
            else:
                out_ref[...] = total.astype(BF16)


def spread(name, terms, part=0, parts=1, homes=None, normed=None):
    rows = terms[0][0].shape[0] // parts
    mid = terms[0][1][0].shape[0]
    tile = mid // 2
    specs, mats = [], []
    for value, pair, start in terms:
        n = value.shape[1]
        specs += [
            pl.BlockSpec((tile, n), lambda j, *s, c=start // n: (jnp.minimum(j, 1), c)),
            pl.BlockSpec((tile, n), lambda j, *s, c=start // n: (jnp.maximum(j - 2, 0), c)),
        ]
        mats += list(pair)
    held = [pl.BlockSpec((rows, v.shape[1]), lambda j, *s: (part, 0)) for v, _, _ in terms]
    wide = sum(v.shape[1] for v, _, _ in terms)
    summed = normed is not None
    shapes = [jax.ShapeDtypeStruct((rows, 2 * mid), BF16)]
    outs = [pl.BlockSpec((rows, tile), lambda j, *s: (0, j))]
    extra = []
    if summed:
        extra = [normed]
        specs.append(pl.BlockSpec((rows, tile), lambda j, *s: (part, j)))
        shapes.append(jax.ShapeDtypeStruct((8, 2 * mid), F32))
        outs.append(pl.BlockSpec((8, tile), lambda j, *s: (0, j)))
    out = pl.pallas_call(
        functools.partial(spread_kernel, 2, len(terms), 0 if homes is None else homes.shape[0], summed),
        out_shape=shapes,
        grid_spec=pltpu.PrefetchScalarGridSpec(
            num_scalar_prefetch=0 if homes is None else 1, grid=(4,), in_specs=held + specs, out_specs=outs
        ),
        compiler_params=params(),
        cost_estimate=cost(4 * rows * mid * wide, 2 * wide * (rows + 2 * mid) + 4 * rows * mid),
        name=name,
    )(*(() if homes is None else (homes,)), *(v for v, _, _ in terms), *mats, *extra)
    return out if summed else out[0]


def feed_kernel(first, count, parts, scalars, a_ref, b_ref, gate_ref, up_ref, gh_ref, *refs):
    refs = refs if first else refs[4:]
    hidden_out, gate_out, up_out, rows_out, part_out, x_ref, acc_ref = refs
    step, size = pl.program_id(0), x_ref.shape[1] // count
    moved = [column_place(scalars, parts, p, size) for p in range(count)]

    @pl.when(step == 0)
    def _():
        rows = a_ref.shape[0]
        rows_out[:rows, :] = a_ref[...]
        rows_out[rows:, :] = b_ref[...]
        for p in range(count):
            x_ref[:rows, moved[p]] = a_ref[:, p * size : (p + 1) * size]
            x_ref[rows:, moved[p]] = b_ref[:, p * size : (p + 1) * size]
        acc_ref[...] = jnp.zeros_like(acc_ref)

    gate = project(x_ref[...], gate_ref[...])
    up = project(x_ref[...], up_ref[...])
    grad = gh_ref[...]
    sig = sigmoid(gate)
    hidden_out[...] = (gate * sig * up).astype(BF16)
    grad_gate = (grad * up * sig * (1.0 + gate * (1.0 - sig))).astype(BF16)
    grad_up = (grad * (gate * sig)).astype(BF16)
    gate_out[...] = grad_gate
    up_out[...] = grad_up
    acc_ref[...] += col_contract(grad_gate, gate_ref[...]) + col_contract(grad_up, up_ref[...])

    @pl.when(step == pl.num_programs(0) - 1)
    def _():
        for p in range(count):
            part_out[:, p * size : (p + 1) * size] = acc_ref[:, moved[p]].astype(BF16)


def feed(scalars, count, parts, part, pieces, mat, grad_hidden, olds):
    span, ff = grad_hidden.shape
    piece, width = pieces[0].shape
    rows = 2 * piece
    tile = 512 if ff % 512 == 0 else ff
    steps = ff // tile
    narrow = width // count % 128
    owners = scalars[parts : parts + count]
    given = [columns(x, jnp.argsort(owners)) for x in pieces] if narrow else pieces
    held = pl.BlockSpec((piece, width), lambda j, s: (0, 0))
    columns_of = lambda shift: pl.BlockSpec((width, tile), lambda j, s: (0, shift + j))
    cols = pl.BlockSpec((rows, tile), lambda j, s: (part, j))
    first = olds is None
    olds = () if first else tuple(olds)
    wide = jax.ShapeDtypeStruct((span, ff), BF16)
    out = pl.pallas_call(
        functools.partial(feed_kernel, first, count, parts),
        out_shape=(
            wide,
            wide,
            wide,
            jax.ShapeDtypeStruct((span, width), BF16),
            jax.ShapeDtypeStruct((rows, width), BF16),
        ),
        grid_spec=pltpu.PrefetchScalarGridSpec(
            num_scalar_prefetch=1,
            grid=(steps,),
            in_specs=[held, held, columns_of(0), columns_of(steps), cols]
            + [pl.BlockSpec(memory_space=pl.ANY)] * len(olds),
            out_specs=(
                cols,
                cols,
                cols,
                pl.BlockSpec((rows, width), lambda j, s: (part, 0)),
                pl.BlockSpec((rows, width), lambda j, s: (0, 0)),
            ),
            scratch_shapes=[pltpu.VMEM((rows, width), BF16), pltpu.VMEM((rows, width), F32)],
        ),
        input_output_aliases={6 + i: i for i in range(len(olds))},
        compiler_params=params(),
        cost_estimate=cost(8 * rows * width * ff, 8 * width * ff, 2 * rows * ff),
        name="feed",
    )(scalars, *given, mat, mat, grad_hidden, *olds)
    return out[:4], columns(out[4], owners) if narrow else out[4]


def descend_kernel(parts, homes, value_ref, mat_ref, out_ref):
    total = col_contract(value_ref[...], mat_ref[...])
    rows = out_ref.shape[0] // parts
    for i in range(parts):
        at = pl.ds(pl.multiple_of(homes[i] * rows, rows), rows)
        out_ref[at, :] = total[i * rows : (i + 1) * rows].astype(BF16)


def descend(homes, owners, value, mat):
    rows, n = value.shape
    width, count, parts = mat.shape[0], owners.shape[0], homes.shape[0]
    narrow = width // count % 128
    steps = 4 if narrow else count
    out = pl.pallas_call(
        functools.partial(descend_kernel, parts),
        out_shape=jax.ShapeDtypeStruct((rows, width), BF16),
        grid_spec=pltpu.PrefetchScalarGridSpec(
            num_scalar_prefetch=1,
            grid=(steps,),
            in_specs=[
                pl.BlockSpec((rows, n), lambda j, s: (0, 0)),
                pl.BlockSpec((width // steps, n), lambda j, s: (s[parts + j], 0)),
            ],
            out_specs=pl.BlockSpec((rows, width // steps), lambda j, s: (0, j)),
        ),
        compiler_params=params(),
        cost_estimate=cost(2 * rows * width * n, 2 * (rows + width) * n + 2 * rows * width),
        name="descend",
    )(jnp.concatenate([homes, jnp.arange(4, dtype=jnp.int32) if narrow else owners]), value, mat)
    return columns(out, owners) if narrow else out


def plane_grads_kernel(counts, *refs):
    out_ref, start, at = refs[-1], 0, len(counts)
    for left, count in zip(refs, counts):
        rights = [r[...] for r in refs[at : at + count]]
        right = rights[0] if count == 1 else jnp.concatenate(rights, axis=1)
        size = right.shape[1]
        out_ref[:, start : start + size] = row_contract(left[...], right).astype(BF16)
        start, at = start + size, at + count


def plane_grads(name, terms, total, old=None):
    span, width = terms[0][0].shape
    tile = 256
    rights = [g for _, pair in terms for g in pair]
    cols = sum(g.shape[1] for g in rights)
    at = 0 if old is None else total // cols - 1
    left = pl.BlockSpec((span, tile), lambda j: (0, j))
    held = [pl.BlockSpec(g.shape, lambda j: (0, 0)) for g in rights]
    olds = () if old is None else (old,)
    return pl.pallas_call(
        functools.partial(plane_grads_kernel, tuple(len(pair) for _, pair in terms)),
        out_shape=jax.ShapeDtypeStruct((width, total), BF16),
        grid=(width // tile,),
        in_specs=[left] * len(terms) + held + [pl.BlockSpec(memory_space=pl.ANY)] * len(olds),
        out_specs=pl.BlockSpec((tile, cols), lambda j: (j, at)),
        input_output_aliases={len(terms) + len(rights): 0} if olds else {},
        compiler_params=params(),
        cost_estimate=cost(2 * span * width * cols, 2 * span * (2 * width + cols) + 2 * width * cols),
        name=name,
    )(*(a for a, _ in terms), *rights, *olds)


def enter_heads_kernel(heads, head_dim, paired, x_ref, near_ref, far_ref, cos_ref, sin_ref, gain_ref, p_out, r_out):
    mid = x_ref.shape[1] // 2
    proj = project(x_ref[:, :mid], near_ref[...]) + project(x_ref[:, mid:], far_ref[...])
    p_out[...] = proj
    for h in range(heads):
        unit, _ = unit_of(proj[:, h * head_dim : (h + 1) * head_dim])
        turned = turn(unit * gain_ref[...], cos_ref, sin_ref, 1.0).astype(BF16)
        at = (2 * h if paired else h) * head_dim
        r_out[:, at : at + head_dim] = turned
        if paired:
            value = proj[:, (heads + h) * head_dim : (heads + h + 1) * head_dim]
            r_out[:, at + head_dim : at + 2 * head_dim] = value.astype(BF16)


def enter_heads(name, heads, head_dim, paired, normed, mats, at, cols, cos, sin, gain):
    span, width = normed.shape
    rows = span // 2
    spec = lambda n: pl.BlockSpec((rows, n), lambda i: (i, 0))
    mat = pl.BlockSpec((width // 2, cols), lambda i: (0, at // cols))
    turned = heads * head_dim * (2 if paired else 1)
    return pl.pallas_call(
        functools.partial(enter_heads_kernel, heads, head_dim, paired),
        out_shape=(jax.ShapeDtypeStruct((span, cols), F32), jax.ShapeDtypeStruct((span, turned), BF16)),
        grid=(2,),
        in_specs=[spec(width), mat, mat, spec(head_dim), spec(head_dim), pl.BlockSpec((1, head_dim), lambda i: (0, 0))],
        out_specs=(spec(cols), spec(turned)),
        compiler_params=params(),
        cost_estimate=cost(2 * span * width * cols, 2 * width * (span + cols) + 6 * span * cols),
        name=name,
    )(normed, *mats, cos, sin, gain)


def unit_of(value):
    inverse = lax.rsqrt(jnp.mean(value * value, axis=-1, keepdims=True) + EPSILON)
    return value * inverse, inverse


def turn(value, cos_ref, sin_ref, sign):
    half = value.shape[-1] // 2
    return value * cos_ref[...] + sign * pltpu.roll(value, half, 1) * sin_ref[...]


def attend_kernel(group, head_dim, turns, first, scalars, q_ref, gate_ref, spot_ref, key_ref, oo_ref, of_ref, *refs):
    blocks = len(turns)
    kv_refs = refs[:blocks]
    rest = refs[blocks:] if first else refs[blocks + 1 :]
    mixed_out, sum_out, gated_out, part_out, acc_ref, total_ref, out_acc = rest
    scale = head_dim**-0.5 * math.log2(math.e)
    own = scalars[0]
    step, mid = pl.program_id(0), out_acc.shape[1] // 2

    @pl.when(step == 0)
    def _():
        out_acc[...] = jnp.zeros_like(out_acc)

    for h in range(group):
        cols = slice(h * head_dim, (h + 1) * head_dim)
        query = q_ref[:, cols]

        def scores(ref):
            return lax.dot_general(query, ref[:, :head_dim], CONTRACT_COLS, preferred_element_type=F32)

        allowed = (key_ref[...] <= spot_ref[...]) & (key_ref[...] < scalars[1])
        terms = jnp.where(allowed, jnp.exp2(scores(kv_refs[0]) * scale), 0.0)
        total_ref[...] = jnp.sum(terms, axis=-1, keepdims=True)
        acc_ref[...] = project(terms.astype(BF16), kv_refs[0][:, head_dim:])
        for place in range(1, blocks):

            @pl.when((own ^ turns[place]) < own)
            def _(ref=kv_refs[place]):
                terms = jnp.exp2(scores(ref) * scale)
                total_ref[...] += jnp.sum(terms, axis=-1, keepdims=True)
                acc_ref[...] += project(terms.astype(BF16), ref[:, head_dim:])

        mixed = acc_ref[...] / total_ref[...]
        mixed_out[:, cols] = mixed
        gated_out[:, cols] = (mixed * sigmoid(gate_ref[:, cols])).astype(BF16)
        sum_out[:, cols] = jnp.broadcast_to(total_ref[...], mixed.shape)
    gated = gated_out[...]
    out_acc[:, :mid] += col_contract(gated, oo_ref[...])
    out_acc[:, mid:] += col_contract(gated, of_ref[...])

    @pl.when(step == pl.num_programs(0) - 1)
    def _():
        part_out[...] = out_acc[...].astype(BF16)


def attend(scalars, part, parts, group, head_dim, turns, query, proj, gate_at, spots, keys, mats, out_at, kvs, old):
    span, width = query.shape
    rows, wide, mid = span // parts, group * head_dim, mats[0].shape[0]
    head = pl.BlockSpec((rows, wide), lambda g, s: (part, g))
    out = pl.BlockSpec((rows, wide), lambda g, s: (0, g))
    mat = pl.BlockSpec((mid, wide), lambda g, s: (0, out_at // wide + g))
    first = old is None
    olds = () if first else (old,)
    return pl.pallas_call(
        functools.partial(attend_kernel, group, head_dim, turns, first),
        out_shape=(
            jax.ShapeDtypeStruct((rows, width), F32),
            jax.ShapeDtypeStruct((rows, width), F32),
            jax.ShapeDtypeStruct((span, width), BF16),
            jax.ShapeDtypeStruct((rows, 2 * mid), BF16),
        ),
        grid_spec=pltpu.PrefetchScalarGridSpec(
            num_scalar_prefetch=1,
            grid=(width // wide,),
            in_specs=[
                head,
                pl.BlockSpec((rows, wide), lambda g, s: (part, gate_at // wide + g)),
                pl.BlockSpec((rows, 1), lambda g, s: (part, 0)),
                pl.BlockSpec((1, span), lambda g, s: (0, 0)),
                mat,
                mat,
            ]
            + [pl.BlockSpec((span, 2 * head_dim), lambda g, s: (0, g))] * len(kvs)
            + [pl.BlockSpec(memory_space=pl.ANY)] * len(olds),
            out_specs=(out, out, head, pl.BlockSpec((rows, 2 * mid), lambda g, s: (0, 0))),
            scratch_shapes=[
                pltpu.VMEM((rows, head_dim), F32),
                pltpu.VMEM((rows, 1), F32),
                pltpu.VMEM((rows, 2 * mid), F32),
            ],
        ),
        input_output_aliases={7 + len(kvs): 2} if olds else {},
        compiler_params=params(),
        cost_estimate=cost(
            4 * rows * width * span * len(kvs) + 4 * rows * width * mid,
            4 * span * width * len(kvs) + 20 * rows * width + 4 * mid * width,
            rows * span * len(kvs) * width // head_dim,
        ),
        name="attend",
    )(scalars, query, proj, spots, keys, *mats, *kvs, *olds)


def attend_back_kernel(group, head_dim, turns, first, count, scalars, *refs):
    blocks = len(turns)
    q_ref, query_ref, gate_ref, mixed_ref, sum_ref, a_ref, b_ref, oo_ref, of_ref = refs[:9]
    spot_ref, key_ref, cos_ref, sin_ref, gain_ref = refs[9:14]
    kv_refs = refs[14 : 14 + blocks]
    rest = refs[14 + blocks :]
    old_refs = () if first else rest[:blocks]
    rest = rest if first else rest[blocks + 3 :]
    gq_out, ggate_out, rows_out, gain_out = rest[:4]
    new_refs = rest[4 : 4 + blocks]
    gq_ref, x_ref = rest[4 + blocks :]
    mid = x_ref.shape[1] // 2

    @pl.when(pl.program_id(0) == 0)
    def _():
        piece = a_ref.shape[0]
        x_ref[:piece, :] = a_ref[...]
        x_ref[piece:, :] = b_ref[...]
        size = x_ref.shape[1] // count
        for p in range(count):
            rows_out[:, column_place(scalars, 2, p, size)] = x_ref[:, p * size : (p + 1) * size]

    all_gated = project(x_ref[:, :mid], oo_ref[...]) + project(x_ref[:, mid:], of_ref[...])
    score_scale = head_dim**-0.5
    scale = score_scale * math.log2(math.e)
    own = scalars[0]
    rows = q_ref.shape[0]

    def as_row(column):
        return jnp.transpose(jnp.broadcast_to(column, (rows, head_dim)))[:1, :]

    for place in range(blocks):
        if first:
            new_refs[place][...] = jnp.zeros_like(new_refs[place])
        else:
            new_refs[place][...] = old_refs[place][...]
    gain_total = jnp.zeros((1, head_dim), F32)
    for h in range(group):
        cols = slice(h * head_dim, (h + 1) * head_dim)
        query = q_ref[:, cols]
        gate = sigmoid(gate_ref[:, cols])
        grad_gated, mixed = all_gated[:, cols], mixed_ref[:, cols]
        grad_mixed = (grad_gated * gate).astype(BF16)
        ggate_out[:, cols] = (grad_gated * mixed * gate * (1.0 - gate)).astype(BF16)
        row_dot = as_row(jnp.sum(grad_mixed.astype(F32) * mixed, axis=-1, keepdims=True))
        row_log = as_row(jnp.log2(sum_ref[:, cols][:, :1]))
        gq_ref[...] = jnp.zeros_like(gq_ref)

        def block(kv_ref, new_ref, masked):
            key, value = kv_ref[:, :head_dim], kv_ref[:, head_dim:]
            scores = lax.dot_general(key, query, CONTRACT_COLS, preferred_element_type=F32)
            probs = jnp.exp2(scores * scale - row_log)
            if masked:
                allowed = (key_ref[...] <= spot_ref[...]) & (key_ref[...] < scalars[1])
                probs = jnp.where(allowed, probs, 0.0)
            grad_probs = lax.dot_general(value, grad_mixed, CONTRACT_COLS, preferred_element_type=F32)
            grad_scores = (probs * (grad_probs - row_dot)).astype(BF16)
            new_ref[:, head_dim:] += project(probs.astype(BF16), grad_mixed)
            new_ref[:, :head_dim] += project(grad_scores, query)
            gq_ref[...] += lax.dot_general(grad_scores, key, CONTRACT_ROWS, preferred_element_type=F32)

        block(kv_refs[0], new_refs[0], True)
        for place in range(1, blocks):

            @pl.when((own ^ turns[place]) < own)
            def _(place=place):
                block(kv_refs[place], new_refs[place], False)

        unit, inverse = unit_of(query_ref[:, cols])
        back = turn(gq_ref[...] * score_scale, cos_ref, sin_ref, -1.0)
        gain_total = gain_total + jnp.sum(back * unit, axis=0, keepdims=True)
        scaled = back * gain_ref[...]
        gq_out[:, cols] = (
            inverse * (scaled - unit * jnp.mean(scaled * unit, axis=-1, keepdims=True))
        ).astype(BF16)
    gain_out[...] = jnp.broadcast_to(gain_total, gain_out.shape)


def attend_back(
    scalars, count, part, parts, group, head_dim, turns, query, proj, gate_at, mixed, sums, pieces, mats, out_at, spots, keys, cos, sin, gain, kvs, olds
):
    span, width = query.shape
    rows, wide = span // parts, group * head_dim
    blocks, mid = len(kvs), mats[0].shape[0]
    mine = pl.BlockSpec((rows, wide), lambda g, s: (part, g))
    local = pl.BlockSpec((rows, wide), lambda g, s: (0, g))
    table = pl.BlockSpec((rows, head_dim), lambda g, s: (part, 0))
    pair = pl.BlockSpec((span, 2 * head_dim), lambda g, s: (0, g))
    piece = pl.BlockSpec(pieces[0].shape, lambda g, s: (0, 0))
    mat = pl.BlockSpec((mid, wide), lambda g, s: (0, out_at // wide + g))
    first = olds is None
    olds = () if first else tuple(olds)
    kv_shape = jax.ShapeDtypeStruct(kvs[0].shape, F32)
    steps = width // wide
    before = 15 + blocks
    out = pl.pallas_call(
        functools.partial(attend_back_kernel, group, head_dim, turns, first, count),
        out_shape=(
            jax.ShapeDtypeStruct((span, width), BF16),
            jax.ShapeDtypeStruct((span, width), BF16),
            jax.ShapeDtypeStruct((span, 2 * mid), BF16),
            jax.ShapeDtypeStruct((8 * steps, head_dim), F32),
        )
        + (kv_shape,) * blocks,
        grid_spec=pltpu.PrefetchScalarGridSpec(
            num_scalar_prefetch=1,
            grid=(steps,),
            in_specs=[
                mine,
                mine,
                pl.BlockSpec((rows, wide), lambda g, s: (part, gate_at // wide + g)),
                local,
                local,
                piece,
                piece,
                mat,
                mat,
                pl.BlockSpec((1, rows), lambda g, s: (0, part)),
                pl.BlockSpec((span, 1), lambda g, s: (0, 0)),
                table,
                table,
                pl.BlockSpec((1, head_dim), lambda g, s: (0, 0)),
            ]
            + [pair] * (blocks + min(len(olds), blocks))
            + [pl.BlockSpec(memory_space=pl.ANY)] * max(len(olds) - blocks, 0),
            out_specs=(
                mine,
                mine,
                pl.BlockSpec((rows, 2 * mid), lambda g, s: (part, 0)),
                pl.BlockSpec((8, head_dim), lambda g, s: (g, 0)),
            )
            + (pair,) * blocks,
            scratch_shapes=[pltpu.VMEM((rows, head_dim), F32), pltpu.VMEM((rows, 2 * mid), BF16)],
        ),
        input_output_aliases={}
        if first
        else {**{before + i: 4 + i for i in range(blocks)}, **{before + blocks + i: i for i in range(3)}},
        compiler_params=params(),
        cost_estimate=cost(
            10 * rows * width * span * blocks + 4 * rows * width * mid,
            20 * span * width * blocks,
            rows * span * blocks * width // head_dim,
        ),
        name="attend_back",
    )(scalars, query, proj, proj, mixed, sums, *pieces, *mats, spots, keys, cos, sin, gain, *kvs, *olds)
    gain_part = sum(out[3][8 * g] for g in range(steps))
    return out[4:], out[:3], gain_part


def keys_back_kernel(kv_heads, head_dim, g_ref, p_ref, cos_ref, sin_ref, gain_ref, k_out, v_out, gain_out):
    gain_total = jnp.zeros((1, head_dim), F32)
    for h in range(kv_heads):
        cols = slice(h * head_dim, (h + 1) * head_dim)
        unit, inverse = unit_of(p_ref[:, cols])
        grad = g_ref[:, 2 * h * head_dim : (2 * h + 1) * head_dim] * head_dim**-0.5
        back = turn(grad, cos_ref, sin_ref, -1.0)
        gain_total = gain_total + jnp.sum(back * unit, axis=0, keepdims=True)
        scaled = back * gain_ref[...]
        k_out[:, cols] = (
            inverse * (scaled - unit * jnp.mean(scaled * unit, axis=-1, keepdims=True))
        ).astype(BF16)
        v_out[:, cols] = g_ref[:, (2 * h + 1) * head_dim : (2 * h + 2) * head_dim].astype(BF16)
    gain_out[...] = jnp.broadcast_to(gain_total, gain_out.shape)


def keys_back(kv_heads, head_dim, grad_kv, proj, key_at, cos, sin, gain):
    span = proj.shape[0]
    cols = kv_heads * head_dim
    key_block = key_at // cols
    whole = lambda a, b: pl.BlockSpec((a, b), lambda i: (0, 0))
    out = pl.pallas_call(
        functools.partial(keys_back_kernel, kv_heads, head_dim),
        out_shape=(
            jax.ShapeDtypeStruct((span, cols), BF16),
            jax.ShapeDtypeStruct((span, cols), BF16),
            jax.ShapeDtypeStruct((8, head_dim), F32),
        ),
        grid=(1,),
        in_specs=[
            whole(span, 2 * cols),
            pl.BlockSpec((span, cols), lambda i: (0, key_block)),
            whole(span, head_dim),
            whole(span, head_dim),
            whole(1, head_dim),
        ],
        out_specs=(whole(span, cols), whole(span, cols), whole(8, head_dim)),
        compiler_params=params(),
        cost_estimate=cost(40 * span * cols, 16 * span * cols),
        name="keys_back",
    )(grad_kv, proj, cos, sin, gain)
    return out[0], out[1], out[2][0]


def norm_back(gradient, unit_vals, inverse, gain_vec):
    scaled = gradient * gain_vec
    return inverse * (scaled - unit_vals * jnp.mean(scaled * unit_vals, axis=-1, keepdims=True))


def per_device(
    links,
    hidden_in,
    lengths,
    attn_gain,
    q_weight,
    gate_weight,
    k_weight,
    v_weight,
    q_gain,
    k_gain,
    o_weight,
    mlp_gain,
    w_gate,
    w_up,
    w_down,
    out_grad,
):
    dp_index, ctx_index, z_index = (lax.axis_index(a) for a in ("dp", "ctx", "tensor"))
    q_cols, k_cols, ff_cols = q_weight.shape[1], k_weight.shape[1], w_down.shape[1]
    span, width = hidden_in.shape
    mid, count = width // 2, 2 * links.half
    shard, head_shard = attn_gain.shape[0], q_gain.shape[0]
    head_dim = head_shard * count
    heads, kv_heads = q_cols // head_dim, k_cols // head_dim
    group = heads // kv_heads
    length = lengths[0]
    low = lambda *mats: jnp.concatenate([m.astype(BF16) for m in mats], axis=1)

    small = jnp.concatenate([attn_gain, mlp_gain, q_gain, k_gain]).astype(BF16)[None, :]
    gains, seen = links.small_gather(small)
    everywhere = lambda block: {p: block for p in range(len(links.bits))}
    paired = lambda half: (half, links.swap(half, "ctx", 1))
    plane = ("dp", "ctx")
    first_own = after(low(q_weight, gate_weight, k_weight, v_weight, o_weight), *seen)
    first_single = links.send_own(everywhere(first_own))
    attn_scale = gains[:, :shard].reshape(1, width).astype(F32)
    mlp_scale = gains[:, shard : 2 * shard].reshape(1, width).astype(F32)
    owners = jnp.stack([links.owner_of(p, dp_index, ctx_index) for p in range(count)]).astype(jnp.int32)
    pick = (owners[None, :] == jnp.arange(count)[:, None]).astype(BF16)
    mesh_gains = project(pick, gains)
    mesh_scale = mesh_gains[:, :shard].reshape(1, width)
    query_scale = mesh_gains[:, 2 * shard : 2 * shard + head_shard].reshape(1, head_dim)
    key_scale = mesh_gains[:, 2 * shard + head_shard :].reshape(1, head_dim)

    parts = 2 * links.tensor
    row_block = span // parts
    row_places = jnp.stack(
        [part * links.tensor + (z_index ^ j) for part in range(2) for j in links.turns]
    ).astype(jnp.int32)
    start = ctx_index * span
    scalars = jnp.concatenate(
        [row_places, owners.astype(jnp.int32), jnp.stack([start, length]).astype(jnp.int32)]
    )
    spots = (start + row_places[:, None] * row_block + jnp.arange(row_block)[None, :]).reshape(span)
    spots = spots.astype(jnp.int32)
    freq_steps = jnp.arange(head_dim // 2, dtype=F32) * (2.0 / head_dim)
    turned = spots.astype(F32)[:, None] * jnp.exp(-math.log(ROPE_BASE) * freq_steps)[None, :]
    cosine, sine = jnp.cos(turned), jnp.sin(turned)
    cos = jnp.concatenate([cosine, cosine], axis=1)
    sin = jnp.concatenate([-sine, sine], axis=1)
    spot_col, spot_row = spots[:, None], spots[None, :]

    stream, grad_out, plain_down, down_grad, plain_normed, normed = enter(
        scalars, count, parts, span, hidden_in, out_grad, after(mesh_scale, first_own)
    )
    feed_low, down_low = low(w_gate, w_up), low(w_down)
    first_single = {q: after(b, normed, feed_low, down_low) for q, b in first_single.items()}
    feed_mat = lax.all_gather(after(feed_low, normed), plane, axis=0, tiled=True)

    first_pairs = links.send_on(first_single)
    first_seen = [b for pair in first_pairs.values() for b in pair]
    down_mat = lax.all_gather(after(down_low, *first_seen), plane, axis=0, tiled=True)
    first_mat = paired(links.assemble(first_own, first_single, first_pairs))
    gate_at, key_at = q_cols, 2 * q_cols
    value_at, out_at = key_at + k_cols, key_at + 2 * k_cols
    kv_proj, kv = enter_heads(
        "enter_keys", kv_heads, head_dim, True, normed, first_mat, key_at, 2 * k_cols, cos, sin, key_scale
    )
    proj, query = enter_heads(
        "enter_queries", heads, head_dim, False, after(normed, kv), first_mat, 0, 2 * q_cols, cos, sin, query_scale
    )
    kvs, turns = [kv], [0]
    mask = links.ctx // 2
    while mask:
        kvs = kvs + [links.swap(b if i == 0 else after(b, query), "ctx", mask) for i, b in enumerate(kvs)]
        turns = turns + [p ^ mask for p in turns]
        mask //= 2
    at = jnp.concatenate([jnp.stack([ctx_index, length]).astype(jnp.int32), owners])
    half_rows = span // 2
    shard_rows = half_rows // links.tensor
    part_of = lambda value, t: value[t * half_rows : (t + 1) * half_rows]
    own_rows = lambda value, t: value[t * shard_rows : (t + 1) * shard_rows]
    live = [(part_of(spot_col, t)[:shard_rows] < length).astype(F32) for t in range(2)]
    mixed, sums, out_part, one = ([None] * 2 for _ in range(4))
    query_now, gated_all = query, None
    for t in range(2):
        mixed[t], sums[t], gated_all, out_part[t] = attend(
            at, t, 2, group, head_dim, turns, query_now, proj, gate_at, spot_col, spot_row, first_mat, out_at, kvs, gated_all
        )
        one[t] = links.scatter_first(out_part[t])
    middle, normed_two, unit_two, inverse_two, two = ([None] * 2 for _ in range(5))
    late = (one[1][1],)
    for t in range(2):
        attn_out, _ = links.scatter_rest(*one[t], late=late)
        middle[t] = own_rows(stream, t).astype(F32) + attn_out * live[t]
        inverse_two[t] = lax.rsqrt(jnp.mean(middle[t] * middle[t], axis=-1, keepdims=True) + EPSILON)
        unit_two[t] = middle[t] * inverse_two[t]
        normed_two[t] = (unit_two[t] * mlp_scale).astype(BF16)
        two[t] = links.gather_first(normed_two[t])
        late = (normed_two[t],)
    pieces_two = [links.gather_rest(*two[0], late=late)]
    pieces_two.append(links.gather_rest(*two[1], late=(pieces_two[0][0],)))

    grad_hidden = project(after(plain_down, one[1][1]), down_mat)
    back_part, three = [None] * 2, [None] * 2
    held = None
    for t in range(2):
        held, back_part[t] = feed(scalars, count, parts, t, pieces_two[t], feed_mat, grad_hidden, held)
        three[t] = links.scatter_first(back_part[t])
    hidden_all, grad_gate_all, grad_up_all, rows_two = held

    halves = lambda value: (value[:, : value.shape[1] // 2], value[:, value.shape[1] // 2 :])

    def grad_others(rows_of, cols, *before):
        left = after(rows_of[:, mid:], *before)
        parts = [row_contract(left, c).astype(BF16) for c in cols]
        return parts, [links.swap(p, "ctx", 1) for p in parts]

    def grad_totals(rows_of, cols, arrived, *before):
        left = after(rows_of[:, :mid], *before)
        return [(row_contract(left, c) + a.astype(F32)).astype(BF16) for c, a in zip(cols, arrived)]

    def grad_rest(firsts, *before):
        return [
            links.reduce_rest(kept, after(came, *before), turn) for turn, (kept, _, came) in enumerate(firsts)
        ]

    scaled_back = lambda back, t: own_rows(grad_out, t).astype(F32) + norm_back(
        back, unit_two[t], inverse_two[t], mlp_scale
    )
    grad_middle, attn_grad, four = ([None] * 2 for _ in range(3))
    back_a, seen_a = links.scatter_rest(*three[0], before=(hidden_all,))
    back_b, seen_b = links.scatter_rest(*three[1])
    feed_cols = [grad_gate_all, grad_up_all]
    over_plane = lambda part: lax.psum_scatter(part, plane, scatter_dimension=0, tiled=True).astype(F32)
    down_grad_part = row_contract(after(plain_down, three[0][1]), hidden_all).astype(BF16)
    grad_down = over_plane(down_grad_part)
    feed_others, feed_came = grad_others(rows_two, feed_cols, down_grad_part)
    homes = jnp.stack([(z_index ^ j) * 2 + part for part in range(2) for j in links.turns]).astype(jnp.int32)
    down_part = descend(homes, owners, after(hidden_all, *feed_others, three[1][1]), down_mat)
    for t, back in enumerate((back_a, back_b)):
        back = after(back, *((down_part,) if t == 0 else (attn_grad[0],)))
        grad_middle[t] = scaled_back(back, t)
        attn_grad[t] = (grad_middle[t] * live[t]).astype(BF16)
        four[t] = links.gather_first(attn_grad[t])
    grad_mlp_gain = sum(jnp.sum(b * unit_two[t], axis=0) for t, b in enumerate((back_a, back_b)))
    attn_shard = attn_grad[1]
    pieces_four = [links.gather_rest(*four[0], late=(attn_shard,))]
    pieces_four.append(links.gather_rest(*four[1]))
    down_sum = lax.psum_scatter(after(down_part, grad_down, pieces_four[0][1], pieces_four[1][0]), "tensor", scatter_dimension=0, tiled=True).astype(F32)
    backward = lambda t, pieces, olds: attend_back(
        at, count, t, 2, group, head_dim, turns, query, proj, gate_at, mixed[t], sums[t], pieces, first_mat, out_at,
        spot_row, spot_col, cos, sin, query_scale, kvs, olds,
    )
    feed_totals = grad_totals(rows_two, feed_cols, feed_came, pieces_four[0][1])
    ready = after(pieces_four[0][1], pieces_four[1][0], grad_down, *feed_totals)
    grad_kvs, held, gain_a = backward(0, (pieces_four[0][0], ready), None)
    back_places = jnp.array(
        [part * links.tensor + o for o in range(links.tensor) for part in range(2)], dtype=jnp.int32
    )
    last = pieces_four[1]
    grad_kvs, held, gain_b = backward(1, last, (*grad_kvs, *held))
    grad_query, grad_gates, attn_all = held
    down_sum = after(down_sum, grad_kvs[0])
    down_shard = jnp.concatenate(middle, axis=0) + down_sum * jnp.concatenate(live, axis=0)
    down_all = lax.all_gather(down_shard.astype(BF16), "tensor", axis=0, tiled=True)
    if width // count % 128:
        attn_all = columns(attn_all, jnp.argsort(owners))
    q_gain_part = gain_a + gain_b
    pieces = dict(zip(turns, grad_kvs))
    mask = 1
    kv_gone, kv_seen = [], []
    while len(pieces) > 1:
        near = [p for p in pieces if not p & mask]
        gone = [pieces[p ^ mask].astype(BF16) for p in near]
        came = links.swap(jnp.concatenate(gone, axis=0), "ctx", mask)
        kv_gone.append(gone)
        kv_seen.append(came)
        pieces = {
            p: pieces[p].astype(F32) + came[i * span : (i + 1) * span].astype(F32) for i, p in enumerate(near)
        }
        mask *= 2
    outer_part = plane_grads(
        "outer_grads", [(after(plain_normed, *kv_gone[-1]), (grad_query, grad_gates)), (attn_all, (gated_all,))],
        3 * q_cols + 2 * k_cols,
    )
    grad_key, grad_value, k_gain_part = keys_back(
        kv_heads, head_dim, after(pieces[0], outer_part, down_shard), kv_proj, 0, cos, sin, key_scale
    )
    feed_first = [links.reduce_first(x, turn, *((grad_key,) if turn else ())) for turn, x in enumerate(feed_totals)]
    seven, eight, in_part, grad_in, attn_gain_part = ([None] * 2 for _ in range(5))
    late_query = grad_query
    for t in range(2):
        terms = [
            (late_query, first_mat, 0),
            (grad_gates, first_mat, gate_at),
            (grad_key, first_mat, key_at),
            (grad_value, first_mat, value_at),
        ]
        in_part[t], gain = spread("spread_in", terms, t, 2, normed=normed)
        attn_gain_part[t] = gain[0] / attn_scale[0]
        seven[t] = links.scatter_first(in_part[t] if t == 0 else after(in_part[1], seven[0][1]))
    inner_part = plane_grads(
        "inner_grads", [(after(plain_normed, attn_gain_part[1]), (grad_key, grad_value))], 3 * q_cols + 2 * k_cols, outer_part
    )
    inner_sum = over_plane(inner_part)
    summed = [links.scatter_rest(*seven[t]) for t in range(2)]
    late = ()
    for t in range(2):
        back = after(summed[t][0], *late)
        x = own_rows(stream, t).astype(F32)
        inverse = lax.rsqrt(jnp.mean(x * x, axis=-1, keepdims=True) + EPSILON)
        unit = x * inverse
        grad_in[t] = (grad_middle[t] + norm_back(back, unit, inverse, attn_scale)).astype(BF16)
        eight[t] = links.gather_first(grad_in[t])
        late = (grad_in[t],)
    feed_rest = grad_rest(feed_first, grad_in[0])
    hidden_out = leave(jnp.concatenate([back_places, scalars[parts:]]), count, parts, [after(down_all, in_part[1])], BF16)
    in_pieces = [*links.gather_rest(*eight[0], late=late)]
    in_pieces += links.gather_rest(*eight[1], late=(in_pieces[0],))
    attn_gain_part = sum(attn_gain_part)
    arrived_one = in_pieces[1]
    in_pieces[1] = after(in_pieces[1], hidden_out, inner_sum, *(r[0] for r in feed_rest))
    grad_in = leave(scalars, count, parts, in_pieces, F32)

    blocks = jnp.stack([attn_gain_part.reshape(count, shard), grad_mlp_gain.reshape(count, shard)])
    to_mesh = (owners[None, :] == jnp.arange(count)[:, None]).astype(F32)
    blocks = jnp.einsum("ap,kpn->kan", to_mesh, blocks, precision=lax.Precision.HIGHEST)
    packed = jnp.concatenate([blocks.reshape(1, -1), q_gain_part[None, :], k_gain_part[None, :]], axis=1)
    packed = links.add_all(packed, arrived_one, hidden_out, *(r[2] for r in feed_rest))[0]
    rank = dp_index * links.ctx + ctx_index
    take = lambda at, size: lax.dynamic_slice_in_dim(packed, at + rank * size, size)
    return (
        hidden_out,
        grad_in,
        take(0, shard),
        inner_sum[:, :q_cols],
        inner_sum[:, q_cols : 2 * q_cols],
        inner_sum[:, 3 * q_cols : 3 * q_cols + k_cols],
        inner_sum[:, 3 * q_cols + k_cols :],
        take(2 * width, head_shard),
        take(2 * width + head_dim, head_shard),
        inner_sum[:, 2 * q_cols : 3 * q_cols],
        take(width, shard),
        feed_rest[0][0],
        feed_rest[1][0],
        grad_down,
    )


def solution(mesh):
    links = Links(dict(mesh.shape))
    rows = P(("dp", "ctx"))
    plain = P(("dp", "ctx"), None)
    split = P(("dp", "ctx"), "tensor")

    def step(*arrays):
        return per_device(links, *arrays)

    return jax.shard_map(
        step,
        mesh=mesh,
        in_specs=(plain, P("dp"), rows, split, split, split, split, rows, rows, split, rows, split, split, split, plain),
        out_specs=(plain, plain, rows, split, split, split, split, rows, rows, split, rows, split, split, split),
        check_vma=False,
    )
```

```python
import functools
import math

import jax
import jax.numpy as jnp
from jax import lax
from jax.experimental import pallas as pl
from jax.experimental.pallas import tpu as pltpu
from jax.sharding import PartitionSpec as P

EPSILON = 1e-06
ROPE_BASE = 1000000.0
CONTRACT_ROWS = (((0,), (0,)), ((), ()))
CONTRACT_COLS = (((1,), (1,)), ((), ()))
F32 = jnp.float32
BF16 = jnp.bfloat16
VMEM_BYTES = 56 * 1024 * 1024


def project(operand, matrix):
    return jnp.dot(operand, matrix, preferred_element_type=F32)


def row_contract(first_op, second_op):
    return lax.dot_general(first_op, second_op, CONTRACT_ROWS, preferred_element_type=F32)


def col_contract(first_op, second_op):
    return lax.dot_general(first_op, second_op, CONTRACT_COLS, preferred_element_type=F32)


def sigmoid(value):
    return 1.0 / (1.0 + jnp.exp(-value))


def after(value, *others):
    if not others:
        return value
    return lax.optimization_barrier((value,) + others)[0]


def cost(flops, moved, exps=0):
    return pl.CostEstimate(flops=int(flops), bytes_accessed=int(moved), transcendentals=int(exps))


def params(**kwargs):
    return pltpu.CompilerParams(vmem_limit_bytes=VMEM_BYTES, **kwargs)


class Links:
    def __init__(self, sizes):
        self.dp, self.ctx, self.tensor = sizes["dp"], sizes["ctx"], sizes["tensor"]
        self.half = self.dp * self.ctx // 2
        ctx_bits = int(math.log2(self.ctx // 2))
        dp_bits = int(math.log2(self.dp))
        self.bits = [("ctx", 2 << i) for i in range(ctx_bits)] + [("dp", 1 << i) for i in range(dp_bits)]
        self.masks = [(2 << i) - 1 for i in range(int(math.log2(self.tensor)))]
        self.turns = [0]
        for mask in reversed(self.masks):
            self.turns = self.turns + [j ^ mask for j in self.turns]

    def swap(self, value, axis, mask):
        count = {"dp": self.dp, "ctx": self.ctx, "tensor": self.tensor}[axis]
        return lax.ppermute(value, axis, [(i, i ^ mask) for i in range(count)])

    def order(self, turn):
        places = list(range(len(self.bits)))
        return places if turn else places[::-1]

    def send_own(self, blocks):
        return {1 << p: self.swap(blocks[p], *self.bits[p]) for p in self.order(0)}

    def send_far(self, block):
        count = self.dp * self.ctx
        single = {}
        for q in range(1, self.half):
            far = (q // (self.ctx // 2)) * self.ctx + (q % (self.ctx // 2)) * 2
            single[q] = lax.ppermute(block, ("dp", "ctx"), [(i, i ^ far) for i in range(count)])
        return single

    def send_on(self, single):
        mid = next(iter(single.values())).shape[1] // 2
        left = {q: b[:, :mid] for q, b in single.items()}
        right = {q: b[:, mid:] for q, b in single.items()}
        for side, places in ((left, self.order(0)), (right, self.order(1))):
            for q in range(1, self.half):
                if q not in single:
                    self.reach(side, q, places)
        return {q: (left[q], right[q]) for q in left if q not in single}

    def assemble(self, block, single, pairs):
        blocks, groups = [], []
        for q in range(self.half):
            members = [block] if q == 0 else [single[q]] if q in single else list(pairs[q])
            groups.append(tuple(range(len(blocks), len(blocks) + len(members))))
            blocks += members
        return stack_blocks(groups, blocks)

    def reach(self, side, q, places):
        if q not in side:
            last = [p for p in places if q & (1 << p)][-1]
            self.reach(side, q ^ (1 << last), places)
            side[q] = self.swap(side[q ^ (1 << last)], *self.bits[last])

    def reduce_first(self, total, turn, *hold):
        rows = total.shape[0] // self.half
        pieces = {q: total[q * rows : (q + 1) * rows] for q in range(self.half)}
        return self.reduce_step(pieces, turn, 0, *hold)

    def reduce_step(self, pieces, turn, step, *hold):
        place = self.order(turn)[step]
        bit = 1 << place
        kept = {q: b for q, b in pieces.items() if not q & bit}
        gone = [pieces[q | bit].astype(BF16) for q in kept]
        sent = after(jnp.concatenate(gone, axis=0), *hold)
        return kept, [sent], self.swap(sent, *self.bits[place])

    def reduce_rest(self, kept, came, turn):
        gone = []
        for step in range(1, len(self.bits) + 1):
            rows = came.shape[0] // len(kept)
            pieces = {
                q: b.astype(F32) + came[i * rows : (i + 1) * rows].astype(F32) for i, (q, b) in enumerate(kept.items())
            }
            if step < len(self.bits):
                kept, sent, came = self.reduce_step(pieces, turn, step)
                gone += sent
        return pieces[0], gone, came

    def small_gather(self, row):
        far = self.send_far(row)
        own = jnp.concatenate([row] + [far[q] for q in range(1, self.half)], axis=0)
        return jnp.concatenate([own, self.swap(own, "ctx", 1)], axis=0), list(far.values())

    def owner_of(self, position, dp_index, ctx_index):
        h, q = position // self.half, position % self.half
        dp_far, ctx_far = q // (self.ctx // 2), (q % (self.ctx // 2)) * 2 + h
        return (dp_index ^ dp_far) * self.ctx + (ctx_index ^ ctx_far)

    def scatter_first(self, part):
        rows = part.shape[0] // 2
        return part[:rows], self.swap(part[rows:], "tensor", self.masks[0])

    def scatter_rest(self, kept, came, before=(), late=()):
        gone = seen = came
        kept = kept.astype(F32) + came.astype(F32)
        for mask in self.masks[1:]:
            rows = kept.shape[0] // 2
            gone = kept[rows:].astype(BF16)
            seen = self.swap(after(gone, *before), "tensor", mask)
            kept = kept[:rows] + after(seen, *late).astype(F32)
        return kept, seen

    def gather_first(self, shard):
        return shard, self.swap(shard, "tensor", self.masks[-1])

    def gather_rest(self, shard, came, late=()):
        came = after(came, *late)
        for mask in self.masks[-2::-1]:
            shard = jnp.concatenate([shard, came], axis=0)
            came = self.swap(shard, "tensor", mask)
        return shard, came

    def add_all(self, value, *before):
        value = after(value, *before)
        value = value + self.swap(value, "ctx", 1)
        value = value + sum(self.send_far(value).values())
        return value + sum(self.swap(value, "tensor", mask) for mask in range(1, self.tensor))


def still(scalars, count, parts):
    owners = scalars[parts : parts + count]
    return owners, lax.dynamic_update_slice(scalars, jnp.arange(count, dtype=scalars.dtype), (parts,))


def columns(value, owners):
    count = owners.shape[0]
    blocks = value.reshape(value.shape[0], count, value.shape[1] // count)
    return jnp.take(blocks, owners, axis=1).reshape(value.shape)


def column_place(scalars, parts, p, size):
    if size % 128:
        return pl.ds(p * size, size)
    return pl.ds(pl.multiple_of(scalars[parts + p] * size, size), size)


def stack_kernel(groups, *refs):
    out_ref = refs[-1]
    for q, group in enumerate(groups):

        @pl.when(pl.program_id(0) == q)
        def _(group=group):
            col = 0
            for i in group:
                out_ref[:, col : col + refs[i].shape[1]] = refs[i][...]
                col += refs[i].shape[1]


def stack_blocks(groups, blocks):
    rows, n = blocks[0].shape
    held = lambda b: pl.BlockSpec(b.shape, lambda i: (0, 0), pipeline_mode=pl.Buffered(1))
    return pl.pallas_call(
        functools.partial(stack_kernel, groups),
        out_shape=jax.ShapeDtypeStruct((rows * len(groups), n), blocks[0].dtype),
        grid=(len(groups),),
        in_specs=[held(b) for b in blocks],
        out_specs=pl.BlockSpec((rows, n), lambda i: (i, 0)),
        compiler_params=params(),
        cost_estimate=cost(0, 4 * rows * len(groups) * n),
        name="stack",
    )(*blocks)


def enter_kernel(
    count, parts, scalars, xa_ref, xb_ref, ga_ref, gb_ref, gain_ref, x_out, g_out, m_out, mine_out, plain_out, n_out
):
    step = pl.program_id(0)
    rows, width = xa_ref.shape
    size = width // count
    moved = [column_place(scalars, parts, p, size) for p in range(count)]
    for part, (x_ref, g_ref) in enumerate(((xa_ref, ga_ref), (xb_ref, gb_ref))):
        if part == 0:

            @pl.when(step % (parts // 4) == 0)
            def _(x_ref=x_ref, g_ref=g_ref):
                for p in range(count):
                    x_out[:, p * size : (p + 1) * size] = x_ref[:, moved[p]]
                    g_out[:, p * size : (p + 1) * size] = g_ref[:, moved[p]]

        place = slice(part * rows, (part + 1) * rows)
        spot = scalars[parts + count] + scalars[2 * step + part] * rows
        live = spot + lax.broadcasted_iota(jnp.int32, (rows, 1), 0) < scalars[parts + count + 1]
        m_out[place, :] = jnp.where(live, g_ref[...].astype(F32), 0.0).astype(BF16)
        wide = x_ref[...].astype(F32)
        inverse = lax.rsqrt(jnp.mean(wide * wide, axis=-1, keepdims=True) + EPSILON)
        plain_out[place, :] = (wide * inverse * gain_ref[...]).astype(BF16)
        for p in range(count):
            n_out[place, p * size : (p + 1) * size] = plain_out[place, moved[p]]
            mine_out[place, p * size : (p + 1) * size] = m_out[place, moved[p]]


def enter(scalars, count, parts, span, hidden_in, out_grad, gain):
    rows, width = span // parts, hidden_in.shape[1]
    narrow = width // count % 128
    owners = scalars[parts : parts + count]
    upper = pl.BlockSpec((rows, width), lambda i, s: (s[2 * i], 0))
    lower = pl.BlockSpec((rows, width), lambda i, s: (s[2 * i + 1], 0))
    own = pl.BlockSpec((rows, width), lambda i, s: (i // (parts // 4), 0))
    plain = pl.BlockSpec((2 * rows, width), lambda i, s: (i, 0))
    shape = jax.ShapeDtypeStruct((span, width), BF16)
    short = jax.ShapeDtypeStruct((2 * rows, width), BF16)
    x, g, m, mine, unmoved, normed = pl.pallas_call(
        functools.partial(enter_kernel, count, parts),
        out_shape=(short, short, shape, shape, shape, shape),
        grid_spec=pltpu.PrefetchScalarGridSpec(
            num_scalar_prefetch=1,
            grid=(parts // 2,),
            in_specs=[upper, lower, upper, lower, pl.BlockSpec((1, width), lambda i, s: (0, 0))],
            out_specs=(own, own, plain, plain, plain, plain),
        ),
        compiler_params=params(),
        cost_estimate=cost(10 * span * width, 8 * span * width),
        name="enter",
    )(scalars, hidden_in, hidden_in, out_grad, out_grad, gain)
    if narrow:
        x, g, mine, normed = (columns(v, owners) for v in (x, g, mine, normed))
    return x, g, m, mine, unmoved, normed


def leave_kernel(count, parts, scalars, *refs):
    pieces, out_ref = refs[:4], refs[4]
    blocks, size = parts // 4, out_ref.shape[1] // count
    rows = out_ref.shape[0] // parts
    for i, in_ref in enumerate(pieces):

        @pl.when(pl.program_id(0) == i)
        def _(i=i, in_ref=in_ref):
            for part in range(blocks):
                at = pl.ds(pl.multiple_of(scalars[i * blocks + part] * rows, rows), rows)
                for p in range(count):
                    block = in_ref[part * rows : (part + 1) * rows, p * size : (p + 1) * size]
                    out_ref[at, column_place(scalars, parts, p, size)] = block.astype(out_ref.dtype)


def leave(scalars, count, parts, pieces, dtype):
    rows, width = pieces[0].shape
    place = lambda k: lambda i, s: (0, 0)
    if len(pieces) == 1:
        rows, pieces = rows // 4, pieces * 4
        place = lambda k: lambda i, s: (k, 0)
    if width // count % 128:
        owners, scalars = still(scalars, count, parts)
        pieces = [columns(piece, jnp.argsort(owners)) for piece in pieces]
    return pl.pallas_call(
        functools.partial(leave_kernel, count, parts),
        out_shape=jax.ShapeDtypeStruct((4 * rows, width), dtype),
        grid_spec=pltpu.PrefetchScalarGridSpec(
            num_scalar_prefetch=1,
            grid=(4,),
            in_specs=[pl.BlockSpec((rows, width), place(k)) for k in range(4)],
            out_specs=pl.BlockSpec((4 * rows, width), lambda i, s: (0, 0)),
        ),
        compiler_params=params(),
        cost_estimate=cost(0, 24 * rows * width),
        name="leave",
    )(scalars, *pieces)


def spread_kernel(tiles, count, parts, summed, *refs):
    homes, refs = (refs[0], refs[1:]) if parts else (None, refs)
    values, out_ref = refs[:count], refs[3 * count + summed]
    for h in range(2):

        @pl.when(pl.program_id(0) // tiles == h)
        def _(h=h):
            total = None
            for k in range(count):
                term = lax.dot_general(
                    values[k][...], refs[count + 2 * k + h][...], CONTRACT_COLS, preferred_element_type=F32
                )
                total = term if total is None else total + term
            if summed:
                norm_ref, sum_ref = refs[3 * count], refs[3 * count + 2]
                gain = jnp.sum(total * norm_ref[...].astype(F32), axis=0, keepdims=True)
                sum_ref[...] = jnp.broadcast_to(gain, sum_ref.shape)
            if parts:
                rows = out_ref.shape[0] // parts
                for i in range(parts):
                    at = pl.ds(pl.multiple_of(homes[i] * rows, rows), rows)
                    out_ref[at, :] = total[i * rows : (i + 1) * rows].astype(BF16)
            else:
                out_ref[...] = total.astype(BF16)


def spread(name, terms, part=0, parts=1, homes=None, normed=None):
    rows = terms[0][0].shape[0] // parts
    mid = terms[0][1][0].shape[0]
    tile = mid // 2
    specs, mats = [], []
    for value, pair, start in terms:
        n = value.shape[1]
        specs += [
            pl.BlockSpec((tile, n), lambda j, *s, c=start // n: (jnp.minimum(j, 1), c)),
            pl.BlockSpec((tile, n), lambda j, *s, c=start // n: (jnp.maximum(j - 2, 0), c)),
        ]
        mats += list(pair)
    held = [pl.BlockSpec((rows, v.shape[1]), lambda j, *s: (part, 0)) for v, _, _ in terms]
    wide = sum(v.shape[1] for v, _, _ in terms)
    summed = normed is not None
    shapes = [jax.ShapeDtypeStruct((rows, 2 * mid), BF16)]
    outs = [pl.BlockSpec((rows, tile), lambda j, *s: (0, j))]
    extra = []
    if summed:
        extra = [normed]
        specs.append(pl.BlockSpec((rows, tile), lambda j, *s: (part, j)))
        shapes.append(jax.ShapeDtypeStruct((8, 2 * mid), F32))
        outs.append(pl.BlockSpec((8, tile), lambda j, *s: (0, j)))
    out = pl.pallas_call(
        functools.partial(spread_kernel, 2, len(terms), 0 if homes is None else homes.shape[0], summed),
        out_shape=shapes,
        grid_spec=pltpu.PrefetchScalarGridSpec(
            num_scalar_prefetch=0 if homes is None else 1, grid=(4,), in_specs=held + specs, out_specs=outs
        ),
        compiler_params=params(),
        cost_estimate=cost(4 * rows * mid * wide, 2 * wide * (rows + 2 * mid) + 4 * rows * mid),
        name=name,
    )(*(() if homes is None else (homes,)), *(v for v, _, _ in terms), *mats, *extra)
    return out if summed else out[0]


def feed_kernel(first, count, parts, scalars, a_ref, b_ref, gate_ref, up_ref, gh_ref, *refs):
    refs = refs if first else refs[4:]
    hidden_out, gate_out, up_out, rows_out, part_out, x_ref, acc_ref = refs
    step, size = pl.program_id(0), x_ref.shape[1] // count
    moved = [column_place(scalars, parts, p, size) for p in range(count)]

    @pl.when(step == 0)
    def _():
        rows = a_ref.shape[0]
        rows_out[:rows, :] = a_ref[...]
        rows_out[rows:, :] = b_ref[...]
        for p in range(count):
            x_ref[:rows, moved[p]] = a_ref[:, p * size : (p + 1) * size]
            x_ref[rows:, moved[p]] = b_ref[:, p * size : (p + 1) * size]
        acc_ref[...] = jnp.zeros_like(acc_ref)

    gate = project(x_ref[...], gate_ref[...])
    up = project(x_ref[...], up_ref[...])
    grad = gh_ref[...]
    sig = sigmoid(gate)
    hidden_out[...] = (gate * sig * up).astype(BF16)
    grad_gate = (grad * up * sig * (1.0 + gate * (1.0 - sig))).astype(BF16)
    grad_up = (grad * (gate * sig)).astype(BF16)
    gate_out[...] = grad_gate
    up_out[...] = grad_up
    acc_ref[...] += col_contract(grad_gate, gate_ref[...]) + col_contract(grad_up, up_ref[...])

    @pl.when(step == pl.num_programs(0) - 1)
    def _():
        for p in range(count):
            part_out[:, p * size : (p + 1) * size] = acc_ref[:, moved[p]].astype(BF16)


def feed(scalars, count, parts, part, pieces, mat, grad_hidden, olds):
    span, ff = grad_hidden.shape
    piece, width = pieces[0].shape
    rows = 2 * piece
    tile = 512 if ff % 512 == 0 else ff
    steps = ff // tile
    narrow = width // count % 128
    owners = scalars[parts : parts + count]
    given = [columns(x, jnp.argsort(owners)) for x in pieces] if narrow else pieces
    held = pl.BlockSpec((piece, width), lambda j, s: (0, 0))
    columns_of = lambda shift: pl.BlockSpec((width, tile), lambda j, s: (0, shift + j))
    cols = pl.BlockSpec((rows, tile), lambda j, s: (part, j))
    first = olds is None
    olds = () if first else tuple(olds)
    wide = jax.ShapeDtypeStruct((span, ff), BF16)
    out = pl.pallas_call(
        functools.partial(feed_kernel, first, count, parts),
        out_shape=(
            wide,
            wide,
            wide,
            jax.ShapeDtypeStruct((span, width), BF16),
            jax.ShapeDtypeStruct((rows, width), BF16),
        ),
        grid_spec=pltpu.PrefetchScalarGridSpec(
            num_scalar_prefetch=1,
            grid=(steps,),
            in_specs=[held, held, columns_of(0), columns_of(steps), cols]
            + [pl.BlockSpec(memory_space=pl.ANY)] * len(olds),
            out_specs=(
                cols,
                cols,
                cols,
                pl.BlockSpec((rows, width), lambda j, s: (part, 0)),
                pl.BlockSpec((rows, width), lambda j, s: (0, 0)),
            ),
            scratch_shapes=[pltpu.VMEM((rows, width), BF16), pltpu.VMEM((rows, width), F32)],
        ),
        input_output_aliases={6 + i: i for i in range(len(olds))},
        compiler_params=params(),
        cost_estimate=cost(8 * rows * width * ff, 8 * width * ff, 2 * rows * ff),
        name="feed",
    )(scalars, *given, mat, mat, grad_hidden, *olds)
    return out[:4], columns(out[4], owners) if narrow else out[4]


def descend_kernel(parts, homes, value_ref, mat_ref, out_ref):
    total = col_contract(value_ref[...], mat_ref[...])
    rows = out_ref.shape[0] // parts
    for i in range(parts):
        at = pl.ds(pl.multiple_of(homes[i] * rows, rows), rows)
        out_ref[at, :] = total[i * rows : (i + 1) * rows].astype(BF16)


def descend(homes, owners, value, mat):
    rows, n = value.shape
    width, count, parts = mat.shape[0], owners.shape[0], homes.shape[0]
    narrow = width // count % 128
    steps = 4 if narrow else count
    out = pl.pallas_call(
        functools.partial(descend_kernel, parts),
        out_shape=jax.ShapeDtypeStruct((rows, width), BF16),
        grid_spec=pltpu.PrefetchScalarGridSpec(
            num_scalar_prefetch=1,
            grid=(steps,),
            in_specs=[
                pl.BlockSpec((rows, n), lambda j, s: (0, 0)),
                pl.BlockSpec((width // steps, n), lambda j, s: (s[parts + j], 0)),
            ],
            out_specs=pl.BlockSpec((rows, width // steps), lambda j, s: (0, j)),
        ),
        compiler_params=params(),
        cost_estimate=cost(2 * rows * width * n, 2 * (rows + width) * n + 2 * rows * width),
        name="descend",
    )(jnp.concatenate([homes, jnp.arange(4, dtype=jnp.int32) if narrow else owners]), value, mat)
    return columns(out, owners) if narrow else out


def plane_grads_kernel(counts, *refs):
    out_ref, start, at = refs[-1], 0, len(counts)
    for left, count in zip(refs, counts):
        rights = [r[...] for r in refs[at : at + count]]
        right = rights[0] if count == 1 else jnp.concatenate(rights, axis=1)
        size = right.shape[1]
        out_ref[:, start : start + size] = row_contract(left[...], right).astype(BF16)
        start, at = start + size, at + count


def plane_grads(name, terms, total, old=None):
    span, width = terms[0][0].shape
    tile = 256
    rights = [g for _, pair in terms for g in pair]
    cols = sum(g.shape[1] for g in rights)
    at = 0 if old is None else total // cols - 1
    left = pl.BlockSpec((span, tile), lambda j: (0, j))
    held = [pl.BlockSpec(g.shape, lambda j: (0, 0)) for g in rights]
    olds = () if old is None else (old,)
    return pl.pallas_call(
        functools.partial(plane_grads_kernel, tuple(len(pair) for _, pair in terms)),
        out_shape=jax.ShapeDtypeStruct((width, total), BF16),
        grid=(width // tile,),
        in_specs=[left] * len(terms) + held + [pl.BlockSpec(memory_space=pl.ANY)] * len(olds),
        out_specs=pl.BlockSpec((tile, cols), lambda j: (j, at)),
        input_output_aliases={len(terms) + len(rights): 0} if olds else {},
        compiler_params=params(),
        cost_estimate=cost(2 * span * width * cols, 2 * span * (2 * width + cols) + 2 * width * cols),
        name=name,
    )(*(a for a, _ in terms), *rights, *olds)


def enter_heads_kernel(heads, head_dim, paired, x_ref, near_ref, far_ref, cos_ref, sin_ref, gain_ref, p_out, r_out):
    mid = x_ref.shape[1] // 2
    proj = project(x_ref[:, :mid], near_ref[...]) + project(x_ref[:, mid:], far_ref[...])
    p_out[...] = proj
    for h in range(heads):
        unit, _ = unit_of(proj[:, h * head_dim : (h + 1) * head_dim])
        turned = turn(unit * gain_ref[...], cos_ref, sin_ref, 1.0).astype(BF16)
        at = (2 * h if paired else h) * head_dim
        r_out[:, at : at + head_dim] = turned
        if paired:
            value = proj[:, (heads + h) * head_dim : (heads + h + 1) * head_dim]
            r_out[:, at + head_dim : at + 2 * head_dim] = value.astype(BF16)


def enter_heads(name, heads, head_dim, paired, normed, mats, at, cols, cos, sin, gain):
    span, width = normed.shape
    rows = span // 2
    spec = lambda n: pl.BlockSpec((rows, n), lambda i: (i, 0))
    mat = pl.BlockSpec((width // 2, cols), lambda i: (0, at // cols))
    turned = heads * head_dim * (2 if paired else 1)
    return pl.pallas_call(
        functools.partial(enter_heads_kernel, heads, head_dim, paired),
        out_shape=(jax.ShapeDtypeStruct((span, cols), F32), jax.ShapeDtypeStruct((span, turned), BF16)),
        grid=(2,),
        in_specs=[spec(width), mat, mat, spec(head_dim), spec(head_dim), pl.BlockSpec((1, head_dim), lambda i: (0, 0))],
        out_specs=(spec(cols), spec(turned)),
        compiler_params=params(),
        cost_estimate=cost(2 * span * width * cols, 2 * width * (span + cols) + 6 * span * cols),
        name=name,
    )(normed, *mats, cos, sin, gain)


def unit_of(value):
    inverse = lax.rsqrt(jnp.mean(value * value, axis=-1, keepdims=True) + EPSILON)
    return value * inverse, inverse


def turn(value, cos_ref, sin_ref, sign):
    half = value.shape[-1] // 2
    return value * cos_ref[...] + sign * pltpu.roll(value, half, 1) * sin_ref[...]


def attend_kernel(group, head_dim, turns, first, scalars, q_ref, gate_ref, spot_ref, key_ref, oo_ref, of_ref, *refs):
    blocks = len(turns)
    kv_refs = refs[:blocks]
    rest = refs[blocks:] if first else refs[blocks + 1 :]
    mixed_out, sum_out, gated_out, part_out, acc_ref, total_ref, out_acc = rest
    scale = head_dim**-0.5 * math.log2(math.e)
    own = scalars[0]
    step, mid = pl.program_id(0), out_acc.shape[1] // 2

    @pl.when(step == 0)
    def _():
        out_acc[...] = jnp.zeros_like(out_acc)

    for h in range(group):
        cols = slice(h * head_dim, (h + 1) * head_dim)
        query = q_ref[:, cols]

        def scores(ref):
            return lax.dot_general(query, ref[:, :head_dim], CONTRACT_COLS, preferred_element_type=F32)

        allowed = (key_ref[...] <= spot_ref[...]) & (key_ref[...] < scalars[1])
        terms = jnp.where(allowed, jnp.exp2(scores(kv_refs[0]) * scale), 0.0)
        total_ref[...] = jnp.sum(terms, axis=-1, keepdims=True)
        acc_ref[...] = project(terms.astype(BF16), kv_refs[0][:, head_dim:])
        for place in range(1, blocks):

            @pl.when((own ^ turns[place]) < own)
            def _(ref=kv_refs[place]):
                terms = jnp.exp2(scores(ref) * scale)
                total_ref[...] += jnp.sum(terms, axis=-1, keepdims=True)
                acc_ref[...] += project(terms.astype(BF16), ref[:, head_dim:])

        mixed = acc_ref[...] / total_ref[...]
        mixed_out[:, cols] = mixed
        gated_out[:, cols] = (mixed * sigmoid(gate_ref[:, cols])).astype(BF16)
        sum_out[:, cols] = jnp.broadcast_to(total_ref[...], mixed.shape)
    gated = gated_out[...]
    out_acc[:, :mid] += col_contract(gated, oo_ref[...])
    out_acc[:, mid:] += col_contract(gated, of_ref[...])

    @pl.when(step == pl.num_programs(0) - 1)
    def _():
        part_out[...] = out_acc[...].astype(BF16)


def attend(scalars, part, parts, group, head_dim, turns, query, proj, gate_at, spots, keys, mats, out_at, kvs, old):
    span, width = query.shape
    rows, wide, mid = span // parts, group * head_dim, mats[0].shape[0]
    head = pl.BlockSpec((rows, wide), lambda g, s: (part, g))
    out = pl.BlockSpec((rows, wide), lambda g, s: (0, g))
    mat = pl.BlockSpec((mid, wide), lambda g, s: (0, out_at // wide + g))
    first = old is None
    olds = () if first else (old,)
    return pl.pallas_call(
        functools.partial(attend_kernel, group, head_dim, turns, first),
        out_shape=(
            jax.ShapeDtypeStruct((rows, width), F32),
            jax.ShapeDtypeStruct((rows, width), F32),
            jax.ShapeDtypeStruct((span, width), BF16),
            jax.ShapeDtypeStruct((rows, 2 * mid), BF16),
        ),
        grid_spec=pltpu.PrefetchScalarGridSpec(
            num_scalar_prefetch=1,
            grid=(width // wide,),
            in_specs=[
                head,
                pl.BlockSpec((rows, wide), lambda g, s: (part, gate_at // wide + g)),
                pl.BlockSpec((rows, 1), lambda g, s: (part, 0)),
                pl.BlockSpec((1, span), lambda g, s: (0, 0)),
                mat,
                mat,
            ]
            + [pl.BlockSpec((span, 2 * head_dim), lambda g, s: (0, g))] * len(kvs)
            + [pl.BlockSpec(memory_space=pl.ANY)] * len(olds),
            out_specs=(out, out, head, pl.BlockSpec((rows, 2 * mid), lambda g, s: (0, 0))),
            scratch_shapes=[
                pltpu.VMEM((rows, head_dim), F32),
                pltpu.VMEM((rows, 1), F32),
                pltpu.VMEM((rows, 2 * mid), F32),
            ],
        ),
        input_output_aliases={7 + len(kvs): 2} if olds else {},
        compiler_params=params(),
        cost_estimate=cost(
            4 * rows * width * span * len(kvs) + 4 * rows * width * mid,
            4 * span * width * len(kvs) + 20 * rows * width + 4 * mid * width,
            rows * span * len(kvs) * width // head_dim,
        ),
        name="attend",
    )(scalars, query, proj, spots, keys, *mats, *kvs, *olds)


def attend_back_kernel(group, head_dim, turns, first, count, scalars, *refs):
    blocks = len(turns)
    q_ref, query_ref, gate_ref, mixed_ref, sum_ref, a_ref, b_ref, oo_ref, of_ref = refs[:9]
    spot_ref, key_ref, cos_ref, sin_ref, gain_ref = refs[9:14]
    kv_refs = refs[14 : 14 + blocks]
    rest = refs[14 + blocks :]
    old_refs = () if first else rest[:blocks]
    rest = rest if first else rest[blocks + 3 :]
    gq_out, ggate_out, rows_out, gain_out = rest[:4]
    new_refs = rest[4 : 4 + blocks]
    gq_ref, x_ref = rest[4 + blocks :]
    mid = x_ref.shape[1] // 2

    @pl.when(pl.program_id(0) == 0)
    def _():
        piece = a_ref.shape[0]
        x_ref[:piece, :] = a_ref[...]
        x_ref[piece:, :] = b_ref[...]
        size = x_ref.shape[1] // count
        for p in range(count):
            rows_out[:, column_place(scalars, 2, p, size)] = x_ref[:, p * size : (p + 1) * size]

    all_gated = project(x_ref[:, :mid], oo_ref[...]) + project(x_ref[:, mid:], of_ref[...])
    score_scale = head_dim**-0.5
    scale = score_scale * math.log2(math.e)
    own = scalars[0]
    rows = q_ref.shape[0]

    def as_row(column):
        return jnp.transpose(jnp.broadcast_to(column, (rows, head_dim)))[:1, :]

    for place in range(blocks):
        if first:
            new_refs[place][...] = jnp.zeros_like(new_refs[place])
        else:
            new_refs[place][...] = old_refs[place][...]
    gain_total = jnp.zeros((1, head_dim), F32)
    for h in range(group):
        cols = slice(h * head_dim, (h + 1) * head_dim)
        query = q_ref[:, cols]
        gate = sigmoid(gate_ref[:, cols])
        grad_gated, mixed = all_gated[:, cols], mixed_ref[:, cols]
        grad_mixed = (grad_gated * gate).astype(BF16)
        ggate_out[:, cols] = (grad_gated * mixed * gate * (1.0 - gate)).astype(BF16)
        row_dot = as_row(jnp.sum(grad_mixed.astype(F32) * mixed, axis=-1, keepdims=True))
        row_log = as_row(jnp.log2(sum_ref[:, cols][:, :1]))
        gq_ref[...] = jnp.zeros_like(gq_ref)

        def block(kv_ref, new_ref, masked):
            key, value = kv_ref[:, :head_dim], kv_ref[:, head_dim:]
            scores = lax.dot_general(key, query, CONTRACT_COLS, preferred_element_type=F32)
            probs = jnp.exp2(scores * scale - row_log)
            if masked:
                allowed = (key_ref[...] <= spot_ref[...]) & (key_ref[...] < scalars[1])
                probs = jnp.where(allowed, probs, 0.0)
            grad_probs = lax.dot_general(value, grad_mixed, CONTRACT_COLS, preferred_element_type=F32)
            grad_scores = (probs * (grad_probs - row_dot)).astype(BF16)
            new_ref[:, head_dim:] += project(probs.astype(BF16), grad_mixed)
            new_ref[:, :head_dim] += project(grad_scores, query)
            gq_ref[...] += lax.dot_general(grad_scores, key, CONTRACT_ROWS, preferred_element_type=F32)

        block(kv_refs[0], new_refs[0], True)
        for place in range(1, blocks):

            @pl.when((own ^ turns[place]) < own)
            def _(place=place):
                block(kv_refs[place], new_refs[place], False)

        unit, inverse = unit_of(query_ref[:, cols])
        back = turn(gq_ref[...] * score_scale, cos_ref, sin_ref, -1.0)
        gain_total = gain_total + jnp.sum(back * unit, axis=0, keepdims=True)
        scaled = back * gain_ref[...]
        gq_out[:, cols] = (
            inverse * (scaled - unit * jnp.mean(scaled * unit, axis=-1, keepdims=True))
        ).astype(BF16)
    gain_out[...] = jnp.broadcast_to(gain_total, gain_out.shape)


def attend_back(
    scalars, count, part, parts, group, head_dim, turns, query, proj, gate_at, mixed, sums, pieces, mats, out_at, spots, keys, cos, sin, gain, kvs, olds
):
    span, width = query.shape
    rows, wide = span // parts, group * head_dim
    blocks, mid = len(kvs), mats[0].shape[0]
    mine = pl.BlockSpec((rows, wide), lambda g, s: (part, g))
    local = pl.BlockSpec((rows, wide), lambda g, s: (0, g))
    table = pl.BlockSpec((rows, head_dim), lambda g, s: (part, 0))
    pair = pl.BlockSpec((span, 2 * head_dim), lambda g, s: (0, g))
    piece = pl.BlockSpec(pieces[0].shape, lambda g, s: (0, 0))
    mat = pl.BlockSpec((mid, wide), lambda g, s: (0, out_at // wide + g))
    first = olds is None
    olds = () if first else tuple(olds)
    kv_shape = jax.ShapeDtypeStruct(kvs[0].shape, F32)
    steps = width // wide
    before = 15 + blocks
    out = pl.pallas_call(
        functools.partial(attend_back_kernel, group, head_dim, turns, first, count),
        out_shape=(
            jax.ShapeDtypeStruct((span, width), BF16),
            jax.ShapeDtypeStruct((span, width), BF16),
            jax.ShapeDtypeStruct((span, 2 * mid), BF16),
            jax.ShapeDtypeStruct((8 * steps, head_dim), F32),
        )
        + (kv_shape,) * blocks,
        grid_spec=pltpu.PrefetchScalarGridSpec(
            num_scalar_prefetch=1,
            grid=(steps,),
            in_specs=[
                mine,
                mine,
                pl.BlockSpec((rows, wide), lambda g, s: (part, gate_at // wide + g)),
                local,
                local,
                piece,
                piece,
                mat,
                mat,
                pl.BlockSpec((1, rows), lambda g, s: (0, part)),
                pl.BlockSpec((span, 1), lambda g, s: (0, 0)),
                table,
                table,
                pl.BlockSpec((1, head_dim), lambda g, s: (0, 0)),
            ]
            + [pair] * (blocks + min(len(olds), blocks))
            + [pl.BlockSpec(memory_space=pl.ANY)] * max(len(olds) - blocks, 0),
            out_specs=(
                mine,
                mine,
                pl.BlockSpec((rows, 2 * mid), lambda g, s: (part, 0)),
                pl.BlockSpec((8, head_dim), lambda g, s: (g, 0)),
            )
            + (pair,) * blocks,
            scratch_shapes=[pltpu.VMEM((rows, head_dim), F32), pltpu.VMEM((rows, 2 * mid), BF16)],
        ),
        input_output_aliases={}
        if first
        else {**{before + i: 4 + i for i in range(blocks)}, **{before + blocks + i: i for i in range(3)}},
        compiler_params=params(),
        cost_estimate=cost(
            10 * rows * width * span * blocks + 4 * rows * width * mid,
            20 * span * width * blocks,
            rows * span * blocks * width // head_dim,
        ),
        name="attend_back",
    )(scalars, query, proj, proj, mixed, sums, *pieces, *mats, spots, keys, cos, sin, gain, *kvs, *olds)
    gain_part = sum(out[3][8 * g] for g in range(steps))
    return out[4:], out[:3], gain_part


def keys_back_kernel(kv_heads, head_dim, g_ref, p_ref, cos_ref, sin_ref, gain_ref, k_out, v_out, gain_out):
    gain_total = jnp.zeros((1, head_dim), F32)
    for h in range(kv_heads):
        cols = slice(h * head_dim, (h + 1) * head_dim)
        unit, inverse = unit_of(p_ref[:, cols])
        grad = g_ref[:, 2 * h * head_dim : (2 * h + 1) * head_dim] * head_dim**-0.5
        back = turn(grad, cos_ref, sin_ref, -1.0)
        gain_total = gain_total + jnp.sum(back * unit, axis=0, keepdims=True)
        scaled = back * gain_ref[...]
        k_out[:, cols] = (
            inverse * (scaled - unit * jnp.mean(scaled * unit, axis=-1, keepdims=True))
        ).astype(BF16)
        v_out[:, cols] = g_ref[:, (2 * h + 1) * head_dim : (2 * h + 2) * head_dim].astype(BF16)
    gain_out[...] = jnp.broadcast_to(gain_total, gain_out.shape)


def keys_back(kv_heads, head_dim, grad_kv, proj, key_at, cos, sin, gain):
    span = proj.shape[0]
    cols = kv_heads * head_dim
    key_block = key_at // cols
    whole = lambda a, b: pl.BlockSpec((a, b), lambda i: (0, 0))
    out = pl.pallas_call(
        functools.partial(keys_back_kernel, kv_heads, head_dim),
        out_shape=(
            jax.ShapeDtypeStruct((span, cols), BF16),
            jax.ShapeDtypeStruct((span, cols), BF16),
            jax.ShapeDtypeStruct((8, head_dim), F32),
        ),
        grid=(1,),
        in_specs=[
            whole(span, 2 * cols),
            pl.BlockSpec((span, cols), lambda i: (0, key_block)),
            whole(span, head_dim),
            whole(span, head_dim),
            whole(1, head_dim),
        ],
        out_specs=(whole(span, cols), whole(span, cols), whole(8, head_dim)),
        compiler_params=params(),
        cost_estimate=cost(40 * span * cols, 16 * span * cols),
        name="keys_back",
    )(grad_kv, proj, cos, sin, gain)
    return out[0], out[1], out[2][0]


def norm_back(gradient, unit_vals, inverse, gain_vec):
    scaled = gradient * gain_vec
    return inverse * (scaled - unit_vals * jnp.mean(scaled * unit_vals, axis=-1, keepdims=True))


def per_device(
    links,
    hidden_in,
    lengths,
    attn_gain,
    q_weight,
    gate_weight,
    k_weight,
    v_weight,
    q_gain,
    k_gain,
    o_weight,
    mlp_gain,
    w_gate,
    w_up,
    w_down,
    out_grad,
):
    dp_index, ctx_index, z_index = (lax.axis_index(a) for a in ("dp", "ctx", "tensor"))
    q_cols, k_cols, ff_cols = q_weight.shape[1], k_weight.shape[1], w_down.shape[1]
    span, width = hidden_in.shape
    mid, count = width // 2, 2 * links.half
    shard, head_shard = attn_gain.shape[0], q_gain.shape[0]
    head_dim = head_shard * count
    heads, kv_heads = q_cols // head_dim, k_cols // head_dim
    group = heads // kv_heads
    length = lengths[0]
    low = lambda *mats: jnp.concatenate([m.astype(BF16) for m in mats], axis=1)

    small = jnp.concatenate([attn_gain, mlp_gain, q_gain, k_gain]).astype(BF16)[None, :]
    gains, seen = links.small_gather(small)
    everywhere = lambda block: {p: block for p in range(len(links.bits))}
    paired = lambda half: (half, links.swap(half, "ctx", 1))
    plane = ("dp", "ctx")
    first_own = after(low(q_weight, gate_weight, k_weight, v_weight, o_weight), *seen)
    first_single = links.send_own(everywhere(first_own))
    attn_scale = gains[:, :shard].reshape(1, width).astype(F32)
    mlp_scale = gains[:, shard : 2 * shard].reshape(1, width).astype(F32)
    owners = jnp.stack([links.owner_of(p, dp_index, ctx_index) for p in range(count)]).astype(jnp.int32)
    pick = (owners[None, :] == jnp.arange(count)[:, None]).astype(BF16)
    mesh_gains = project(pick, gains)
    mesh_scale = mesh_gains[:, :shard].reshape(1, width)
    query_scale = mesh_gains[:, 2 * shard : 2 * shard + head_shard].reshape(1, head_dim)
    key_scale = mesh_gains[:, 2 * shard + head_shard :].reshape(1, head_dim)

    parts = 2 * links.tensor
    row_block = span // parts
    row_places = jnp.stack(
        [part * links.tensor + (z_index ^ j) for part in range(2) for j in links.turns]
    ).astype(jnp.int32)
    start = ctx_index * span
    scalars = jnp.concatenate(
        [row_places, owners.astype(jnp.int32), jnp.stack([start, length]).astype(jnp.int32)]
    )
    spots = (start + row_places[:, None] * row_block + jnp.arange(row_block)[None, :]).reshape(span)
    spots = spots.astype(jnp.int32)
    freq_steps = jnp.arange(head_dim // 2, dtype=F32) * (2.0 / head_dim)
    turned = spots.astype(F32)[:, None] * jnp.exp(-math.log(ROPE_BASE) * freq_steps)[None, :]
    cosine, sine = jnp.cos(turned), jnp.sin(turned)
    cos = jnp.concatenate([cosine, cosine], axis=1)
    sin = jnp.concatenate([-sine, sine], axis=1)
    spot_col, spot_row = spots[:, None], spots[None, :]

    stream, grad_out, plain_down, down_grad, plain_normed, normed = enter(
        scalars, count, parts, span, hidden_in, out_grad, after(mesh_scale, first_own)
    )
    feed_low, down_low = low(w_gate, w_up), low(w_down)
    first_single = {q: after(b, normed, feed_low, down_low) for q, b in first_single.items()}
    feed_mat = lax.all_gather(after(feed_low, normed), plane, axis=0, tiled=True)

    first_pairs = links.send_on(first_single)
    first_seen = [b for pair in first_pairs.values() for b in pair]
    down_mat = lax.all_gather(after(down_low, *first_seen), plane, axis=0, tiled=True)
    first_mat = paired(links.assemble(first_own, first_single, first_pairs))
    gate_at, key_at = q_cols, 2 * q_cols
    value_at, out_at = key_at + k_cols, key_at + 2 * k_cols
    kv_proj, kv = enter_heads(
        "enter_keys", kv_heads, head_dim, True, normed, first_mat, key_at, 2 * k_cols, cos, sin, key_scale
    )
    proj, query = enter_heads(
        "enter_queries", heads, head_dim, False, after(normed, kv), first_mat, 0, 2 * q_cols, cos, sin, query_scale
    )
    kvs, turns = [kv], [0]
    mask = links.ctx // 2
    while mask:
        kvs = kvs + [links.swap(b if i == 0 else after(b, query), "ctx", mask) for i, b in enumerate(kvs)]
        turns = turns + [p ^ mask for p in turns]
        mask //= 2
    at = jnp.concatenate([jnp.stack([ctx_index, length]).astype(jnp.int32), owners])
    half_rows = span // 2
    shard_rows = half_rows // links.tensor
    part_of = lambda value, t: value[t * half_rows : (t + 1) * half_rows]
    own_rows = lambda value, t: value[t * shard_rows : (t + 1) * shard_rows]
    live = [(part_of(spot_col, t)[:shard_rows] < length).astype(F32) for t in range(2)]
    mixed, sums, out_part, one = ([None] * 2 for _ in range(4))
    query_now, gated_all = query, None
    for t in range(2):
        mixed[t], sums[t], gated_all, out_part[t] = attend(
            at, t, 2, group, head_dim, turns, query_now, proj, gate_at, spot_col, spot_row, first_mat, out_at, kvs, gated_all
        )
        one[t] = links.scatter_first(out_part[t])
    middle, normed_two, unit_two, inverse_two, two = ([None] * 2 for _ in range(5))
    late = (one[1][1],)
    for t in range(2):
        attn_out, _ = links.scatter_rest(*one[t], late=late)
        middle[t] = own_rows(stream, t).astype(F32) + attn_out * live[t]
        inverse_two[t] = lax.rsqrt(jnp.mean(middle[t] * middle[t], axis=-1, keepdims=True) + EPSILON)
        unit_two[t] = middle[t] * inverse_two[t]
        normed_two[t] = (unit_two[t] * mlp_scale).astype(BF16)
        two[t] = links.gather_first(normed_two[t])
        late = (normed_two[t],)
    pieces_two = [links.gather_rest(*two[0], late=late)]
    pieces_two.append(links.gather_rest(*two[1], late=(pieces_two[0][0],)))

    grad_hidden = project(after(plain_down, one[1][1]), down_mat)
    back_part, three = [None] * 2, [None] * 2
    held = None
    for t in range(2):
        held, back_part[t] = feed(scalars, count, parts, t, pieces_two[t], feed_mat, grad_hidden, held)
        three[t] = links.scatter_first(back_part[t])
    hidden_all, grad_gate_all, grad_up_all, rows_two = held

    halves = lambda value: (value[:, : value.shape[1] // 2], value[:, value.shape[1] // 2 :])

    def grad_others(rows_of, cols, *before):
        left = after(rows_of[:, mid:], *before)
        parts = [row_contract(left, c).astype(BF16) for c in cols]
        return parts, [links.swap(p, "ctx", 1) for p in parts]

    def grad_totals(rows_of, cols, arrived, *before):
        left = after(rows_of[:, :mid], *before)
        return [(row_contract(left, c) + a.astype(F32)).astype(BF16) for c, a in zip(cols, arrived)]

    def grad_rest(firsts, *before):
        return [
            links.reduce_rest(kept, after(came, *before), turn) for turn, (kept, _, came) in enumerate(firsts)
        ]

    scaled_back = lambda back, t: own_rows(grad_out, t).astype(F32) + norm_back(
        back, unit_two[t], inverse_two[t], mlp_scale
    )
    grad_middle, attn_grad, four = ([None] * 2 for _ in range(3))
    back_a, seen_a = links.scatter_rest(*three[0], before=(hidden_all,))
    back_b, seen_b = links.scatter_rest(*three[1])
    feed_cols = [grad_gate_all, grad_up_all]
    over_plane = lambda part: lax.psum_scatter(part, plane, scatter_dimension=0, tiled=True).astype(F32)
    down_grad_part = row_contract(after(plain_down, three[0][1]), hidden_all).astype(BF16)
    grad_down = over_plane(down_grad_part)
    feed_others, feed_came = grad_others(rows_two, feed_cols, down_grad_part)
    homes = jnp.stack([(z_index ^ j) * 2 + part for part in range(2) for j in links.turns]).astype(jnp.int32)
    down_part = descend(homes, owners, after(hidden_all, *feed_others, three[1][1]), down_mat)
    for t, back in enumerate((back_a, back_b)):
        back = after(back, *((down_part,) if t == 0 else (attn_grad[0],)))
        grad_middle[t] = scaled_back(back, t)
        attn_grad[t] = (grad_middle[t] * live[t]).astype(BF16)
        four[t] = links.gather_first(attn_grad[t])
    grad_mlp_gain = sum(jnp.sum(b * unit_two[t], axis=0) for t, b in enumerate((back_a, back_b)))
    attn_shard = attn_grad[1]
    pieces_four = [links.gather_rest(*four[0], late=(attn_shard,))]
    pieces_four.append(links.gather_rest(*four[1]))
    down_sum = lax.psum_scatter(after(down_part, grad_down, pieces_four[0][1], pieces_four[1][0]), "tensor", scatter_dimension=0, tiled=True).astype(F32)
    backward = lambda t, pieces, olds: attend_back(
        at, count, t, 2, group, head_dim, turns, query, proj, gate_at, mixed[t], sums[t], pieces, first_mat, out_at,
        spot_row, spot_col, cos, sin, query_scale, kvs, olds,
    )
    feed_totals = grad_totals(rows_two, feed_cols, feed_came, pieces_four[0][1])
    ready = after(pieces_four[0][1], pieces_four[1][0], grad_down, *feed_totals)
    grad_kvs, held, gain_a = backward(0, (pieces_four[0][0], ready), None)
    back_places = jnp.array(
        [part * links.tensor + o for o in range(links.tensor) for part in range(2)], dtype=jnp.int32
    )
    last = pieces_four[1]
    grad_kvs, held, gain_b = backward(1, last, (*grad_kvs, *held))
    grad_query, grad_gates, attn_all = held
    down_sum = after(down_sum, grad_kvs[0])
    down_shard = jnp.concatenate(middle, axis=0) + down_sum * jnp.concatenate(live, axis=0)
    down_all = lax.all_gather(down_shard.astype(BF16), "tensor", axis=0, tiled=True)
    if width // count % 128:
        attn_all = columns(attn_all, jnp.argsort(owners))
    q_gain_part = gain_a + gain_b
    pieces = dict(zip(turns, grad_kvs))
    mask = 1
    kv_gone, kv_seen = [], []
    while len(pieces) > 1:
        near = [p for p in pieces if not p & mask]
        gone = [pieces[p ^ mask].astype(BF16) for p in near]
        came = links.swap(jnp.concatenate(gone, axis=0), "ctx", mask)
        kv_gone.append(gone)
        kv_seen.append(came)
        pieces = {
            p: pieces[p].astype(F32) + came[i * span : (i + 1) * span].astype(F32) for i, p in enumerate(near)
        }
        mask *= 2
    outer_part = plane_grads(
        "outer_grads", [(after(plain_normed, *kv_gone[-1]), (grad_query, grad_gates)), (attn_all, (gated_all,))],
        3 * q_cols + 2 * k_cols,
    )
    grad_key, grad_value, k_gain_part = keys_back(
        kv_heads, head_dim, after(pieces[0], outer_part, down_shard), kv_proj, 0, cos, sin, key_scale
    )
    feed_first = [links.reduce_first(x, turn, *((grad_key,) if turn else ())) for turn, x in enumerate(feed_totals)]
    seven, eight, in_part, grad_in, attn_gain_part = ([None] * 2 for _ in range(5))
    late_query = grad_query
    for t in range(2):
        terms = [
            (late_query, first_mat, 0),
            (grad_gates, first_mat, gate_at),
            (grad_key, first_mat, key_at),
            (grad_value, first_mat, value_at),
        ]
        in_part[t], gain = spread("spread_in", terms, t, 2, normed=normed)
        attn_gain_part[t] = gain[0] / attn_scale[0]
        seven[t] = links.scatter_first(in_part[t] if t == 0 else after(in_part[1], seven[0][1]))
    inner_part = plane_grads(
        "inner_grads", [(after(plain_normed, attn_gain_part[1]), (grad_key, grad_value))], 3 * q_cols + 2 * k_cols, outer_part
    )
    inner_sum = over_plane(inner_part)
    summed = [links.scatter_rest(*seven[t]) for t in range(2)]
    late = ()
    for t in range(2):
        back = after(summed[t][0], *late)
        x = own_rows(stream, t).astype(F32)
        inverse = lax.rsqrt(jnp.mean(x * x, axis=-1, keepdims=True) + EPSILON)
        unit = x * inverse
        grad_in[t] = (grad_middle[t] + norm_back(back, unit, inverse, attn_scale)).astype(BF16)
        eight[t] = links.gather_first(grad_in[t])
        late = (grad_in[t],)
    feed_rest = grad_rest(feed_first, grad_in[0])
    hidden_out = leave(jnp.concatenate([back_places, scalars[parts:]]), count, parts, [after(down_all, in_part[1])], BF16)
    in_pieces = [*links.gather_rest(*eight[0], late=late)]
    in_pieces += links.gather_rest(*eight[1], late=(in_pieces[0],))
    attn_gain_part = sum(attn_gain_part)
    arrived_one = in_pieces[1]
    in_pieces[1] = after(in_pieces[1], hidden_out, *(r[0] for r in feed_rest))
    grad_in = leave(scalars, count, parts, in_pieces, F32)

    blocks = jnp.stack([attn_gain_part.reshape(count, shard), grad_mlp_gain.reshape(count, shard)])
    to_mesh = (owners[None, :] == jnp.arange(count)[:, None]).astype(F32)
    blocks = jnp.einsum("ap,kpn->kan", to_mesh, blocks, precision=lax.Precision.HIGHEST)
    packed = jnp.concatenate([blocks.reshape(1, -1), q_gain_part[None, :], k_gain_part[None, :]], axis=1)
    packed = links.add_all(packed, in_pieces[3], arrived_one, hidden_out, *(r[2] for r in feed_rest))[0]
    rank = dp_index * links.ctx + ctx_index
    take = lambda at, size: lax.dynamic_slice_in_dim(packed, at + rank * size, size)
    return (
        hidden_out,
        grad_in,
        take(0, shard),
        inner_sum[:, :q_cols],
        inner_sum[:, q_cols : 2 * q_cols],
        inner_sum[:, 3 * q_cols : 3 * q_cols + k_cols],
        inner_sum[:, 3 * q_cols + k_cols :],
        take(2 * width, head_shard),
        take(2 * width + head_dim, head_shard),
        inner_sum[:, 2 * q_cols : 3 * q_cols],
        take(width, shard),
        feed_rest[0][0],
        feed_rest[1][0],
        grad_down,
    )


def solution(mesh):
    links = Links(dict(mesh.shape))
    rows = P(("dp", "ctx"))
    plain = P(("dp", "ctx"), None)
    split = P(("dp", "ctx"), "tensor")

    def step(*arrays):
        return per_device(links, *arrays)

    return jax.shard_map(
        step,
        mesh=mesh,
        in_specs=(plain, P("dp"), rows, split, split, split, split, rows, rows, split, rows, split, split, split, plain),
        out_specs=(plain, plain, rows, split, split, split, split, rows, rows, split, rows, split, split, split),
        check_vma=False,
    )
```

```python
import functools
import math

import jax
import jax.numpy as jnp
from jax import lax
from jax.experimental import pallas as pl
from jax.experimental.pallas import tpu as pltpu
from jax.sharding import PartitionSpec as P

EPSILON = 1e-06
ROPE_BASE = 1000000.0
CONTRACT_ROWS = (((0,), (0,)), ((), ()))
CONTRACT_COLS = (((1,), (1,)), ((), ()))
F32 = jnp.float32
BF16 = jnp.bfloat16
VMEM_BYTES = 56 * 1024 * 1024


def project(operand, matrix):
    return jnp.dot(operand, matrix, preferred_element_type=F32)


def row_contract(first_op, second_op):
    return lax.dot_general(first_op, second_op, CONTRACT_ROWS, preferred_element_type=F32)


def col_contract(first_op, second_op):
    return lax.dot_general(first_op, second_op, CONTRACT_COLS, preferred_element_type=F32)


def sigmoid(value):
    return 1.0 / (1.0 + jnp.exp(-value))


def after(value, *others):
    if not others:
        return value
    return lax.optimization_barrier((value,) + others)[0]


def cost(flops, moved, exps=0):
    return pl.CostEstimate(flops=int(flops), bytes_accessed=int(moved), transcendentals=int(exps))


def params(**kwargs):
    return pltpu.CompilerParams(vmem_limit_bytes=VMEM_BYTES, **kwargs)


class Links:
    def __init__(self, sizes):
        self.dp, self.ctx, self.tensor = sizes["dp"], sizes["ctx"], sizes["tensor"]
        self.half = self.dp * self.ctx // 2
        ctx_bits = int(math.log2(self.ctx // 2))
        dp_bits = int(math.log2(self.dp))
        self.bits = [("ctx", 2 << i) for i in range(ctx_bits)] + [("dp", 1 << i) for i in range(dp_bits)]
        self.masks = [(2 << i) - 1 for i in range(int(math.log2(self.tensor)))]
        self.turns = [0]
        for mask in reversed(self.masks):
            self.turns = self.turns + [j ^ mask for j in self.turns]

    def swap(self, value, axis, mask):
        count = {"dp": self.dp, "ctx": self.ctx, "tensor": self.tensor}[axis]
        return lax.ppermute(value, axis, [(i, i ^ mask) for i in range(count)])

    def order(self, turn):
        places = list(range(len(self.bits)))
        return places if turn else places[::-1]

    def send_own(self, blocks):
        return {1 << p: self.swap(blocks[p], *self.bits[p]) for p in self.order(0)}

    def send_far(self, block):
        count = self.dp * self.ctx
        single = {}
        for q in range(1, self.half):
            far = (q // (self.ctx // 2)) * self.ctx + (q % (self.ctx // 2)) * 2
            single[q] = lax.ppermute(block, ("dp", "ctx"), [(i, i ^ far) for i in range(count)])
        return single

    def send_on(self, single):
        mid = next(iter(single.values())).shape[1] // 2
        left = {q: b[:, :mid] for q, b in single.items()}
        right = {q: b[:, mid:] for q, b in single.items()}
        for side, places in ((left, self.order(0)), (right, self.order(1))):
            for q in range(1, self.half):
                if q not in single:
                    self.reach(side, q, places)
        return {q: (left[q], right[q]) for q in left if q not in single}

    def assemble(self, block, single, pairs):
        blocks, groups = [], []
        for q in range(self.half):
            members = [block] if q == 0 else [single[q]] if q in single else list(pairs[q])
            groups.append(tuple(range(len(blocks), len(blocks) + len(members))))
            blocks += members
        return stack_blocks(groups, blocks)

    def reach(self, side, q, places):
        if q not in side:
            last = [p for p in places if q & (1 << p)][-1]
            self.reach(side, q ^ (1 << last), places)
            side[q] = self.swap(side[q ^ (1 << last)], *self.bits[last])

    def reduce_first(self, total, turn, *hold):
        rows = total.shape[0] // self.half
        pieces = {q: total[q * rows : (q + 1) * rows] for q in range(self.half)}
        return self.reduce_step(pieces, turn, 0, *hold)

    def reduce_step(self, pieces, turn, step, *hold):
        place = self.order(turn)[step]
        bit = 1 << place
        kept = {q: b for q, b in pieces.items() if not q & bit}
        gone = [pieces[q | bit].astype(BF16) for q in kept]
        sent = after(jnp.concatenate(gone, axis=0), *hold)
        return kept, [sent], self.swap(sent, *self.bits[place])

    def reduce_rest(self, kept, came, turn):
        gone = []
        for step in range(1, len(self.bits) + 1):
            rows = came.shape[0] // len(kept)
            pieces = {
                q: b.astype(F32) + came[i * rows : (i + 1) * rows].astype(F32) for i, (q, b) in enumerate(kept.items())
            }
            if step < len(self.bits):
                kept, sent, came = self.reduce_step(pieces, turn, step)
                gone += sent
        return pieces[0], gone, came

    def small_gather(self, row):
        far = self.send_far(row)
        own = jnp.concatenate([row] + [far[q] for q in range(1, self.half)], axis=0)
        return jnp.concatenate([own, self.swap(own, "ctx", 1)], axis=0), list(far.values())

    def owner_of(self, position, dp_index, ctx_index):
        h, q = position // self.half, position % self.half
        dp_far, ctx_far = q // (self.ctx // 2), (q % (self.ctx // 2)) * 2 + h
        return (dp_index ^ dp_far) * self.ctx + (ctx_index ^ ctx_far)

    def scatter_first(self, part):
        rows = part.shape[0] // 2
        return part[:rows], self.swap(part[rows:], "tensor", self.masks[0])

    def scatter_rest(self, kept, came, before=(), late=()):
        gone = seen = came
        kept = kept.astype(F32) + came.astype(F32)
        for mask in self.masks[1:]:
            rows = kept.shape[0] // 2
            gone = kept[rows:].astype(BF16)
            seen = self.swap(after(gone, *before), "tensor", mask)
            kept = kept[:rows] + after(seen, *late).astype(F32)
        return kept, seen

    def gather_first(self, shard):
        return shard, self.swap(shard, "tensor", self.masks[-1])

    def gather_rest(self, shard, came, late=()):
        came = after(came, *late)
        for mask in self.masks[-2::-1]:
            shard = jnp.concatenate([shard, came], axis=0)
            came = self.swap(shard, "tensor", mask)
        return shard, came

    def add_all(self, value, *before):
        value = after(value, *before)
        value = value + self.swap(value, "ctx", 1)
        value = value + sum(self.send_far(value).values())
        return value + sum(self.swap(value, "tensor", mask) for mask in range(1, self.tensor))


def still(scalars, count, parts):
    owners = scalars[parts : parts + count]
    return owners, lax.dynamic_update_slice(scalars, jnp.arange(count, dtype=scalars.dtype), (parts,))


def columns(value, owners):
    count = owners.shape[0]
    blocks = value.reshape(value.shape[0], count, value.shape[1] // count)
    return jnp.take(blocks, owners, axis=1).reshape(value.shape)


def column_place(scalars, parts, p, size):
    if size % 128:
        return pl.ds(p * size, size)
    return pl.ds(pl.multiple_of(scalars[parts + p] * size, size), size)


def stack_kernel(groups, *refs):
    out_ref = refs[-1]
    for q, group in enumerate(groups):

        @pl.when(pl.program_id(0) == q)
        def _(group=group):
            col = 0
            for i in group:
                out_ref[:, col : col + refs[i].shape[1]] = refs[i][...]
                col += refs[i].shape[1]


def stack_blocks(groups, blocks):
    rows, n = blocks[0].shape
    held = lambda b: pl.BlockSpec(b.shape, lambda i: (0, 0), pipeline_mode=pl.Buffered(1))
    return pl.pallas_call(
        functools.partial(stack_kernel, groups),
        out_shape=jax.ShapeDtypeStruct((rows * len(groups), n), blocks[0].dtype),
        grid=(len(groups),),
        in_specs=[held(b) for b in blocks],
        out_specs=pl.BlockSpec((rows, n), lambda i: (i, 0)),
        compiler_params=params(),
        cost_estimate=cost(0, 4 * rows * len(groups) * n),
        name="stack",
    )(*blocks)


def enter_kernel(
    count, parts, scalars, xa_ref, xb_ref, ga_ref, gb_ref, gain_ref, x_out, g_out, m_out, mine_out, plain_out, n_out
):
    step = pl.program_id(0)
    rows, width = xa_ref.shape
    size = width // count
    moved = [column_place(scalars, parts, p, size) for p in range(count)]
    for part, (x_ref, g_ref) in enumerate(((xa_ref, ga_ref), (xb_ref, gb_ref))):
        if part == 0:

            @pl.when(step % (parts // 4) == 0)
            def _(x_ref=x_ref, g_ref=g_ref):
                for p in range(count):
                    x_out[:, p * size : (p + 1) * size] = x_ref[:, moved[p]]
                    g_out[:, p * size : (p + 1) * size] = g_ref[:, moved[p]]

        place = slice(part * rows, (part + 1) * rows)
        spot = scalars[parts + count] + scalars[2 * step + part] * rows
        live = spot + lax.broadcasted_iota(jnp.int32, (rows, 1), 0) < scalars[parts + count + 1]
        m_out[place, :] = jnp.where(live, g_ref[...].astype(F32), 0.0).astype(BF16)
        wide = x_ref[...].astype(F32)
        inverse = lax.rsqrt(jnp.mean(wide * wide, axis=-1, keepdims=True) + EPSILON)
        plain_out[place, :] = (wide * inverse * gain_ref[...]).astype(BF16)
        for p in range(count):
            n_out[place, p * size : (p + 1) * size] = plain_out[place, moved[p]]
            mine_out[place, p * size : (p + 1) * size] = m_out[place, moved[p]]


def enter(scalars, count, parts, span, hidden_in, out_grad, gain):
    rows, width = span // parts, hidden_in.shape[1]
    narrow = width // count % 128
    owners = scalars[parts : parts + count]
    upper = pl.BlockSpec((rows, width), lambda i, s: (s[2 * i], 0))
    lower = pl.BlockSpec((rows, width), lambda i, s: (s[2 * i + 1], 0))
    own = pl.BlockSpec((rows, width), lambda i, s: (i // (parts // 4), 0))
    plain = pl.BlockSpec((2 * rows, width), lambda i, s: (i, 0))
    shape = jax.ShapeDtypeStruct((span, width), BF16)
    short = jax.ShapeDtypeStruct((2 * rows, width), BF16)
    x, g, m, mine, unmoved, normed = pl.pallas_call(
        functools.partial(enter_kernel, count, parts),
        out_shape=(short, short, shape, shape, shape, shape),
        grid_spec=pltpu.PrefetchScalarGridSpec(
            num_scalar_prefetch=1,
            grid=(parts // 2,),
            in_specs=[upper, lower, upper, lower, pl.BlockSpec((1, width), lambda i, s: (0, 0))],
            out_specs=(own, own, plain, plain, plain, plain),
        ),
        compiler_params=params(),
        cost_estimate=cost(10 * span * width, 8 * span * width),
        name="enter",
    )(scalars, hidden_in, hidden_in, out_grad, out_grad, gain)
    if narrow:
        x, g, mine, normed = (columns(v, owners) for v in (x, g, mine, normed))
    return x, g, m, mine, unmoved, normed


def leave_kernel(count, parts, scalars, *refs):
    pieces, out_ref = refs[:4], refs[4]
    blocks, size = parts // 4, out_ref.shape[1] // count
    rows = out_ref.shape[0] // parts
    for i, in_ref in enumerate(pieces):

        @pl.when(pl.program_id(0) == i)
        def _(i=i, in_ref=in_ref):
            for part in range(blocks):
                at = pl.ds(pl.multiple_of(scalars[i * blocks + part] * rows, rows), rows)
                for p in range(count):
                    block = in_ref[part * rows : (part + 1) * rows, p * size : (p + 1) * size]
                    out_ref[at, column_place(scalars, parts, p, size)] = block.astype(out_ref.dtype)


def leave(scalars, count, parts, pieces, dtype):
    rows, width = pieces[0].shape
    place = lambda k: lambda i, s: (0, 0)
    if len(pieces) == 1:
        rows, pieces = rows // 4, pieces * 4
        place = lambda k: lambda i, s: (k, 0)
    if width // count % 128:
        owners, scalars = still(scalars, count, parts)
        pieces = [columns(piece, jnp.argsort(owners)) for piece in pieces]
    return pl.pallas_call(
        functools.partial(leave_kernel, count, parts),
        out_shape=jax.ShapeDtypeStruct((4 * rows, width), dtype),
        grid_spec=pltpu.PrefetchScalarGridSpec(
            num_scalar_prefetch=1,
            grid=(4,),
            in_specs=[pl.BlockSpec((rows, width), place(k)) for k in range(4)],
            out_specs=pl.BlockSpec((4 * rows, width), lambda i, s: (0, 0)),
        ),
        compiler_params=params(),
        cost_estimate=cost(0, 24 * rows * width),
        name="leave",
    )(scalars, *pieces)


def spread_kernel(tiles, count, parts, summed, *refs):
    homes, refs = (refs[0], refs[1:]) if parts else (None, refs)
    values, out_ref = refs[:count], refs[3 * count + summed]
    for h in range(2):

        @pl.when(pl.program_id(0) // tiles == h)
        def _(h=h):
            total = None
            for k in range(count):
                term = lax.dot_general(
                    values[k][...], refs[count + 2 * k + h][...], CONTRACT_COLS, preferred_element_type=F32
                )
                total = term if total is None else total + term
            if summed:
                norm_ref, sum_ref = refs[3 * count], refs[3 * count + 2]
                gain = jnp.sum(total * norm_ref[...].astype(F32), axis=0, keepdims=True)
                sum_ref[...] = jnp.broadcast_to(gain, sum_ref.shape)
            if parts:
                rows = out_ref.shape[0] // parts
                for i in range(parts):
                    at = pl.ds(pl.multiple_of(homes[i] * rows, rows), rows)
                    out_ref[at, :] = total[i * rows : (i + 1) * rows].astype(BF16)
            else:
                out_ref[...] = total.astype(BF16)


def spread(name, terms, part=0, parts=1, homes=None, normed=None):
    rows = terms[0][0].shape[0] // parts
    mid = terms[0][1][0].shape[0]
    tile = mid // 2
    specs, mats = [], []
    for value, pair, start in terms:
        n = value.shape[1]
        specs += [
            pl.BlockSpec((tile, n), lambda j, *s, c=start // n: (jnp.minimum(j, 1), c)),
            pl.BlockSpec((tile, n), lambda j, *s, c=start // n: (jnp.maximum(j - 2, 0), c)),
        ]
        mats += list(pair)
    held = [pl.BlockSpec((rows, v.shape[1]), lambda j, *s: (part, 0)) for v, _, _ in terms]
    wide = sum(v.shape[1] for v, _, _ in terms)
    summed = normed is not None
    shapes = [jax.ShapeDtypeStruct((rows, 2 * mid), BF16)]
    outs = [pl.BlockSpec((rows, tile), lambda j, *s: (0, j))]
    extra = []
    if summed:
        extra = [normed]
        specs.append(pl.BlockSpec((rows, tile), lambda j, *s: (part, j)))
        shapes.append(jax.ShapeDtypeStruct((8, 2 * mid), F32))
        outs.append(pl.BlockSpec((8, tile), lambda j, *s: (0, j)))
    out = pl.pallas_call(
        functools.partial(spread_kernel, 2, len(terms), 0 if homes is None else homes.shape[0], summed),
        out_shape=shapes,
        grid_spec=pltpu.PrefetchScalarGridSpec(
            num_scalar_prefetch=0 if homes is None else 1, grid=(4,), in_specs=held + specs, out_specs=outs
        ),
        compiler_params=params(),
        cost_estimate=cost(4 * rows * mid * wide, 2 * wide * (rows + 2 * mid) + 4 * rows * mid),
        name=name,
    )(*(() if homes is None else (homes,)), *(v for v, _, _ in terms), *mats, *extra)
    return out if summed else out[0]


def feed_kernel(first, count, parts, scalars, a_ref, b_ref, gate_ref, up_ref, gh_ref, *refs):
    refs = refs if first else refs[4:]
    hidden_out, gate_out, up_out, rows_out, part_out, x_ref, acc_ref = refs
    step, size = pl.program_id(0), x_ref.shape[1] // count
    moved = [column_place(scalars, parts, p, size) for p in range(count)]

    @pl.when(step == 0)
    def _():
        rows = a_ref.shape[0]
        rows_out[:rows, :] = a_ref[...]
        rows_out[rows:, :] = b_ref[...]
        for p in range(count):
            x_ref[:rows, moved[p]] = a_ref[:, p * size : (p + 1) * size]
            x_ref[rows:, moved[p]] = b_ref[:, p * size : (p + 1) * size]
        acc_ref[...] = jnp.zeros_like(acc_ref)

    gate = project(x_ref[...], gate_ref[...])
    up = project(x_ref[...], up_ref[...])
    grad = gh_ref[...]
    sig = sigmoid(gate)
    hidden_out[...] = (gate * sig * up).astype(BF16)
    grad_gate = (grad * up * sig * (1.0 + gate * (1.0 - sig))).astype(BF16)
    grad_up = (grad * (gate * sig)).astype(BF16)
    gate_out[...] = grad_gate
    up_out[...] = grad_up
    acc_ref[...] += col_contract(grad_gate, gate_ref[...]) + col_contract(grad_up, up_ref[...])

    @pl.when(step == pl.num_programs(0) - 1)
    def _():
        for p in range(count):
            part_out[:, p * size : (p + 1) * size] = acc_ref[:, moved[p]].astype(BF16)


def feed(scalars, count, parts, part, pieces, mat, grad_hidden, olds):
    span, ff = grad_hidden.shape
    piece, width = pieces[0].shape
    rows = 2 * piece
    tile = 512 if ff % 512 == 0 else ff
    steps = ff // tile
    narrow = width // count % 128
    owners = scalars[parts : parts + count]
    given = [columns(x, jnp.argsort(owners)) for x in pieces] if narrow else pieces
    held = pl.BlockSpec((piece, width), lambda j, s: (0, 0))
    columns_of = lambda shift: pl.BlockSpec((width, tile), lambda j, s: (0, shift + j))
    cols = pl.BlockSpec((rows, tile), lambda j, s: (part, j))
    first = olds is None
    olds = () if first else tuple(olds)
    wide = jax.ShapeDtypeStruct((span, ff), BF16)
    out = pl.pallas_call(
        functools.partial(feed_kernel, first, count, parts),
        out_shape=(
            wide,
            wide,
            wide,
            jax.ShapeDtypeStruct((span, width), BF16),
            jax.ShapeDtypeStruct((rows, width), BF16),
        ),
        grid_spec=pltpu.PrefetchScalarGridSpec(
            num_scalar_prefetch=1,
            grid=(steps,),
            in_specs=[held, held, columns_of(0), columns_of(steps), cols]
            + [pl.BlockSpec(memory_space=pl.ANY)] * len(olds),
            out_specs=(
                cols,
                cols,
                cols,
                pl.BlockSpec((rows, width), lambda j, s: (part, 0)),
                pl.BlockSpec((rows, width), lambda j, s: (0, 0)),
            ),
            scratch_shapes=[pltpu.VMEM((rows, width), BF16), pltpu.VMEM((rows, width), F32)],
        ),
        input_output_aliases={6 + i: i for i in range(len(olds))},
        compiler_params=params(),
        cost_estimate=cost(8 * rows * width * ff, 8 * width * ff, 2 * rows * ff),
        name="feed",
    )(scalars, *given, mat, mat, grad_hidden, *olds)
    return out[:4], columns(out[4], owners) if narrow else out[4]


def descend_kernel(parts, homes, value_ref, mat_ref, out_ref):
    total = col_contract(value_ref[...], mat_ref[...])
    rows = out_ref.shape[0] // parts
    for i in range(parts):
        at = pl.ds(pl.multiple_of(homes[i] * rows, rows), rows)
        out_ref[at, :] = total[i * rows : (i + 1) * rows].astype(BF16)


def descend(homes, owners, value, mat):
    rows, n = value.shape
    width, count, parts = mat.shape[0], owners.shape[0], homes.shape[0]
    narrow = width // count % 128
    steps = 4 if narrow else count
    out = pl.pallas_call(
        functools.partial(descend_kernel, parts),
        out_shape=jax.ShapeDtypeStruct((rows, width), BF16),
        grid_spec=pltpu.PrefetchScalarGridSpec(
            num_scalar_prefetch=1,
            grid=(steps,),
            in_specs=[
                pl.BlockSpec((rows, n), lambda j, s: (0, 0)),
                pl.BlockSpec((width // steps, n), lambda j, s: (s[parts + j], 0)),
            ],
            out_specs=pl.BlockSpec((rows, width // steps), lambda j, s: (0, j)),
        ),
        compiler_params=params(),
        cost_estimate=cost(2 * rows * width * n, 2 * (rows + width) * n + 2 * rows * width),
        name="descend",
    )(jnp.concatenate([homes, jnp.arange(4, dtype=jnp.int32) if narrow else owners]), value, mat)
    return columns(out, owners) if narrow else out


def plane_grads_kernel(counts, *refs):
    out_ref, start, at = refs[-1], 0, len(counts)
    for left, count in zip(refs, counts):
        rights = [r[...] for r in refs[at : at + count]]
        right = rights[0] if count == 1 else jnp.concatenate(rights, axis=1)
        size = right.shape[1]
        out_ref[:, start : start + size] = row_contract(left[...], right).astype(BF16)
        start, at = start + size, at + count


def plane_grads(name, terms, total, old=None):
    span, width = terms[0][0].shape
    tile = 256
    rights = [g for _, pair in terms for g in pair]
    cols = sum(g.shape[1] for g in rights)
    at = 0 if old is None else total // cols - 1
    left = pl.BlockSpec((span, tile), lambda j: (0, j))
    held = [pl.BlockSpec(g.shape, lambda j: (0, 0)) for g in rights]
    olds = () if old is None else (old,)
    return pl.pallas_call(
        functools.partial(plane_grads_kernel, tuple(len(pair) for _, pair in terms)),
        out_shape=jax.ShapeDtypeStruct((width, total), BF16),
        grid=(width // tile,),
        in_specs=[left] * len(terms) + held + [pl.BlockSpec(memory_space=pl.ANY)] * len(olds),
        out_specs=pl.BlockSpec((tile, cols), lambda j: (j, at)),
        input_output_aliases={len(terms) + len(rights): 0} if olds else {},
        compiler_params=params(),
        cost_estimate=cost(2 * span * width * cols, 2 * span * (2 * width + cols) + 2 * width * cols),
        name=name,
    )(*(a for a, _ in terms), *rights, *olds)


def enter_heads_kernel(heads, head_dim, paired, x_ref, near_ref, far_ref, cos_ref, sin_ref, gain_ref, p_out, r_out):
    mid = x_ref.shape[1] // 2
    proj = project(x_ref[:, :mid], near_ref[...]) + project(x_ref[:, mid:], far_ref[...])
    p_out[...] = proj
    for h in range(heads):
        unit, _ = unit_of(proj[:, h * head_dim : (h + 1) * head_dim])
        turned = turn(unit * gain_ref[...], cos_ref, sin_ref, 1.0).astype(BF16)
        at = (2 * h if paired else h) * head_dim
        r_out[:, at : at + head_dim] = turned
        if paired:
            value = proj[:, (heads + h) * head_dim : (heads + h + 1) * head_dim]
            r_out[:, at + head_dim : at + 2 * head_dim] = value.astype(BF16)


def enter_heads(name, heads, head_dim, paired, normed, mats, at, cols, cos, sin, gain):
    span, width = normed.shape
    rows = span // 2
    spec = lambda n: pl.BlockSpec((rows, n), lambda i: (i, 0))
    mat = pl.BlockSpec((width // 2, cols), lambda i: (0, at // cols))
    turned = heads * head_dim * (2 if paired else 1)
    return pl.pallas_call(
        functools.partial(enter_heads_kernel, heads, head_dim, paired),
        out_shape=(jax.ShapeDtypeStruct((span, cols), F32), jax.ShapeDtypeStruct((span, turned), BF16)),
        grid=(2,),
        in_specs=[spec(width), mat, mat, spec(head_dim), spec(head_dim), pl.BlockSpec((1, head_dim), lambda i: (0, 0))],
        out_specs=(spec(cols), spec(turned)),
        compiler_params=params(),
        cost_estimate=cost(2 * span * width * cols, 2 * width * (span + cols) + 6 * span * cols),
        name=name,
    )(normed, *mats, cos, sin, gain)


def unit_of(value):
    inverse = lax.rsqrt(jnp.mean(value * value, axis=-1, keepdims=True) + EPSILON)
    return value * inverse, inverse


def turn(value, cos_ref, sin_ref, sign):
    half = value.shape[-1] // 2
    return value * cos_ref[...] + sign * pltpu.roll(value, half, 1) * sin_ref[...]


def attend_kernel(group, head_dim, turns, first, scalars, q_ref, gate_ref, spot_ref, key_ref, oo_ref, of_ref, *refs):
    blocks = len(turns)
    kv_refs = refs[:blocks]
    rest = refs[blocks:] if first else refs[blocks + 1 :]
    mixed_out, sum_out, gated_out, part_out, acc_ref, total_ref, out_acc = rest
    scale = head_dim**-0.5 * math.log2(math.e)
    own = scalars[0]
    step, mid = pl.program_id(0), out_acc.shape[1] // 2

    @pl.when(step == 0)
    def _():
        out_acc[...] = jnp.zeros_like(out_acc)

    for h in range(group):
        cols = slice(h * head_dim, (h + 1) * head_dim)
        query = q_ref[:, cols]

        def scores(ref):
            return lax.dot_general(query, ref[:, :head_dim], CONTRACT_COLS, preferred_element_type=F32)

        allowed = (key_ref[...] <= spot_ref[...]) & (key_ref[...] < scalars[1])
        terms = jnp.where(allowed, jnp.exp2(scores(kv_refs[0]) * scale), 0.0)
        total_ref[...] = jnp.sum(terms, axis=-1, keepdims=True)
        acc_ref[...] = project(terms.astype(BF16), kv_refs[0][:, head_dim:])
        for place in range(1, blocks):

            @pl.when((own ^ turns[place]) < own)
            def _(ref=kv_refs[place]):
                terms = jnp.exp2(scores(ref) * scale)
                total_ref[...] += jnp.sum(terms, axis=-1, keepdims=True)
                acc_ref[...] += project(terms.astype(BF16), ref[:, head_dim:])

        mixed = acc_ref[...] / total_ref[...]
        mixed_out[:, cols] = mixed
        gated_out[:, cols] = (mixed * sigmoid(gate_ref[:, cols])).astype(BF16)
        sum_out[:, cols] = jnp.broadcast_to(total_ref[...], mixed.shape)
    gated = gated_out[...]
    out_acc[:, :mid] += col_contract(gated, oo_ref[...])
    out_acc[:, mid:] += col_contract(gated, of_ref[...])

    @pl.when(step == pl.num_programs(0) - 1)
    def _():
        part_out[...] = out_acc[...].astype(BF16)


def attend(scalars, part, parts, group, head_dim, turns, query, proj, gate_at, spots, keys, mats, out_at, kvs, old):
    span, width = query.shape
    rows, wide, mid = span // parts, group * head_dim, mats[0].shape[0]
    head = pl.BlockSpec((rows, wide), lambda g, s: (part, g))
    out = pl.BlockSpec((rows, wide), lambda g, s: (0, g))
    mat = pl.BlockSpec((mid, wide), lambda g, s: (0, out_at // wide + g))
    first = old is None
    olds = () if first else (old,)
    return pl.pallas_call(
        functools.partial(attend_kernel, group, head_dim, turns, first),
        out_shape=(
            jax.ShapeDtypeStruct((rows, width), F32),
            jax.ShapeDtypeStruct((rows, width), F32),
            jax.ShapeDtypeStruct((span, width), BF16),
            jax.ShapeDtypeStruct((rows, 2 * mid), BF16),
        ),
        grid_spec=pltpu.PrefetchScalarGridSpec(
            num_scalar_prefetch=1,
            grid=(width // wide,),
            in_specs=[
                head,
                pl.BlockSpec((rows, wide), lambda g, s: (part, gate_at // wide + g)),
                pl.BlockSpec((rows, 1), lambda g, s: (part, 0)),
                pl.BlockSpec((1, span), lambda g, s: (0, 0)),
                mat,
                mat,
            ]
            + [pl.BlockSpec((span, 2 * head_dim), lambda g, s: (0, g))] * len(kvs)
            + [pl.BlockSpec(memory_space=pl.ANY)] * len(olds),
            out_specs=(out, out, head, pl.BlockSpec((rows, 2 * mid), lambda g, s: (0, 0))),
            scratch_shapes=[
                pltpu.VMEM((rows, head_dim), F32),
                pltpu.VMEM((rows, 1), F32),
                pltpu.VMEM((rows, 2 * mid), F32),
            ],
        ),
        input_output_aliases={7 + len(kvs): 2} if olds else {},
        compiler_params=params(),
        cost_estimate=cost(
            4 * rows * width * span * len(kvs) + 4 * rows * width * mid,
            4 * span * width * len(kvs) + 20 * rows * width + 4 * mid * width,
            rows * span * len(kvs) * width // head_dim,
        ),
        name="attend",
    )(scalars, query, proj, spots, keys, *mats, *kvs, *olds)


def attend_back_kernel(group, head_dim, turns, first, count, scalars, *refs):
    blocks = len(turns)
    q_ref, query_ref, gate_ref, mixed_ref, sum_ref, a_ref, b_ref, oo_ref, of_ref = refs[:9]
    spot_ref, key_ref, cos_ref, sin_ref, gain_ref = refs[9:14]
    kv_refs = refs[14 : 14 + blocks]
    rest = refs[14 + blocks :]
    old_refs = () if first else rest[:blocks]
    rest = rest if first else rest[blocks + 3 :]
    gq_out, ggate_out, rows_out, gain_out = rest[:4]
    new_refs = rest[4 : 4 + blocks]
    gq_ref, x_ref = rest[4 + blocks :]
    mid = x_ref.shape[1] // 2

    @pl.when(pl.program_id(0) == 0)
    def _():
        piece = a_ref.shape[0]
        x_ref[:piece, :] = a_ref[...]
        x_ref[piece:, :] = b_ref[...]
        size = x_ref.shape[1] // count
        for p in range(count):
            rows_out[:, column_place(scalars, 2, p, size)] = x_ref[:, p * size : (p + 1) * size]

    all_gated = project(x_ref[:, :mid], oo_ref[...]) + project(x_ref[:, mid:], of_ref[...])
    score_scale = head_dim**-0.5
    scale = score_scale * math.log2(math.e)
    own = scalars[0]
    rows = q_ref.shape[0]

    def as_row(column):
        return jnp.transpose(jnp.broadcast_to(column, (rows, head_dim)))[:1, :]

    for place in range(blocks):
        if first:
            new_refs[place][...] = jnp.zeros_like(new_refs[place])
        else:
            new_refs[place][...] = old_refs[place][...]
    gain_total = jnp.zeros((1, head_dim), F32)
    for h in range(group):
        cols = slice(h * head_dim, (h + 1) * head_dim)
        query = q_ref[:, cols]
        gate = sigmoid(gate_ref[:, cols])
        grad_gated, mixed = all_gated[:, cols], mixed_ref[:, cols]
        grad_mixed = (grad_gated * gate).astype(BF16)
        ggate_out[:, cols] = (grad_gated * mixed * gate * (1.0 - gate)).astype(BF16)
        row_dot = as_row(jnp.sum(grad_mixed.astype(F32) * mixed, axis=-1, keepdims=True))
        row_log = as_row(jnp.log2(sum_ref[:, cols][:, :1]))
        gq_ref[...] = jnp.zeros_like(gq_ref)

        def block(kv_ref, new_ref, masked):
            key, value = kv_ref[:, :head_dim], kv_ref[:, head_dim:]
            scores = lax.dot_general(key, query, CONTRACT_COLS, preferred_element_type=F32)
            probs = jnp.exp2(scores * scale - row_log)
            if masked:
                allowed = (key_ref[...] <= spot_ref[...]) & (key_ref[...] < scalars[1])
                probs = jnp.where(allowed, probs, 0.0)
            grad_probs = lax.dot_general(value, grad_mixed, CONTRACT_COLS, preferred_element_type=F32)
            grad_scores = (probs * (grad_probs - row_dot)).astype(BF16)
            new_ref[:, head_dim:] += project(probs.astype(BF16), grad_mixed)
            new_ref[:, :head_dim] += project(grad_scores, query)
            gq_ref[...] += lax.dot_general(grad_scores, key, CONTRACT_ROWS, preferred_element_type=F32)

        block(kv_refs[0], new_refs[0], True)
        for place in range(1, blocks):

            @pl.when((own ^ turns[place]) < own)
            def _(place=place):
                block(kv_refs[place], new_refs[place], False)

        unit, inverse = unit_of(query_ref[:, cols])
        back = turn(gq_ref[...] * score_scale, cos_ref, sin_ref, -1.0)
        gain_total = gain_total + jnp.sum(back * unit, axis=0, keepdims=True)
        scaled = back * gain_ref[...]
        gq_out[:, cols] = (
            inverse * (scaled - unit * jnp.mean(scaled * unit, axis=-1, keepdims=True))
        ).astype(BF16)
    gain_out[...] = jnp.broadcast_to(gain_total, gain_out.shape)


def attend_back(
    scalars, count, part, parts, group, head_dim, turns, query, proj, gate_at, mixed, sums, pieces, mats, out_at, spots, keys, cos, sin, gain, kvs, olds
):
    span, width = query.shape
    rows, wide = span // parts, group * head_dim
    blocks, mid = len(kvs), mats[0].shape[0]
    mine = pl.BlockSpec((rows, wide), lambda g, s: (part, g))
    local = pl.BlockSpec((rows, wide), lambda g, s: (0, g))
    table = pl.BlockSpec((rows, head_dim), lambda g, s: (part, 0))
    pair = pl.BlockSpec((span, 2 * head_dim), lambda g, s: (0, g))
    piece = pl.BlockSpec(pieces[0].shape, lambda g, s: (0, 0))
    mat = pl.BlockSpec((mid, wide), lambda g, s: (0, out_at // wide + g))
    first = olds is None
    olds = () if first else tuple(olds)
    kv_shape = jax.ShapeDtypeStruct(kvs[0].shape, F32)
    steps = width // wide
    before = 15 + blocks
    out = pl.pallas_call(
        functools.partial(attend_back_kernel, group, head_dim, turns, first, count),
        out_shape=(
            jax.ShapeDtypeStruct((span, width), BF16),
            jax.ShapeDtypeStruct((span, width), BF16),
            jax.ShapeDtypeStruct((span, 2 * mid), BF16),
            jax.ShapeDtypeStruct((8 * steps, head_dim), F32),
        )
        + (kv_shape,) * blocks,
        grid_spec=pltpu.PrefetchScalarGridSpec(
            num_scalar_prefetch=1,
            grid=(steps,),
            in_specs=[
                mine,
                mine,
                pl.BlockSpec((rows, wide), lambda g, s: (part, gate_at // wide + g)),
                local,
                local,
                piece,
                piece,
                mat,
                mat,
                pl.BlockSpec((1, rows), lambda g, s: (0, part)),
                pl.BlockSpec((span, 1), lambda g, s: (0, 0)),
                table,
                table,
                pl.BlockSpec((1, head_dim), lambda g, s: (0, 0)),
            ]
            + [pair] * (blocks + min(len(olds), blocks))
            + [pl.BlockSpec(memory_space=pl.ANY)] * max(len(olds) - blocks, 0),
            out_specs=(
                mine,
                mine,
                pl.BlockSpec((rows, 2 * mid), lambda g, s: (part, 0)),
                pl.BlockSpec((8, head_dim), lambda g, s: (g, 0)),
            )
            + (pair,) * blocks,
            scratch_shapes=[pltpu.VMEM((rows, head_dim), F32), pltpu.VMEM((rows, 2 * mid), BF16)],
        ),
        input_output_aliases={}
        if first
        else {**{before + i: 4 + i for i in range(blocks)}, **{before + blocks + i: i for i in range(3)}},
        compiler_params=params(),
        cost_estimate=cost(
            10 * rows * width * span * blocks + 4 * rows * width * mid,
            20 * span * width * blocks,
            rows * span * blocks * width // head_dim,
        ),
        name="attend_back",
    )(scalars, query, proj, proj, mixed, sums, *pieces, *mats, spots, keys, cos, sin, gain, *kvs, *olds)
    gain_part = sum(out[3][8 * g] for g in range(steps))
    return out[4:], out[:3], gain_part


def keys_back_kernel(kv_heads, head_dim, g_ref, p_ref, cos_ref, sin_ref, gain_ref, k_out, v_out, gain_out):
    gain_total = jnp.zeros((1, head_dim), F32)
    for h in range(kv_heads):
        cols = slice(h * head_dim, (h + 1) * head_dim)
        unit, inverse = unit_of(p_ref[:, cols])
        grad = g_ref[:, 2 * h * head_dim : (2 * h + 1) * head_dim] * head_dim**-0.5
        back = turn(grad, cos_ref, sin_ref, -1.0)
        gain_total = gain_total + jnp.sum(back * unit, axis=0, keepdims=True)
        scaled = back * gain_ref[...]
        k_out[:, cols] = (
            inverse * (scaled - unit * jnp.mean(scaled * unit, axis=-1, keepdims=True))
        ).astype(BF16)
        v_out[:, cols] = g_ref[:, (2 * h + 1) * head_dim : (2 * h + 2) * head_dim].astype(BF16)
    gain_out[...] = jnp.broadcast_to(gain_total, gain_out.shape)


def keys_back(kv_heads, head_dim, grad_kv, proj, key_at, cos, sin, gain):
    span = proj.shape[0]
    cols = kv_heads * head_dim
    key_block = key_at // cols
    whole = lambda a, b: pl.BlockSpec((a, b), lambda i: (0, 0))
    out = pl.pallas_call(
        functools.partial(keys_back_kernel, kv_heads, head_dim),
        out_shape=(
            jax.ShapeDtypeStruct((span, cols), BF16),
            jax.ShapeDtypeStruct((span, cols), BF16),
            jax.ShapeDtypeStruct((8, head_dim), F32),
        ),
        grid=(1,),
        in_specs=[
            whole(span, 2 * cols),
            pl.BlockSpec((span, cols), lambda i: (0, key_block)),
            whole(span, head_dim),
            whole(span, head_dim),
            whole(1, head_dim),
        ],
        out_specs=(whole(span, cols), whole(span, cols), whole(8, head_dim)),
        compiler_params=params(),
        cost_estimate=cost(40 * span * cols, 16 * span * cols),
        name="keys_back",
    )(grad_kv, proj, cos, sin, gain)
    return out[0], out[1], out[2][0]


def norm_back(gradient, unit_vals, inverse, gain_vec):
    scaled = gradient * gain_vec
    return inverse * (scaled - unit_vals * jnp.mean(scaled * unit_vals, axis=-1, keepdims=True))


def per_device(
    links,
    hidden_in,
    lengths,
    attn_gain,
    q_weight,
    gate_weight,
    k_weight,
    v_weight,
    q_gain,
    k_gain,
    o_weight,
    mlp_gain,
    w_gate,
    w_up,
    w_down,
    out_grad,
):
    dp_index, ctx_index, z_index = (lax.axis_index(a) for a in ("dp", "ctx", "tensor"))
    q_cols, k_cols, ff_cols = q_weight.shape[1], k_weight.shape[1], w_down.shape[1]
    span, width = hidden_in.shape
    mid, count = width // 2, 2 * links.half
    shard, head_shard = attn_gain.shape[0], q_gain.shape[0]
    head_dim = head_shard * count
    heads, kv_heads = q_cols // head_dim, k_cols // head_dim
    group = heads // kv_heads
    length = lengths[0]
    low = lambda *mats: jnp.concatenate([m.astype(BF16) for m in mats], axis=1)

    small = jnp.concatenate([attn_gain, mlp_gain, q_gain, k_gain]).astype(BF16)[None, :]
    gains, seen = links.small_gather(small)
    everywhere = lambda block: {p: block for p in range(len(links.bits))}
    paired = lambda half: (half, links.swap(half, "ctx", 1))
    plane = ("dp", "ctx")
    first_own = after(low(q_weight, gate_weight, k_weight, v_weight, o_weight), *seen)
    first_single = links.send_own(everywhere(first_own))
    attn_scale = gains[:, :shard].reshape(1, width).astype(F32)
    mlp_scale = gains[:, shard : 2 * shard].reshape(1, width).astype(F32)
    owners = jnp.stack([links.owner_of(p, dp_index, ctx_index) for p in range(count)]).astype(jnp.int32)
    pick = (owners[None, :] == jnp.arange(count)[:, None]).astype(BF16)
    mesh_gains = project(pick, gains)
    mesh_scale = mesh_gains[:, :shard].reshape(1, width)
    query_scale = mesh_gains[:, 2 * shard : 2 * shard + head_shard].reshape(1, head_dim)
    key_scale = mesh_gains[:, 2 * shard + head_shard :].reshape(1, head_dim)

    parts = 2 * links.tensor
    row_block = span // parts
    row_places = jnp.stack(
        [part * links.tensor + (z_index ^ j) for part in range(2) for j in links.turns]
    ).astype(jnp.int32)
    start = ctx_index * span
    scalars = jnp.concatenate(
        [row_places, owners.astype(jnp.int32), jnp.stack([start, length]).astype(jnp.int32)]
    )
    spots = (start + row_places[:, None] * row_block + jnp.arange(row_block)[None, :]).reshape(span)
    spots = spots.astype(jnp.int32)
    freq_steps = jnp.arange(head_dim // 2, dtype=F32) * (2.0 / head_dim)
    turned = spots.astype(F32)[:, None] * jnp.exp(-math.log(ROPE_BASE) * freq_steps)[None, :]
    cosine, sine = jnp.cos(turned), jnp.sin(turned)
    cos = jnp.concatenate([cosine, cosine], axis=1)
    sin = jnp.concatenate([-sine, sine], axis=1)
    spot_col, spot_row = spots[:, None], spots[None, :]

    stream, grad_out, plain_down, down_grad, plain_normed, normed = enter(
        scalars, count, parts, span, hidden_in, out_grad, after(mesh_scale, first_own)
    )
    feed_low, down_low = low(w_gate, w_up), low(w_down)
    first_single = {q: after(b, normed, feed_low, down_low) for q, b in first_single.items()}
    feed_mat = lax.all_gather(after(feed_low, normed), plane, axis=0, tiled=True)

    first_pairs = links.send_on(first_single)
    first_seen = [b for pair in first_pairs.values() for b in pair]
    down_mat = lax.all_gather(after(down_low, *first_seen), plane, axis=0, tiled=True)
    first_mat = paired(links.assemble(first_own, first_single, first_pairs))
    gate_at, key_at = q_cols, 2 * q_cols
    value_at, out_at = key_at + k_cols, key_at + 2 * k_cols
    kv_proj, kv = enter_heads(
        "enter_keys", kv_heads, head_dim, True, normed, first_mat, key_at, 2 * k_cols, cos, sin, key_scale
    )
    proj, query = enter_heads(
        "enter_queries", heads, head_dim, False, after(normed, kv), first_mat, 0, 2 * q_cols, cos, sin, query_scale
    )
    kvs, turns = [kv], [0]
    mask = links.ctx // 2
    while mask:
        kvs = kvs + [links.swap(b if i == 0 else after(b, query), "ctx", mask) for i, b in enumerate(kvs)]
        turns = turns + [p ^ mask for p in turns]
        mask //= 2
    at = jnp.concatenate([jnp.stack([ctx_index, length]).astype(jnp.int32), owners])
    half_rows = span // 2
    shard_rows = half_rows // links.tensor
    part_of = lambda value, t: value[t * half_rows : (t + 1) * half_rows]
    own_rows = lambda value, t: value[t * shard_rows : (t + 1) * shard_rows]
    live = [(part_of(spot_col, t)[:shard_rows] < length).astype(F32) for t in range(2)]
    mixed, sums, out_part, one = ([None] * 2 for _ in range(4))
    query_now, gated_all = query, None
    for t in range(2):
        mixed[t], sums[t], gated_all, out_part[t] = attend(
            at, t, 2, group, head_dim, turns, query_now, proj, gate_at, spot_col, spot_row, first_mat, out_at, kvs, gated_all
        )
        one[t] = links.scatter_first(out_part[t])
    middle, normed_two, unit_two, inverse_two, two = ([None] * 2 for _ in range(5))
    late = (one[1][1],)
    for t in range(2):
        attn_out, _ = links.scatter_rest(*one[t], late=late)
        middle[t] = own_rows(stream, t).astype(F32) + attn_out * live[t]
        inverse_two[t] = lax.rsqrt(jnp.mean(middle[t] * middle[t], axis=-1, keepdims=True) + EPSILON)
        unit_two[t] = middle[t] * inverse_two[t]
        normed_two[t] = (unit_two[t] * mlp_scale).astype(BF16)
        two[t] = links.gather_first(normed_two[t])
        late = (normed_two[t],)
    pieces_two = [links.gather_rest(*two[0], late=late)]
    pieces_two.append(links.gather_rest(*two[1], late=(pieces_two[0][0],)))

    grad_hidden = project(after(plain_down, one[1][1]), down_mat)
    back_part, three = [None] * 2, [None] * 2
    held = None
    for t in range(2):
        held, back_part[t] = feed(scalars, count, parts, t, pieces_two[t], feed_mat, grad_hidden, held)
        three[t] = links.scatter_first(back_part[t])
    hidden_all, grad_gate_all, grad_up_all, rows_two = held

    halves = lambda value: (value[:, : value.shape[1] // 2], value[:, value.shape[1] // 2 :])

    def grad_others(rows_of, cols, *before):
        left = after(rows_of[:, mid:], *before)
        parts = [row_contract(left, c).astype(BF16) for c in cols]
        return parts, [links.swap(p, "ctx", 1) for p in parts]

    def grad_totals(rows_of, cols, arrived, *before):
        left = after(rows_of[:, :mid], *before)
        return [(row_contract(left, c) + a.astype(F32)).astype(BF16) for c, a in zip(cols, arrived)]

    def grad_rest(firsts, *before):
        return [
            links.reduce_rest(kept, after(came, *before), turn) for turn, (kept, _, came) in enumerate(firsts)
        ]

    scaled_back = lambda back, t: own_rows(grad_out, t).astype(F32) + norm_back(
        back, unit_two[t], inverse_two[t], mlp_scale
    )
    grad_middle, attn_grad, four = ([None] * 2 for _ in range(3))
    back_a, seen_a = links.scatter_rest(*three[0], before=(hidden_all,))
    back_b, seen_b = links.scatter_rest(*three[1])
    feed_cols = [grad_gate_all, grad_up_all]
    over_plane = lambda part: lax.psum_scatter(part, plane, scatter_dimension=0, tiled=True).astype(F32)
    down_grad_part = row_contract(after(plain_down, three[0][1]), hidden_all).astype(BF16)
    grad_down = over_plane(down_grad_part)
    feed_others, feed_came = grad_others(rows_two, feed_cols, down_grad_part)
    homes = jnp.stack([(z_index ^ j) * 2 + part for part in range(2) for j in links.turns]).astype(jnp.int32)
    down_part = descend(homes, owners, after(hidden_all, *feed_others, three[1][1]), down_mat)
    for t, back in enumerate((back_a, back_b)):
        back = after(back, *((down_part,) if t == 0 else (attn_grad[0],)))
        grad_middle[t] = scaled_back(back, t)
        attn_grad[t] = (grad_middle[t] * live[t]).astype(BF16)
        four[t] = links.gather_first(attn_grad[t])
    grad_mlp_gain = sum(jnp.sum(b * unit_two[t], axis=0) for t, b in enumerate((back_a, back_b)))
    attn_shard = attn_grad[1]
    pieces_four = [links.gather_rest(*four[0], late=(attn_shard,))]
    pieces_four.append(links.gather_rest(*four[1]))
    down_sum = lax.psum_scatter(after(down_part, grad_down, pieces_four[0][1], pieces_four[1][0]), "tensor", scatter_dimension=0, tiled=True).astype(F32)
    backward = lambda t, pieces, olds: attend_back(
        at, count, t, 2, group, head_dim, turns, query, proj, gate_at, mixed[t], sums[t], pieces, first_mat, out_at,
        spot_row, spot_col, cos, sin, query_scale, kvs, olds,
    )
    feed_totals = grad_totals(rows_two, feed_cols, feed_came, pieces_four[0][1])
    ready = after(pieces_four[0][1], pieces_four[1][0], grad_down, *feed_totals)
    grad_kvs, held, gain_a = backward(0, (pieces_four[0][0], ready), None)
    back_places = jnp.array(
        [part * links.tensor + o for o in range(links.tensor) for part in range(2)], dtype=jnp.int32
    )
    last = pieces_four[1]
    grad_kvs, held, gain_b = backward(1, last, (*grad_kvs, *held))
    grad_query, grad_gates, attn_all = held
    down_sum = after(down_sum, grad_kvs[0])
    down_shard = jnp.concatenate(middle, axis=0) + down_sum * jnp.concatenate(live, axis=0)
    down_all = lax.all_gather(down_shard.astype(BF16), "tensor", axis=0, tiled=True)
    if width // count % 128:
        attn_all = columns(attn_all, jnp.argsort(owners))
    q_gain_part = gain_a + gain_b
    pieces = dict(zip(turns, grad_kvs))
    mask = 1
    kv_gone, kv_seen = [], []
    while len(pieces) > 1:
        near = [p for p in pieces if not p & mask]
        gone = [pieces[p ^ mask].astype(BF16) for p in near]
        came = links.swap(jnp.concatenate(gone, axis=0), "ctx", mask)
        kv_gone.append(gone)
        kv_seen.append(came)
        pieces = {
            p: pieces[p].astype(F32) + came[i * span : (i + 1) * span].astype(F32) for i, p in enumerate(near)
        }
        mask *= 2
    outer_part = plane_grads(
        "outer_grads", [(after(plain_normed, *kv_gone[-1]), (grad_query, grad_gates)), (attn_all, (gated_all,))],
        3 * q_cols + 2 * k_cols,
    )
    grad_key, grad_value, k_gain_part = keys_back(
        kv_heads, head_dim, after(pieces[0], outer_part, down_shard), kv_proj, 0, cos, sin, key_scale
    )
    feed_first = [links.reduce_first(x, turn, *((grad_key,) if turn else ())) for turn, x in enumerate(feed_totals)]
    seven, eight, in_part, grad_in, attn_gain_part = ([None] * 2 for _ in range(5))
    late_query = grad_query
    for t in range(2):
        terms = [
            (late_query, first_mat, 0),
            (grad_gates, first_mat, gate_at),
            (grad_key, first_mat, key_at),
            (grad_value, first_mat, value_at),
        ]
        in_part[t], gain = spread("spread_in", terms, t, 2, normed=normed)
        attn_gain_part[t] = gain[0] / attn_scale[0]
        seven[t] = links.scatter_first(in_part[t] if t == 0 else after(in_part[1], seven[0][1]))
    inner_part = plane_grads(
        "inner_grads", [(after(plain_normed, attn_gain_part[1]), (grad_key, grad_value))], 3 * q_cols + 2 * k_cols, outer_part
    )
    inner_sum = over_plane(inner_part)
    summed = [links.scatter_rest(*seven[t]) for t in range(2)]
    late = ()
    for t in range(2):
        back = after(summed[t][0], *late)
        x = own_rows(stream, t).astype(F32)
        inverse = lax.rsqrt(jnp.mean(x * x, axis=-1, keepdims=True) + EPSILON)
        unit = x * inverse
        grad_in[t] = (grad_middle[t] + norm_back(back, unit, inverse, attn_scale)).astype(BF16)
        eight[t] = links.gather_first(grad_in[t])
        late = (grad_in[t],)
    feed_rest = grad_rest(feed_first, grad_in[0])
    hidden_out = leave(jnp.concatenate([back_places, scalars[parts:]]), count, parts, [after(down_all, in_part[1])], BF16)
    in_pieces = [*links.gather_rest(*eight[0], late=late)]
    in_pieces += links.gather_rest(*eight[1], late=(in_pieces[0],))
    attn_gain_part = sum(attn_gain_part)
    arrived_one = in_pieces[1]
    in_pieces[1] = after(in_pieces[1], hidden_out, inner_sum, *(r[0] for r in feed_rest))
    grad_in = leave(scalars, count, parts, in_pieces, F32)

    blocks = jnp.stack([attn_gain_part.reshape(count, shard), grad_mlp_gain.reshape(count, shard)])
    to_mesh = (owners[None, :] == jnp.arange(count)[:, None]).astype(F32)
    blocks = jnp.einsum("ap,kpn->kan", to_mesh, blocks, precision=lax.Precision.HIGHEST)
    packed = jnp.concatenate([blocks.reshape(1, -1), q_gain_part[None, :], k_gain_part[None, :]], axis=1)
    packed = links.add_all(packed, arrived_one, hidden_out, *(r[2] for r in feed_rest))[0]
    rank = dp_index * links.ctx + ctx_index
    take = lambda at, size: lax.dynamic_slice_in_dim(packed, at + rank * size, size)
    return (
        hidden_out,
        grad_in,
        take(0, shard),
        inner_sum[:, :q_cols],
        inner_sum[:, q_cols : 2 * q_cols],
        inner_sum[:, 3 * q_cols : 3 * q_cols + k_cols],
        inner_sum[:, 3 * q_cols + k_cols :],
        take(2 * width, head_shard),
        take(2 * width + head_dim, head_shard),
        inner_sum[:, 2 * q_cols : 3 * q_cols],
        take(width, shard),
        feed_rest[0][0],
        feed_rest[1][0],
        grad_down,
    )


def solution(mesh):
    links = Links(dict(mesh.shape))
    rows = P(("dp", "ctx"))
    plain = P(("dp", "ctx"), None)
    split = P(("dp", "ctx"), "tensor")

    def step(*arrays):
        return per_device(links, *arrays)

    return jax.shard_map(
        step,
        mesh=mesh,
        in_specs=(plain, P("dp"), rows, split, split, split, split, rows, rows, split, rows, split, split, split, plain),
        out_specs=(plain, plain, rows, split, split, split, split, rows, rows, split, rows, split, split, split),
        check_vma=False,
    )
```
